32 devices in a mesh: batch: 8 (over z, x), head: 4 (over y, core).
Axes of the slice: x: 2, y: 2, z: 4, core: 2. Of those that a mesh axis runs over, the one named last changes fastest.
Arguments:
- tokens: bfloat16 [16384, 768], P(('batch', 'head')), may hold values from -6 to 6
- cotangent: bfloat16 [16384, 768], P(('batch', 'head')), may hold values from -6 to 6
- lengths: int32 [8, 3], P('batch'), may hold values from 1 to 1024, 2048 in all within a row
- input_weight: float32 [2304, 768], P(('batch', 'head')), may hold values from -0.21875 to 0.21875
- output_weight: float32 [768, 768], P(('batch', 'head')), may hold values from -0.875 to 0.875
- expand_weight: float32 [3072, 768], P(('batch', 'head')), may hold values from -0.21875 to 0.21875
- contract_weight: float32 [768, 3072], P(('batch', 'head')), may hold values from -0.109375 to 0.109375
- vector_params: float32 [9216], replicated, may hold values from -0.8 to 1.6, as said below
- input_first: float32 [2304, 768], P(('batch', 'head')), may hold values from -0.005859375 to 0.005859375
- input_second: float32 [2304, 768], P(('batch', 'head')), may hold values from 1.4128508e-07 to 5.6514034e-07
- output_first: float32 [768, 768], P(('batch', 'head')), may hold values from -0.005859375 to 0.005859375
- output_second: float32 [768, 768], P(('batch', 'head')), may hold values from 1.4128508e-07 to 5.6514034e-07
- expand_first: float32 [3072, 768], P(('batch', 'head')), may hold values from -0.005859375 to 0.005859375
- expand_second: float32 [3072, 768], P(('batch', 'head')), may hold values from 1.4128508e-07 to 5.6514034e-07
- contract_first: float32 [768, 3072], P(('batch', 'head')), may hold values from -0.005859375 to 0.005859375
- contract_second: float32 [768, 3072], P(('batch', 'head')), may hold values from 1.4128508e-07 to 5.6514034e-07
- vector_first: float32 [9216], replicated, may hold values from -0.0234375 to 0.0234375
- vector_second: float32 [9216], replicated, may hold values from 2.2605614e-06 to 9.042245e-06
Outputs:
- block_out: bfloat16 [16384, 768], P(('batch', 'head'))
- input_grad: bfloat16 [16384, 768], P(('batch', 'head'))
- grad_norm: float32 [], replicated
- matrix_norms: float32 [8], replicated
- input_first_new: float32 [2304, 768], P(('batch', 'head'))
- input_second_new: float32 [2304, 768], P(('batch', 'head'))
- input_weight_new: float32 [2304, 768], P(('batch', 'head'))
- input_weight_low: bfloat16 [2304, 768], P(('batch', 'head'))
- output_first_new: float32 [768, 768], P(('batch', 'head'))
- output_second_new: float32 [768, 768], P(('batch', 'head'))
- output_weight_new: float32 [768, 768], P(('batch', 'head'))
- output_weight_low: bfloat16 [768, 768], P(('batch', 'head'))
- expand_first_new: float32 [3072, 768], P(('batch', 'head'))
- expand_second_new: float32 [3072, 768], P(('batch', 'head'))
- expand_weight_new: float32 [3072, 768], P(('batch', 'head'))
- expand_weight_low: bfloat16 [3072, 768], P(('batch', 'head'))
- contract_first_new: float32 [768, 3072], P(('batch', 'head'))
- contract_second_new: float32 [768, 3072], P(('batch', 'head'))
- contract_weight_new: float32 [768, 3072], P(('batch', 'head'))
- contract_weight_low: bfloat16 [768, 3072], P(('batch', 'head'))
- vector_first_new: float32 [9216], replicated
- vector_second_new: float32 [9216], replicated
- vector_params_new: float32 [9216], replicated
The draws below stay inside these ranges and needn't reach their ends.
Inputs may be any that keep to these rules, and one draw needn't show every extreme that they name: Each row holds 3 lengths summing to 2048; the longest in every row is exactly half of 2048. `vector_params`: entries 0 to 767 and 1536 to 2303 are norm gains near 1; the rest are shifts and biases.
All inputs are finite; a program needn't handle non-finite values.
Results may differ from the reference program's by a relative error of at most 0.012.
Values may be sent and summed in bfloat16 or wider, within the bound.
No kernel may reach another device: no remote copies, remote signals or barrier semaphores. Data moves between devices by JAX's collectives and lax.ppermute only.
A program may use at most 192 MiB of HBM per device.

```python
import math
import jax
import jax.numpy as jnp
import numpy as np
from jax import lax

D = 768
H = 12
HD = 64
FF = 3072
GROUP_TOK = 2048
DOCS = 3
STEP = 5
TOKENS = 16384
N_BATCH = 8


def draw_vector_params(key, part):
    noise = jnp.clip(jax.random.normal(key, (8 * D + FF,), jnp.float32), -4.0, 4.0)
    positions = jnp.arange(8 * D + FF)
    is_gain = (positions < D) | (positions >= 2 * D) & (positions < 3 * D)
    return jnp.where(is_gain, 1.0 + 0.15 * noise, 0.2 * noise)


def block_scale(own_key, extent, shards, smallest, largest):
    def one(dim, parts):
        heights = jax.random.uniform(jax.random.fold_in(jax.random.fold_in(own_key, 6), dim), (parts,), jnp.float32, smallest / len(shards), largest / len(shards))
        return jnp.repeat(jnp.exp(heights), extent[dim] // parts).reshape((-1,) + (1,) * (len(extent) - dim - 1))

    loudness = one(*shards[0])
    for cut in shards[1:]:
        loudness = loudness * one(*cut)
    return loudness


def length_profile(number_of, total, reach, slope):
    loads = [(1 << 20) // math.isqrt(standing ** slope) + 1 for standing in range(2, number_of + 1)]
    surplus, given = total - reach - (number_of - 1), [1] * (number_of - 1)
    while surplus > 0:
        movable = [i for i in range(number_of - 1) if given[i] < reach]
        mass, budget = sum([loads[i] for i in movable]), surplus
        for i in movable:
            addition = min(reach - given[i], max(1, budget * loads[i] // mass), surplus)
            given[i] = given[i] + addition
            surplus = surplus - addition
    return np.array([reach] + given)


def uneven_parts(own_key, number_of, total, limit, skew):
    if number_of == 2:
        one = jax.random.randint(own_key, (), max(1, total - limit), min(limit, total - 1) + 1)
        return jnp.stack([one, total - one])
    sizes = jnp.asarray(length_profile(number_of, total, limit, skew), jnp.int32)
    pairs = (number_of - 1) // 2
    donor, taker = sizes[1:1 + 2 * pairs:2], sizes[2:2 + 2 * pairs:2]
    room = jnp.minimum(donor - 1, limit - taker)
    passed = jax.random.randint(jax.random.fold_in(own_key, 1), (pairs,), 0, 1 << 20) % (room + 1)
    sizes = sizes.at[1:1 + 2 * pairs:2].set(donor - passed).at[2:2 + 2 * pairs:2].set(taker + passed)
    return sizes[jax.random.permutation(jax.random.fold_in(own_key, 2), number_of)]


def normal_values(rng, shape, scale, limit, cuts=(), held_as=jnp.bfloat16):
    level = block_scale(rng, shape, cuts, -0.22, 0.18) if cuts else 1.0
    entries = jax.random.normal(rng, shape, jnp.float32) * scale * level
    return jnp.minimum(jnp.maximum(entries, -limit), limit).astype(held_as)


def setup_inputs(seed: int = 0) -> dict:
    arg_keys = jax.random.split(jax.random.key(seed), 19)
    tokens = normal_values(arg_keys[0], (TOKENS, D), 1.0, 6.0, ((0, 32),))
    cotangent = normal_values(arg_keys[1], (TOKENS, D), 1.0, 6.0, ((0, 32),))
    lengths = jax.vmap(lambda own: uneven_parts(own, DOCS, GROUP_TOK, GROUP_TOK // 2, 0))(jax.random.split(arg_keys[2], N_BATCH)).reshape((N_BATCH, DOCS)).astype(jnp.int32)
    input_weight = normal_values(arg_keys[3], (3 * D, D), D ** -0.5, 0.21875, ((0, 32),), jnp.float32)
    output_weight = normal_values(arg_keys[4], (D, D), (D // 16) ** -0.5, 0.875, ((0, 32),), jnp.float32)
    expand_weight = normal_values(arg_keys[5], (FF, D), D ** -0.5, 0.21875, ((0, 32),), jnp.float32)
    contract_weight = normal_values(arg_keys[6], (D, FF), FF ** -0.5, 0.109375, ((0, 32),), jnp.float32)
    vector_params = draw_vector_params(jax.random.fold_in(arg_keys[18], 71), 0)
    input_first = normal_values(arg_keys[8], (3 * D, D), ((4 * D * D + 2 * FF * D) ** -0.5), 0.005859375, ((0, 32),), jnp.float32)
    input_second = jnp.clip(jnp.exp(math.log(5.651403398587718e-07) - 1.3862944 * jax.random.uniform(arg_keys[9], (3 * D, D), jnp.float32) ** block_scale(arg_keys[9], (3 * D, D), ((0, 32),), -0.2, 0.2)), 1.4128508496469294e-07, 5.651403398587718e-07)
    output_first = normal_values(arg_keys[10], (D, D), ((4 * D * D + 2 * FF * D) ** -0.5), 0.005859375, ((0, 32),), jnp.float32)
    output_second = jnp.clip(jnp.exp(math.log(5.651403398587718e-07) - 1.3862944 * jax.random.uniform(arg_keys[11], (D, D), jnp.float32) ** block_scale(arg_keys[11], (D, D), ((0, 32),), -0.2, 0.2)), 1.4128508496469294e-07, 5.651403398587718e-07)
    expand_first = normal_values(arg_keys[12], (FF, D), ((4 * D * D + 2 * FF * D) ** -0.5), 0.005859375, ((0, 32),), jnp.float32)
    expand_second = jnp.clip(jnp.exp(math.log(5.651403398587718e-07) - 1.3862944 * jax.random.uniform(arg_keys[13], (FF, D), jnp.float32) ** block_scale(arg_keys[13], (FF, D), ((0, 32),), -0.2, 0.2)), 1.4128508496469294e-07, 5.651403398587718e-07)
    contract_first = normal_values(arg_keys[14], (D, FF), ((4 * D * D + 2 * FF * D) ** -0.5), 0.005859375, ((0, 32),), jnp.float32)
    contract_second = jnp.clip(jnp.exp(math.log(5.651403398587718e-07) - 1.3862944 * jax.random.uniform(arg_keys[15], (D, FF), jnp.float32) ** block_scale(arg_keys[15], (D, FF), ((0, 32),), -0.2, 0.2)), 1.4128508496469294e-07, 5.651403398587718e-07)
    vector_first = normal_values(arg_keys[16], (8 * D + FF,), (4 * (4 * D * D + 2 * FF * D) ** -0.5), 0.0234375, (), jnp.float32)
    vector_second = jnp.clip(jnp.exp(jax.random.uniform(arg_keys[17], (8 * D + FF,), jnp.float32, math.log(2.260561359435087e-06), math.log(9.042245437740348e-06))), 2.260561359435087e-06, 9.042245437740348e-06)
    return {"tokens": tokens, "cotangent": cotangent, "lengths": lengths, "input_weight": input_weight, "output_weight": output_weight, "expand_weight": expand_weight, "contract_weight": contract_weight, "vector_params": vector_params, "input_first": input_first, "input_second": input_second, "output_first": output_first, "output_second": output_second, "expand_first": expand_first, "expand_second": expand_second, "contract_first": contract_first, "contract_second": contract_second, "vector_first": vector_first, "vector_second": vector_second}


@jax.custom_vjp
def low(v):
    return lax.optimization_barrier(v.astype(jnp.bfloat16)).astype(jnp.float32)

@jax.custom_vjp
def low_back(v):
    return v

def low_keep(v):
    return (low(v), None)

def low_pass(kept, grad):
    return (grad,)

def back_keep(v):
    return (v, None)

def back_low(kept, grad):
    return (low(grad),)
low.defvjp(low_keep, low_pass)
low_back.defvjp(back_keep, back_low)
HIGHEST = lax.Precision.HIGHEST
NORM_EPS = 1e-05
ADAM_EPS = 1e-06
DECAY_RATE = 0.01
MATRIX_RATE = 0.5
VECTOR_RATE = 0.1

def layer_norm(values, gain_vec, bias_vec):
    row_mean = lax.optimization_barrier(jnp.mean(values, axis=-1, keepdims=True))
    centered = values - row_mean
    variance = lax.optimization_barrier(jnp.mean(centered * centered, axis=-1, keepdims=True))
    return centered * lax.rsqrt(variance + NORM_EPS) * gain_vec + bias_vec

def unpack_vector(params):
    pieces = [params[position * D:(position + 1) * D] for position in range(8)]
    return pieces + [params[8 * D:8 * D + FF]]

def segment_ids(length_row):
    doc_ends = jnp.cumsum(length_row).astype(jnp.int32)
    positions = jnp.arange(GROUP_TOK, dtype=jnp.int32)
    return lax.optimization_barrier(jnp.sum((positions[:, None] >= doc_ends[None, :]).astype(jnp.int32), axis=1)).astype(jnp.int32)

def attend_block(query_block, offset, key_rows, value_rows, segment, block_rows):
    scores = jnp.einsum('qhd,khd->hqk', query_block, key_rows, precision=HIGHEST) * HD ** (-0.5)
    scores = low_back(scores)
    query_pos = offset + jnp.arange(block_rows, dtype=jnp.int32)
    key_pos = jnp.arange(GROUP_TOK, dtype=jnp.int32)
    query_seg = lax.dynamic_slice_in_dim(segment, offset, block_rows, 0)
    allowed = (key_pos[None, :] <= query_pos[:, None]) & (query_seg[:, None] == segment[None, :])
    scores = jnp.where(allowed[None], scores, -1e+30)
    row_max = lax.optimization_barrier(jnp.max(scores, axis=-1, keepdims=True))
    exponent = jnp.exp(scores - row_max)
    soft_weights = low(exponent / lax.optimization_barrier(jnp.sum(exponent, axis=-1, keepdims=True)))
    return jnp.einsum('hqk,khd->qhd', soft_weights, value_rows, precision=HIGHEST)

def group_forward(group_in, segment, stacked_input, used_output, used_expand, used_contract, params):
    gain_one, bias_one, gain_two, bias_two, bias_query, bias_value, bias_output, bias_contract, bias_expand = unpack_vector(params)
    normed_one = low(layer_norm(group_in, gain_one, bias_one))
    projected = jnp.einsum('td,cod->cto', normed_one, stacked_input, precision=HIGHEST)
    projected = projected + jnp.stack([bias_query, jnp.zeros_like(bias_query), bias_value])[:, None, :]
    projected = low(low_back(projected))
    queries = projected[0].reshape(GROUP_TOK, H, HD)
    key_rows = projected[1].reshape(GROUP_TOK, H, HD)
    value_rows = projected[2].reshape(GROUP_TOK, H, HD)
    block_rows = min(512, GROUP_TOK)
    block_count = GROUP_TOK // block_rows
    query_blocks = queries.reshape(block_count, block_rows, H, HD)
    offsets = jnp.arange(block_count, dtype=jnp.int32) * block_rows

    def one_block(block_item):
        return attend_block(block_item[0], block_item[1], key_rows, value_rows, segment, block_rows)
    attended = lax.map(jax.checkpoint(one_block), (query_blocks, offsets)).reshape(GROUP_TOK, D)
    attended = low(low_back(attended))
    branch = low_back(jnp.dot(attended, used_output.T, precision=HIGHEST) + bias_output)
    middle = group_in + branch
    normed_two = low(layer_norm(middle, gain_two, bias_two))
    expanded = low_back(jnp.dot(normed_two, used_expand.T, precision=HIGHEST) + bias_expand)
    activated = low(jax.nn.gelu(expanded, approximate=True))
    return middle + jnp.dot(activated, used_contract.T, precision=HIGHEST) + bias_contract

def forward_all(tokens_f, input_weight, output_weight, expand_weight, contract_weight, params, segments):
    stacked_input = low(input_weight).reshape(3, D, D)
    used_output = low(output_weight)
    used_expand = low(expand_weight)
    used_contract = low(contract_weight)
    groups_in = tokens_f.reshape(N_BATCH, GROUP_TOK, D)

    def one_group(group_in, segment):
        return group_forward(group_in, segment, stacked_input, used_output, used_expand, used_contract, params)
    checked = jax.checkpoint(one_group)

    def scan_step(carried, scan_item):
        return (carried, checked(scan_item[0], scan_item[1]))
    unused_carry, outputs = lax.scan(scan_step, jnp.float32(0.0), (groups_in, segments))
    return outputs.reshape(TOKENS, D)

def adam_direction(gradient, first_old, second_old, master, clip_factor):
    clipped = gradient * clip_factor
    first_new = 0.5 * first_old + 0.5 * clipped
    second_new = 0.5 * second_old + 0.5 * clipped * clipped
    correction = 1.0 - 0.5 ** STEP
    direction = first_new / correction / (jnp.sqrt(second_new / correction) + ADAM_EPS) + DECAY_RATE * master
    return (first_new, second_new, direction)

def reference(tokens, cotangent, lengths, input_weight, output_weight, expand_weight, contract_weight, vector_params, input_first, input_second, output_first, output_second, expand_first, expand_second, contract_first, contract_second, vector_first, vector_second):
    segments = jax.vmap(segment_ids)(lengths)

    def forward_fn(tokens_f, weight_in, weight_out, weight_expand, weight_contract, params):
        return forward_all(tokens_f, weight_in, weight_out, weight_expand, weight_contract, params, segments)
    outputs, pullback = jax.vjp(forward_fn, tokens.astype(jnp.float32), input_weight, output_weight, expand_weight, contract_weight, vector_params)
    grad_tokens, grad_input, grad_output, grad_expand, grad_contract, grad_vector = pullback(cotangent.astype(jnp.float32))
    matrix_grads = [grad_input, grad_output, grad_expand, grad_contract]
    masters = [input_weight, output_weight, expand_weight, contract_weight]
    firsts = [input_first, output_first, expand_first, contract_first]
    seconds = [input_second, output_second, expand_second, contract_second]
    total_sq = jnp.sum(grad_vector * grad_vector)
    for gradient in matrix_grads:
        total_sq = total_sq + jnp.sum(gradient * gradient)
    grad_norm = jnp.sqrt(total_sq)
    clip_factor = jnp.minimum(1.0, 1.0 / grad_norm)
    results = []
    weight_norms = []
    update_norms = []
    for gradient, first_old, second_old, master in zip(matrix_grads, firsts, seconds, masters):
        first_new, second_new, direction = adam_direction(gradient, first_old, second_old, master, clip_factor)
        weight_norm = jnp.sqrt(jnp.sum(master * master))
        update_norm = jnp.sqrt(jnp.sum(direction * direction))
        new_master = master - MATRIX_RATE * (weight_norm / update_norm) * direction
        weight_norms.append(weight_norm)
        update_norms.append(update_norm)
        results.append((first_new, second_new, new_master, new_master.astype(jnp.bfloat16)))
    vector_first_new, vector_second_new, vector_direction = adam_direction(grad_vector, vector_first, vector_second, vector_params, clip_factor)
    vector_new = vector_params - VECTOR_RATE * vector_direction
    matrix_norms = jnp.stack(weight_norms + update_norms)
    return (outputs.astype(jnp.bfloat16), grad_tokens.astype(jnp.bfloat16), grad_norm, matrix_norms, results[0][0], results[0][1], results[0][2], results[0][3], results[1][0], results[1][1], results[1][2], results[1][3], results[2][0], results[2][1], results[2][2], results[2][3], results[3][0], results[3][1], results[3][2], results[3][3], vector_first_new, vector_second_new, vector_new)
```

```python
from functools import partial

import jax
import jax.numpy as jnp
from jax import lax
from jax.sharding import PartitionSpec as P

D = 768
HD = 64
FF = 3072
STEP = 5


NORM_EPS = 1e-05
ADAM_EPS = 1e-06
DECAY_RATE = 0.01
MATRIX_RATE = 0.5
VECTOR_RATE = 0.1


def layer_norm(values, gain_vec, bias_vec):
    row_mean = jnp.mean(values, axis=-1, keepdims=True)
    centered = values - row_mean
    variance = jnp.mean(centered * centered, axis=-1, keepdims=True)
    return centered * lax.rsqrt(variance + NORM_EPS) * gain_vec + bias_vec


def unpack_vector(params):
    pieces = [params[position * D : (position + 1) * D] for position in range(8)]
    return pieces + [params[8 * D : 8 * D + FF]]


def masked_scores(query_block, key_rows, segment, offset, block_rows, score_scale):
    scores = (
        jnp.einsum("qhd,khd->hqk", query_block, key_rows, preferred_element_type=jnp.float32)
        * score_scale
    )
    query_pos = offset + jnp.arange(block_rows, dtype=jnp.int32)
    key_pos = jnp.arange(key_rows.shape[0], dtype=jnp.int32)
    query_seg = lax.dynamic_slice_in_dim(segment, offset, block_rows, 0)
    allowed = (key_pos[None, :] <= query_pos[:, None]) & (query_seg[:, None] == segment[None, :])
    return jnp.where(allowed[None], scores, -1e30)


def head_forward(head_inputs, segment, block_count, block_rows, score_scale):
    group_rows = head_inputs.shape[1]
    heads_here = head_inputs.shape[2] // HD
    queries = head_inputs[0].reshape(group_rows, heads_here, HD)
    key_rows = head_inputs[1].reshape(group_rows, heads_here, HD)
    value_rows = head_inputs[2].reshape(group_rows, heads_here, HD)

    def one_block(block_index):
        offset = block_index * block_rows
        query_block = lax.dynamic_slice_in_dim(queries, offset, block_rows, 0)
        scores = masked_scores(query_block, key_rows, segment, offset, block_rows, score_scale)
        row_max = jnp.max(scores, axis=-1, keepdims=True)
        exponent = jnp.exp(scores - row_max)
        row_total = jnp.sum(exponent, axis=-1, keepdims=True)
        soft_weights = (exponent / row_total).astype(jnp.bfloat16)
        attended = jnp.einsum(
            "hqk,khd->qhd", soft_weights, value_rows, preferred_element_type=jnp.float32
        )
        return (attended.astype(jnp.bfloat16), row_max + jnp.log(row_total))

    attended, log_totals = lax.map(one_block, jnp.arange(block_count, dtype=jnp.int32))
    return (attended.reshape(group_rows, heads_here * HD), log_totals)


def head_backward(
    head_inputs, grad_heads, log_totals, segment, block_count, block_rows, score_scale
):
    group_rows = head_inputs.shape[1]
    heads_here = head_inputs.shape[2] // HD
    queries = head_inputs[0].reshape(group_rows, heads_here, HD)
    key_rows = head_inputs[1].reshape(group_rows, heads_here, HD)
    value_rows = head_inputs[2].reshape(group_rows, heads_here, HD)
    grad_out = grad_heads.reshape(group_rows, heads_here, HD)

    def one_block(state_pair, scan_item):
        grad_keys, grad_values = state_pair
        block_index, block_logs = scan_item
        offset = block_index * block_rows
        query_block = lax.dynamic_slice_in_dim(queries, offset, block_rows, 0)
        grad_block = lax.dynamic_slice_in_dim(grad_out, offset, block_rows, 0)
        scores = masked_scores(query_block, key_rows, segment, offset, block_rows, score_scale)
        probs = jnp.exp(scores - block_logs)
        grad_values = grad_values + jnp.einsum(
            "hqk,qhd->khd",
            probs.astype(jnp.bfloat16),
            grad_block,
            preferred_element_type=jnp.float32,
        )
        grad_probs = jnp.einsum(
            "qhd,khd->hqk", grad_block, value_rows, preferred_element_type=jnp.float32
        )
        row_delta = jnp.sum(probs * grad_probs, axis=-1, keepdims=True)
        grad_scores = (probs * (grad_probs - row_delta)).astype(jnp.bfloat16)
        grad_queries = (
            jnp.einsum("hqk,khd->qhd", grad_scores, key_rows, preferred_element_type=jnp.float32)
            * score_scale
        )
        grad_keys = (
            grad_keys
            + jnp.einsum(
                "hqk,qhd->khd", grad_scores, query_block, preferred_element_type=jnp.float32
            )
            * score_scale
        )
        return ((grad_keys, grad_values), grad_queries)

    zero_state = jnp.zeros((group_rows, heads_here, HD), jnp.float32)
    final_state, grad_queries = lax.scan(
        one_block, (zero_state, zero_state), (jnp.arange(block_count, dtype=jnp.int32), log_totals)
    )
    width_here = heads_here * HD
    stacked = jnp.stack(
        [
            grad_queries.reshape(group_rows, width_here),
            final_state[0].reshape(group_rows, width_here),
            final_state[1].reshape(group_rows, width_here),
        ]
    )
    return stacked.astype(jnp.bfloat16)


def adam_direction(gradient, first_old, second_old, master, clip_factor):
    clipped = gradient * clip_factor
    first_new = 0.5 * first_old + 0.5 * clipped
    second_new = 0.5 * second_old + 0.5 * clipped * clipped
    correction = 1.0 - 0.5**STEP
    direction = (
        first_new / correction / (jnp.sqrt(second_new / correction) + ADAM_EPS)
        + DECAY_RATE * master
    )
    return (first_new, second_new, direction)


def on_device(
    tokens,
    cotangent,
    lengths,
    input_weight,
    output_weight,
    expand_weight,
    contract_weight,
    vector_params,
    input_first,
    input_second,
    output_first,
    output_second,
    expand_first,
    expand_second,
    contract_first,
    contract_second,
    vector_first,
    vector_second,
):
    head_count = lax.axis_size("head")
    local_rows = tokens.shape[0]
    group_rows = local_rows * head_count
    block_rows = min(512, group_rows)
    block_count = group_rows // block_rows
    score_scale = HD ** (-0.5)
    (
        gain_one,
        bias_one,
        gain_two,
        bias_two,
        bias_query,
        bias_value,
        bias_output,
        bias_contract,
        bias_expand,
    ) = unpack_vector(vector_params)
    full_input, full_output, full_expand, full_contract = (
        lax.all_gather(input_weight.astype(jnp.bfloat16), ("batch", "head"), axis=0, tiled=True),
        lax.all_gather(output_weight.astype(jnp.bfloat16), ("batch", "head"), axis=0, tiled=True),
        lax.all_gather(expand_weight.astype(jnp.bfloat16), ("batch", "head"), axis=0, tiled=True),
        lax.all_gather(contract_weight.astype(jnp.bfloat16), ("batch", "head"), axis=0, tiled=True),
    )
    stacked_input = full_input.reshape(3, D, D)
    doc_ends = jnp.stack([jnp.sum(lengths[0, : position + 1]) for position in range(lengths.shape[1])])
    positions = jnp.arange(group_rows, dtype=jnp.int32)
    segment = jnp.sum((positions[:, None] >= doc_ends[None, :]).astype(jnp.int32), axis=1)
    resid_in = tokens.astype(jnp.float32)
    normed_one = layer_norm(resid_in, gain_one, bias_one).astype(jnp.bfloat16)
    input_bias = jnp.stack([bias_query, jnp.zeros_like(bias_query), bias_value])[:, None, :]
    projected = (
        jnp.einsum("td,cod->cto", normed_one, stacked_input, preferred_element_type=jnp.float32)
        + input_bias
    ).astype(jnp.bfloat16)
    head_inputs = lax.all_to_all(projected, "head", split_axis=2, concat_axis=1, tiled=True)
    head_out, log_totals = head_forward(head_inputs, segment, block_count, block_rows, score_scale)
    attended = lax.all_to_all(head_out, "head", split_axis=0, concat_axis=1, tiled=True)
    branch = (
        jnp.einsum("tc,oc->to", attended, full_output, preferred_element_type=jnp.float32)
        + bias_output
    )
    resid_mid = resid_in + branch
    normed_two = layer_norm(resid_mid, gain_two, bias_two).astype(jnp.bfloat16)
    expanded = (
        jnp.einsum("td,fd->tf", normed_two, full_expand, preferred_element_type=jnp.float32)
        + bias_expand
    )
    activated = jax.nn.gelu(expanded, approximate=True).astype(jnp.bfloat16)
    block_out = (
        resid_mid
        + jnp.einsum("tf,of->to", activated, full_contract, preferred_element_type=jnp.float32)
        + bias_contract
    ).astype(jnp.bfloat16)
    upstream = cotangent.astype(jnp.float32)
    grad_contract = jnp.einsum(
        "to,tf->of", cotangent, activated, preferred_element_type=jnp.float32
    )
    grad_activated = jnp.einsum(
        "to,of->tf", cotangent, full_contract, preferred_element_type=jnp.float32
    )
    unused_gelu, gelu_pull = jax.vjp(partial(jax.nn.gelu, approximate=True), expanded)
    grad_expanded = gelu_pull(grad_activated)[0].astype(jnp.bfloat16)
    grad_expand = jnp.einsum(
        "tf,td->fd", grad_expanded, normed_two, preferred_element_type=jnp.float32
    )
    grad_normed_two = jnp.einsum(
        "tf,fd->td", grad_expanded, full_expand, preferred_element_type=jnp.float32
    )
    unused_second, norm_pull_two = jax.vjp(layer_norm, resid_mid, gain_two, bias_two)
    grad_mid_norm, grad_gain_two, grad_bias_two = norm_pull_two(grad_normed_two)
    grad_mid = upstream + grad_mid_norm
    grad_branch = grad_mid.astype(jnp.bfloat16)
    grad_output = jnp.einsum("to,tc->oc", grad_branch, attended, preferred_element_type=jnp.float32)
    grad_attended = jnp.einsum(
        "to,oc->tc", grad_branch, full_output, preferred_element_type=jnp.float32
    ).astype(jnp.bfloat16)
    grad_heads = lax.all_to_all(grad_attended, "head", split_axis=1, concat_axis=0, tiled=True)
    grad_projected_heads = head_backward(
        head_inputs, grad_heads, log_totals, segment, block_count, block_rows, score_scale
    )
    grad_projected = lax.all_to_all(
        grad_projected_heads, "head", split_axis=1, concat_axis=2, tiled=True
    )
    grad_input = jnp.einsum(
        "cto,td->cod", grad_projected, normed_one, preferred_element_type=jnp.float32
    ).reshape(3 * D, D)
    grad_normed_one = jnp.einsum(
        "cto,cod->td", grad_projected, stacked_input, preferred_element_type=jnp.float32
    )
    unused_first, norm_pull_one = jax.vjp(layer_norm, resid_in, gain_one, bias_one)
    grad_in_norm, grad_gain_one, grad_bias_one = norm_pull_one(grad_normed_one)
    input_grad = (grad_mid + grad_in_norm).astype(jnp.bfloat16)
    projected_sums = jnp.sum(grad_projected.astype(jnp.float32), axis=1)
    vector_local = jnp.concatenate(
        [
            grad_gain_one,
            grad_bias_one,
            grad_gain_two,
            grad_bias_two,
            projected_sums[0],
            projected_sums[2],
            jnp.sum(grad_branch.astype(jnp.float32), axis=0),
            jnp.sum(upstream, axis=0),
            jnp.sum(grad_expanded.astype(jnp.float32), axis=0),
        ]
    )
    shard_grads = (
        lax.psum_scatter(grad_input, ("batch", "head"), scatter_dimension=0, tiled=True),
        lax.psum_scatter(grad_output, ("batch", "head"), scatter_dimension=0, tiled=True),
        lax.psum_scatter(grad_expand, ("batch", "head"), scatter_dimension=0, tiled=True),
        lax.psum_scatter(grad_contract, ("batch", "head"), scatter_dimension=0, tiled=True),
    )
    vector_grads = lax.psum(vector_local, ("batch", "head"))
    masters = (input_weight, output_weight, expand_weight, contract_weight)
    firsts = (input_first, output_first, expand_first, contract_first)
    seconds = (input_second, output_second, expand_second, contract_second)
    local_grad_sq = jnp.sum(
        jnp.stack([jnp.sum(piece_grad * piece_grad) for piece_grad in shard_grads])
    )
    weight_sq = jnp.stack([jnp.sum(master * master) for master in masters])
    grad_total = lax.psum(local_grad_sq, ("batch", "head"))
    grad_norm = jnp.sqrt(grad_total + jnp.sum(vector_grads * vector_grads))
    clip_factor = jnp.minimum(1.0, 1.0 / grad_norm)
    updated = [
        adam_direction(piece_grad, first_old, second_old, master, clip_factor)
        for piece_grad, first_old, second_old, master in zip(shard_grads, firsts, seconds, masters)
    ]
    update_sq = jnp.stack([jnp.sum(entry[2] * entry[2]) for entry in updated])
    weight_total, update_total = lax.psum((weight_sq, update_sq), ("batch", "head"))
    weight_norms = jnp.sqrt(weight_total)
    update_norms = jnp.sqrt(update_total)
    matrix_norms = jnp.concatenate([weight_norms, update_norms])
    results = []
    for position in range(4):
        first_new, second_new, direction = updated[position]
        new_master = (
            masters[position]
            - MATRIX_RATE * (weight_norms[position] / update_norms[position]) * direction
        )
        results.append((first_new, second_new, new_master, new_master.astype(jnp.bfloat16)))
    vector_first_new, vector_second_new, vector_direction = adam_direction(
        vector_grads, vector_first, vector_second, vector_params, clip_factor
    )
    vector_new = vector_params - VECTOR_RATE * vector_direction
    return (
        block_out,
        input_grad,
        grad_norm,
        matrix_norms,
        results[0][0],
        results[0][1],
        results[0][2],
        results[0][3],
        results[1][0],
        results[1][1],
        results[1][2],
        results[1][3],
        results[2][0],
        results[2][1],
        results[2][2],
        results[2][3],
        results[3][0],
        results[3][1],
        results[3][2],
        results[3][3],
        vector_first_new,
        vector_second_new,
        vector_new,
    )


def solution(mesh):
    placed = (
        P(("batch", "head"), None),
        P(("batch", "head"), None),
        P("batch", None),
        P(("batch", "head"), None),
        P(("batch", "head"), None),
        P(("batch", "head"), None),
        P(("batch", "head"), None),
        P(),
        P(("batch", "head"), None),
        P(("batch", "head"), None),
        P(("batch", "head"), None),
        P(("batch", "head"), None),
        P(("batch", "head"), None),
        P(("batch", "head"), None),
        P(("batch", "head"), None),
        P(("batch", "head"), None),
        P(),
        P(),
    )
    return jax.shard_map(
        on_device,
        mesh=mesh,
        in_specs=placed,
        out_specs=(
            P(("batch", "head"), None),
            P(("batch", "head"), None),
            P(),
            P(),
            P(("batch", "head"), None),
            P(("batch", "head"), None),
            P(("batch", "head"), None),
            P(("batch", "head"), None),
            P(("batch", "head"), None),
            P(("batch", "head"), None),
            P(("batch", "head"), None),
            P(("batch", "head"), None),
            P(("batch", "head"), None),
            P(("batch", "head"), None),
            P(("batch", "head"), None),
            P(("batch", "head"), None),
            P(("batch", "head"), None),
            P(("batch", "head"), None),
            P(("batch", "head"), None),
            P(("batch", "head"), None),
            P(),
            P(),
            P(),
        ),
        check_vma=False,
    )
```

```python
from functools import partial
import jax
import jax.numpy as jnp
from jax import lax
from jax.experimental import pallas as pl
from jax.experimental.pallas import tpu as pltpu
from jax.sharding import PartitionSpec as P

D = 768
HD = 64
FF = 3072
STEP = 5
BLOCK = 256
LANES = 256
NT = (((1,), (1,)), ((), ()))
NN = (((1,), (0,)), ((), ()))
F32 = jnp.float32
BF16 = jnp.bfloat16


def mm(a, b, dims):
    return lax.dot_general(a, b, dims, preferred_element_type=F32)


def block_start(index, per_piece, me):
    piece = index // per_piece
    return pl.multiple_of(((piece ^ me) * per_piece + index % per_piece) * BLOCK, BLOCK)


def starts_of(scalars, docs, positions):
    first = jnp.zeros_like(positions)
    for doc in range(docs - 1):
        end = scalars[1 + doc]
        first = jnp.where(positions >= end, end, first)
    return first


def first_block(scalars, docs, index):
    position = index * BLOCK
    first = jnp.int32(0)
    for doc in range(docs - 1):
        end = scalars[1 + doc]
        first = jnp.where(position >= end, end, first)
    return first // BLOCK


def head_lanes(block, heads):
    lane = lax.broadcasted_iota(jnp.int32, block.shape, 1) // HD
    return [jnp.where(lane == j, block, jnp.zeros_like(block)) for j in range(heads)]


def allowed_mask(index, key_block, doc_first):
    query = index * BLOCK + lax.broadcasted_iota(jnp.int32, (1, BLOCK), 1)
    key = key_block * BLOCK + lax.broadcasted_iota(jnp.int32, (BLOCK, BLOCK), 0)
    return (key <= query) & (key >= doc_first)


def forward_body(heads, docs, per_piece, blocks, scalars, qkv, keep_out, send_out, log_out, values_t, out_t):
    me = scalars[0]
    width = heads * HD

    def transpose_values(i, carry):
        v = qkv[pl.ds(block_start(i, per_piece, me), BLOCK), 2 * LANES : 3 * LANES]
        values_t[:, pl.ds(pl.multiple_of(i * BLOCK, BLOCK), BLOCK)] = v.T[:width]
        return carry

    lax.fori_loop(0, blocks, transpose_values, 0)

    def query_block(i, carry):
        row = block_start(i, per_piece, me)
        q = qkv[pl.ds(row, BLOCK), 0:LANES] * BF16(HD ** -0.5)
        q_heads = head_lanes(q, heads)
        positions = i * BLOCK + lax.broadcasted_iota(jnp.int32, (1, BLOCK), 1)
        doc_first = starts_of(scalars, docs, positions)

        def key_step(kb, state):
            allowed = allowed_mask(i, kb, doc_first)
            k = qkv[pl.ds(block_start(kb, per_piece, me), BLOCK), LANES : 2 * LANES]
            column = pl.ds(pl.multiple_of(kb * BLOCK, BLOCK), BLOCK)
            new = []
            for j in range(heads):
                top, total, acc = state[j]
                s = jnp.where(allowed, mm(k, q_heads[j], NT), -1e30)
                top_new = jnp.maximum(top, jnp.max(s, axis=0, keepdims=True))
                p = jnp.exp(s - top_new)
                fade = jnp.exp(top - top_new)
                total = total * fade + jnp.sum(p, axis=0, keepdims=True)
                v_t = values_t[j * HD : (j + 1) * HD, column]
                acc = acc * fade + mm(v_t, p.astype(BF16), NN)
                new.append((top_new, total, acc))
            return tuple(new)

        init = tuple(
            (jnp.full((1, BLOCK), -1e30, F32), jnp.zeros((1, BLOCK), F32), jnp.zeros((HD, BLOCK), F32))
            for _ in range(heads)
        )
        state = key_step(i, init)
        state = lax.fori_loop(first_block(scalars, docs, i), i, key_step, state)
        column = pl.ds(row, BLOCK)
        for j in range(heads):
            top, total, acc = state[j]
            out_t[j * HD : (j + 1) * HD, column] = (acc / total).astype(BF16)
            log_out[j : j + 1, pl.ds(pl.multiple_of(i * BLOCK, BLOCK), BLOCK)] = top + jnp.log(total)
        return carry

    lax.fori_loop(0, blocks, query_block, 0)
    half = out_t.shape[1] // 2
    keep_out[...] = out_t[:, :half]
    send_out[...] = out_t[:, half:]


def attention_forward(scalars, qkv, heads, docs, piece_rows):
    rows = qkv.shape[0]
    width = heads * HD
    vmem = pl.BlockSpec(memory_space=pltpu.VMEM)
    return pl.pallas_call(
        partial(forward_body, heads, docs, piece_rows // BLOCK, rows // BLOCK),
        out_shape=(
            jax.ShapeDtypeStruct((width, rows // 2), BF16),
            jax.ShapeDtypeStruct((width, rows // 2), BF16),
            jax.ShapeDtypeStruct((8, rows), F32),
        ),
        in_specs=[pl.BlockSpec(memory_space=pltpu.SMEM), vmem],
        out_specs=(vmem, vmem, vmem),
        scratch_shapes=[pltpu.VMEM((width, rows), BF16), pltpu.VMEM((width, rows), BF16)],
        compiler_params=pltpu.CompilerParams(vmem_limit_bytes=40 * 2**20),
        cost_estimate=pl.CostEstimate(flops=4 * rows * rows * width, bytes_accessed=8 * rows * width, transcendentals=rows * rows),
        name="attention_forward",
    )(scalars, qkv)


def backward_body(
    heads, docs, per_piece, blocks, scalars, qkv, out_keep, out_send, grad_keep, grad_recv, logs, d_qkv,
    keys_t, out_t, grad_t, d_keys, d_values
):
    me = scalars[0]
    width = heads * HD
    scale = HD ** -0.5
    half = out_keep.shape[1]
    out_t[:, :half] = out_keep[...]
    out_t[:, half:] = out_send[...]
    grad_t[:, :half] = grad_keep[...]
    grad_t[:, half:] = grad_recv[...]
    d_keys[...] = jnp.zeros_like(d_keys)
    d_values[...] = jnp.zeros_like(d_values)

    def transpose_keys(i, carry):
        k = qkv[pl.ds(block_start(i, per_piece, me), BLOCK), LANES : 2 * LANES]
        keys_t[:, pl.ds(pl.multiple_of(i * BLOCK, BLOCK), BLOCK)] = k.T[:width]
        return carry

    lax.fori_loop(0, blocks, transpose_keys, 0)

    def query_block(i, carry):
        row = block_start(i, per_piece, me)
        q_heads = head_lanes(qkv[pl.ds(row, BLOCK), 0:LANES] * BF16(scale), heads)
        o_t = out_t[:, pl.ds(row, BLOCK)]
        g_t = grad_t[:, pl.ds(row, BLOCK)]
        product = o_t.astype(F32) * g_t.astype(F32)
        deltas = [jnp.sum(product[j * HD : (j + 1) * HD], axis=0, keepdims=True) for j in range(heads)]
        padded = jnp.concatenate([g_t, jnp.zeros((LANES - width, BLOCK), BF16)], axis=0)
        g_heads = head_lanes(padded.T, heads)
        natural = pl.ds(pl.multiple_of(i * BLOCK, BLOCK), BLOCK)
        log_rows = [logs[j : j + 1, natural] for j in range(heads)]
        positions = i * BLOCK + lax.broadcasted_iota(jnp.int32, (1, BLOCK), 1)
        doc_first = starts_of(scalars, docs, positions)

        def key_step(kb, d_q):
            allowed = allowed_mask(i, kb, doc_first)
            key_row = pl.ds(block_start(kb, per_piece, me), BLOCK)
            k = qkv[key_row, LANES : 2 * LANES]
            v = qkv[key_row, 2 * LANES : 3 * LANES]
            column = pl.ds(pl.multiple_of(kb * BLOCK, BLOCK), BLOCK)
            d_k = d_keys[key_row, :]
            d_v = d_values[key_row, :]
            new = []
            for j in range(heads):
                s = jnp.where(allowed, mm(k, q_heads[j], NT), -1e30)
                p = jnp.exp(s - log_rows[j])
                d_v = d_v + mm(p.astype(BF16), g_heads[j], NN)
                d_p = mm(v, g_heads[j], NT)
                d_s = (p * (d_p - deltas[j])).astype(BF16)
                d_k = d_k + mm(d_s, q_heads[j], NN)
                new.append(d_q[j] + mm(keys_t[j * HD : (j + 1) * HD, column], d_s, NN))
            d_keys[key_row, :] = d_k
            d_values[key_row, :] = d_v
            return tuple(new)

        d_q = key_step(i, tuple(jnp.zeros((HD, BLOCK), F32) for _ in range(heads)))
        d_q = lax.fori_loop(first_block(scalars, docs, i), i, key_step, d_q)
        stacked = jnp.concatenate([*d_q, jnp.zeros((LANES - width, BLOCK), F32)], axis=0) * scale
        d_qkv[pl.ds(row, BLOCK), 0:LANES] = stacked.T.astype(BF16)
        return carry

    lax.fori_loop(0, blocks, query_block, 0)
    d_qkv[:, LANES : 2 * LANES] = d_keys[...].astype(BF16)
    d_qkv[:, 2 * LANES : 3 * LANES] = d_values[...].astype(BF16)


def attention_backward(scalars, qkv, out_keep, out_send, grad_keep, grad_recv, logs, heads, docs, piece_rows):
    rows = qkv.shape[0]
    width = heads * HD
    vmem = pl.BlockSpec(memory_space=pltpu.VMEM)
    return pl.pallas_call(
        partial(backward_body, heads, docs, piece_rows // BLOCK, rows // BLOCK),
        out_shape=jax.ShapeDtypeStruct((rows, 3 * LANES), BF16),
        in_specs=[pl.BlockSpec(memory_space=pltpu.SMEM)] + [vmem] * 6,
        out_specs=vmem,
        scratch_shapes=[pltpu.VMEM((width, rows), BF16)] * 3 + [pltpu.VMEM((rows, LANES), F32)] * 2,
        compiler_params=pltpu.CompilerParams(vmem_limit_bytes=48 * 2**20),
        cost_estimate=pl.CostEstimate(flops=10 * rows * rows * width, bytes_accessed=16 * rows * width, transcendentals=rows * rows),
        name="attention_backward",
    )(scalars, qkv, out_keep, out_send, grad_keep, grad_recv, logs)


NORM_EPS = 1e-05
ADAM_EPS = 1e-06
DECAY_RATE = 0.01
MATRIX_RATE = 0.5
VECTOR_RATE = 0.1
ROOT_TWO_OVER_PI = (2.0 / 3.141592653589793) ** 0.5
BOTH = ("batch", "head")
PARTNER = 1
ACROSS = 2


def layer_norm_parts(values):
    row_mean = jnp.mean(values, axis=-1, keepdims=True)
    centered = values - row_mean
    variance = jnp.mean(centered * centered, axis=-1, keepdims=True)
    inverse = lax.rsqrt(variance + NORM_EPS)
    return centered * inverse, inverse


def layer_norm_backward(upstream, normalized, inverse, gain):
    scaled = upstream * gain
    first = jnp.mean(scaled, axis=-1, keepdims=True)
    second = jnp.mean(scaled * normalized, axis=-1, keepdims=True)
    return inverse * (scaled - first - normalized * second)


def unpack_vector(params):
    pieces = [params[position * D : (position + 1) * D] for position in range(8)]
    return pieces + [params[8 * D : 8 * D + FF]]


def dot(a, b, dims):
    return lax.dot_general(a, b, (dims, ((), ())), preferred_element_type=F32)


def swap(values, axis, mask):
    size = lax.axis_size(axis)
    return lax.ppermute(values, axis, [(place, place ^ mask) for place in range(size)])


def bit_of(axis, mask):
    return (lax.axis_index(axis) & mask) != 0


def gather_step(values, axis, mask, position):
    other = swap(values, axis, mask)
    high = bit_of(axis, mask)
    return jnp.stack(
        [jnp.where(high, other, values), jnp.where(high, values, other)], axis=position
    )


def scatter_step(values, axis, mask, position):
    high = bit_of(axis, mask).astype(jnp.int32)
    kept = lax.dynamic_index_in_dim(values, high, position, keepdims=False)
    sent = lax.dynamic_index_in_dim(values, 1 - high, position, keepdims=False)
    arrived = swap(sent.astype(BF16), axis, mask)
    return kept.astype(F32) + arrived.astype(F32)


def all_sum(values):
    for axis in ("head", "batch"):
        mask = 1
        while mask < lax.axis_size(axis):
            values = values + swap(values, axis, mask)
            mask *= 2
    return values


def batch_masks():
    return [1 << bit for bit in range((lax.axis_size("batch") - 1).bit_length())]


def gather_chips(values, across_last):
    masks = batch_masks()[::-1]
    early, late = masks[:-1], masks[-1]
    position = 0
    for mask in early:
        values = gather_step(values, "batch", mask, position)
        position += 1
    if across_last:
        values = gather_step(values, "batch", late, position)
        values = gather_step(values, "head", ACROSS, position + 1)
    else:
        values = gather_step(values, "head", ACROSS, position)
        values = gather_step(values, "batch", late, position)
    return values.reshape((-1,) + values.shape[position + 2 :])


def scatter_chips(values, across_first):
    masks = batch_masks()
    shape = values.shape[1:]
    values = values.reshape((2,) * (len(masks) + 1) + shape)
    position = len(masks)
    if across_first:
        values = scatter_step(values, "head", ACROSS, position)
        values = scatter_step(values, "batch", masks[0], position - 1)
    else:
        values = scatter_step(values, "batch", masks[0], position - 1)
        values = scatter_step(values, "head", ACROSS, position - 1)
    for step, mask in enumerate(masks[1:]):
        values = scatter_step(values, "batch", mask, position - 2 - step)
    return values


def gather_batch(values, position):
    for mask in batch_masks()[::-1]:
        values = gather_step(values, "batch", mask, position)
        position += 1
    return values


def scatter_batch(values, position):
    masks = batch_masks()
    shape = values.shape
    values = values.reshape(
        shape[:position] + (2,) * len(masks) + shape[position + 1 :]
    )
    for step, mask in enumerate(masks):
        values = scatter_step(values, "batch", mask, position + len(masks) - 1 - step)
    return values


def block_permutation(slot, to_owner):
    rows, heads = lax.axis_size("batch"), lax.axis_size("head")
    total = rows * heads
    pairs = []
    for owner in range(total):
        place = (3 * owner + slot) % total
        holder = (place % rows) * heads + place // rows
        pairs.append((holder, owner) if to_owner else (owner, holder))
    return pairs


def holder_place():
    return lax.axis_size("batch") * lax.axis_index("head") + lax.axis_index("batch")


def blocks_to_holders(shard):
    total = lax.axis_size("batch") * lax.axis_size("head")
    blocks = shard.reshape(3, -1, D)
    arrived = jnp.stack(
        [lax.ppermute(blocks[slot], BOTH, block_permutation(slot, False)) for slot in range(3)]
    )
    place = holder_place()
    return jnp.stack(
        [
            lax.dynamic_index_in_dim(arrived, (total * kind + place) % 3, 0, keepdims=False)
            for kind in range(3)
        ]
    )


def blocks_to_owners(blocks):
    total = lax.axis_size("batch") * lax.axis_size("head")
    place = holder_place()
    arrived = []
    for slot in range(3):
        kind = ((slot + 3 * total - place) * total) % 3
        sent = lax.dynamic_index_in_dim(blocks, kind, 0, keepdims=False)
        arrived.append(lax.ppermute(sent, BOTH, block_permutation(slot, True)))
    return jnp.concatenate(arrived, axis=0)


def adam_direction(gradient, first_old, second_old, master, clip_factor):
    clipped = gradient * clip_factor
    first_new = 0.5 * first_old + 0.5 * clipped
    second_new = 0.5 * second_old + 0.5 * clipped * clipped
    correction = 1.0 - 0.5**STEP
    direction = (
        first_new / correction / (jnp.sqrt(second_new / correction) + ADAM_EPS)
        + DECAY_RATE * master
    )
    return (first_new, second_new, direction)


def on_device(
    tokens,
    cotangent,
    lengths,
    input_weight,
    output_weight,
    expand_weight,
    contract_weight,
    vector_params,
    input_first,
    input_second,
    output_first,
    output_second,
    expand_first,
    expand_second,
    contract_first,
    contract_second,
    vector_first,
    vector_second,
):
    rows_of_devices = lax.axis_size("batch")
    head_count = lax.axis_size("head")
    chips = rows_of_devices * head_count // 2
    here = lax.axis_index("head")
    core = here % 2
    side = here // 2
    width = D // head_count
    heads = width // HD
    piece = tokens.shape[0]
    docs = lengths.shape[1]
    hidden_block = FF // (2 * chips)
    half = FF // 2
    (
        gain_one,
        bias_one,
        gain_two,
        bias_two,
        bias_query,
        bias_value,
        bias_output,
        bias_contract,
        bias_expand,
    ) = unpack_vector(vector_params)

    ends = [jnp.sum(lengths[0, : doc + 1]) for doc in range(docs)]
    scalars = jnp.stack([here, *ends]).astype(jnp.int32)

    resid_in = tokens.astype(F32)
    unit_one, inverse_one = layer_norm_parts(resid_in)
    normed_own = (unit_one * gain_one + bias_one).astype(BF16)
    normed_across = swap(normed_own, "head", ACROSS)
    normed_partner = swap(normed_own, "head", PARTNER)
    normed_both = swap(normed_across, "head", PARTNER)
    normed_one = jnp.concatenate([normed_own, normed_partner, normed_across, normed_both])

    kinds = gather_batch(blocks_to_holders(input_weight.astype(BF16)), 1).reshape(3, width, D)
    weight_in = jnp.pad(kinds, ((0, 0), (0, LANES - width), (0, 0))).reshape(3 * LANES, D)

    def of_heads(vector):
        return jnp.pad(lax.dynamic_slice_in_dim(vector, here * width, width), (0, LANES - width))

    bias_in = jnp.concatenate([of_heads(bias_query), jnp.zeros(LANES, F32), of_heads(bias_value)])
    projected = (dot(normed_one, weight_in, ((1,), (1,))) + bias_in).astype(BF16)

    def split_columns(shard, parts):
        return shard.reshape(shard.shape[0], parts, 2, -1)

    def exchange_columns(shard, parts):
        cut = split_columns(shard, parts)
        mine = lax.dynamic_index_in_dim(cut, core, 2, keepdims=False)
        other = swap(lax.dynamic_index_in_dim(cut, 1 - core, 2, keepdims=False), "head", PARTNER)
        high = core == 1
        return jnp.stack([jnp.where(high, other, mine), jnp.where(high, mine, other)])

    out_rows = output_weight.shape[0]
    output_shard = exchange_columns(output_weight.astype(BF16), 2).reshape(2 * out_rows, 2, width)
    output_half = gather_chips(output_shard.transpose(1, 0, 2), True)
    output_half = output_half.transpose(1, 0, 2, 3).reshape(2, D, width)
    output_own = lax.dynamic_index_in_dim(output_half, side, 0, keepdims=False)
    output_across = lax.dynamic_index_in_dim(output_half, 1 - side, 0, keepdims=False)
    expand_half = gather_chips(expand_weight.astype(BF16), True).reshape(half, D)
    contract_shard = exchange_columns(contract_weight.astype(BF16), chips).reshape(2 * out_rows, half)
    contract_half = gather_chips(contract_shard, False).reshape(D, half)
    bias_half = lax.dynamic_index_in_dim(
        bias_expand.reshape(chips, 2, hidden_block), core, 1, keepdims=False
    ).reshape(half)
    upstream_pair = jnp.concatenate([cotangent, swap(cotangent, "head", PARTNER)])

    keep_t, send_t, logs = attention_forward(scalars, projected, heads, docs, piece)
    across_t = swap(send_t, "head", ACROSS)
    branch_pair = dot(keep_t, output_own, ((0,), (1,))) + dot(across_t, output_across, ((0,), (1,)))
    branch = branch_pair[:piece] + swap(branch_pair[piece:], "head", PARTNER) + bias_output
    resid_mid = resid_in + branch
    unit_two, inverse_two = layer_norm_parts(resid_mid)
    normed_two_own = (unit_two * gain_two + bias_two).astype(BF16)
    normed_two = jnp.concatenate([normed_two_own, swap(normed_two_own, "head", PARTNER)])

    expanded = dot(normed_two, expand_half, ((1,), (1,))) + bias_half
    squared = expanded * expanded
    bent = jnp.tanh(ROOT_TWO_OVER_PI * (expanded + 0.044715 * expanded * squared))
    activated = (0.5 * expanded * (1.0 + bent)).astype(BF16)
    slope = 0.5 * (1.0 + bent) + 0.5 * expanded * (1.0 - bent * bent) * ROOT_TWO_OVER_PI * (
        1.0 + 3.0 * 0.044715 * squared
    )
    grad_expanded_wide = dot(upstream_pair, contract_half, ((1,), (0,))) * slope
    grad_expanded = grad_expanded_wide.astype(BF16)
    contract_pair = dot(activated, contract_half, ((1,), (1,)))
    block_out = (
        resid_mid + contract_pair[:piece] + swap(contract_pair[piece:], "head", PARTNER) + bias_contract
    ).astype(BF16)
    grad_normed_pair = dot(grad_expanded, expand_half, ((1,), (0,)))
    grad_normed_two = grad_normed_pair[:piece] + swap(grad_normed_pair[piece:], "head", PARTNER)
    upstream = cotangent.astype(F32)
    grad_mid = upstream + layer_norm_backward(grad_normed_two, unit_two, inverse_two, gain_two)
    grad_gain_two = jnp.sum(grad_normed_two * unit_two, axis=0)
    grad_bias_two = jnp.sum(grad_normed_two, axis=0)
    grad_branch = grad_mid.astype(BF16)
    grad_branch_pair = jnp.concatenate([grad_branch, swap(grad_branch, "head", PARTNER)])

    grad_across_t = dot(output_across, grad_branch_pair, ((0,), (1,))).astype(BF16)
    grad_arrived_t = swap(grad_across_t, "head", ACROSS)
    grad_keep_t = dot(output_own, grad_branch_pair, ((0,), (1,))).astype(BF16)
    grad_projected = attention_backward(
        scalars, projected, keep_t, send_t, grad_keep_t, grad_arrived_t, logs, heads, docs, piece
    )

    expand_sum = dot(grad_expanded, normed_two, ((0,), (0,))).reshape(chips, hidden_block, D)
    expand_grad = scatter_chips(expand_sum, False)
    contract_sum = dot(upstream_pair, activated, ((0,), (0,))).reshape(chips, 2 * out_rows, half)
    contract_mixed = scatter_chips(contract_sum, True)
    own_columns = dot(grad_branch_pair, keep_t, ((0,), (1,)))
    across_columns = dot(grad_branch_pair, across_t, ((0,), (1,)))
    output_sum = jnp.stack(
        [
            jnp.where(side == 1, across_columns, own_columns),
            jnp.where(side == 1, own_columns, across_columns),
        ]
    ).reshape(2, chips, 2 * out_rows, width)
    output_mixed = scatter_chips(output_sum.transpose(1, 0, 2, 3), True)
    output_mixed = output_mixed.transpose(1, 0, 2)

    def return_columns(mixed, parts):
        cut = mixed.reshape(2, out_rows, parts, -1)
        mine = lax.dynamic_index_in_dim(cut, core, 0, keepdims=False)
        other = swap(lax.dynamic_index_in_dim(cut, 1 - core, 0, keepdims=False), "head", PARTNER)
        high = core == 1
        return jnp.stack(
            [jnp.where(high, other, mine), jnp.where(high, mine, other)], axis=2
        ).reshape(out_rows, -1)

    contract_grad = return_columns(contract_mixed, chips)
    output_grad = return_columns(output_mixed, 2)

    grad_normed_all = dot(grad_projected, weight_in, ((1,), (0,))).reshape(4, piece, D)
    reduced_across = grad_normed_all[2] + swap(grad_normed_all[3].astype(BF16), "head", PARTNER).astype(F32)
    arrived_across = swap(reduced_across.astype(BF16), "head", ACROSS)
    grad_normed_one = (
        grad_normed_all[0]
        + swap(grad_normed_all[1].astype(BF16), "head", PARTNER).astype(F32)
        + arrived_across.astype(F32)
    )
    grad_in_sum = dot(grad_projected, normed_one, ((0,), (0,))).reshape(3, LANES, D)[:, :width]
    grad_in_blocks = scatter_batch(grad_in_sum.reshape(3, rows_of_devices, -1, D), 1)
    input_piece_grad = blocks_to_owners(grad_in_blocks)
    input_grad = (grad_mid + layer_norm_backward(grad_normed_one, unit_one, inverse_one, gain_one)).astype(BF16)

    projected_sums = jnp.sum(grad_projected.astype(F32), axis=0).reshape(3, LANES)[:, :width]

    def place_heads(vector):
        return lax.dynamic_update_slice_in_dim(jnp.zeros(D, F32), vector, here * width, 0)

    hidden_sums = jnp.sum(grad_expanded.astype(F32), axis=0).reshape(chips, 1, hidden_block)
    hidden_sums = lax.dynamic_update_slice_in_dim(
        jnp.zeros((chips, 2, hidden_block), F32), hidden_sums, core, 1
    ).reshape(FF)
    masters = (input_weight, output_weight, expand_weight, contract_weight)
    firsts = (input_first, output_first, expand_first, contract_first)
    seconds = (input_second, output_second, expand_second, contract_second)
    shard_grads = (input_piece_grad, output_grad, expand_grad, contract_grad)
    local_sq = jnp.sum(grad_in_blocks * grad_in_blocks) + sum(
        jnp.sum(piece_grad * piece_grad) for piece_grad in shard_grads[1:]
    )
    weight_sq = [jnp.sum(master * master) for master in masters]
    scalars_sq = jnp.pad(jnp.stack([local_sq, *weight_sq]), (0, 1024 - 5))
    local = jnp.concatenate(
        [
            jnp.sum(grad_normed_one * unit_one, axis=0),
            jnp.sum(grad_normed_one, axis=0),
            grad_gain_two,
            grad_bias_two,
            place_heads(projected_sums[0]),
            place_heads(projected_sums[2]),
            jnp.sum(grad_branch.astype(F32), axis=0),
            jnp.sum(upstream, axis=0),
            hidden_sums,
            scalars_sq,
        ]
    ).reshape(-1, 128)
    summed = all_sum(local).reshape(-1)
    vector_grads = summed[: 8 * D + FF]
    grad_norm = jnp.sqrt(summed[8 * D + FF] + jnp.sum(vector_grads * vector_grads))
    weight_norms = jnp.sqrt(summed[8 * D + FF + 1 : 8 * D + FF + 5])
    clip_factor = jnp.minimum(1.0, 1.0 / grad_norm)
    updated = [
        adam_direction(piece_grad, first_old, second_old, master, clip_factor)
        for piece_grad, first_old, second_old, master in zip(shard_grads, firsts, seconds, masters)
    ]
    update_sq = jnp.stack([jnp.sum(entry[2] * entry[2]) for entry in updated])
    update_norms = jnp.sqrt(all_sum(jnp.pad(update_sq, (0, 1020)).reshape(8, 128))[0, :4])
    matrix_norms = jnp.concatenate([weight_norms, update_norms])
    results = []
    for position in range(4):
        first_new, second_new, direction = updated[position]
        new_master = (
            masters[position]
            - MATRIX_RATE * (weight_norms[position] / update_norms[position]) * direction
        )
        results += [first_new, second_new, new_master, new_master.astype(BF16)]
    vector_first_new, vector_second_new, vector_direction = adam_direction(
        vector_grads, vector_first, vector_second, vector_params, clip_factor
    )
    vector_new = vector_params - VECTOR_RATE * vector_direction
    return (
        block_out,
        input_grad,
        grad_norm,
        matrix_norms,
        *results,
        vector_first_new,
        vector_second_new,
        vector_new,
    )


def solution(mesh):
    split = P(BOTH, None)
    return jax.shard_map(
        on_device,
        mesh=mesh,
        in_specs=(split, split, P("batch", None)) + (split,) * 4 + (P(),) + (split,) * 8 + (P(), P()),
        out_specs=(split, split, P(), P()) + (split,) * 16 + (P(), P(), P()),
        check_vma=False,
    )
```

```python
from functools import partial
import jax
import jax.numpy as jnp
from jax import lax
from jax.experimental import pallas as pl
from jax.experimental.pallas import tpu as pltpu
from jax.sharding import PartitionSpec as P

D = 768
HD = 64
FF = 3072
STEP = 5
NORM_EPS = 1e-05
ADAM_EPS = 1e-06
DECAY_RATE = 0.01
MATRIX_RATE = 0.5
VECTOR_RATE = 0.1
ROOT_TWO_OVER_PI = (2.0 / 3.141592653589793) ** 0.5
BLOCK = 256
LANES = 256
NT = (((1,), (1,)), ((), ()))
NN = (((1,), (0,)), ((), ()))
F32 = jnp.float32
BF16 = jnp.bfloat16


def mm(a, b, dims):
    return lax.dot_general(a, b, dims, preferred_element_type=F32)


def block_start(index, per_piece, me):
    piece = index // per_piece
    return pl.multiple_of(((piece ^ me) * per_piece + index % per_piece) * BLOCK, BLOCK)


def starts_of(scalars, docs, positions):
    first = jnp.zeros_like(positions)
    for doc in range(docs - 1):
        end = scalars[ENDS + doc]
        first = jnp.where(positions >= end, end, first)
    return first


def first_block(scalars, docs, index):
    position = index * BLOCK
    first = jnp.int32(0)
    for doc in range(docs - 1):
        end = scalars[ENDS + doc]
        first = jnp.where(position >= end, end, first)
    return first // BLOCK


def head_lanes(block, heads):
    if heads == 1:
        return [block]
    lane = lax.broadcasted_iota(jnp.int32, block.shape, 1) // HD
    return [jnp.where(lane == j, block, jnp.zeros_like(block)) for j in range(heads)]


def allowed_mask(index, key_block, doc_first):
    query = index * BLOCK + lax.broadcasted_iota(jnp.int32, (1, BLOCK), 1)
    key = key_block * BLOCK + lax.broadcasted_iota(jnp.int32, (BLOCK, BLOCK), 0)
    return (key <= query) & (key >= doc_first)


def group_lanes(group, kind):
    start = kind * LANES + group * HEAD_LANES
    return slice(start, start + HEAD_LANES)


def forward_body(heads, group, docs, per_piece, blocks, cuts, scalars, qkv, *refs):
    pairs, refs = refs[: 2 * len(cuts)], refs[2 * len(cuts) :]
    keep_out, send_out, log_out = refs[:3]
    values_t, out_t = refs[-2:]
    join_pairs(pairs, refs[3:-2], cuts)
    me = scalars[HERE]
    width = heads * HD

    def transpose_values(i, carry):
        v = qkv[pl.ds(block_start(i, per_piece, me), BLOCK), group_lanes(group, 2)]
        values_t[:, pl.ds(pl.multiple_of(i * BLOCK, BLOCK), BLOCK)] = v.T[:width]
        return carry

    lax.fori_loop(0, blocks, transpose_values, 0)

    def query_block(i, carry):
        row = block_start(i, per_piece, me)
        q_heads = head_lanes(qkv[pl.ds(row, BLOCK), group_lanes(group, 0)] * BF16(HD ** -0.5), heads)
        positions = i * BLOCK + lax.broadcasted_iota(jnp.int32, (1, BLOCK), 1)
        doc_first = starts_of(scalars, docs, positions)

        def key_step(kb, state):
            allowed = allowed_mask(i, kb, doc_first)
            k = qkv[pl.ds(block_start(kb, per_piece, me), BLOCK), group_lanes(group, 1)]
            column = pl.ds(pl.multiple_of(kb * BLOCK, BLOCK), BLOCK)
            new = []
            for j in range(heads):
                top, total, acc = state[j]
                s = jnp.where(allowed, mm(k, q_heads[j], NT), -1e30)
                top_new = jnp.maximum(top, jnp.max(s, axis=0, keepdims=True))
                p = jnp.exp(s - top_new)
                fade = jnp.exp(top - top_new)
                total = total * fade + jnp.sum(p, axis=0, keepdims=True)
                v_t = values_t[j * HD : (j + 1) * HD, column]
                acc = acc * fade + mm(v_t, p.astype(BF16), NN)
                new.append((top_new, total, acc))
            return tuple(new)

        init = tuple(
            (jnp.full((1, BLOCK), -1e30, F32), jnp.zeros((1, BLOCK), F32), jnp.zeros((HD, BLOCK), F32))
            for _ in range(heads)
        )
        state = key_step(i, init)
        state = lax.fori_loop(first_block(scalars, docs, i), i, key_step, state)
        column = pl.ds(row, BLOCK)
        for j in range(heads):
            top, total, acc = state[j]
            out_t[j * HD : (j + 1) * HD, column] = (acc / total).astype(BF16)
            log_out[j : j + 1, pl.ds(pl.multiple_of(i * BLOCK, BLOCK), BLOCK)] = top + jnp.log(total)
        return carry

    lax.fori_loop(0, blocks, query_block, 0)
    half = out_t.shape[1] // 2
    keep_out[...] = out_t[:, :half]
    send_out[...] = out_t[:, half:]


def attention_forward(scalars, qkv, heads, group, docs, piece, pairs, cuts):
    rows = qkv.shape[0]
    width = heads * HD
    flat = [x for pair in pairs for x in pair]
    found = call(
        partial(forward_body, heads, group, docs, piece // BLOCK, rows // BLOCK, cuts),
        [scalars, qkv, *flat],
        [
            shape((width, rows // 2), BF16),
            shape((width, rows // 2), BF16),
            shape((8, rows), F32),
            *join_shapes(pairs, cuts),
        ],
        [pltpu.VMEM((width, rows), BF16), pltpu.VMEM((width, rows), BF16)],
        24,
        "attention_forward",
    )
    return found[:3], found[3:]


def backward_body(
    heads, group, docs, per_piece, blocks, scalars, qkv, out_keep, out_send, grad_keep, grad_recv, logs, grads,
    sums, keys_t, out_t, grad_t, d_keys, d_values
):
    me = scalars[HERE]
    width = heads * HD
    scale = HD ** -0.5
    half = out_keep.shape[1]
    out_t[:, :half] = out_keep[...]
    out_t[:, half:] = out_send[...]
    grad_t[:, :half] = grad_keep[...]
    grad_t[:, half:] = grad_recv[...]
    d_keys[...] = jnp.zeros_like(d_keys)
    d_values[...] = jnp.zeros_like(d_values)

    def transpose_keys(i, carry):
        k = qkv[pl.ds(block_start(i, per_piece, me), BLOCK), group_lanes(group, 1)]
        keys_t[:, pl.ds(pl.multiple_of(i * BLOCK, BLOCK), BLOCK)] = k.T[:width]
        return carry

    lax.fori_loop(0, blocks, transpose_keys, 0)

    def padded(rows, kind):
        if width == HEAD_LANES:
            return rows
        return jnp.concatenate([rows, jnp.zeros((HEAD_LANES - width, BLOCK), kind)], axis=0)

    def query_block(i, carry):
        row = block_start(i, per_piece, me)
        q_heads = head_lanes(qkv[pl.ds(row, BLOCK), group_lanes(group, 0)] * BF16(scale), heads)
        o_t = out_t[:, pl.ds(row, BLOCK)]
        g_t = grad_t[:, pl.ds(row, BLOCK)]
        product = o_t.astype(F32) * g_t.astype(F32)
        deltas = [jnp.sum(product[j * HD : (j + 1) * HD], axis=0, keepdims=True) for j in range(heads)]
        g_heads = head_lanes(padded(g_t, BF16).T, heads)
        natural = pl.ds(pl.multiple_of(i * BLOCK, BLOCK), BLOCK)
        log_rows = [logs[j : j + 1, natural] for j in range(heads)]
        positions = i * BLOCK + lax.broadcasted_iota(jnp.int32, (1, BLOCK), 1)
        doc_first = starts_of(scalars, docs, positions)

        def key_step(kb, d_q):
            allowed = allowed_mask(i, kb, doc_first)
            key_row = pl.ds(block_start(kb, per_piece, me), BLOCK)
            k = qkv[key_row, group_lanes(group, 1)]
            v = qkv[key_row, group_lanes(group, 2)]
            column = pl.ds(pl.multiple_of(kb * BLOCK, BLOCK), BLOCK)
            d_k = d_keys[key_row, :]
            d_v = d_values[key_row, :]
            new = []
            for j in range(heads):
                s = jnp.where(allowed, mm(k, q_heads[j], NT), -1e30)
                p = jnp.exp(s - log_rows[j])
                d_v = d_v + mm(p.astype(BF16), g_heads[j], NN)
                d_p = mm(v, g_heads[j], NT)
                d_s = (p * (d_p - deltas[j])).astype(BF16)
                d_k = d_k + mm(d_s, q_heads[j], NN)
                new.append(d_q[j] + mm(keys_t[j * HD : (j + 1) * HD, column], d_s, NN))
            d_keys[key_row, :] = d_k
            d_values[key_row, :] = d_v
            return tuple(new)

        d_q = key_step(i, tuple(jnp.zeros((HD, BLOCK), F32) for _ in range(heads)))
        d_q = lax.fori_loop(first_block(scalars, docs, i), i, key_step, d_q)
        stacked = padded(jnp.concatenate(d_q, axis=0), F32) * scale
        grads[pl.ds(row, BLOCK), 0:HEAD_LANES] = stacked.T.astype(BF16)
        return carry

    lax.fori_loop(0, blocks, query_block, 0)
    grads[:, HEAD_LANES : 2 * HEAD_LANES] = d_keys[...].astype(BF16)
    grads[:, 2 * HEAD_LANES : 3 * HEAD_LANES] = d_values[...].astype(BF16)
    sums[...] = jnp.zeros_like(sums)
    for line, kind in enumerate((0, 2)):
        columns = grads[:, kind * HEAD_LANES : (kind + 1) * HEAD_LANES].astype(F32)
        sums[line : line + 1, :] = jnp.sum(columns, axis=0, keepdims=True)


def attention_backward(scalars, qkv, outs, grads, logs, heads, group, docs, piece, markers=()):
    rows = qkv.shape[0]
    width = heads * HD
    return call(
        partial(backward_body, heads, group, docs, piece // BLOCK, rows // BLOCK),
        [scalars, qkv, *outs, *grads, logs],
        [shape((rows, 3 * HEAD_LANES), BF16), shape((8, HEAD_LANES), F32)],
        [pltpu.VMEM((width, rows), BF16)] * 3 + [pltpu.VMEM((rows, HEAD_LANES), F32)] * 2,
        26,
        "attention_backward",
        markers=markers,
    )


MICROSECONDS = {
    "prepare": 2,
    "block_kinds": 1,
    "join": 2,
    "project": 5,
    "attention_forward": 16,
    "branch": 2,
    "middle_norm": 2,
    "feed_forward": 18,
    "head_gradients": 2,
    "output_weight_gradient": 2,
    "attention_backward": 32,
    "first_norm_gradient": 2,
    "input_weight_gradient": 4,
    "add_arrived": 1,
    "middle_gradient": 2,
    "first_gradient": 4,
    "payload": 2,
    "moments": 4,
    "weights": 3,
}
COST_SCALE = 4.0


def cost(name):
    flops = int(MICROSECONDS[name] * COST_SCALE * 1.0e9)
    return pl.CostEstimate(flops=flops, bytes_accessed=0, transcendentals=0)


VMEM = pl.BlockSpec(memory_space=pltpu.VMEM)
SMEM = pl.BlockSpec(memory_space=pltpu.SMEM)
LEFT = pl.BlockSpec(memory_space=pl.ANY)
TN = (((0,), (0,)), ((), ()))
HERE, CHIP, ROW, CORE, SIDE, PLACE = range(6)
ENDS = 6


class Places:
    def __init__(self, lengths=None):
        self.lengths = lengths

    def __getitem__(self, number):
        here, row = lax.axis_index("head"), lax.axis_index("batch")
        heads, rows = lax.axis_size("head"), lax.axis_size("batch")
        if number == HERE:
            return here
        if number == CHIP:
            return row * (heads // 2) + here // 2
        if number == ROW:
            return row
        if number == CORE:
            return here % 2
        if number == SIDE:
            return here // 2
        if number == PLACE:
            return rows * here + row
        return sum(self.lengths[0, doc] for doc in range(number - ENDS + 1))


def call(body, inputs, outputs, scratch, mib, name, markers=()):
    lengths, inputs = inputs[0].lengths, inputs[1:]
    lead = [] if lengths is None else [lengths]
    count = len(lead) + len(inputs)

    def whole(*refs):
        places = Places(refs[0] if lead else None)
        body(places, *refs[len(lead) : count], *refs[count + len(markers) :])

    return pl.pallas_call(
        whole,
        out_shape=tuple(outputs),
        in_specs=[SMEM] * len(lead) + [VMEM] * len(inputs) + [LEFT] * len(markers),
        out_specs=(VMEM,) * len(outputs),
        scratch_shapes=scratch,
        compiler_params=pltpu.CompilerParams(vmem_limit_bytes=mib * 2**20),
        cost_estimate=cost(name),
        name=name,
    )(*lead, *inputs, *markers)


def lines_row(lines, first, count):
    return jnp.concatenate([lines[pl.ds(first + i, 1), :] for i in range(count)], axis=1)


def vector_row(lines, number):
    return lines_row(lines, number * (D // 128), D // 128)


def heads_row(lines, number, here):
    width = D // lax.axis_size("head")
    row = lines_row(lines, number * (D // 128) + (width * here) // 128, LANES // 128)
    row = jnp.where((width * here) % 128 != 0, pltpu.roll(row, LANES - HD, 1), row)
    lane = lax.broadcasted_iota(jnp.int32, row.shape, 1)
    return jnp.where(lane < width, row, 0.0)


def shape(dims, kind):
    return jax.ShapeDtypeStruct(tuple(dims), kind)


def join_pairs(ins, outs, cuts):
    outs = list(outs)
    for i, cut in enumerate(cuts):
        own, arrived = ins[2 * i], ins[2 * i + 1]
        half = own.shape[0]
        if cut == 0:
            out = outs.pop(0)
            out[:half] = own[...]
            out[half:] = arrived[...]
            continue
        rows = own.shape[1] // cut
        for part in range(cut):
            out = outs.pop(0)
            out[:half] = own[:, part * rows : (part + 1) * rows]
            out[half:] = arrived[:, part * rows : (part + 1) * rows]


def join_body(cuts, scalars, *refs):
    count = 2 * len(cuts)
    join_pairs(refs[:count], refs[count:], cuts)


def join_shapes(pairs, cuts):
    shapes = []
    for (own, _), cut in zip(pairs, cuts):
        dims = (2 * own.shape[0],) + own.shape[1:]
        if cut == 0:
            shapes.append(shape(dims, own.dtype))
        else:
            shapes += [shape((dims[0], dims[1] // cut, dims[2]), own.dtype)] * cut
    return shapes


def join(scalars, pairs, cuts, markers=()):
    flat = [x for pair in pairs for x in pair]
    return call(
        partial(join_body, cuts), [scalars, *flat], join_shapes(pairs, cuts), [], 24, "join", markers=markers
    )


def prepare_body(scalars, weight_in, weight_expand, weight_out, tokens, lines, *outs):
    blocks, (expand, mine, other, normed) = outs[:3], outs[3:]
    rows = blocks[0].shape[0]
    for slot, out in enumerate(blocks):
        out[...] = weight_in[slot * rows : (slot + 1) * rows, :].astype(BF16)
    expand[...] = weight_expand[...].astype(BF16)
    quarter = D // 4
    wide = weight_out[...]
    even = jnp.concatenate([wide[:, :quarter], wide[:, 2 * quarter : 3 * quarter]], axis=1)
    odd = jnp.concatenate([wide[:, quarter : 2 * quarter], wide[:, 3 * quarter :]], axis=1)
    high = scalars[CORE] == 1
    mine[...] = jnp.where(high, odd, even).astype(BF16)
    other[...] = jnp.where(high, even, odd).astype(BF16)
    gain, shift = vector_row(lines, 0), vector_row(lines, 1)
    step = min(128, tokens.shape[0])
    for start in range(0, tokens.shape[0], step):
        unit, _ = row_norm(tokens[start : start + step, :].astype(F32))
        normed[start : start + step, :] = (unit * gain + shift).astype(BF16)


def prepare(scalars, weight_in, weight_expand, weight_out, tokens, lines):
    rows, out_rows = weight_in.shape[0] // 3, weight_out.shape[0]
    return call(
        prepare_body,
        [scalars, weight_in, weight_expand, weight_out, tokens, lines],
        [shape((rows, D), BF16)] * 3
        + [
            shape(weight_expand.shape, BF16),
            shape((out_rows, D // 2), BF16),
            shape((out_rows, D // 2), BF16),
            shape(tokens.shape, BF16),
        ],
        [],
        60,
        "prepare",
    )


def kinds_body(total, scalars, first, second, third, out):
    place = scalars[PLACE]
    rows = first.shape[0]
    for slot, block in enumerate((first, second, third)):
        kind = ((slot + 3 * total - place) * total) % 3
        out[kind] = block[...]


def block_kinds(scalars, blocks, total):
    rows = blocks[0].shape[0]
    outs = [shape((3, rows, D), BF16)]
    return call(partial(kinds_body, total), [scalars, *blocks], outs, [], 8, "block_kinds")[0]


def spread(scalars, base, parts, masks, put):
    origin = scalars[base] if base is not None else 0
    for ref, own in zip(parts, masks):
        for r, mask in enumerate(own):
            put(origin ^ mask if base is not None else mask, ref[r])


def project_body(base, masks, cuts, scalars, mine, other, lines, *refs):
    parts, refs = refs[: len(masks)], refs[len(masks) :]
    pairs, refs = refs[: 2 * len(cuts)], refs[2 * len(cuts) :]
    out, weight_out, weight = refs[0], refs[1], refs[-1]
    join_pairs(pairs, refs[2:-1], cuts)
    weight[...] = jnp.zeros_like(weight)

    def put(place, chunk):
        rows = chunk.shape[0] // 3
        wide = chunk.astype(F32)
        for kind in range(3):
            start = kind * LANES + place * rows
            if base is not None:
                start = pl.multiple_of(start, 8)
            weight[pl.ds(start, rows), :] = wide[kind * rows : (kind + 1) * rows]

    spread(scalars, base, parts, masks, put)
    low = weight[...].astype(BF16)
    weight_out[...] = low
    piece = mine.shape[0] // 2
    here = scalars[HERE]
    bias = jnp.concatenate(
        [heads_row(lines, 4, here), jnp.zeros((1, LANES), F32), heads_row(lines, 5, here)], axis=1
    )
    for place, (source, lead) in enumerate(((mine, 0), (other, 0), (mine, piece), (other, piece))):
        rows = source[lead : lead + piece, :]
        out[place * piece : (place + 1) * piece, :] = (mm(rows, low, NT) + bias).astype(BF16)


def project(scalars, mine, other, lines, base, parts, masks, pairs, cuts, markers):
    rows = 2 * mine.shape[0]
    flat = [x for pair in pairs for x in pair]
    outs = [shape((rows, 3 * LANES), BF16), shape((3 * LANES, D), BF16), *join_shapes(pairs, cuts)]
    found = call(
        partial(project_body, base, masks, cuts),
        [scalars, mine, other, lines, *parts, *flat],
        outs,
        [pltpu.VMEM((3 * LANES, D), F32)],
        24,
        "project",
        markers=markers,
    )
    return found[0], found[1], found[2:]


def branch_body(base, masks, scalars, keep, across_t, *refs):
    parts, refs = refs[: len(masks)], refs[len(masks) :]
    sent_a, sent_b, kept, own_out, across_out, weight = refs
    width = own_out.shape[1]

    def put(place, chunk):
        rows = chunk.shape[0]
        start = pl.multiple_of(place * rows, 16) if base is not None else place * rows
        for group in range(2):
            weight[group, pl.ds(start, rows), :] = chunk[:, group * width : (group + 1) * width]

    spread(scalars, base, parts, masks, put)
    side = scalars[SIDE]
    own_out[...] = weight[side]
    across_out[...] = weight[1 - side]
    piece = kept.shape[0]
    def rows_of(columns):
        return mm(keep[:, columns].T, own_out[...], NT) + mm(across_t[:, columns].T, across_out[...], NT)

    half = piece // 2
    sent_a[...] = rows_of(slice(piece, piece + half)).astype(BF16)
    sent_b[...] = rows_of(slice(piece + half, 2 * piece)).astype(BF16)
    kept[...] = rows_of(slice(0, piece))


def middle_norm_body(scalars, tokens, kept, arrived_a, arrived_b, lines, middle, normed_a, normed_b):
    bias, gain, shift = vector_row(lines, 6), vector_row(lines, 2), vector_row(lines, 3)
    half = normed_a.shape[0]
    step = min(128, half)
    for lead, arrived, normed in ((0, arrived_a, normed_a), (half, arrived_b, normed_b)):
        for start in range(0, half, step):
            rows = slice(lead + start, lead + start + step)
            values = tokens[rows, :].astype(F32) + kept[rows, :]
            values = values + arrived[start : start + step, :].astype(F32) + bias
            middle[rows, :] = values
            unit, _ = row_norm(values)
            normed[start : start + step, :] = (unit * gain + shift).astype(BF16)


def middle_norm(scalars, tokens, kept, arrived, lines):
    piece = tokens.shape[0]
    return call(
        middle_norm_body,
        [scalars, tokens, kept, *arrived, lines],
        [shape((piece, D), F32), shape((piece // 2, D), BF16), shape((piece // 2, D), BF16)],
        [],
        16,
        "middle_norm",
    )


def branch(scalars, keep, across_t, base, parts, masks, markers):
    width, rows = keep.shape
    piece = rows // 2
    return call(
        partial(branch_body, base, masks),
        [scalars, keep, across_t, *parts],
        [shape((piece // 2, D), BF16)] * 2
        + [shape((piece, D), F32), shape((D, width), BF16), shape((D, width), BF16)],
        [pltpu.VMEM((2, D, width), BF16)],
        24,
        "branch",
        markers=markers,
    )


MLP_ROWS = 256
MLP_LANES = 512


def feed_body(
    bases, masks, count, scalars, own_a, own_b, other_a, other_b, grad_own, grad_other, lines, *refs
):
    parts, refs = refs[: sum(map(len, masks))], refs[sum(map(len, masks)) :]
    activated, grad_hidden, normed_sent, normed_kept, out_sent, out_kept, sums, pair, grad_pair = refs[:9]
    expand, contract = refs[9:]
    half = expand.shape[0]
    piece = grad_own.shape[0]
    for lead, rows in enumerate((own_a, own_b, other_a, other_b)):
        pair[lead * (piece // 2) : (lead + 1) * (piece // 2), :] = rows[...]
    grad_pair[:piece, :] = grad_own[...]
    grad_pair[piece:, :] = grad_other[...]
    bias = lines_row(lines, 8 * (D // 128) + scalars[CORE] * (half // 128), half // 128)

    def put_expand(index):
        def put(place, chunk):
            rows = chunk.shape[0]
            start = place * 2 * rows + index * rows
            if bases[index] is not None:
                start = pl.multiple_of(start, 16)
            expand[pl.ds(start, rows), :] = chunk

        return put

    def put_contract(place, chunk):
        rows = chunk.shape[0]
        start = pl.multiple_of(place * rows, 16) if bases[-1] is not None else place * rows
        contract[pl.ds(start, rows), :] = chunk

    taken = 0
    for index, own_masks in enumerate(masks):
        put = put_contract if index == len(masks) - 1 else put_expand(index)
        spread(scalars, bases[index], parts[taken : taken + len(own_masks)], own_masks, put)
        taken += len(own_masks)
    sums[...] = jnp.zeros_like(sums)
    step = min(MLP_ROWS, piece)

    def block(start, lead, normed_out, contract_out):
        rows = pl.ds(start, step)
        target = pl.ds(pl.multiple_of(lead + start, step), step)
        normed = pair[target, :]
        grad = grad_pair[target, :]
        back = jnp.zeros((step, D), F32)
        result = jnp.zeros((step, D), F32)
        for lanes in range(0, half, MLP_LANES):
            span = slice(lanes, lanes + MLP_LANES)
            expanded = mm(normed, expand[span, :], NT) + bias[:, span]
            squared = expanded * expanded
            bent = jnp.tanh(ROOT_TWO_OVER_PI * (expanded + 0.044715 * (expanded * squared)))
            rise = 0.5 * (1.0 + bent)
            act = (expanded * rise).astype(BF16)
            slope = rise + (0.5 * ROOT_TWO_OVER_PI) * expanded * (1.0 - bent * bent) * (
                1.0 + (3.0 * 0.044715) * squared
            )
            hidden = (mm(grad, contract[:, span], NN) * slope).astype(BF16)
            activated[target, span] = act
            grad_hidden[target, span] = hidden
            sums[0:1, span] += jnp.sum(hidden.astype(F32), axis=0, keepdims=True)
            back = back + mm(hidden, expand[span, :], NN)
            result = result + mm(act, contract[:, span], NT)
        normed_out[rows, :] = back.astype(normed_out.dtype)
        contract_out[rows, :] = result.astype(contract_out.dtype)

    def own_block(i, carry):
        start = pl.multiple_of(i * step, step)
        block(start, 0, normed_kept, out_kept)
        return carry

    def other_block(i, carry):
        start = pl.multiple_of(i * step, step)
        block(start, piece, normed_sent, out_sent)
        return carry

    lax.fori_loop(0, piece // step, other_block, 0)
    lax.fori_loop(0, piece // step, own_block, 0)


def feed_forward(scalars, normed, grads, lines, bases, parts, masks):
    piece = grads[0].shape[0]
    half = FF // 2
    flat = [x for group in parts for x in group]
    return call(
        partial(feed_body, bases, masks, len(flat)),
        [scalars, *normed, *grads, lines, *flat],
        [
            shape((2 * piece, half), BF16),
            shape((2 * piece, half), BF16),
            shape((piece, D), BF16),
            shape((piece, D), F32),
            shape((piece, D), BF16),
            shape((piece, D), F32),
            shape((8, half), F32),
            shape((2 * piece, D), BF16),
            shape((2 * piece, D), BF16),
        ],
        [pltpu.VMEM((half, D), BF16), pltpu.VMEM((D, half), BF16)],
        36,
        "feed_forward",
    )


def head_grads_body(scalars, own, other, weight_own, weight_across, keep, sent):
    piece = own.shape[0]
    for matrix, out in ((weight_across, sent), (weight_own, keep)):
        for place, rows in enumerate((own, other)):
            features = mm(rows[...], matrix[...], NN).T.astype(BF16)
            out[:, place * piece : (place + 1) * piece] = features


def head_grads(scalars, grads, weight_own, weight_across):
    piece = grads[0].shape[0]
    outs = [shape((weight_own.shape[1], 2 * piece), BF16)] * 2
    return call(head_grads_body, [scalars, *grads, weight_own, weight_across], outs, [], 24, "head_gradients")


def output_weight_body(scalars, own, other, keep, across_t, out, stacked):
    side = scalars[SIDE]
    piece = own.shape[0]
    width = keep.shape[0]
    for place, features in ((side, keep), (1 - side, across_t)):
        product = mm(features[:, :piece], own[...], NN) + mm(features[:, piece:], other[...], NN)
        stacked[pl.ds(pl.multiple_of(place * width, 8), width), :] = product
    out[...] = stacked[...].T.astype(out.dtype)


def output_weight_grad(scalars, grads, keep, across_t, markers):
    width = keep.shape[0]
    return call(
        output_weight_body,
        [scalars, *grads, keep, across_t],
        [shape((D, 2 * width), BF16)],
        [pltpu.VMEM((2 * width, D), F32)],
        24,
        "output_weight_gradient",
        markers=markers,
    )[0]


def input_weight_body(aligned, rows_of_devices, scalars, grads, mine, other, *refs):
    total = refs[-1]
    piece = mine.shape[0] // 2
    step = min(MLP_ROWS, piece)
    total[...] = jnp.zeros_like(total)
    for place, (source, lead) in enumerate(((mine, 0), (other, 0), (mine, piece), (other, piece))):
        for start in range(0, piece, step):
            rows = grads[place * piece + start : place * piece + start + step, :]
            total[...] += mm(rows.T, source[lead + start : lead + start + step, :], NN)
    if not aligned:
        natural = refs[0]
        for kind in range(3):
            natural[kind] = total[kind * LANES : kind * LANES + natural.shape[1], :]
        return
    rows = refs[0].shape[1]
    half = D // 2
    row = scalars[ROW]
    for part, position in enumerate((0, 1)):
        sent, kept = refs[2 * part], refs[2 * part + 1]
        columns = slice(part * half, (part + 1) * half)
        low = 1 << position
        bit = (row >> position) & 1
        count = rows_of_devices // 2
        for kind in range(3):
            for e in range(count):
                base = (e // low) * 2 * low + e % low
                for out, chosen in ((sent, 1 - bit), (kept, bit)):
                    start = kind * LANES + (base + chosen * low) * rows
                    block = total[pl.ds(pl.multiple_of(start, 8), rows), columns]
                    out[kind * count + e] = block.astype(out.dtype)


def input_weight_grad(scalars, grads, mine, other, rows_of_devices, block):
    aligned = block % 8 == 0
    part = (3 * rows_of_devices // 2, block, D // 2)
    outs = [shape(part, BF16), shape(part, F32)] * 2
    if not aligned:
        outs = [shape((3, block * rows_of_devices, D), F32)]
    return call(
        partial(input_weight_body, aligned, rows_of_devices),
        [scalars, grads, mine, other],
        outs,
        [pltpu.VMEM((3 * LANES, D), F32)],
        32,
        "input_weight_gradient",
    )


def first_grads_body(places, scalars, grads, weight, *refs):
    *far, sent, kept = refs
    piece = sent.shape[0]
    if far:
        far_kept, far_arrived, reduced = far
        reduced[...] = (far_kept[...] + far_arrived[...].astype(F32)).astype(BF16)
    for place, out in zip(places, (sent, kept)):
        out[...] = mm(grads[place * piece : (place + 1) * piece, :], weight[...], NN).astype(out.dtype)


def first_grads(scalars, grads, weight, places, far=(), markers=()):
    piece = grads.shape[0] // 4
    outs = [shape((piece, D), BF16), shape((piece, D), F32)]
    return call(
        partial(first_grads_body, places),
        [scalars, grads, weight, *far],
        outs[:1] * bool(far) + outs,
        [],
        20,
        "first_norm_gradient",
        markers=markers,
    )


def payload_body(hidden_rows, scalars, left, right, expand, contract, first, middle, heads, hidden, out):
    six = D // 128
    out[...] = jnp.zeros_like(out)
    out[: 2 * six, :] = first[: 2 * six, :]
    out[2 * six : 4 * six, :] = middle[: 2 * six, :]
    out[6 * six : 8 * six, :] = middle[2 * six : 4 * six, :]
    here = scalars[HERE]
    for line in range(2):
        row = heads[line : line + 1, :]
        row = jnp.where(here % 2 == 1, pltpu.roll(row, HD, 1), row)
        start = (4 + line) * six + (3 * here) // 2
        for part in range(2):
            out[pl.ds(start + part, 1), :] = row[:, part * 128 : (part + 1) * 128]
    for part in range(hidden_rows):
        line = 8 * six + scalars[CORE] * hidden_rows + part
        out[pl.ds(line, 1), :] = hidden[0:1, part * 128 : (part + 1) * 128]
    total = jnp.zeros((1, 1), F32)
    for gradients in (left, right, expand, contract):
        for i in range(gradients.shape[0]):
            values = gradients[i]
            rows = jnp.sum(values * values, axis=1, keepdims=True)
            total += jnp.sum(rows, axis=0, keepdims=True)
    lane = lax.broadcasted_iota(jnp.int32, (1, 128), 1)
    out[VECTOR_ROWS : VECTOR_ROWS + 1, :] = jnp.where(lane == 0, total, 0.0)


def make_payload(scalars, gradients, first, middle, heads, hidden):
    return call(
        partial(payload_body, hidden.shape[1] // 128),
        [scalars, *gradients, first, middle, heads, hidden],
        [shape((VECTOR_ROWS + 8, 128), F32)],
        [],
        16,
        "payload",
    )[0]


def reduce_body(plans, scalars, *refs):
    count = 2 * sum(len(sources) for sources, _ in plans)
    ins, outs = list(refs[:count]), list(refs[count:])
    for sources, split in plans:
        terms = []
        column = 0
        for full in sources:
            kept, arrived = ins.pop(0), ins.pop(0)
            columns = slice(column, column + arrived.shape[2])
            column += arrived.shape[2]

            def total(index, kept=kept, arrived=arrived, full=full):
                source = index
                if full is not None:
                    which, shift, size = full
                    bit = (scalars[which] >> shift) & 1
                    source = (index // size) * 2 * size + bit * size + index % size
                return kept[source].astype(F32) + arrived[index].astype(F32)

            terms.append((columns, total))
        if split is None:
            out = outs.pop(0)

            def whole(m, carry, out=out, terms=terms):
                for columns, total in terms:
                    out[m, :, columns] = total(m)
                return carry

            lax.fori_loop(0, out.shape[0], whole, 0)
        else:
            which, shift, size = split
            sent_out, kept_out = outs.pop(0), outs.pop(0)

            def halves(m, carry, sent_out=sent_out, kept_out=kept_out, terms=terms):
                bit = (scalars[which] >> shift) & 1
                base = (m // size) * 2 * size + m % size
                for columns, total in terms:
                    kept_out[m, :, columns] = total(base + bit * size)
                    sent_out[m, :, columns] = total(base + (1 - bit) * size).astype(BF16)
                return carry

            lax.fori_loop(0, kept_out.shape[0], halves, 0)


HEAD_LANES = LANES


VECTOR_ROWS = (8 * D + FF) // 128


def row_norm(values):
    mean = jnp.mean(values, axis=1, keepdims=True)
    centered = values - mean
    variance = jnp.mean(centered * centered, axis=1, keepdims=True)
    inverse = lax.rsqrt(variance + NORM_EPS)
    return centered * inverse, inverse


def norm_input_gradient(upstream, values, gain):
    unit, inverse = row_norm(values)
    scaled = upstream * gain
    first = jnp.mean(scaled, axis=1, keepdims=True)
    second = jnp.mean(scaled * unit, axis=1, keepdims=True)
    return inverse * (scaled - first - unit * second), unit


def stack_rows(sums, rows):
    for place, row in enumerate(rows):
        total = jnp.sum(row, axis=0, keepdims=True)
        for part in range(D // 128):
            line = place * (D // 128) + part
            sums[line : line + 1, :] += total[:, part * 128 : (part + 1) * 128]


def middle_body(own, arrived, middle, cotangent, lines, grad_mid, grad_branch, sums):
    @pl.when(pl.program_id(0) == 0)
    def _():
        sums[...] = jnp.zeros_like(sums)

    upstream = own[...] + arrived[...].astype(F32)
    passed, unit = norm_input_gradient(upstream, middle[...], vector_row(lines, 2))
    outer = cotangent[...].astype(F32)
    total = outer + passed
    rounded = total.astype(BF16)
    grad_mid[...] = total
    grad_branch[...] = rounded
    stack_rows(sums, [upstream * unit, upstream, rounded.astype(F32), outer])


def first_body(own, arrived, across, tokens, grad_mid, lines, input_grad, sums):
    @pl.when(pl.program_id(0) == 0)
    def _():
        sums[...] = jnp.zeros_like(sums)

    upstream = own[...] + arrived[...].astype(F32) + across[...].astype(F32)
    passed, unit = norm_input_gradient(upstream, tokens[...].astype(F32), vector_row(lines, 0))
    input_grad[...] = (grad_mid[...] + passed).astype(BF16)
    stack_rows(sums, [upstream * unit, upstream])


def norm_backward(body, arrays, lines, outputs, name):
    rows = arrays[0].shape[0]
    step = min(128, rows)
    tile = pl.BlockSpec((step, D), lambda i: (i, 0))
    row = pl.BlockSpec(lines.shape, lambda i: (0, 0))
    sums = pl.BlockSpec((24, 128), lambda i: (0, 0))
    return pl.pallas_call(
        body,
        grid=(rows // step,),
        out_shape=tuple(jax.ShapeDtypeStruct((rows, D), kind) for kind in outputs)
        + (jax.ShapeDtypeStruct((24, 128), F32),),
        in_specs=[tile] * len(arrays) + [row],
        out_specs=tuple(tile for _ in outputs) + (sums,),
        compiler_params=pltpu.CompilerParams(vmem_limit_bytes=24 * 2**20),
        cost_estimate=cost(name),
        name=name,
    )(*arrays, lines)


def moments_body(*refs):
    payload, refs = refs[0], refs[1:]
    grads, firsts, seconds, masters = refs[0:5], refs[5:10], refs[10:15], refs[15:20]
    first_outs, second_outs, direction_outs = refs[20:25], refs[25:30], refs[30:35]
    squares = refs[35]
    vector = payload[0:VECTOR_ROWS, :]
    total = payload[VECTOR_ROWS : VECTOR_ROWS + 1, 0:1] + jnp.sum(
        jnp.sum(vector * vector, axis=1, keepdims=True), axis=0, keepdims=True
    )
    clip = jnp.minimum(1.0, 1.0 / jnp.sqrt(total))
    correction = 1.0 - 0.5**STEP
    lane = lax.broadcasted_iota(jnp.int32, squares.shape, 1)
    row = lax.broadcasted_iota(jnp.int32, squares.shape, 0)
    found = jnp.zeros(squares.shape, F32)
    for place in range(5):
        gradient = grads[place][...] if place < 4 else vector
        master = masters[place][...]
        clipped = gradient * clip
        first_new = 0.5 * firsts[place][...] + 0.5 * clipped
        second_new = 0.5 * seconds[place][...] + 0.5 * clipped * clipped
        direction = (
            first_new / correction / (jnp.sqrt(second_new / correction) + ADAM_EPS)
            + DECAY_RATE * master
        )
        first_outs[place][...] = first_new
        second_outs[place][...] = second_new
        if place < 4:
            direction_outs[place][...] = direction
            for offset, values in ((0, direction), (4, master)):
                square = jnp.sum(
                    jnp.sum(values * values, axis=1, keepdims=True), axis=0, keepdims=True
                )
                found = found + jnp.where((lane == place + offset) & (row == 0), square, 0.0)
        else:
            direction_outs[place][...] = master - VECTOR_RATE * direction
    squares[...] = found


def moments_step(payload, grads, firsts, seconds, masters):
    vmem = pl.BlockSpec(memory_space=pltpu.VMEM)
    shapes = [jax.ShapeDtypeStruct(master.shape, F32) for master in masters]
    outs = pl.pallas_call(
        moments_body,
        out_shape=tuple(shapes * 3) + (jax.ShapeDtypeStruct((8, 128), F32),),
        in_specs=[vmem] * 21,
        out_specs=(vmem,) * 16,
        compiler_params=pltpu.CompilerParams(vmem_limit_bytes=60 * 2**20),
        cost_estimate=cost("moments"),
        name="moments",
    )(payload, *grads, payload, *firsts, *seconds, *masters)
    return outs[0:5], outs[5:10], outs[10:15], outs[15]


def weights_body(*refs):
    squares, refs = refs[0], refs[1:]
    directions, masters, outs, lows = refs[0:4], refs[4:8], refs[8:12], refs[12:16]
    norms = refs[16]
    norms[...] = jnp.zeros_like(norms)
    weight = jnp.sqrt(squares[0:1, 4:8])
    update = jnp.sqrt(squares[0:1, 0:4])
    for place in range(4):
        ratio = MATRIX_RATE * (weight[:, place : place + 1] / update[:, place : place + 1])
        new = masters[place][...] - ratio * directions[place][...]
        outs[place][...] = new
        lows[place][...] = new.astype(BF16)
    norms[0:1, 0:4] = weight
    norms[1:2, 0:4] = update


def weights_step(squares, directions, masters):
    vmem = pl.BlockSpec(memory_space=pltpu.VMEM)
    outs = pl.pallas_call(
        weights_body,
        out_shape=tuple(jax.ShapeDtypeStruct(m.shape, F32) for m in masters)
        + tuple(jax.ShapeDtypeStruct(m.shape, BF16) for m in masters)
        + (jax.ShapeDtypeStruct((8, 128), F32),),
        in_specs=[vmem] * 9,
        out_specs=(vmem,) * 9,
        compiler_params=pltpu.CompilerParams(vmem_limit_bytes=60 * 2**20),
        cost_estimate=cost("weights"),
        name="weights",
    )(squares, *directions, *masters)
    return outs[0:4], outs[4:8], outs[8]


BOTH = ("batch", "head")
PARTNER = 1
ACROSS = 2


def dot(a, b, dims):
    return lax.dot_general(a, b, (dims, ((), ())), preferred_element_type=F32)


def swap(values, axis, mask):
    size = lax.axis_size(axis)
    return lax.ppermute(values, axis, [(place, place ^ mask) for place in range(size)])


def partner(values):
    return swap(values, "head", PARTNER)


def across(values):
    return swap(values, "head", ACROSS)


def batch_masks():
    return [1 << bit for bit in range((lax.axis_size("batch") - 1).bit_length())][::-1]


class Chain:
    def __init__(self, scalars, chunk, order, chips):
        self.scalars, self.values, self.order, self.chips = scalars, chunk[None], list(order), chips
        self.masks, self.flip, self.arrived = [0], 0, None

    def start(self):
        axis, mask = self.order.pop(0)
        self.flip = mask if not self.chips else (2 * mask if axis == "batch" else 1)
        self.arrived = swap(self.values, axis, mask)

    def pair(self):
        return self.values, self.arrived

    def take(self, joined):
        self.values = joined
        self.masks = self.masks + [mask ^ self.flip for mask in self.masks]
        self.arrived = None
        if self.order:
            self.start()

    def drain(self, left):
        while len(self.order) > left:
            self.take(join(self.scalars, [self.pair()], [0])[0])

    def halves(self, joined, orders):
        chains = []
        for values, order in zip(joined, orders):
            chain = Chain(self.scalars, values[0], order, self.chips)
            chain.values = values
            chain.masks = self.masks + [mask ^ self.flip for mask in self.masks]
            chain.start()
            chains.append(chain)
        return chains

    def parts(self, multiple, kinds=1):
        rows = self.values.shape[1] // kinds
        source = CHIP if self.chips else ROW
        arrays, masks = [self.values], [self.masks]
        if self.arrived is not None:
            arrays.append(self.arrived)
            masks.append([mask ^ self.flip for mask in self.masks])
        if rows % multiple == 0:
            return source, arrays, masks
        chunks = [array[r] for array in arrays for r in range(array.shape[0])]
        order = [mask for group in masks for mask in group]
        count = len(order)
        natural = jnp.stack([chunks[order.index(place)] for place in range(count)])
        size = 1
        while size < count:
            cut = natural.reshape((-1, 2, size) + natural.shape[1:])
            flipped = jnp.concatenate([cut[:, 1:], cut[:, :1]], axis=1)
            cut = jnp.where((self.scalars[source] & size) != 0, flipped, cut)
            natural = cut.reshape(natural.shape)
            size *= 2
        natural = natural.reshape(count, kinds, rows, -1).transpose(1, 0, 2, 3)
        return None, [natural.reshape(1, kinds * count * rows, -1)], [[0]]


def join_all(scalars, chains, extra=(), markers=()):
    pairs = [chain.pair() for chain in chains] + list(extra)
    joined = join(scalars, pairs, [0] * len(pairs), markers)
    for chain, values in zip(chains, joined):
        chain.take(values)
    return joined[len(chains) :]


def bit_source(bit):
    axis, mask = bit
    return (ROW, mask.bit_length() - 1) if axis == "batch" else (SIDE, 0)


class Reduce:
    def __init__(self, bits, order, *values):
        self.left, self.order, self.values, self.full = list(bits), list(order), values, None

    def split(self):
        bit = self.order.pop(0)
        size = 1 << (len(self.left) - 1 - self.left.index(bit))
        self.left.remove(bit)
        self.bit = bit
        return (*bit_source(bit), size)

    def begin(self, scalars):
        self.full = self.split()
        self.sources = []
        for values in self.values:
            self.send(scalars, values)

    def send(self, scalars, values):
        which, shift, size = self.full
        bit = (scalars[which] >> shift) & 1
        rows = values.shape[1:]
        cut = values.reshape((-1, 2, size) + rows)
        sent = lax.dynamic_index_in_dim(cut, 1 - bit, 1, keepdims=False).reshape((-1,) + rows)
        self.sources.append((values, swap(sent.astype(BF16), *self.bit)))

    def begin_with(self, sent, kept):
        self.full = None
        self.sources = [(kept, swap(sent, *self.bit))]

    @property
    def kept(self):
        return self.sources[0][0]


def reduce_all(scalars, chains, markers=()):
    plans, inputs, outs = [], [scalars], []
    for chain in chains:
        full = chain.full
        for source in chain.sources:
            inputs += source
        plan = chain.split() if chain.order else None
        plans.append(([full] * len(chain.sources), plan))
        count, rows, _ = chain.sources[0][1].shape
        columns = sum(arrived.shape[2] for _, arrived in chain.sources)
        if plan is None:
            outs.append(shape((count, rows, columns), F32))
        else:
            outs.append(shape((count // 2, rows, columns), BF16))
            outs.append(shape((count // 2, rows, columns), F32))
    found = list(call(partial(reduce_body, plans), inputs, outs, [], 40, "add_arrived", markers=markers))
    for chain, (_, plan) in zip(chains, plans):
        if plan is None:
            chain.values = found.pop(0)
        else:
            sent, kept = found.pop(0), found.pop(0)
            chain.begin_with(sent, kept)


def all_sum(values):
    for mask in (PARTNER, ACROSS):
        values = values + swap(values, "head", mask)
    masks = batch_masks()[::-1]
    if len(masks) % 2:
        values = values + swap(values, "batch", masks[0])
        masks = masks[1:]
    for low, high in zip(masks[::2], masks[1::2]):
        near = values + swap(values, "batch", low)
        far = swap(values, "batch", high) + swap(values, "batch", low | high)
        values = near + far
    return values


def block_permutation(slot, to_owner):
    rows, heads = lax.axis_size("batch"), lax.axis_size("head")
    total = rows * heads
    pairs = []
    for owner in range(total):
        place = (3 * owner + slot) % total
        holder = (place % rows) * heads + place // rows
        pairs.append((holder, owner) if to_owner else (owner, holder))
    return pairs


def holder_place():
    return lax.axis_size("batch") * lax.axis_index("head") + lax.axis_index("batch")


def blocks_to_holders(shard):
    blocks = shard.reshape(3, -1, D)
    return [lax.ppermute(blocks[slot], BOTH, block_permutation(slot, False)) for slot in range(3)]


def blocks_to_owners(blocks):
    total = lax.axis_size("batch") * lax.axis_size("head")
    place = holder_place()
    arrived = []
    for slot in range(3):
        kind = ((slot + 3 * total - place) * total) % 3
        sent = lax.dynamic_index_in_dim(blocks, kind, 0, keepdims=False)
        arrived.append(lax.ppermute(sent, BOTH, block_permutation(slot, True)))
    return jnp.concatenate(arrived, axis=0)


def on_device(
    tokens,
    cotangent,
    lengths,
    input_weight,
    output_weight,
    expand_weight,
    contract_weight,
    vector_params,
    input_first,
    input_second,
    output_first,
    output_second,
    expand_first,
    expand_second,
    contract_first,
    contract_second,
    vector_first,
    vector_second,
):
    rows_of_devices = lax.axis_size("batch")
    head_count = lax.axis_size("head")
    chips = rows_of_devices * head_count // 2
    here = lax.axis_index("head")
    core = here % 2
    side = here // 2
    width = D // head_count
    heads = width // HD
    piece = tokens.shape[0]
    docs = lengths.shape[1]
    hidden_block = FF // (2 * chips)
    half = FF // 2
    out_rows = output_weight.shape[0]
    total_devices = rows_of_devices * head_count
    batch_bits = [("batch", mask) for mask in batch_masks()]
    far, near = batch_bits[:-1], batch_bits[-1]
    side_bit = ("head", ACROSS)
    bits = batch_bits + [side_bit]
    bias_contract = vector_params[7 * D : 8 * D]

    def by_core(mine, other, axis):
        high = core == 1
        return jnp.stack([jnp.where(high, other, mine), jnp.where(high, mine, other)], axis=axis)

    def pick(values, index, axis):
        return lax.dynamic_index_in_dim(values, index, axis, keepdims=False)

    scalars, sequences = Places(), Places(lengths)
    lines = vector_params.reshape(VECTOR_ROWS, 128)

    *in_blocks, expand_low, output_mine, output_cut, normed_own = prepare(
        scalars, input_weight, expand_weight, output_weight, tokens, lines
    )
    in_arrived = [
        lax.ppermute(block, BOTH, block_permutation(slot, False)) for slot, block in enumerate(in_blocks)
    ]
    expands = Chain(scalars, expand_low, far, True)
    expands.start()
    normed_across = across(normed_own)
    output_other = partner(output_cut)
    contract_cut = contract_weight.astype(BF16).reshape(out_rows, chips, 2, hidden_block)
    contract_other = partner(pick(contract_cut, 1 - core, 2))
    contract_shard = by_core(pick(contract_cut, core, 2), contract_other, 0).reshape(2 * out_rows, half)
    output_shard = by_core(output_mine, output_other, 0).reshape(2 * out_rows, 2 * width)
    contracts = Chain(scalars, contract_shard, [near, side_bit] + far, True)
    contracts.start()

    kinds = block_kinds(scalars, in_arrived, total_devices).reshape(-1, D)
    inputs = Chain(scalars, kinds, batch_bits, False)
    outputs = Chain(scalars, output_shard, far + [near, side_bit], True)
    inputs.start()
    outputs.start()
    inputs.drain(2)
    outputs.drain(3)
    join_all(scalars, [inputs, outputs, contracts], (), (expands.arrived,))
    expands.drain(1)
    (normed_mine,) = join_all(
        scalars, [inputs, outputs, contracts, expands], [(normed_own, normed_across)]
    )
    contracts.drain(1)
    normed_other = partner(normed_mine)

    def cores_first(vectors):
        hidden = vectors[:, 8 * D :].reshape(-1, chips, 2, hidden_block).transpose(0, 2, 1, 3)
        return jnp.concatenate([vectors[:, : 8 * D], hidden.reshape(-1, FF)], axis=1).reshape(-1, VECTOR_ROWS, 128)

    def cores_back(rows):
        vectors = rows.reshape(-1, 8 * D + FF)
        hidden = vectors[:, 8 * D :].reshape(-1, 2, chips, hidden_block).transpose(0, 2, 1, 3)
        return jnp.concatenate([vectors[:, : 8 * D], hidden.reshape(-1, FF)], axis=1)

    vector_state = cores_first(jnp.stack([vector_first, vector_second, vector_params]))
    projected, weight_in, joined = project(
        scalars,
        normed_mine,
        normed_other,
        lines,
        *inputs.parts(8, 3),
        [outputs.pair(), expands.pair()],
        [0, 2],
        (vector_state,),
    )
    outputs.take(joined[0])
    expands = expands.halves(joined[1:], ([near, side_bit], [side_bit, near]))

    keep_t, send_t, logs = attention_forward(sequences, projected, heads, 0, docs, piece, [], [])[0]
    across_t = across(send_t)
    join_all(scalars, [*expands, contracts, outputs], (), (keep_t,))
    *branch_sent, branch_kept, output_own, output_across = branch(
        scalars, keep_t, across_t, *outputs.parts(16), (contracts.values,)
    )
    resid_mid, *normed_two = middle_norm(
        scalars, tokens, branch_kept, [partner(rows) for rows in branch_sent], lines
    )
    arrived_two = [partner(rows) for rows in normed_two]
    cotangent_other = partner(cotangent)

    found = [chain.parts(16) for chain in (*expands, contracts)]
    activated, grad_hidden, normed_sent, normed_kept, out_sent, out_kept, hidden_sums, *pairs = feed_forward(
        scalars,
        (*normed_two, *arrived_two),
        (cotangent, cotangent_other),
        vector_state[2],
        [part[0] for part in found],
        [part[1] for part in found],
        [part[2] for part in found],
    )
    normed_arrived = partner(normed_sent)
    out_arrived = partner(out_sent)
    block_out = (resid_mid + out_kept + out_arrived.astype(F32) + bias_contract).astype(BF16)

    normed_pair, cotangent_pair = pairs
    expand_sum = Reduce(
        bits,
        [near] + far[-1:] + [side_bit] + far[:-1][::-1],
        dot(grad_hidden, normed_pair, ((0,), (0,))).astype(BF16).reshape(chips, hidden_block, D),
    )
    expand_sum.begin(scalars)
    grad_mid, grad_branch, middle_sums = norm_backward(
        middle_body,
        [normed_kept, normed_arrived, resid_mid, cotangent],
        lines,
        (F32, BF16),
        "middle_gradient",
    )
    grads = (grad_branch, partner(grad_branch))
    contract_total = dot(cotangent_pair, activated, ((0,), (0,))).astype(BF16)
    contract_sum = Reduce(
        bits, far[-1:] + [near, side_bit] + far[:-1][::-1], contract_total.reshape(chips, 2 * out_rows, half)
    )
    contract_sum.begin(scalars)

    grad_keep_t, grad_sent_t = head_grads(scalars, grads, output_own, output_across)
    grad_arrived_t = across(grad_sent_t)
    output_total = output_weight_grad(scalars, grads, keep_t, across_t, (grad_sent_t,))
    contract_sum.send(scalars, output_total.reshape(chips, 2 * out_rows, 2 * width))
    sums = [expand_sum, contract_sum]
    grad_heads, head_sums = attention_backward(
        sequences, projected, (keep_t, send_t), (grad_keep_t, grad_arrived_t), logs, heads, 0, docs, piece,
        [chain.sources[-1][0] for chain in sums],
    )

    far_sent, far_kept = first_grads(scalars, grad_heads, weight_in, (3, 2))
    far_arrived = partner(far_sent)
    in_found = input_weight_grad(
        scalars, grad_heads, normed_mine, normed_other, rows_of_devices, D // total_devices
    )
    in_orders = ([near] + far[::-1], far[::-1] + [near])
    if len(in_found) == 4:
        in_sums = [Reduce(batch_bits, order) for order in in_orders]
        for part, sent, kept in zip(in_sums, in_found[::2], in_found[1::2]):
            part.split()
            part.begin_with(sent, kept)
    else:
        natural = in_found[0].reshape(3 * rows_of_devices, -1, D)
        in_sums = [
            Reduce(batch_bits, in_orders[0], natural[..., : D // 2]),
            Reduce(batch_bits, in_orders[1], natural[..., D // 2 :]),
        ]
        for part in in_sums:
            part.begin(scalars)
    reduced_far, near_sent, near_kept = first_grads(
        scalars, grad_heads, weight_in, (1, 0), (far_kept, far_arrived), (in_sums[0].kept,)
    )
    first_arrived = across(reduced_far)
    near_arrived = partner(near_sent)
    reduce_all(scalars, sums, (reduced_far,))
    while in_sums[0].order:
        reduce_all(scalars, in_sums, (sums[0].kept,))
        if sums[0].order:
            reduce_all(scalars, sums, (in_sums[0].kept,))
    while sums[0].order:
        reduce_all(scalars, sums)
    reduce_all(scalars, in_sums, (first_arrived,))
    reduce_all(scalars, sums, (in_sums[0].values,))
    expand_grad = expand_sum.values.reshape(hidden_block, D)
    contract_mixed = contract_sum.values[0, :, :half]
    output_mixed = contract_sum.values[0, :, half:]
    in_blocks = jnp.concatenate([part.values for part in in_sums], axis=-1)

    def columns_other(mixed, parts):
        cut = mixed.reshape(2, out_rows, parts, -1)
        return pick(cut, core, 0), partner(pick(cut, 1 - core, 0))

    contract_grad = by_core(*columns_other(contract_mixed, chips), 2).reshape(out_rows, -1)
    output_grad = by_core(*columns_other(output_mixed, 2), 2).reshape(out_rows, -1)
    input_piece_grad = blocks_to_owners(in_blocks)
    input_grad, first_sums = norm_backward(
        first_body,
        [near_kept, near_arrived, first_arrived, tokens, grad_mid],
        lines,
        (BF16,),
        "first_gradient",
    )

    masters = (input_weight, output_weight, expand_weight, contract_weight)
    gradients = [part.values for part in (*in_sums, expand_sum, contract_sum)]
    payload = all_sum(
        make_payload(scalars, gradients, first_sums, middle_sums, head_sums, hidden_sums)
    )
    vector_grads = payload[:VECTOR_ROWS]
    grad_norm = jnp.sqrt(payload[VECTOR_ROWS, 0] + jnp.sum(vector_grads * vector_grads))
    first_new, second_new, directions, squares = moments_step(
        payload,
        (input_piece_grad, output_grad, expand_grad, contract_grad),
        (input_first, output_first, expand_first, contract_first, vector_state[0]),
        (input_second, output_second, expand_second, contract_second, vector_state[1]),
        (*masters, vector_state[2]),
    )
    squares = all_sum(squares)
    vector_news = cores_back(jnp.stack([first_new[4], second_new[4], directions[4]]))
    news, lows, norms = weights_step(squares, directions[:4], masters)
    results = []
    for position in range(4):
        results += [first_new[position], second_new[position], news[position], lows[position]]
    return (
        block_out,
        input_grad,
        grad_norm,
        norms[:2, :4].reshape(8),
        *results,
        vector_news[0],
        vector_news[1],
        vector_news[2],
    )


def solution(mesh):
    split = P(BOTH, None)
    return jax.shard_map(
        on_device,
        mesh=mesh,
        in_specs=(split, split, P("batch", None)) + (split,) * 4 + (P(),) + (split,) * 8 + (P(), P()),
        out_specs=(split, split, P(), P()) + (split,) * 16 + (P(), P(), P()),
        check_vma=False,
    )
```

```python
from functools import partial
import jax
import jax.numpy as jnp
from jax import lax
from jax.experimental import pallas as pl
from jax.experimental.pallas import tpu as pltpu
from jax.sharding import PartitionSpec as P

D = 768
HD = 64
FF = 3072
STEP = 5
NORM_EPS = 1e-05
ADAM_EPS = 1e-06
DECAY_RATE = 0.01
MATRIX_RATE = 0.5
VECTOR_RATE = 0.1
ROOT_TWO_OVER_PI = (2.0 / 3.141592653589793) ** 0.5
BLOCK = 256
LANES = 256
NT = (((1,), (1,)), ((), ()))
NN = (((1,), (0,)), ((), ()))
F32 = jnp.float32
BF16 = jnp.bfloat16


def mm(a, b, dims):
    return lax.dot_general(a, b, dims, preferred_element_type=F32)


def block_start(index, per_piece, me):
    piece = index // per_piece
    return pl.multiple_of(((piece ^ me) * per_piece + index % per_piece) * BLOCK, BLOCK)


def starts_of(scalars, docs, positions):
    first = jnp.zeros_like(positions)
    for doc in range(docs - 1):
        end = scalars[ENDS + doc]
        first = jnp.where(positions >= end, end, first)
    return first


def first_block(scalars, docs, index):
    position = index * BLOCK
    first = jnp.int32(0)
    for doc in range(docs - 1):
        end = scalars[ENDS + doc]
        first = jnp.where(position >= end, end, first)
    return first // BLOCK


def head_lanes(block, heads):
    if heads == 1:
        return [block]
    lane = lax.broadcasted_iota(jnp.int32, block.shape, 1) // HD
    return [jnp.where(lane == j, block, jnp.zeros_like(block)) for j in range(heads)]


def allowed_mask(index, key_block, doc_first):
    query = index * BLOCK + lax.broadcasted_iota(jnp.int32, (1, BLOCK), 1)
    key = key_block * BLOCK + lax.broadcasted_iota(jnp.int32, (BLOCK, BLOCK), 0)
    return (key <= query) & (key >= doc_first)


def group_lanes(group, kind):
    start = kind * LANES + group * HEAD_LANES
    return slice(start, start + HEAD_LANES)


def forward_body(heads, group, docs, per_piece, blocks, cuts, scalars, qkv, *refs):
    pairs, refs = refs[: 2 * len(cuts)], refs[2 * len(cuts) :]
    keep_out, send_out, log_out = refs[:3]
    values_t, out_t = refs[-2:]
    join_pairs(pairs, refs[3:-2], cuts)
    me = scalars[HERE]
    width = heads * HD

    def transpose_values(i, carry):
        v = qkv[pl.ds(block_start(i, per_piece, me), BLOCK), group_lanes(group, 2)]
        values_t[:, pl.ds(pl.multiple_of(i * BLOCK, BLOCK), BLOCK)] = v.T[:width]
        return carry

    lax.fori_loop(0, blocks, transpose_values, 0)

    def query_block(i, carry):
        row = block_start(i, per_piece, me)
        q_heads = head_lanes(qkv[pl.ds(row, BLOCK), group_lanes(group, 0)] * BF16(HD ** -0.5), heads)
        positions = i * BLOCK + lax.broadcasted_iota(jnp.int32, (1, BLOCK), 1)
        doc_first = starts_of(scalars, docs, positions)

        def key_step(kb, state):
            allowed = allowed_mask(i, kb, doc_first)
            k = qkv[pl.ds(block_start(kb, per_piece, me), BLOCK), group_lanes(group, 1)]
            column = pl.ds(pl.multiple_of(kb * BLOCK, BLOCK), BLOCK)
            new = []
            for j in range(heads):
                top, total, acc = state[j]
                s = jnp.where(allowed, mm(k, q_heads[j], NT), -1e30)
                top_new = jnp.maximum(top, jnp.max(s, axis=0, keepdims=True))
                p = jnp.exp(s - top_new)
                fade = jnp.exp(top - top_new)
                total = total * fade + jnp.sum(p, axis=0, keepdims=True)
                v_t = values_t[j * HD : (j + 1) * HD, column]
                acc = acc * fade + mm(v_t, p.astype(BF16), NN)
                new.append((top_new, total, acc))
            return tuple(new)

        init = tuple(
            (jnp.full((1, BLOCK), -1e30, F32), jnp.zeros((1, BLOCK), F32), jnp.zeros((HD, BLOCK), F32))
            for _ in range(heads)
        )
        state = key_step(i, init)
        state = lax.fori_loop(first_block(scalars, docs, i), i, key_step, state)
        column = pl.ds(row, BLOCK)
        for j in range(heads):
            top, total, acc = state[j]
            out_t[j * HD : (j + 1) * HD, column] = (acc / total).astype(BF16)
            log_out[j : j + 1, pl.ds(pl.multiple_of(i * BLOCK, BLOCK), BLOCK)] = top + jnp.log(total)
        return carry

    lax.fori_loop(0, blocks, query_block, 0)
    half = out_t.shape[1] // 2
    keep_out[...] = out_t[:, :half]
    send_out[...] = out_t[:, half:]


def attention_forward(scalars, qkv, heads, group, docs, piece, pairs, cuts):
    rows = qkv.shape[0]
    width = heads * HD
    flat = [x for pair in pairs for x in pair]
    found = call(
        partial(forward_body, heads, group, docs, piece // BLOCK, rows // BLOCK, cuts),
        [scalars, qkv, *flat],
        [
            shape((width, rows // 2), BF16),
            shape((width, rows // 2), BF16),
            shape((8, rows), F32),
            *join_shapes(pairs, cuts),
        ],
        [pltpu.VMEM((width, rows), BF16), pltpu.VMEM((width, rows), BF16)],
        14,
        "attention_forward",
    )
    return found[:3], found[3:]


def backward_body(
    heads, docs, per_piece, span, final, scalars, qkv, out_keep, out_send, grad_keep, grad_recv, logs, *refs
):
    if span[0] > 0:
        refs = refs[3:]
    grads, d_keys, d_values, sums, keys_t, out_t, grad_t = refs
    me = scalars[HERE]
    width = heads * HD
    scale = HD ** -0.5
    half = out_keep.shape[1]
    out_t[:, :half] = out_keep[...]
    out_t[:, half:] = out_send[...]
    grad_t[:, :half] = grad_keep[...]
    grad_t[:, half:] = grad_recv[...]
    if span[0] == 0:
        d_keys[...] = jnp.zeros_like(d_keys)
        d_values[...] = jnp.zeros_like(d_values)

    def transpose_keys(i, carry):
        k = qkv[pl.ds(block_start(i, per_piece, me), BLOCK), group_lanes(0, 1)]
        keys_t[:, pl.ds(pl.multiple_of(i * BLOCK, BLOCK), BLOCK)] = k.T[:width]
        return carry

    lax.fori_loop(0, span[1], transpose_keys, 0)

    def padded(rows, kind):
        return jnp.concatenate([rows, jnp.zeros((LANES - width, BLOCK), kind)], axis=0)

    def query_block(i, carry):
        row = block_start(i, per_piece, me)
        q_heads = head_lanes(qkv[pl.ds(row, BLOCK), group_lanes(0, 0)] * BF16(scale), heads)
        o_t = out_t[:, pl.ds(row, BLOCK)]
        g_t = grad_t[:, pl.ds(row, BLOCK)]
        product = o_t.astype(F32) * g_t.astype(F32)
        deltas = [jnp.sum(product[j * HD : (j + 1) * HD], axis=0, keepdims=True) for j in range(heads)]
        g_heads = head_lanes(padded(g_t, BF16).T, heads)
        natural = pl.ds(pl.multiple_of(i * BLOCK, BLOCK), BLOCK)
        log_rows = [logs[j : j + 1, natural] for j in range(heads)]
        positions = i * BLOCK + lax.broadcasted_iota(jnp.int32, (1, BLOCK), 1)
        doc_first = starts_of(scalars, docs, positions)

        def key_step(kb, d_q):
            allowed = allowed_mask(i, kb, doc_first)
            key_row = pl.ds(block_start(kb, per_piece, me), BLOCK)
            k = qkv[key_row, group_lanes(0, 1)]
            v = qkv[key_row, group_lanes(0, 2)]
            column = pl.ds(pl.multiple_of(kb * BLOCK, BLOCK), BLOCK)
            d_k = d_keys[key_row, :]
            d_v = d_values[key_row, :]
            new = []
            for j in range(heads):
                s = jnp.where(allowed, mm(k, q_heads[j], NT), -1e30)
                p = jnp.exp(s - log_rows[j])
                d_v = d_v + mm(p.astype(BF16), g_heads[j], NN)
                d_p = mm(v, g_heads[j], NT)
                d_s = (p * (d_p - deltas[j])).astype(BF16)
                d_k = d_k + mm(d_s, q_heads[j], NN)
                new.append(d_q[j] + mm(keys_t[j * HD : (j + 1) * HD, column], d_s, NN))
            d_keys[key_row, :] = d_k
            d_values[key_row, :] = d_v
            return tuple(new)

        d_q = key_step(i, tuple(jnp.zeros((HD, BLOCK), F32) for _ in range(heads)))
        d_q = lax.fori_loop(first_block(scalars, docs, i), i, key_step, d_q)
        stacked = padded(jnp.concatenate(d_q, axis=0), F32) * scale
        grads[pl.ds(row, BLOCK), 0:LANES] = stacked.T.astype(BF16)
        return carry

    lax.fori_loop(span[0], span[1], query_block, 0)
    sums[...] = jnp.zeros_like(sums)
    if final:
        grads[:, LANES : 2 * LANES] = d_keys[...].astype(BF16)
        grads[:, 2 * LANES : 3 * LANES] = d_values[...].astype(BF16)
        for line, kind in enumerate((0, 2)):
            columns = grads[:, kind * LANES : (kind + 1) * LANES].astype(F32)
            sums[line : line + 1, :] = jnp.sum(columns, axis=0, keepdims=True)


def attention_backward(scalars, qkv, outs, grads, logs, heads, docs, piece, span, before=(), markers=()):
    rows = qkv.shape[0]
    width = heads * HD
    final = span[1] == rows // BLOCK
    inputs = [scalars, qkv, *outs, *grads, logs, *before]
    return call(
        partial(backward_body, heads, docs, piece // BLOCK, span, final),
        inputs,
        [
            shape((rows, 3 * LANES), BF16),
            shape((rows, LANES), F32),
            shape((rows, LANES), F32),
            shape((8, LANES), F32),
        ],
        [pltpu.VMEM((width, rows), BF16)] * 3,
        19,
        "attention_backward",
        markers=markers,
        aliases={len(inputs) - 3 + i: i for i in range(3)} if before else {},
    )


MICROSECONDS = {
    "prepare": 2.8,
    "block_kinds": 0.5,
    "join": 1.2,
    "project": 5,
    "attention_forward": 16,
    "branch": 1.3,
    "middle_norm": 1,
    "feed_forward": 16,
    "head_gradients": 1,
    "output_weight_gradient": 1,
    "attention_backward": 3,
    "first_norm_gradient": 1.5,
    "input_weight_gradient": 3,
    "add_arrived": 1.2,
    "middle_gradient": 3,
    "first_gradient": 2.5,
    "payload": 1,
    "expand_gradient": 3,
    "contract_gradient": 3,
    "moments": 2,
    "directions": 1,
    "weights": 1.5,
}
COST_SCALE = 1.0


def cost(name):
    flops = int(MICROSECONDS[name] * COST_SCALE * 1.0e9)
    return pl.CostEstimate(flops=flops, bytes_accessed=0, transcendentals=0)


VMEM = pl.BlockSpec(memory_space=pltpu.VMEM)
SMEM = pl.BlockSpec(memory_space=pltpu.SMEM)
LEFT = pl.BlockSpec(memory_space=pl.ANY)
TN = (((0,), (0,)), ((), ()))
HERE, CHIP, ROW, CORE, SIDE, PLACE = range(6)
ENDS = 6


class Places:
    def __init__(self, lengths=None):
        self.lengths = lengths

    def __getitem__(self, number):
        here, row = lax.axis_index("head"), lax.axis_index("batch")
        heads, rows = lax.axis_size("head"), lax.axis_size("batch")
        if number == HERE:
            return here
        if number == CHIP:
            return row * (heads // 2) + here // 2
        if number == ROW:
            return row
        if number == CORE:
            return here % 2
        if number == SIDE:
            return here // 2
        if number == PLACE:
            return rows * here + row
        return sum(self.lengths[0, doc] for doc in range(number - ENDS + 1))


def call(body, inputs, outputs, scratch, mib, name, markers=(), aliases={}):
    lengths, inputs = inputs[0].lengths, inputs[1:]
    lead = [] if lengths is None else [lengths]
    count = len(lead) + len(inputs)

    def whole(*refs):
        places = Places(refs[0] if lead else None)
        body(places, *refs[len(lead) : count], *refs[count + len(markers) :])

    return pl.pallas_call(
        whole,
        out_shape=tuple(outputs),
        in_specs=[SMEM] * len(lead) + [VMEM] * len(inputs) + [LEFT] * len(markers),
        out_specs=(VMEM,) * len(outputs),
        scratch_shapes=scratch,
        input_output_aliases=aliases,
        compiler_params=pltpu.CompilerParams(vmem_limit_bytes=mib * 2**20),
        cost_estimate=cost(name),
        name=name,
    )(*lead, *inputs, *markers)


def lines_row(lines, first, count):
    return jnp.concatenate([lines[pl.ds(first + i, 1), :] for i in range(count)], axis=1)


def vector_row(lines, number):
    return lines_row(lines, number * (D // 128), D // 128)


def heads_row(lines, number, here):
    width = D // lax.axis_size("head")
    row = lines_row(lines, number * (D // 128) + (width * here) // 128, LANES // 128)
    row = jnp.where((width * here) % 128 != 0, pltpu.roll(row, LANES - HD, 1), row)
    lane = lax.broadcasted_iota(jnp.int32, row.shape, 1)
    return jnp.where(lane < width, row, 0.0)


def shape(dims, kind):
    return jax.ShapeDtypeStruct(tuple(dims), kind)


def join_pairs(ins, outs, cuts):
    outs = list(outs)
    for i, cut in enumerate(cuts):
        own, arrived = ins[2 * i], ins[2 * i + 1]
        half = own.shape[0]
        if cut == 0:
            out = outs.pop(0)
            out[:half] = own[...]
            out[half:] = arrived[...]
            continue
        rows = own.shape[1] // cut
        for part in range(cut):
            out = outs.pop(0)
            out[:half] = own[:, part * rows : (part + 1) * rows]
            out[half:] = arrived[:, part * rows : (part + 1) * rows]


def join_body(cuts, scalars, *refs):
    count = 2 * len(cuts)
    join_pairs(refs[:count], refs[count:], cuts)


def join_shapes(pairs, cuts):
    shapes = []
    for (own, _), cut in zip(pairs, cuts):
        dims = (2 * own.shape[0],) + own.shape[1:]
        if cut == 0:
            shapes.append(shape(dims, own.dtype))
        else:
            shapes += [shape((dims[0], dims[1] // cut, dims[2]), own.dtype)] * cut
    return shapes


def join(scalars, pairs, cuts, markers=()):
    flat = [x for pair in pairs for x in pair]
    return call(
        partial(join_body, cuts), [scalars, *flat], join_shapes(pairs, cuts), [], 24, "join", markers=markers
    )


def prepare_body(scalars, weight_in, weight_expand, weight_out, weight_back, tokens, lines, *outs):
    blocks, (expand, mine, other, back, normed) = outs[:3], outs[3:]
    back[...] = weight_back[...].astype(BF16)
    rows = blocks[0].shape[0]
    for slot, out in enumerate(blocks):
        out[...] = weight_in[slot * rows : (slot + 1) * rows, :].astype(BF16)
    expand[...] = weight_expand[...].astype(BF16)
    quarter = D // 4
    wide = weight_out[...]
    even = jnp.concatenate([wide[:, :quarter], wide[:, 2 * quarter : 3 * quarter]], axis=1)
    odd = jnp.concatenate([wide[:, quarter : 2 * quarter], wide[:, 3 * quarter :]], axis=1)
    high = scalars[CORE] == 1
    mine[...] = jnp.where(high, odd, even).astype(BF16)
    other[...] = jnp.where(high, even, odd).astype(BF16)
    gain, shift = vector_row(lines, 0), vector_row(lines, 1)
    step = min(128, tokens.shape[0])
    for start in range(0, tokens.shape[0], step):
        unit, _ = row_norm(tokens[start : start + step, :].astype(F32))
        normed[start : start + step, :] = (unit * gain + shift).astype(BF16)


def prepare(scalars, weight_in, weight_expand, weight_out, weight_back, tokens, lines):
    rows, out_rows = weight_in.shape[0] // 3, weight_out.shape[0]
    return call(
        prepare_body,
        [scalars, weight_in, weight_expand, weight_out, weight_back, tokens, lines],
        [shape((rows, D), BF16)] * 3
        + [
            shape(weight_expand.shape, BF16),
            shape((out_rows, D // 2), BF16),
            shape((out_rows, D // 2), BF16),
            shape(weight_back.shape, BF16),
            shape(tokens.shape, BF16),
        ],
        [],
        60,
        "prepare",
    )


def kinds_body(total, scalars, first, second, third, out):
    place = scalars[PLACE]
    rows = first.shape[0]
    for slot, block in enumerate((first, second, third)):
        kind = ((slot + 3 * total - place) * total) % 3
        out[kind] = block[...]


def block_kinds(scalars, blocks, total):
    rows = blocks[0].shape[0]
    outs = [shape((3, rows, D), BF16)]
    return call(partial(kinds_body, total), [scalars, *blocks], outs, [], 8, "block_kinds")[0]


def spread(scalars, base, parts, masks, put):
    origin = scalars[base] if base is not None else 0
    for ref, own in zip(parts, masks):
        for r, mask in enumerate(own):
            put(origin ^ mask if base is not None else mask, ref[r])


def project_body(base, masks, cuts, scalars, mine, other, lines, *refs):
    parts, refs = refs[: len(masks)], refs[len(masks) :]
    pairs, refs = refs[: 2 * len(cuts)], refs[2 * len(cuts) :]
    out, weight_out, weight = refs[0], refs[1], refs[-1]
    join_pairs(pairs, refs[2:-1], cuts)
    weight[...] = jnp.zeros_like(weight)

    def put(place, chunk):
        rows = chunk.shape[0] // 3
        wide = chunk.astype(F32)
        for kind in range(3):
            start = kind * LANES + place * rows
            if base is not None:
                start = pl.multiple_of(start, 8)
            weight[pl.ds(start, rows), :] = wide[kind * rows : (kind + 1) * rows]

    spread(scalars, base, parts, masks, put)
    low = weight[...].astype(BF16)
    weight_out[...] = low
    piece = mine.shape[0] // 2
    here = scalars[HERE]
    bias = jnp.concatenate(
        [heads_row(lines, 4, here), jnp.zeros((1, LANES), F32), heads_row(lines, 5, here)], axis=1
    )
    for place, (source, lead) in enumerate(((mine, 0), (other, 0), (mine, piece), (other, piece))):
        rows = source[lead : lead + piece, :]
        out[place * piece : (place + 1) * piece, :] = (mm(rows, low, NT) + bias).astype(BF16)


def project(scalars, mine, other, lines, base, parts, masks, pairs, cuts, markers):
    rows = 2 * mine.shape[0]
    flat = [x for pair in pairs for x in pair]
    outs = [shape((rows, 3 * LANES), BF16), shape((3 * LANES, D), BF16), *join_shapes(pairs, cuts)]
    found = call(
        partial(project_body, base, masks, cuts),
        [scalars, mine, other, lines, *parts, *flat],
        outs,
        [pltpu.VMEM((3 * LANES, D), F32)],
        24,
        "project",
        markers=markers,
    )
    return found[0], found[1], found[2:]


def branch_body(base, masks, scalars, keep, across_t, *refs):
    parts, refs = refs[: len(masks)], refs[len(masks) :]
    sent_a, sent_b, kept, own_out, across_out, weight = refs
    width = own_out.shape[1]

    def put(place, chunk):
        rows = chunk.shape[0]
        start = pl.multiple_of(place * rows, 16) if base is not None else place * rows
        for group in range(2):
            weight[group, pl.ds(start, rows), :] = chunk[:, group * width : (group + 1) * width]

    spread(scalars, base, parts, masks, put)
    side = scalars[SIDE]
    own_out[...] = weight[side]
    across_out[...] = weight[1 - side]
    piece = kept.shape[0]
    def rows_of(columns):
        return mm(keep[:, columns].T, own_out[...], NT) + mm(across_t[:, columns].T, across_out[...], NT)

    half = piece // 2
    sent_a[...] = rows_of(slice(piece, piece + half)).astype(BF16)
    sent_b[...] = rows_of(slice(piece + half, 2 * piece)).astype(BF16)
    kept[...] = rows_of(slice(0, piece))


def middle_norm_body(scalars, tokens, kept, arrived_a, arrived_b, lines, middle, normed_a, normed_b):
    bias, gain, shift = vector_row(lines, 6), vector_row(lines, 2), vector_row(lines, 3)
    half = normed_a.shape[0]
    step = min(128, half)
    for lead, arrived, normed in ((0, arrived_a, normed_a), (half, arrived_b, normed_b)):
        for start in range(0, half, step):
            rows = slice(lead + start, lead + start + step)
            values = tokens[rows, :].astype(F32) + kept[rows, :]
            values = values + arrived[start : start + step, :].astype(F32) + bias
            middle[rows, :] = values
            unit, _ = row_norm(values)
            normed[start : start + step, :] = (unit * gain + shift).astype(BF16)


def middle_norm(scalars, tokens, kept, arrived, lines):
    piece = tokens.shape[0]
    return call(
        middle_norm_body,
        [scalars, tokens, kept, *arrived, lines],
        [shape((piece, D), F32), shape((piece // 2, D), BF16), shape((piece // 2, D), BF16)],
        [],
        16,
        "middle_norm",
    )


def branch(scalars, keep, across_t, base, parts, masks, markers):
    width, rows = keep.shape
    piece = rows // 2
    return call(
        partial(branch_body, base, masks),
        [scalars, keep, across_t, *parts],
        [shape((piece // 2, D), BF16)] * 2
        + [shape((piece, D), F32), shape((D, width), BF16), shape((D, width), BF16)],
        [pltpu.VMEM((2, D, width), BF16)],
        24,
        "branch",
        markers=markers,
    )


MLP_ROWS = 256
MLP_LANES = 512


def feed_body(
    bases, masks, count, scalars, own_a, own_b, other_a, other_b, grad_own, grad_other, lines, *refs
):
    parts, refs = refs[: sum(map(len, masks))], refs[sum(map(len, masks)) :]
    activated, grad_hidden, normed_sent, normed_kept, out_sent, out_kept, sums, pair, grad_pair = refs[:9]
    expand, contract = refs[9:]
    half = expand.shape[0]
    piece = grad_own.shape[0]
    for lead, rows in enumerate((own_a, own_b, other_a, other_b)):
        pair[lead * (piece // 2) : (lead + 1) * (piece // 2), :] = rows[...]
    grad_pair[:piece, :] = grad_own[...]
    grad_pair[piece:, :] = grad_other[...]
    bias = lines_row(lines, 8 * (D // 128) + scalars[CORE] * (half // 128), half // 128)

    def put_expand(index):
        def put(place, chunk):
            rows = chunk.shape[0]
            start = place * 2 * rows + index * rows
            if bases[index] is not None:
                start = pl.multiple_of(start, 16)
            expand[pl.ds(start, rows), :] = chunk

        return put

    def put_contract(place, chunk):
        rows = chunk.shape[0]
        start = pl.multiple_of(place * rows, 16) if bases[-1] is not None else place * rows
        contract[pl.ds(start, rows), :] = chunk

    taken = 0
    for index, own_masks in enumerate(masks):
        put = put_contract if index == len(masks) - 1 else put_expand(index)
        spread(scalars, bases[index], parts[taken : taken + len(own_masks)], own_masks, put)
        taken += len(own_masks)
    sums[...] = jnp.zeros_like(sums)
    step = min(MLP_ROWS, piece)

    def block(start, lead, normed_out, contract_out):
        rows = pl.ds(start, step)
        target = pl.ds(pl.multiple_of(lead + start, step), step)
        normed = pair[target, :]
        grad = grad_pair[target, :]
        back = jnp.zeros((step, D), F32)
        result = jnp.zeros((step, D), F32)
        for lanes in range(0, half, MLP_LANES):
            span = slice(lanes, lanes + MLP_LANES)
            expanded = mm(normed, expand[span, :], NT) + bias[:, span]
            squared = expanded * expanded
            bent = jnp.tanh(ROOT_TWO_OVER_PI * (expanded + 0.044715 * (expanded * squared)))
            rise = 0.5 * (1.0 + bent)
            act = (expanded * rise).astype(BF16)
            slope = rise + (0.5 * ROOT_TWO_OVER_PI) * expanded * (1.0 - bent * bent) * (
                1.0 + (3.0 * 0.044715) * squared
            )
            hidden = (mm(grad, contract[:, span], NN) * slope).astype(BF16)
            activated[target, span] = act
            grad_hidden[target, span] = hidden
            sums[0:1, span] += jnp.sum(hidden.astype(F32), axis=0, keepdims=True)
            back = back + mm(hidden, expand[span, :], NN)
            result = result + mm(act, contract[:, span], NT)
        normed_out[rows, :] = back.astype(normed_out.dtype)
        contract_out[rows, :] = result.astype(contract_out.dtype)

    def own_block(i, carry):
        start = pl.multiple_of(i * step, step)
        block(start, 0, normed_kept, out_kept)
        return carry

    def other_block(i, carry):
        start = pl.multiple_of(i * step, step)
        block(start, piece, normed_sent, out_sent)
        return carry

    lax.fori_loop(0, piece // step, other_block, 0)
    lax.fori_loop(0, piece // step, own_block, 0)


def feed_forward(scalars, normed, grads, lines, bases, parts, masks):
    piece = grads[0].shape[0]
    half = FF // 2
    flat = [x for group in parts for x in group]
    return call(
        partial(feed_body, bases, masks, len(flat)),
        [scalars, *normed, *grads, lines, *flat],
        [
            shape((2 * piece, half), BF16),
            shape((2 * piece, half), BF16),
            shape((piece, D), BF16),
            shape((piece, D), F32),
            shape((piece, D), BF16),
            shape((piece, D), F32),
            shape((8, half), F32),
            shape((2 * piece, D), BF16),
            shape((2 * piece, D), BF16),
        ],
        [pltpu.VMEM((half, D), BF16), pltpu.VMEM((D, half), BF16)],
        31,
        "feed_forward",
    )


def head_grads_body(scalars, own, other, weight_own, weight_across, keep, sent):
    piece = own.shape[0]
    for matrix, out in ((weight_across, sent), (weight_own, keep)):
        for place, rows in enumerate((own, other)):
            features = mm(rows[...], matrix[...], NN).T.astype(BF16)
            out[:, place * piece : (place + 1) * piece] = features


def head_grads(scalars, grads, weight_own, weight_across, markers):
    piece = grads[0].shape[0]
    outs = [shape((weight_own.shape[1], 2 * piece), BF16)] * 2
    return call(head_grads_body, [scalars, *grads, weight_own, weight_across], outs, [], 16, "head_gradients", markers)


def split_rows(total, plan, scalars, sent, kept):
    which, shift, size = plan
    bit = (scalars[which] >> shift) & 1
    rows = sent.shape[1]

    def one(m, carry):
        base = (m // size) * 2 * size + m % size
        for out, chosen in ((sent, 1 - bit), (kept, bit)):
            start = pl.multiple_of((base + chosen * size) * rows, 8)
            out[m] = total[pl.ds(start, rows), :].astype(out.dtype)
        return carry

    lax.fori_loop(0, sent.shape[0], one, 0)


def split_shapes(chips, rows, columns):
    dims = (chips // 2, rows, columns)
    return [shape(dims, BF16), shape(dims, F32)]


def output_weight_body(plan, scalars, own, other, keep, across_t, *refs):
    *outs, stacked, total = refs
    side = scalars[SIDE]
    piece = own.shape[0]
    width = keep.shape[0]
    for place, features in ((side, keep), (1 - side, across_t)):
        product = mm(features[:, :piece], own[...], NN) + mm(features[:, piece:], other[...], NN)
        stacked[pl.ds(pl.multiple_of(place * width, 8), width), :] = product
    total[...] = stacked[...].T
    if plan is None:
        outs[0][...] = total[...].astype(BF16)
    else:
        split_rows(total, plan, scalars, *outs)


def output_weight_grad(scalars, grads, keep, across_t, plan, chips, markers):
    width = keep.shape[0]
    outs = [shape((D, 2 * width), BF16)] if plan is None else split_shapes(chips, D // chips, 2 * width)
    return call(
        partial(output_weight_body, plan),
        [scalars, *grads, keep, across_t],
        outs,
        [pltpu.VMEM((2 * width, D), F32), pltpu.VMEM((D, 2 * width), F32)],
        16,
        "output_weight_gradient",
        markers=markers,
    )


def product_body(plan, lanes, scalars, left, right, sent, kept, total):
    for start in range(0, left.shape[1], lanes):
        block = left[:, start : start + lanes].T
        for column in range(0, right.shape[1], D):
            columns = slice(column, column + D)
            total[start : start + lanes, columns] = mm(block, right[:, columns], NN)
    split_rows(total, plan, scalars, sent, kept)


def product_grad(scalars, left, right, plan, chips, name, markers=()):
    rows, columns = left.shape[1], right.shape[1]
    return call(
        partial(product_body, plan, 256),
        [scalars, left, right],
        split_shapes(chips, rows // chips, columns),
        [pltpu.VMEM((rows, columns), F32)],
        24,
        name,
        markers=markers,
    )


def input_weight_body(aligned, rows_of_devices, scalars, grads, mine, other, *refs):
    total = refs[-1]
    piece = mine.shape[0] // 2
    step = min(MLP_ROWS, piece)
    total[...] = jnp.zeros_like(total)
    for place, (source, lead) in enumerate(((mine, 0), (other, 0), (mine, piece), (other, piece))):
        for start in range(0, piece, step):
            rows = grads[place * piece + start : place * piece + start + step, :]
            total[...] += mm(rows.T, source[lead + start : lead + start + step, :], NN)
    if not aligned:
        natural = refs[0]
        for kind in range(3):
            natural[kind] = total[kind * LANES : kind * LANES + natural.shape[1], :]
        return
    rows = refs[0].shape[1]
    half = D // 2
    row = scalars[ROW]
    for part, position in enumerate((0, 1)):
        sent, kept = refs[2 * part], refs[2 * part + 1]
        columns = slice(part * half, (part + 1) * half)
        low = 1 << position
        bit = (row >> position) & 1
        count = rows_of_devices // 2
        for kind in range(3):
            for e in range(count):
                base = (e // low) * 2 * low + e % low
                for out, chosen in ((sent, 1 - bit), (kept, bit)):
                    start = kind * LANES + (base + chosen * low) * rows
                    block = total[pl.ds(pl.multiple_of(start, 8), rows), columns]
                    out[kind * count + e] = block.astype(out.dtype)


def input_weight_grad(scalars, grads, mine, other, rows_of_devices, block):
    aligned = block % 8 == 0
    part = (3 * rows_of_devices // 2, block, D // 2)
    outs = [shape(part, BF16), shape(part, F32)] * 2
    if not aligned:
        outs = [shape((3, block * rows_of_devices, D), F32)]
    return call(
        partial(input_weight_body, aligned, rows_of_devices),
        [scalars, grads, mine, other],
        outs,
        [pltpu.VMEM((3 * LANES, D), F32)],
        16,
        "input_weight_gradient",
    )


def first_grads_body(places, scalars, grads, weight, *refs):
    *far, sent_a, sent_b, kept = refs
    piece = kept.shape[0]
    half = piece // 2
    if far:
        far_kept, arrived_a, arrived_b, reduced = far
        for lead, arrived in ((0, arrived_a), (half, arrived_b)):
            rows = slice(lead, lead + half)
            reduced[rows, :] = (far_kept[rows, :] + arrived[...].astype(F32)).astype(BF16)
    sent, stay = places
    for lead, out in ((0, sent_a), (half, sent_b)):
        rows = grads[sent * piece + lead : sent * piece + lead + half, :]
        out[...] = mm(rows, weight[...], NN).astype(BF16)
    kept[...] = mm(grads[stay * piece : (stay + 1) * piece, :], weight[...], NN)


def first_grads(scalars, grads, weight, places, far=(), markers=()):
    piece = grads.shape[0] // 4
    outs = [shape((piece, D), BF16)] * bool(far) + [shape((piece // 2, D), BF16)] * 2
    return call(
        partial(first_grads_body, places),
        [scalars, grads, weight, *far],
        outs + [shape((piece, D), F32)],
        [],
        16,
        "first_norm_gradient",
        markers=markers,
    )


def payload_body(hidden_rows, scalars, left, right, expand, contract, first, middle, heads, hidden, out, blocks):
    six = D // 128
    out[...] = jnp.zeros_like(out)
    out[: 2 * six, :] = first[: 2 * six, :]
    out[2 * six : 4 * six, :] = middle[: 2 * six, :]
    out[6 * six : 8 * six, :] = middle[2 * six : 4 * six, :]
    here = scalars[HERE]
    for line in range(2):
        row = heads[line : line + 1, :]
        row = jnp.where(here % 2 == 1, pltpu.roll(row, HD, 1), row)
        start = (4 + line) * six + (3 * here) // 2
        for part in range(2):
            out[pl.ds(start + part, 1), :] = row[:, part * 128 : (part + 1) * 128]
    for part in range(hidden_rows):
        line = 8 * six + scalars[CORE] * hidden_rows + part
        out[pl.ds(line, 1), :] = hidden[0:1, part * 128 : (part + 1) * 128]
    total = jnp.zeros((1, 1), F32)
    for gradients in (left, right, expand, contract):
        for i in range(gradients.shape[0]):
            values = gradients[i]
            rows = jnp.sum(values * values, axis=1, keepdims=True)
            total += jnp.sum(rows, axis=0, keepdims=True)
    blocks[:, :, : D // 2] = left[...]
    blocks[:, :, D // 2 :] = right[...]
    lane = lax.broadcasted_iota(jnp.int32, (1, 128), 1)
    out[VECTOR_ROWS : VECTOR_ROWS + 1, :] = jnp.where(lane == 0, total, 0.0)


def make_payload(scalars, gradients, first, middle, heads, hidden):
    return call(
        partial(payload_body, hidden.shape[1] // 128),
        [scalars, *gradients, first, middle, heads, hidden],
        [shape((VECTOR_ROWS + 8, 128), F32), shape(gradients[0].shape[:2] + (D,), F32)],
        [],
        12,
        "payload",
    )


def reduce_body(plans, scalars, *refs):
    count = 2 * sum(len(sources) for sources, _ in plans)
    ins, outs = list(refs[:count]), list(refs[count:])
    for sources, split in plans:
        terms = []
        column = 0
        for full in sources:
            kept, arrived = ins.pop(0), ins.pop(0)
            columns = slice(column, column + arrived.shape[2])
            column += arrived.shape[2]

            def total(index, kept=kept, arrived=arrived, full=full):
                source = index
                if full is not None:
                    which, shift, size = full
                    bit = (scalars[which] >> shift) & 1
                    source = (index // size) * 2 * size + bit * size + index % size
                return kept[source].astype(F32) + arrived[index].astype(F32)

            terms.append((columns, total))
        if split is None:
            out = outs.pop(0)

            def whole(m, carry, out=out, terms=terms):
                for columns, total in terms:
                    out[m, :, columns] = total(m)
                return carry

            lax.fori_loop(0, out.shape[0], whole, 0)
        else:
            which, shift, size = split
            sent_out, kept_out = outs.pop(0), outs.pop(0)

            def halves(m, carry, sent_out=sent_out, kept_out=kept_out, terms=terms):
                bit = (scalars[which] >> shift) & 1
                base = (m // size) * 2 * size + m % size
                for columns, total in terms:
                    kept_out[m, :, columns] = total(base + bit * size)
                    sent_out[m, :, columns] = total(base + (1 - bit) * size).astype(BF16)
                return carry

            lax.fori_loop(0, kept_out.shape[0], halves, 0)


HEAD_LANES = LANES


VECTOR_ROWS = (8 * D + FF) // 128


def row_norm(values):
    mean = jnp.mean(values, axis=1, keepdims=True)
    centered = values - mean
    variance = jnp.mean(centered * centered, axis=1, keepdims=True)
    inverse = lax.rsqrt(variance + NORM_EPS)
    return centered * inverse, inverse


def norm_input_gradient(upstream, values, gain):
    unit, inverse = row_norm(values)
    scaled = upstream * gain
    first = jnp.mean(scaled, axis=1, keepdims=True)
    second = jnp.mean(scaled * unit, axis=1, keepdims=True)
    return inverse * (scaled - first - unit * second), unit


def stack_rows(sums, rows):
    for place, row in enumerate(rows):
        total = jnp.sum(row, axis=0, keepdims=True)
        for part in range(D // 128):
            line = place * (D // 128) + part
            sums[line : line + 1, :] += total[:, part * 128 : (part + 1) * 128]


def middle_body(own, arrived, middle, cotangent, lines, grad_mid, grad_branch, sums):
    @pl.when(pl.program_id(0) == 0)
    def _():
        sums[...] = jnp.zeros_like(sums)

    upstream = own[...] + arrived[...].astype(F32)
    passed, unit = norm_input_gradient(upstream, middle[...], vector_row(lines, 2))
    outer = cotangent[...].astype(F32)
    total = outer + passed
    rounded = total.astype(BF16)
    grad_mid[...] = total
    grad_branch[...] = rounded
    stack_rows(sums, [upstream * unit, upstream, rounded.astype(F32), outer])


def first_body(own, arrived, across, tokens, grad_mid, lines, input_grad, sums):
    @pl.when(pl.program_id(0) == 0)
    def _():
        sums[...] = jnp.zeros_like(sums)

    upstream = own[...] + arrived[...].astype(F32) + across[...].astype(F32)
    passed, unit = norm_input_gradient(upstream, tokens[...].astype(F32), vector_row(lines, 0))
    input_grad[...] = (grad_mid[...] + passed).astype(BF16)
    stack_rows(sums, [upstream * unit, upstream])


def norm_backward(body, arrays, lines, outputs, name, markers=()):
    rows = arrays[0].shape[0]
    step = min(128, rows)
    tile = pl.BlockSpec((step, D), lambda i: (i, 0))
    row = pl.BlockSpec(lines.shape, lambda i: (0, 0))
    sums = pl.BlockSpec((24, 128), lambda i: (0, 0))
    count = len(arrays) + 1

    def whole(*refs):
        body(*refs[:count], *refs[count + len(markers) :])

    return pl.pallas_call(
        whole,
        grid=(rows // step,),
        out_shape=tuple(jax.ShapeDtypeStruct((rows, D), kind) for kind in outputs)
        + (jax.ShapeDtypeStruct((24, 128), F32),),
        in_specs=[tile] * len(arrays) + [row] + [LEFT] * len(markers),
        out_specs=tuple(tile for _ in outputs) + (sums,),
        compiler_params=pltpu.CompilerParams(vmem_limit_bytes=10 * 2**20),
        cost_estimate=cost(name),
        name=name,
    )(*arrays, lines, *markers)


def moments_body(*refs):
    payload, refs = refs[0], refs[1:]
    grads, firsts, seconds, masters = refs[0:4], refs[4:9], refs[9:14], refs[14:19]
    first_outs, second_outs, direction_outs = refs[20:25], refs[25:30], refs[30:35]
    clip = clip_of(payload)
    for place in range(5):
        gradient = grads[place][...] if place < 4 else payload[0:VECTOR_ROWS, :]
        master = masters[place][...]
        first_new, second_new, direction = direction_of(
            gradient, firsts[place][...], seconds[place][...], master, clip
        )
        first_outs[place][...] = first_new
        second_outs[place][...] = second_new
        direction_outs[place][...] = direction if place < 4 else master - VECTOR_RATE * direction


def clip_of(payload):
    vector = payload[0:VECTOR_ROWS, :]
    total = payload[VECTOR_ROWS : VECTOR_ROWS + 1, 0:1] + jnp.sum(
        jnp.sum(vector * vector, axis=1, keepdims=True), axis=0, keepdims=True
    )
    return jnp.minimum(1.0, 1.0 / jnp.sqrt(total))


def direction_of(gradient, first_old, second_old, master, clip):
    clipped = gradient * clip
    first_new = 0.5 * first_old + 0.5 * clipped
    second_new = 0.5 * second_old + 0.5 * clipped * clipped
    correction = 1.0 - 0.5**STEP
    direction = (
        first_new / correction / (jnp.sqrt(second_new / correction) + ADAM_EPS) + DECAY_RATE * master
    )
    return first_new, second_new, direction


def directions_body(*refs):
    payload, squares, refs = refs[0], refs[-1], refs[1:-1]
    grads, firsts, seconds, masters = refs[0:4], refs[4:8], refs[8:12], refs[12:16]
    clip = clip_of(payload)
    lane = lax.broadcasted_iota(jnp.int32, squares.shape, 1)
    row = lax.broadcasted_iota(jnp.int32, squares.shape, 0)
    found = jnp.zeros(squares.shape, F32)
    for place in range(4):
        master = masters[place][...]
        _, _, direction = direction_of(
            grads[place][...], firsts[place][...], seconds[place][...], master, clip
        )
        for offset, values in ((0, direction), (4, master)):
            square = jnp.sum(jnp.sum(values * values, axis=1, keepdims=True), axis=0, keepdims=True)
            found = found + jnp.where((lane == place + offset) & (row == 0), square, 0.0)
    squares[...] = found


def directions_step(payload, grads, firsts, seconds, masters):
    vmem = pl.BlockSpec(memory_space=pltpu.VMEM)
    return pl.pallas_call(
        directions_body,
        out_shape=jax.ShapeDtypeStruct((8, 128), F32),
        in_specs=[vmem] * 17,
        out_specs=vmem,
        compiler_params=pltpu.CompilerParams(vmem_limit_bytes=16 * 2**20),
        cost_estimate=cost("directions"),
        name="directions",
    )(payload, *grads, *firsts, *seconds, *masters)


def moments_step(payload, grads, firsts, seconds, masters, marker):
    vmem = pl.BlockSpec(memory_space=pltpu.VMEM)
    shapes = [jax.ShapeDtypeStruct(master.shape, F32) for master in masters]
    outs = pl.pallas_call(
        moments_body,
        out_shape=tuple(shapes * 3),
        in_specs=[vmem] * 21,
        out_specs=(vmem,) * 15,
        compiler_params=pltpu.CompilerParams(vmem_limit_bytes=16 * 2**20),
        cost_estimate=cost("moments"),
        name="moments",
    )(payload, *grads, *firsts, *seconds, *masters, marker)
    return outs[0:5], outs[5:10], outs[10:15]


def weights_body(*refs):
    squares, refs = refs[0], refs[1:]
    directions, masters, outs, lows = refs[0:4], refs[4:8], refs[8:12], refs[12:16]
    norms = refs[16]
    norms[...] = jnp.zeros_like(norms)
    weight = jnp.sqrt(squares[0:1, 4:8])
    update = jnp.sqrt(squares[0:1, 0:4])
    for place in range(4):
        ratio = MATRIX_RATE * (weight[:, place : place + 1] / update[:, place : place + 1])
        new = masters[place][...] - ratio * directions[place][...]
        outs[place][...] = new
        lows[place][...] = new.astype(BF16)
    norms[0:1, 0:4] = weight
    norms[1:2, 0:4] = update


def weights_step(squares, directions, masters):
    vmem = pl.BlockSpec(memory_space=pltpu.VMEM)
    outs = pl.pallas_call(
        weights_body,
        out_shape=tuple(jax.ShapeDtypeStruct(m.shape, F32) for m in masters)
        + tuple(jax.ShapeDtypeStruct(m.shape, BF16) for m in masters)
        + (jax.ShapeDtypeStruct((8, 128), F32),),
        in_specs=[vmem] * 9,
        out_specs=(vmem,) * 9,
        compiler_params=pltpu.CompilerParams(vmem_limit_bytes=16 * 2**20),
        cost_estimate=cost("weights"),
        name="weights",
    )(squares, *directions, *masters)
    return outs[0:4], outs[4:8], outs[8]


BOTH = ("batch", "head")
PARTNER = 1
ACROSS = 2


def dot(a, b, dims):
    return lax.dot_general(a, b, (dims, ((), ())), preferred_element_type=F32)


def swap(values, axis, mask):
    size = lax.axis_size(axis)
    return lax.ppermute(values, axis, [(place, place ^ mask) for place in range(size)])


def partner(values):
    return swap(values, "head", PARTNER)


def across(values):
    return swap(values, "head", ACROSS)


def batch_masks():
    return [1 << bit for bit in range((lax.axis_size("batch") - 1).bit_length())][::-1]


class Chain:
    def __init__(self, scalars, chunk, order, chips):
        self.scalars, self.values, self.order, self.chips = scalars, chunk[None], list(order), chips
        self.masks, self.flip, self.arrived = [0], 0, None

    def start(self):
        axis, mask = self.order.pop(0)
        self.flip = mask if not self.chips else (2 * mask if axis == "batch" else 1)
        self.arrived = swap(self.values, axis, mask)

    def pair(self):
        return self.values, self.arrived

    def take(self, joined):
        self.values = joined
        self.masks = self.masks + [mask ^ self.flip for mask in self.masks]
        self.arrived = None
        if self.order:
            self.start()

    def drain(self, left):
        while len(self.order) > left:
            self.take(join(self.scalars, [self.pair()], [0])[0])

    def halves(self, joined, orders):
        chains = []
        for values, order in zip(joined, orders):
            chain = Chain(self.scalars, values[0], order, self.chips)
            chain.values = values
            chain.masks = self.masks + [mask ^ self.flip for mask in self.masks]
            chain.start()
            chains.append(chain)
        return chains

    def parts(self, multiple, kinds=1):
        rows = self.values.shape[1] // kinds
        source = CHIP if self.chips else ROW
        arrays, masks = [self.values], [self.masks]
        if self.arrived is not None:
            arrays.append(self.arrived)
            masks.append([mask ^ self.flip for mask in self.masks])
        if rows % multiple == 0:
            return source, arrays, masks
        chunks = [array[r] for array in arrays for r in range(array.shape[0])]
        order = [mask for group in masks for mask in group]
        count = len(order)
        natural = jnp.stack([chunks[order.index(place)] for place in range(count)])
        size = 1
        while size < count:
            cut = natural.reshape((-1, 2, size) + natural.shape[1:])
            flipped = jnp.concatenate([cut[:, 1:], cut[:, :1]], axis=1)
            cut = jnp.where((self.scalars[source] & size) != 0, flipped, cut)
            natural = cut.reshape(natural.shape)
            size *= 2
        natural = natural.reshape(count, kinds, rows, -1).transpose(1, 0, 2, 3)
        return None, [natural.reshape(1, kinds * count * rows, -1)], [[0]]


def join_all(scalars, chains, extra=(), markers=()):
    pairs = [chain.pair() for chain in chains] + list(extra)
    joined = join(scalars, pairs, [0] * len(pairs), markers)
    for chain, values in zip(chains, joined):
        chain.take(values)
    return joined[len(chains) :]


def bit_source(bit):
    axis, mask = bit
    return (ROW, mask.bit_length() - 1) if axis == "batch" else (SIDE, 0)


class Reduce:
    def __init__(self, bits, order, *values):
        self.left, self.order, self.values, self.full = list(bits), list(order), values, None

    def split(self):
        bit = self.order.pop(0)
        size = 1 << (len(self.left) - 1 - self.left.index(bit))
        self.left.remove(bit)
        self.bit = bit
        return (*bit_source(bit), size)

    def begin(self, scalars):
        self.full = self.split()
        self.sources = []
        for values in self.values:
            self.send(scalars, values)

    def send(self, scalars, values):
        which, shift, size = self.full
        bit = (scalars[which] >> shift) & 1
        rows = values.shape[1:]
        cut = values.reshape((-1, 2, size) + rows)
        sent = lax.dynamic_index_in_dim(cut, 1 - bit, 1, keepdims=False).reshape((-1,) + rows)
        self.sources.append((values, swap(sent.astype(BF16), *self.bit)))

    def begin_with(self, *pairs):
        self.full = None
        self.sources = [(kept, swap(sent, *self.bit)) for sent, kept in pairs]

    def add_source(self, sent, kept):
        self.sources.append((kept, swap(sent, *self.bit)))

    @property
    def kept(self):
        return self.sources[0][0]


def reduce_all(scalars, chains, markers=()):
    plans, inputs, outs = [], [scalars], []
    for chain in chains:
        full = chain.full
        for source in chain.sources:
            inputs += source
        plan = chain.split() if chain.order else None
        plans.append(([full] * len(chain.sources), plan))
        count, rows, _ = chain.sources[0][1].shape
        columns = sum(arrived.shape[2] for _, arrived in chain.sources)
        if plan is None:
            outs.append(shape((count, rows, columns), F32))
        else:
            outs.append(shape((count // 2, rows, columns), BF16))
            outs.append(shape((count // 2, rows, columns), F32))
    found = list(call(partial(reduce_body, plans), inputs, outs, [], 16, "add_arrived", markers=markers))
    for chain, (_, plan) in zip(chains, plans):
        if plan is None:
            chain.values = found.pop(0)
        else:
            sent, kept = found.pop(0), found.pop(0)
            chain.begin_with((sent, kept))


def all_sum(values):
    for mask in (PARTNER, ACROSS):
        values = values + swap(values, "head", mask)
    masks = batch_masks()[::-1]
    if len(masks) % 2:
        values = values + swap(values, "batch", masks[0])
        masks = masks[1:]
    for low, high in zip(masks[::2], masks[1::2]):
        near = values + swap(values, "batch", low)
        far = swap(values, "batch", high) + swap(values, "batch", low | high)
        values = near + far
    return values


def block_permutation(slot, to_owner):
    rows, heads = lax.axis_size("batch"), lax.axis_size("head")
    total = rows * heads
    pairs = []
    for owner in range(total):
        place = (3 * owner + slot) % total
        holder = (place % rows) * heads + place // rows
        pairs.append((holder, owner) if to_owner else (owner, holder))
    return pairs


def holder_place():
    return lax.axis_size("batch") * lax.axis_index("head") + lax.axis_index("batch")


def blocks_to_holders(shard):
    blocks = shard.reshape(3, -1, D)
    return [lax.ppermute(blocks[slot], BOTH, block_permutation(slot, False)) for slot in range(3)]


def blocks_to_owners(blocks):
    total = lax.axis_size("batch") * lax.axis_size("head")
    place = holder_place()
    arrived = []
    for slot in range(3):
        kind = ((slot + 3 * total - place) * total) % 3
        sent = lax.dynamic_index_in_dim(blocks, kind, 0, keepdims=False)
        arrived.append(lax.ppermute(sent, BOTH, block_permutation(slot, True)))
    return jnp.concatenate(arrived, axis=0)


def on_device(
    tokens,
    cotangent,
    lengths,
    input_weight,
    output_weight,
    expand_weight,
    contract_weight,
    vector_params,
    input_first,
    input_second,
    output_first,
    output_second,
    expand_first,
    expand_second,
    contract_first,
    contract_second,
    vector_first,
    vector_second,
):
    rows_of_devices = lax.axis_size("batch")
    head_count = lax.axis_size("head")
    chips = rows_of_devices * head_count // 2
    here = lax.axis_index("head")
    core = here % 2
    side = here // 2
    width = D // head_count
    heads = width // HD
    piece = tokens.shape[0]
    docs = lengths.shape[1]
    hidden_block = FF // (2 * chips)
    half = FF // 2
    out_rows = output_weight.shape[0]
    total_devices = rows_of_devices * head_count
    batch_bits = [("batch", mask) for mask in batch_masks()]
    far, near = batch_bits[:-1], batch_bits[-1]
    side_bit = ("head", ACROSS)
    bits = batch_bits + [side_bit]
    bias_contract = vector_params[7 * D : 8 * D]

    def by_core(mine, other, axis):
        high = core == 1
        return jnp.stack([jnp.where(high, other, mine), jnp.where(high, mine, other)], axis=axis)

    def pick(values, index, axis):
        return lax.dynamic_index_in_dim(values, index, axis, keepdims=False)

    scalars, sequences = Places(), Places(lengths)
    lines = vector_params.reshape(VECTOR_ROWS, 128)

    *in_blocks, expand_low, output_mine, output_cut, contract_low, normed_own = prepare(
        scalars, input_weight, expand_weight, output_weight, contract_weight, tokens, lines
    )
    in_arrived = [
        lax.ppermute(block, BOTH, block_permutation(slot, False)) for slot, block in enumerate(in_blocks)
    ]
    expands = Chain(scalars, expand_low, far, True)
    expands.start()
    normed_across = across(normed_own)
    contract_cut = contract_low.reshape(out_rows, chips, 2, hidden_block)
    sent = jnp.concatenate([pick(contract_cut, 1 - core, 2).reshape(out_rows, half), output_cut], axis=1)
    columns_arrived = partner(sent)
    contract_mine = pick(contract_cut, core, 2).reshape(out_rows, half)
    contract_shard = by_core(contract_mine, columns_arrived[:, :half], 0).reshape(2 * out_rows, half)
    output_shard = by_core(output_mine, columns_arrived[:, half:], 0).reshape(2 * out_rows, 2 * width)
    contracts = Chain(scalars, contract_shard, [near, side_bit] + far, True)
    contracts.start()

    kinds = block_kinds(scalars, in_arrived, total_devices).reshape(-1, D)
    inputs = Chain(scalars, kinds, batch_bits, False)
    outputs = Chain(scalars, output_shard, far + [side_bit, near], True)
    inputs.start()
    outputs.start()
    inputs.drain(2)
    outputs.drain(3)
    join_all(scalars, [inputs, outputs, contracts], (), (expands.arrived,))
    expands.drain(1)
    (normed_mine,) = join_all(
        scalars, [inputs, outputs, contracts, expands], [(normed_own, normed_across)]
    )
    contracts.drain(1)
    normed_other = partner(normed_mine)

    def cores_first(vectors):
        hidden = vectors[:, 8 * D :].reshape(-1, chips, 2, hidden_block).transpose(0, 2, 1, 3)
        return jnp.concatenate([vectors[:, : 8 * D], hidden.reshape(-1, FF)], axis=1).reshape(-1, VECTOR_ROWS, 128)

    def cores_back(rows):
        vectors = rows.reshape(-1, 8 * D + FF)
        hidden = vectors[:, 8 * D :].reshape(-1, 2, chips, hidden_block).transpose(0, 2, 1, 3)
        return jnp.concatenate([vectors[:, : 8 * D], hidden.reshape(-1, FF)], axis=1)

    vector_state = cores_first(jnp.stack([vector_first, vector_second, vector_params]))
    projected, weight_in, joined = project(
        scalars,
        normed_mine,
        normed_other,
        lines,
        *inputs.parts(8, 3),
        [outputs.pair(), expands.pair()],
        [0, 2],
        (vector_state,),
    )
    outputs.take(joined[0])
    expands = expands.halves(joined[1:], ([near, side_bit], [side_bit, near]))

    keep_t, send_t, logs = attention_forward(sequences, projected, heads, 0, docs, piece, [], [])[0]
    across_t = across(send_t)
    cotangent_other = partner(cotangent)
    join_all(scalars, [*expands, contracts, outputs], (), (keep_t, cotangent_other))
    *branch_sent, branch_kept, output_own, output_across = branch(
        scalars, keep_t, across_t, *outputs.parts(16), (contracts.values,)
    )
    resid_mid, *normed_two = middle_norm(
        scalars, tokens, branch_kept, [partner(rows) for rows in branch_sent], lines
    )
    arrived_two = [partner(rows) for rows in normed_two]

    found = [chain.parts(16) for chain in (*expands, contracts)]
    activated, grad_hidden, normed_sent, normed_kept, out_sent, out_kept, hidden_sums, *pairs = feed_forward(
        scalars,
        (*normed_two, *arrived_two),
        (cotangent, cotangent_other),
        vector_state[2],
        [part[0] for part in found],
        [part[1] for part in found],
        [part[2] for part in found],
    )
    normed_arrived = partner(normed_sent)
    out_arrived = partner(out_sent)
    block_out = (resid_mid + out_kept + out_arrived.astype(F32) + bias_contract).astype(BF16)

    normed_pair, cotangent_pair = pairs
    expand_sum = Reduce(bits, [near] + far[-1:] + [side_bit] + far[:-1][::-1])
    contract_sum = Reduce(bits, far[-1:] + [side_bit, near] + far[:-1][::-1])
    sums = [expand_sum, contract_sum]
    aligned = hidden_block % 8 == 0 and 2 * out_rows % 8 == 0
    if aligned:
        plans = [chain.split() for chain in sums]
        contract_sum.begin_with(
            product_grad(scalars, cotangent_pair, activated, plans[1], chips, "contract_gradient")
        )
    else:
        expand_total = dot(grad_hidden, normed_pair, ((0,), (0,))).astype(BF16)
        contract_total = dot(cotangent_pair, activated, ((0,), (0,))).astype(BF16)
        expand_sum.values = (expand_total.reshape(chips, hidden_block, D),)
        contract_sum.values = (contract_total.reshape(chips, 2 * out_rows, half),)
        for chain in sums:
            chain.begin(scalars)
    grad_mid, grad_branch, middle_sums = norm_backward(
        middle_body,
        [normed_kept, normed_arrived, resid_mid, cotangent],
        lines,
        (F32, BF16),
        "middle_gradient",
        (contract_sum.kept,),
    )
    grads = (grad_branch, partner(grad_branch))
    if aligned:
        expand_sum.begin_with(
            product_grad(scalars, grad_hidden, normed_pair, plans[0], chips, "expand_gradient")
        )

    grad_keep_t, grad_sent_t = head_grads(scalars, grads, output_own, output_across, (expand_sum.kept,))
    grad_arrived_t = across(grad_sent_t)
    output_found = output_weight_grad(
        scalars, grads, keep_t, across_t, plans[1] if aligned else None, chips, (grad_sent_t,)
    )
    if aligned:
        contract_sum.add_source(*output_found)
    else:
        contract_sum.send(scalars, output_found[0].reshape(chips, 2 * out_rows, 2 * width))
    blocks = 4 * piece // BLOCK
    inputs = (sequences, projected, (keep_t, send_t), (grad_keep_t, grad_arrived_t), logs, heads, docs, piece)
    *before, _ = attention_backward(
        *inputs, (0, blocks // 2), (), [chain.sources[-1][0] for chain in sums]
    )
    reduce_all(scalars, sums, (before[0],))
    grad_heads, _, _, head_sums = attention_backward(
        *inputs, (blocks // 2, blocks), before, [chain.kept for chain in sums]
    )

    reduce_all(scalars, sums, (grad_heads,))
    *far_sent, far_kept = first_grads(
        scalars, grad_heads, weight_in, (3, 2), (), [chain.kept for chain in sums]
    )
    far_arrived = [partner(rows) for rows in far_sent]
    in_found = input_weight_grad(
        scalars, grad_heads, normed_mine, normed_other, rows_of_devices, D // total_devices
    )
    in_orders = ([near] + far[::-1], far[::-1] + [near])
    if len(in_found) == 4:
        in_sums = [Reduce(batch_bits, order) for order in in_orders]
        for part, sent, kept in zip(in_sums, in_found[::2], in_found[1::2]):
            part.split()
            part.begin_with((sent, kept))
    else:
        natural = in_found[0].reshape(3 * rows_of_devices, -1, D)
        in_sums = [
            Reduce(batch_bits, in_orders[0], natural[..., : D // 2]),
            Reduce(batch_bits, in_orders[1], natural[..., D // 2 :]),
        ]
        for part in in_sums:
            part.begin(scalars)
    reduced_far, *near_sent, near_kept = first_grads(
        scalars, grad_heads, weight_in, (1, 0), (far_kept, *far_arrived), (in_sums[0].kept,)
    )
    first_arrived = across(reduced_far)
    near_arrived = jnp.concatenate([partner(rows) for rows in near_sent])
    while sums[0].order:
        reduce_all(scalars, sums, (reduced_far,))
        if in_sums[0].order:
            reduce_all(scalars, in_sums, (sums[0].kept,))
    while in_sums[0].order:
        reduce_all(scalars, in_sums)
    reduce_all(scalars, in_sums, (first_arrived,))
    reduce_all(scalars, sums, (in_sums[0].values,))
    expand_grad = expand_sum.values.reshape(hidden_block, D)
    contract_mixed = contract_sum.values[0, :, :half]
    output_mixed = contract_sum.values[0, :, half:]

    def columns_other(mixed, parts):
        cut = mixed.reshape(2, out_rows, parts, -1)
        return pick(cut, core, 0), partner(pick(cut, 1 - core, 0))

    contract_grad = by_core(*columns_other(contract_mixed, chips), 2).reshape(out_rows, -1)
    output_grad = by_core(*columns_other(output_mixed, 2), 2).reshape(out_rows, -1)
    input_grad, first_sums = norm_backward(
        first_body,
        [near_kept, near_arrived, first_arrived, tokens, grad_mid],
        lines,
        (BF16,),
        "first_gradient",
    )

    masters = (input_weight, output_weight, expand_weight, contract_weight)
    gradients = [part.values for part in (*in_sums, expand_sum, contract_sum)]
    payload, in_blocks = make_payload(
        scalars, gradients, first_sums, middle_sums, head_sums, hidden_sums
    )
    payload = all_sum(payload)
    input_piece_grad = blocks_to_owners(in_blocks)
    vector_grads = payload[:VECTOR_ROWS]
    grad_norm = jnp.sqrt(payload[VECTOR_ROWS, 0] + jnp.sum(vector_grads * vector_grads))
    shard_grads = (input_piece_grad, output_grad, expand_grad, contract_grad)
    firsts = (input_first, output_first, expand_first, contract_first)
    seconds = (input_second, output_second, expand_second, contract_second)
    squares = directions_step(payload, shard_grads, firsts, seconds, masters)
    first_new, second_new, directions = moments_step(
        payload,
        shard_grads,
        (*firsts, vector_state[0]),
        (*seconds, vector_state[1]),
        (*masters, vector_state[2]),
        squares,
    )
    squares = all_sum(squares)
    vector_news = cores_back(jnp.stack([first_new[4], second_new[4], directions[4]]))
    news, lows, norms = weights_step(squares, directions[:4], masters)
    results = []
    for position in range(4):
        results += [first_new[position], second_new[position], news[position], lows[position]]
    return (
        block_out,
        input_grad,
        grad_norm,
        norms[:2, :4].reshape(8),
        *results,
        vector_news[0],
        vector_news[1],
        vector_news[2],
    )


def solution(mesh):
    split = P(BOTH, None)
    return jax.shard_map(
        on_device,
        mesh=mesh,
        in_specs=(split, split, P("batch", None)) + (split,) * 4 + (P(),) + (split,) * 8 + (P(), P()),
        out_specs=(split, split, P(), P()) + (split,) * 16 + (P(), P(), P()),
        check_vma=False,
    )
```

```python
from functools import partial
import jax
import jax.numpy as jnp
from jax import lax
from jax.experimental import pallas as pl
from jax.experimental.pallas import tpu as pltpu
from jax.sharding import PartitionSpec as P

D = 768
HD = 64
FF = 3072
STEP = 5
NORM_EPS = 1e-05
ADAM_EPS = 1e-06
DECAY_RATE = 0.01
MATRIX_RATE = 0.5
VECTOR_RATE = 0.1
ROOT_TWO_OVER_PI = (2.0 / 3.141592653589793) ** 0.5
BLOCK = 256
LANES = 256
NT = (((1,), (1,)), ((), ()))
NN = (((1,), (0,)), ((), ()))
F32 = jnp.float32
BF16 = jnp.bfloat16


def mm(a, b, dims):
    return lax.dot_general(a, b, dims, preferred_element_type=F32)


def block_start(index, per_piece, me):
    piece = index // per_piece
    return pl.multiple_of(((piece ^ me) * per_piece + index % per_piece) * BLOCK, BLOCK)


def starts_of(scalars, docs, positions):
    first = jnp.zeros_like(positions)
    for doc in range(docs - 1):
        end = scalars[ENDS + doc]
        first = jnp.where(positions >= end, end, first)
    return first


def first_block(scalars, docs, index):
    position = index * BLOCK
    first = jnp.int32(0)
    for doc in range(docs - 1):
        end = scalars[ENDS + doc]
        first = jnp.where(position >= end, end, first)
    return first // BLOCK


def head_lanes(block, heads):
    if heads == 1:
        return [block]
    lane = lax.broadcasted_iota(jnp.int32, block.shape, 1) // HD
    return [jnp.where(lane == j, block, jnp.zeros_like(block)) for j in range(heads)]


def allowed_mask(index, key_block, doc_first):
    key = key_block * BLOCK + lax.broadcasted_iota(jnp.int32, (BLOCK, BLOCK), 0)
    if index is None:
        return key >= doc_first
    query = index * BLOCK + lax.broadcasted_iota(jnp.int32, (1, BLOCK), 1)
    return (key <= query) & (key >= doc_first)


def over_keys(first, last, key_step, state):
    pairs = (last - first) // 2

    def two(p, state):
        return key_step(first + 2 * p + 1, key_step(first + 2 * p, state))

    state = lax.fori_loop(0, pairs, two, state)
    return lax.fori_loop(first + 2 * pairs, last, key_step, state)


def group_lanes(group, kind):
    start = kind * LANES + group * HEAD_LANES
    return slice(start, start + HEAD_LANES)


def forward_body(heads, group, docs, per_piece, blocks, cuts, scalars, qkv, *refs):
    pairs, refs = refs[: 2 * len(cuts)], refs[2 * len(cuts) :]
    keep_out, send_out, log_out = refs[:3]
    values_t, out_t = refs[-2:]
    join_pairs(pairs, refs[3:-2], cuts)
    me = scalars[HERE]
    width = heads * HD

    def transpose_values(i, carry):
        v = qkv[pl.ds(block_start(i, per_piece, me), BLOCK), group_lanes(group, 2)]
        values_t[:, pl.ds(pl.multiple_of(i * BLOCK, BLOCK), BLOCK)] = v.T[:width]
        return carry

    lax.fori_loop(0, blocks, transpose_values, 0)

    def query_block(i, carry):
        row = block_start(i, per_piece, me)
        q_heads = head_lanes(qkv[pl.ds(row, BLOCK), group_lanes(group, 0)] * BF16(HD ** -0.5), heads)
        positions = i * BLOCK + lax.broadcasted_iota(jnp.int32, (1, BLOCK), 1)
        doc_first = starts_of(scalars, docs, positions)

        def key_step(kb, state, query=None):
            allowed = allowed_mask(query, kb, doc_first)
            k = qkv[pl.ds(block_start(kb, per_piece, me), BLOCK), group_lanes(group, 1)]
            column = pl.ds(pl.multiple_of(kb * BLOCK, BLOCK), BLOCK)
            new = []
            for j in range(heads):
                top, total, acc = state[j]
                s = jnp.where(allowed, mm(k, q_heads[j], NT), -1e30)
                top_new = jnp.maximum(top, jnp.max(s, axis=0, keepdims=True))
                p = jnp.exp(s - top_new)
                fade = jnp.exp(top - top_new)
                total = total * fade + jnp.sum(p, axis=0, keepdims=True)
                v_t = values_t[j * HD : (j + 1) * HD, column]
                acc = acc * fade + mm(v_t, p.astype(BF16), NN)
                new.append((top_new, total, acc))
            return tuple(new)

        init = tuple(
            (jnp.full((1, BLOCK), -1e30, F32), jnp.zeros((1, BLOCK), F32), jnp.zeros((HD, BLOCK), F32))
            for _ in range(heads)
        )
        state = key_step(i, init, i)
        state = lax.fori_loop(first_block(scalars, docs, i), i, key_step, state)
        column = pl.ds(row, BLOCK)
        for j in range(heads):
            top, total, acc = state[j]
            out_t[j * HD : (j + 1) * HD, column] = (acc / total).astype(BF16)
            log_out[j : j + 1, pl.ds(pl.multiple_of(i * BLOCK, BLOCK), BLOCK)] = top + jnp.log(total)
        return carry

    lax.fori_loop(0, blocks, query_block, 0)
    half = out_t.shape[1] // 2
    keep_out[...] = out_t[:, :half]
    send_out[...] = out_t[:, half:]


def attention_forward(scalars, qkv, heads, group, docs, piece, pairs, cuts):
    rows = qkv.shape[0]
    width = heads * HD
    flat = [x for pair in pairs for x in pair]
    found = call(
        partial(forward_body, heads, group, docs, piece // BLOCK, rows // BLOCK, cuts),
        [scalars, qkv, *flat],
        [
            shape((width, rows // 2), BF16),
            shape((width, rows // 2), BF16),
            shape((8, rows), F32),
            *join_shapes(pairs, cuts),
        ],
        [pltpu.VMEM((width, rows), BF16), pltpu.VMEM((width, rows), BF16)],
        14,
        "attention_forward",
    )
    return found[:3], found[3:]


def backward_body(
    heads, docs, per_piece, span, final, scalars, qkv, out_keep, out_send, grad_keep, grad_recv, logs, *refs
):
    if span[0] > 0:
        refs = refs[3:]
    grads, d_keys, d_values, sums, keys_t, out_t, grad_t = refs
    me = scalars[HERE]
    width = heads * HD
    scale = HD ** -0.5
    half = out_keep.shape[1]
    out_t[:, :half] = out_keep[...]
    out_t[:, half:] = out_send[...]
    grad_t[:, :half] = grad_keep[...]
    grad_t[:, half:] = grad_recv[...]
    if span[0] == 0:
        d_keys[...] = jnp.zeros_like(d_keys)
        d_values[...] = jnp.zeros_like(d_values)

    def transpose_keys(i, carry):
        k = qkv[pl.ds(block_start(i, per_piece, me), BLOCK), group_lanes(0, 1)]
        keys_t[:, pl.ds(pl.multiple_of(i * BLOCK, BLOCK), BLOCK)] = k.T[:width]
        return carry

    lax.fori_loop(0, span[1], transpose_keys, 0)

    def padded(rows, kind):
        return jnp.concatenate([rows, jnp.zeros((LANES - width, BLOCK), kind)], axis=0)

    def query_block(i, carry):
        row = block_start(i, per_piece, me)
        q_heads = head_lanes(qkv[pl.ds(row, BLOCK), group_lanes(0, 0)] * BF16(scale), heads)
        o_t = out_t[:, pl.ds(row, BLOCK)]
        g_t = grad_t[:, pl.ds(row, BLOCK)]
        product = o_t.astype(F32) * g_t.astype(F32)
        deltas = [jnp.sum(product[j * HD : (j + 1) * HD], axis=0, keepdims=True) for j in range(heads)]
        g_heads = head_lanes(padded(g_t, BF16).T, heads)
        natural = pl.ds(pl.multiple_of(i * BLOCK, BLOCK), BLOCK)
        log_rows = [logs[j : j + 1, natural] for j in range(heads)]
        positions = i * BLOCK + lax.broadcasted_iota(jnp.int32, (1, BLOCK), 1)
        doc_first = starts_of(scalars, docs, positions)

        def key_step(kb, d_q, query=None):
            allowed = allowed_mask(query, kb, doc_first)
            key_row = pl.ds(block_start(kb, per_piece, me), BLOCK)
            k = qkv[key_row, group_lanes(0, 1)]
            v = qkv[key_row, group_lanes(0, 2)]
            column = pl.ds(pl.multiple_of(kb * BLOCK, BLOCK), BLOCK)
            d_k = d_keys[key_row, :]
            d_v = d_values[key_row, :]
            new = []
            for j in range(heads):
                s = jnp.where(allowed, mm(k, q_heads[j], NT), -1e30)
                p = jnp.exp(s - log_rows[j])
                d_v = d_v + mm(p.astype(BF16), g_heads[j], NN)
                d_p = mm(v, g_heads[j], NT)
                d_s = (p * (d_p - deltas[j])).astype(BF16)
                d_k = d_k + mm(d_s, q_heads[j], NN)
                new.append(d_q[j] + mm(keys_t[j * HD : (j + 1) * HD, column], d_s, NN))
            d_keys[key_row, :] = d_k
            d_values[key_row, :] = d_v
            return tuple(new)

        d_q = key_step(i, tuple(jnp.zeros((HD, BLOCK), F32) for _ in range(heads)), i)
        d_q = over_keys(first_block(scalars, docs, i), i, key_step, d_q)
        stacked = padded(jnp.concatenate(d_q, axis=0), F32) * scale
        grads[pl.ds(row, BLOCK), 0:LANES] = stacked.T.astype(BF16)
        return carry

    lax.fori_loop(span[0], span[1], query_block, 0)
    sums[...] = jnp.zeros_like(sums)
    if final:
        grads[:, LANES : 2 * LANES] = d_keys[...].astype(BF16)
        grads[:, 2 * LANES : 3 * LANES] = d_values[...].astype(BF16)
        for line, kind in enumerate((0, 2)):
            columns = grads[:, kind * LANES : (kind + 1) * LANES].astype(F32)
            sums[line : line + 1, :] = jnp.sum(columns, axis=0, keepdims=True)


def attention_backward(scalars, qkv, outs, grads, logs, heads, docs, piece, span, before=(), markers=()):
    rows = qkv.shape[0]
    width = heads * HD
    final = span[1] == rows // BLOCK
    inputs = [scalars, qkv, *outs, *grads, logs, *before]
    return call(
        partial(backward_body, heads, docs, piece // BLOCK, span, final),
        inputs,
        [
            shape((rows, 3 * LANES), BF16),
            shape((rows, LANES), F32),
            shape((rows, LANES), F32),
            shape((8, LANES), F32),
        ],
        [pltpu.VMEM((width, rows), BF16)] * 3,
        19,
        "attention_backward",
        markers=markers,
        aliases={len(inputs) - 3 + i: i for i in range(3)} if before else {},
    )


MICROSECONDS = {
    "prepare": 2.8,
    "block_kinds": 0.5,
    "join": 1.2,
    "project": 5,
    "attention_forward": 16,
    "branch": 1.3,
    "middle_norm": 0.2,
    "rise": 0.1,
    "feed_forward": 11,
    "head_gradients": 0.2,
    "output_weight_gradient": 0.2,
    "attention_backward": 2,
    "first_norm_gradient": 0.5,
    "input_weight_gradient": 1,
    "add_arrived": 0.05,
    "middle_gradient": 0.4,
    "first_gradient": 2.5,
    "payload": 1,
    "expand_gradient": 0.4,
    "contract_gradient": 0.4,
    "moments": 2,
    "directions": 1,
    "weights": 1.5,
}
COST_SCALE = 1.0


def cost(name):
    flops = int(MICROSECONDS[name] * COST_SCALE * 1.0e9)
    return pl.CostEstimate(flops=flops, bytes_accessed=0, transcendentals=0)


VMEM = pl.BlockSpec(memory_space=pltpu.VMEM)
SMEM = pl.BlockSpec(memory_space=pltpu.SMEM)
LEFT = pl.BlockSpec(memory_space=pl.ANY)
TN = (((0,), (0,)), ((), ()))
HERE, CHIP, ROW, CORE, SIDE, PLACE = range(6)
ENDS = 6


class Places:
    def __init__(self, lengths=None):
        self.lengths = lengths

    def __getitem__(self, number):
        here, row = lax.axis_index("head"), lax.axis_index("batch")
        heads, rows = lax.axis_size("head"), lax.axis_size("batch")
        if number == HERE:
            return here
        if number == CHIP:
            return row * (heads // 2) + here // 2
        if number == ROW:
            return row
        if number == CORE:
            return here % 2
        if number == SIDE:
            return here // 2
        if number == PLACE:
            return rows * here + row
        return sum(self.lengths[0, doc] for doc in range(number - ENDS + 1))


def call(body, inputs, outputs, scratch, mib, name, markers=(), aliases={}):
    lengths, inputs = inputs[0].lengths, inputs[1:]
    lead = [] if lengths is None else [lengths]
    count = len(lead) + len(inputs)

    def whole(*refs):
        places = Places(refs[0] if lead else None)
        body(places, *refs[len(lead) : count], *refs[count + len(markers) :])

    return pl.pallas_call(
        whole,
        out_shape=tuple(outputs),
        in_specs=[SMEM] * len(lead) + [VMEM] * len(inputs) + [LEFT] * len(markers),
        out_specs=(VMEM,) * len(outputs),
        scratch_shapes=scratch,
        input_output_aliases=aliases,
        compiler_params=pltpu.CompilerParams(vmem_limit_bytes=mib * 2**20),
        cost_estimate=cost(name),
        name=name,
    )(*lead, *inputs, *markers)


def lines_row(lines, first, count):
    return jnp.concatenate([lines[pl.ds(first + i, 1), :] for i in range(count)], axis=1)


def vector_row(lines, number):
    return lines_row(lines, number * (D // 128), D // 128)


def heads_row(lines, number, here):
    width = D // lax.axis_size("head")
    row = lines_row(lines, number * (D // 128) + (width * here) // 128, LANES // 128)
    row = jnp.where((width * here) % 128 != 0, pltpu.roll(row, LANES - HD, 1), row)
    lane = lax.broadcasted_iota(jnp.int32, row.shape, 1)
    return jnp.where(lane < width, row, 0.0)


def shape(dims, kind):
    return jax.ShapeDtypeStruct(tuple(dims), kind)


def join_pairs(ins, outs, cuts):
    outs = list(outs)
    for i, cut in enumerate(cuts):
        own, arrived = ins[2 * i], ins[2 * i + 1]
        half = own.shape[0]
        if cut == 0:
            out = outs.pop(0)
            out[:half] = own[...]
            out[half:] = arrived[...]
            continue
        rows = own.shape[1] // cut
        for part in range(cut):
            out = outs.pop(0)
            out[:half] = own[:, part * rows : (part + 1) * rows]
            out[half:] = arrived[:, part * rows : (part + 1) * rows]


def join_body(cuts, scalars, *refs):
    count = 2 * len(cuts)
    join_pairs(refs[:count], refs[count:], cuts)


def join_shapes(pairs, cuts):
    shapes = []
    for (own, _), cut in zip(pairs, cuts):
        dims = (2 * own.shape[0],) + own.shape[1:]
        if cut == 0:
            shapes.append(shape(dims, own.dtype))
        else:
            shapes += [shape((dims[0], dims[1] // cut, dims[2]), own.dtype)] * cut
    return shapes


def join(scalars, pairs, cuts, markers=()):
    flat = [x for pair in pairs for x in pair]
    return call(
        partial(join_body, cuts), [scalars, *flat], join_shapes(pairs, cuts), [], 24, "join", markers=markers
    )


def prepare_body(scalars, weight_in, weight_expand, weight_out, weight_back, tokens, lines, *outs):
    blocks, (expand, mine, other, back, normed) = outs[:3], outs[3:]
    back[...] = weight_back[...].astype(BF16)
    rows = blocks[0].shape[0]
    for slot, out in enumerate(blocks):
        out[...] = weight_in[slot * rows : (slot + 1) * rows, :].astype(BF16)
    expand[...] = weight_expand[...].astype(BF16)
    quarter = D // 4
    wide = weight_out[...]
    even = jnp.concatenate([wide[:, :quarter], wide[:, 2 * quarter : 3 * quarter]], axis=1)
    odd = jnp.concatenate([wide[:, quarter : 2 * quarter], wide[:, 3 * quarter :]], axis=1)
    high = scalars[CORE] == 1
    mine[...] = jnp.where(high, odd, even).astype(BF16)
    other[...] = jnp.where(high, even, odd).astype(BF16)
    gain, shift = vector_row(lines, 0), vector_row(lines, 1)
    step = min(128, tokens.shape[0])
    for start in range(0, tokens.shape[0], step):
        unit, _ = row_norm(tokens[start : start + step, :].astype(F32))
        normed[start : start + step, :] = (unit * gain + shift).astype(BF16)


def prepare(scalars, weight_in, weight_expand, weight_out, weight_back, tokens, lines):
    rows, out_rows = weight_in.shape[0] // 3, weight_out.shape[0]
    return call(
        prepare_body,
        [scalars, weight_in, weight_expand, weight_out, weight_back, tokens, lines],
        [shape((rows, D), BF16)] * 3
        + [
            shape(weight_expand.shape, BF16),
            shape((out_rows, D // 2), BF16),
            shape((out_rows, D // 2), BF16),
            shape(weight_back.shape, BF16),
            shape(tokens.shape, BF16),
        ],
        [],
        60,
        "prepare",
    )


def kinds_body(total, scalars, first, second, third, out):
    place = scalars[PLACE]
    rows = first.shape[0]
    for slot, block in enumerate((first, second, third)):
        kind = ((slot + 3 * total - place) * total) % 3
        out[kind] = block[...]


def block_kinds(scalars, blocks, total):
    rows = blocks[0].shape[0]
    outs = [shape((3, rows, D), BF16)]
    return call(partial(kinds_body, total), [scalars, *blocks], outs, [], 8, "block_kinds")[0]


def spread(scalars, base, parts, masks, put):
    origin = scalars[base] if base is not None else 0
    for ref, own in zip(parts, masks):
        for r, mask in enumerate(own):
            put(origin ^ mask if base is not None else mask, ref[r])


def project_body(base, masks, cuts, scalars, mine, other, lines, *refs):
    parts, refs = refs[: len(masks)], refs[len(masks) :]
    pairs, refs = refs[: 2 * len(cuts)], refs[2 * len(cuts) :]
    out, weight_out, weight = refs[0], refs[1], refs[-1]
    join_pairs(pairs, refs[2:-1], cuts)
    weight[...] = jnp.zeros_like(weight)

    def put(place, chunk):
        rows = chunk.shape[0] // 3
        wide = chunk.astype(F32)
        for kind in range(3):
            start = kind * LANES + place * rows
            if base is not None:
                start = pl.multiple_of(start, 8)
            weight[pl.ds(start, rows), :] = wide[kind * rows : (kind + 1) * rows]

    spread(scalars, base, parts, masks, put)
    low = weight[...].astype(BF16)
    weight_out[...] = low
    piece = mine.shape[0] // 2
    here = scalars[HERE]
    bias = jnp.concatenate(
        [heads_row(lines, 4, here), jnp.zeros((1, LANES), F32), heads_row(lines, 5, here)], axis=1
    )
    for place, (source, lead) in enumerate(((mine, 0), (other, 0), (mine, piece), (other, piece))):
        rows = source[lead : lead + piece, :]
        out[place * piece : (place + 1) * piece, :] = (mm(rows, low, NT) + bias).astype(BF16)


def project(scalars, mine, other, lines, base, parts, masks, pairs, cuts, markers):
    rows = 2 * mine.shape[0]
    flat = [x for pair in pairs for x in pair]
    outs = [shape((rows, 3 * LANES), BF16), shape((3 * LANES, D), BF16), *join_shapes(pairs, cuts)]
    found = call(
        partial(project_body, base, masks, cuts),
        [scalars, mine, other, lines, *parts, *flat],
        outs,
        [pltpu.VMEM((3 * LANES, D), F32)],
        24,
        "project",
        markers=markers,
    )
    return found[0], found[1], found[2:]


def branch_body(base, masks, scalars, keep, across_t, *refs):
    parts, refs = refs[: len(masks)], refs[len(masks) :]
    sent_a, sent_b, kept, own_out, across_out, weight = refs
    width = own_out.shape[1]

    def put(place, chunk):
        rows = chunk.shape[0]
        start = pl.multiple_of(place * rows, 16) if base is not None else place * rows
        for group in range(2):
            weight[group, pl.ds(start, rows), :] = chunk[:, group * width : (group + 1) * width]

    spread(scalars, base, parts, masks, put)
    side = scalars[SIDE]
    own_out[...] = weight[side]
    across_out[...] = weight[1 - side]
    piece = kept.shape[0]
    def rows_of(columns):
        return mm(keep[:, columns].T, own_out[...], NT) + mm(across_t[:, columns].T, across_out[...], NT)

    half = piece // 2
    sent_a[...] = rows_of(slice(piece, piece + half)).astype(BF16)
    sent_b[...] = rows_of(slice(piece + half, 2 * piece)).astype(BF16)
    kept[...] = rows_of(slice(0, piece))


def middle_norm_body(scalars, tokens, kept, arrived_a, arrived_b, lines, middle, normed_a, normed_b):
    bias, gain, shift = vector_row(lines, 6), vector_row(lines, 2), vector_row(lines, 3)
    half = normed_a.shape[0]
    step = min(128, half)
    for lead, arrived, normed in ((0, arrived_a, normed_a), (half, arrived_b, normed_b)):
        for start in range(0, half, step):
            rows = slice(lead + start, lead + start + step)
            values = tokens[rows, :].astype(F32) + kept[rows, :]
            values = values + arrived[start : start + step, :].astype(F32) + bias
            middle[rows, :] = values
            unit, _ = row_norm(values)
            normed[start : start + step, :] = (unit * gain + shift).astype(BF16)


def middle_norm(scalars, tokens, kept, arrived, lines):
    piece = tokens.shape[0]
    return call(
        middle_norm_body,
        [scalars, tokens, kept, *arrived, lines],
        [shape((piece, D), F32), shape((piece // 2, D), BF16), shape((piece // 2, D), BF16)],
        [],
        16,
        "middle_norm",
    )


def branch(scalars, keep, across_t, base, parts, masks, markers):
    width, rows = keep.shape
    piece = rows // 2
    return call(
        partial(branch_body, base, masks),
        [scalars, keep, across_t, *parts],
        [shape((piece // 2, D), BF16)] * 2
        + [shape((piece, D), F32), shape((D, width), BF16), shape((D, width), BF16)],
        [pltpu.VMEM((2, D, width), BF16)],
        24,
        "branch",
        markers=markers,
    )


MLP_ROWS = 256
MLP_LANES = 512


def rise_body(bases, masks, scalars, own_a, own_b, other_a, other_b, grad_own, grad_other, lines, *refs):
    count = sum(map(len, masks))
    parts, (activated, slopes, expand, pair, grad_pair) = refs[:count], refs[count:]
    half = expand.shape[0]
    piece = grad_own.shape[0]
    for lead, rows in enumerate((own_a, own_b, other_a, other_b)):
        pair[lead * (piece // 2) : (lead + 1) * (piece // 2), :] = rows[...]
    grad_pair[:piece, :] = grad_own[...]
    grad_pair[piece:, :] = grad_other[...]
    bias = lines_row(lines, 8 * (D // 128) + scalars[CORE] * (half // 128), half // 128)

    def put_expand(index):
        def put(place, chunk):
            rows = chunk.shape[0]
            start = place * 2 * rows + index * rows
            if bases[index] is not None:
                start = pl.multiple_of(start, 16)
            expand[pl.ds(start, rows), :] = chunk

        return put

    taken = 0
    for index, own_masks in enumerate(masks):
        spread(scalars, bases[index], parts[taken : taken + len(own_masks)], own_masks, put_expand(index))
        taken += len(own_masks)
    step = min(MLP_ROWS, piece)

    def block(i, carry):
        rows = pl.ds(pl.multiple_of(i * step, step), step)
        normed = pair[rows, :]
        for lanes in range(0, half, MLP_LANES):
            span = slice(lanes, lanes + MLP_LANES)
            expanded = mm(normed, expand[span, :], NT) + bias[:, span]
            squared = expanded * expanded
            bent = jnp.tanh(ROOT_TWO_OVER_PI * (expanded + 0.044715 * (expanded * squared)))
            rise = 0.5 * (1.0 + bent)
            activated[rows, span] = (expanded * rise).astype(BF16)
            slopes[rows, span] = rise + (0.5 * ROOT_TWO_OVER_PI) * expanded * (1.0 - bent * bent) * (
                1.0 + (3.0 * 0.044715) * squared
            )
        return carry

    lax.fori_loop(0, 2 * piece // step, block, 0)


def rise(scalars, normed, grads, lines, bases, parts, masks):
    piece = grads[0].shape[0]
    half = FF // 2
    flat = [x for group in parts for x in group]
    return call(
        partial(rise_body, bases, masks),
        [scalars, *normed, *grads, lines, *flat],
        [
            shape((2 * piece, half), BF16),
            shape((2 * piece, half), F32),
            shape((half, D), BF16),
            shape((2 * piece, D), BF16),
            shape((2 * piece, D), BF16),
        ],
        [],
        14,
        "rise",
    )


def feed_body(base, masks, scalars, activated, slopes, expand, grad_pair, *refs):
    parts, refs = refs[: len(masks)], refs[len(masks) :]
    grad_hidden, normed_sent, normed_kept, out_sent, out_kept, sums, contract = refs
    half = expand.shape[0]
    piece = normed_kept.shape[0]

    def put_contract(place, chunk):
        rows = chunk.shape[0]
        start = pl.multiple_of(place * rows, 16) if base is not None else place * rows
        contract[pl.ds(start, rows), :] = chunk

    spread(scalars, base, parts, masks, put_contract)
    sums[...] = jnp.zeros_like(sums)
    step = min(MLP_ROWS, piece)

    def block(start, lead, normed_out, contract_out):
        rows = pl.ds(start, step)
        target = pl.ds(pl.multiple_of(lead + start, step), step)
        grad = grad_pair[target, :]
        back = jnp.zeros((step, D), F32)
        result = jnp.zeros((step, D), F32)
        for lanes in range(0, half, MLP_LANES):
            span = slice(lanes, lanes + MLP_LANES)
            hidden = (mm(grad, contract[:, span], NN) * slopes[target, span]).astype(BF16)
            grad_hidden[target, span] = hidden
            sums[0:1, span] += jnp.sum(hidden.astype(F32), axis=0, keepdims=True)
            back = back + mm(hidden, expand[span, :], NN)
            result = result + mm(activated[target, span], contract[:, span], NT)
        normed_out[rows, :] = back.astype(normed_out.dtype)
        contract_out[rows, :] = result.astype(contract_out.dtype)

    def own_block(i, carry):
        block(pl.multiple_of(i * step, step), 0, normed_kept, out_kept)
        return carry

    def other_block(i, carry):
        block(pl.multiple_of(i * step, step), piece, normed_sent, out_sent)
        return carry

    lax.fori_loop(0, piece // step, other_block, 0)
    lax.fori_loop(0, piece // step, own_block, 0)


def feed_forward(scalars, activated, slopes, expand, grad_pair, base, parts, masks):
    half = expand.shape[0]
    piece = grad_pair.shape[0] // 2
    return call(
        partial(feed_body, base, masks),
        [scalars, activated, slopes, expand, grad_pair, *parts],
        [
            shape((2 * piece, half), BF16),
            shape((piece, D), BF16),
            shape((piece, D), F32),
            shape((piece, D), BF16),
            shape((piece, D), F32),
            shape((8, half), F32),
        ],
        [pltpu.VMEM((D, half), BF16)],
        18,
        "feed_forward",
    )


def head_grads_body(scalars, own, other, weight_own, weight_across, keep, sent):
    piece = own.shape[0]
    for matrix, out in ((weight_across, sent), (weight_own, keep)):
        for place, rows in enumerate((own, other)):
            features = mm(rows[...], matrix[...], NN).T.astype(BF16)
            out[:, place * piece : (place + 1) * piece] = features


def head_grads(scalars, grads, weight_own, weight_across, markers):
    piece = grads[0].shape[0]
    outs = [shape((weight_own.shape[1], 2 * piece), BF16)] * 2
    return call(head_grads_body, [scalars, *grads, weight_own, weight_across], outs, [], 16, "head_gradients", markers)


def split_rows(total, plan, scalars, sent, kept):
    which, shift, size = plan
    bit = (scalars[which] >> shift) & 1
    rows = sent.shape[1]

    def one(m, carry):
        base = (m // size) * 2 * size + m % size
        for out, chosen in ((sent, 1 - bit), (kept, bit)):
            start = pl.multiple_of((base + chosen * size) * rows, 8)
            out[m] = total[pl.ds(start, rows), :].astype(out.dtype)
        return carry

    lax.fori_loop(0, sent.shape[0], one, 0)


def split_shapes(chips, rows, columns):
    dims = (chips // 2, rows, columns)
    return [shape(dims, BF16), shape(dims, F32)]


def output_weight_body(plan, scalars, own, other, keep, across_t, *refs):
    *outs, stacked, total = refs
    side = scalars[SIDE]
    piece = own.shape[0]
    width = keep.shape[0]
    for place, features in ((side, keep), (1 - side, across_t)):
        product = mm(features[:, :piece], own[...], NN) + mm(features[:, piece:], other[...], NN)
        stacked[pl.ds(pl.multiple_of(place * width, 8), width), :] = product
    total[...] = stacked[...].T
    if plan is None:
        outs[0][...] = total[...].astype(BF16)
    else:
        split_rows(total, plan, scalars, *outs)


def output_weight_grad(scalars, grads, keep, across_t, plan, chips, markers):
    width = keep.shape[0]
    outs = [shape((D, 2 * width), BF16)] if plan is None else split_shapes(chips, D // chips, 2 * width)
    return call(
        partial(output_weight_body, plan),
        [scalars, *grads, keep, across_t],
        outs,
        [pltpu.VMEM((2 * width, D), F32), pltpu.VMEM((D, 2 * width), F32)],
        16,
        "output_weight_gradient",
        markers=markers,
    )


def product_body(plan, lanes, scalars, left, right, sent, kept, total):
    for start in range(0, left.shape[1], lanes):
        block = left[:, start : start + lanes].T
        for column in range(0, right.shape[1], D):
            columns = slice(column, column + D)
            total[start : start + lanes, columns] = mm(block, right[:, columns], NN)
    split_rows(total, plan, scalars, sent, kept)


def product_grad(scalars, left, right, plan, chips, name, markers=()):
    rows, columns = left.shape[1], right.shape[1]
    return call(
        partial(product_body, plan, 256),
        [scalars, left, right],
        split_shapes(chips, rows // chips, columns),
        [pltpu.VMEM((rows, columns), F32)],
        24,
        name,
        markers=markers,
    )


def input_weight_body(aligned, rows_of_devices, scalars, grads, mine, other, *refs):
    total = refs[-1]
    piece = mine.shape[0] // 2
    step = min(MLP_ROWS, piece)
    total[...] = jnp.zeros_like(total)
    for place, (source, lead) in enumerate(((mine, 0), (other, 0), (mine, piece), (other, piece))):
        for start in range(0, piece, step):
            rows = grads[place * piece + start : place * piece + start + step, :]
            total[...] += mm(rows.T, source[lead + start : lead + start + step, :], NN)
    if not aligned:
        natural = refs[0]
        for kind in range(3):
            natural[kind] = total[kind * LANES : kind * LANES + natural.shape[1], :]
        return
    sent, kept = refs[0], refs[1]
    rows = sent.shape[1]
    bit = (scalars[ROW] >> 1) & 1
    count = rows_of_devices // 2
    for kind in range(3):
        for e in range(count):
            for out, chosen in ((sent, 1 - bit), (kept, bit)):
                start = kind * LANES + ((e // 2) * 4 + e % 2 + 2 * chosen) * rows
                out[kind * count + e] = total[pl.ds(pl.multiple_of(start, 8), rows), :].astype(out.dtype)


def input_weight_grad(scalars, grads, mine, other, rows_of_devices, block):
    aligned = block % 8 == 0
    part = (3 * rows_of_devices // 2, block, D)
    outs = [shape(part, BF16), shape(part, F32)]
    if not aligned:
        outs = [shape((3, block * rows_of_devices, D), F32)]
    return call(
        partial(input_weight_body, aligned, rows_of_devices),
        [scalars, grads, mine, other],
        outs,
        [pltpu.VMEM((3 * LANES, D), F32)],
        16,
        "input_weight_gradient",
    )


def first_grads_body(places, scalars, grads, weight, *refs):
    *far, kept = refs
    piece = kept.shape[0]
    half = piece // 2
    halves = len(far) == 2
    if halves:
        outs = ((0, far[0]), (half, far[1]))
    else:
        far_kept, arrived_a, arrived_b, reduced, whole = far
        outs = ((0, whole),)
        for lead, arrived in ((0, arrived_a), (half, arrived_b)):
            rows = slice(lead, lead + half)
            reduced[rows, :] = (far_kept[rows, :] + arrived[...].astype(F32)).astype(BF16)
    sent, stay = places
    for lead, out in outs:
        rows = grads[sent * piece + lead : sent * piece + lead + out.shape[0], :]
        out[...] = mm(rows, weight[...], NN).astype(BF16)
    kept[...] = mm(grads[stay * piece : (stay + 1) * piece, :], weight[...], NN)


def first_grads(scalars, grads, weight, places, far=(), markers=()):
    piece = grads.shape[0] // 4
    outs = [shape((piece, D), BF16)] * 2 if far else [shape((piece // 2, D), BF16)] * 2
    return call(
        partial(first_grads_body, places),
        [scalars, grads, weight, *far],
        outs + [shape((piece, D), F32)],
        [],
        16,
        "first_norm_gradient",
        markers=markers,
    )


def payload_body(hidden_rows, scalars, inputs, expand, contract, first, middle, heads, hidden, out):
    six = D // 128
    out[...] = jnp.zeros_like(out)
    out[: 2 * six, :] = first[: 2 * six, :]
    out[2 * six : 4 * six, :] = middle[: 2 * six, :]
    out[6 * six : 8 * six, :] = middle[2 * six : 4 * six, :]
    here = scalars[HERE]
    for line in range(2):
        row = heads[line : line + 1, :]
        row = jnp.where(here % 2 == 1, pltpu.roll(row, HD, 1), row)
        start = (4 + line) * six + (3 * here) // 2
        for part in range(2):
            out[pl.ds(start + part, 1), :] = row[:, part * 128 : (part + 1) * 128]
    for part in range(hidden_rows):
        line = 8 * six + scalars[CORE] * hidden_rows + part
        out[pl.ds(line, 1), :] = hidden[0:1, part * 128 : (part + 1) * 128]
    total = jnp.zeros((1, 1), F32)
    for gradients in (inputs, expand, contract):
        for i in range(gradients.shape[0]):
            values = gradients[i]
            rows = jnp.sum(values * values, axis=1, keepdims=True)
            total += jnp.sum(rows, axis=0, keepdims=True)
    lane = lax.broadcasted_iota(jnp.int32, (1, 128), 1)
    out[VECTOR_ROWS : VECTOR_ROWS + 1, :] = jnp.where(lane == 0, total, 0.0)


def make_payload(scalars, gradients, first, middle, heads, hidden):
    return call(
        partial(payload_body, hidden.shape[1] // 128),
        [scalars, *gradients, first, middle, heads, hidden],
        [shape((VECTOR_ROWS + 8, 128), F32)],
        [],
        12,
        "payload",
    )[0]


def reduce_body(plans, scalars, *refs):
    count = 2 * sum(len(sources) for sources, _ in plans)
    ins, outs = list(refs[:count]), list(refs[count:])
    for sources, split in plans:
        terms = []
        column = 0
        for full in sources:
            kept, arrived = ins.pop(0), ins.pop(0)
            columns = slice(column, column + arrived.shape[2])
            column += arrived.shape[2]

            def total(index, kept=kept, arrived=arrived, full=full):
                source = index
                if full is not None:
                    which, shift, size = full
                    bit = (scalars[which] >> shift) & 1
                    source = (index // size) * 2 * size + bit * size + index % size
                return kept[source].astype(F32) + arrived[index].astype(F32)

            terms.append((columns, total))
        if split is None:
            out = outs.pop(0)

            def whole(m, carry, out=out, terms=terms):
                for columns, total in terms:
                    out[m, :, columns] = total(m)
                return carry

            lax.fori_loop(0, out.shape[0], whole, 0)
        else:
            which, shift, size = split
            sent_out, kept_out = outs.pop(0), outs.pop(0)

            def halves(m, carry, sent_out=sent_out, kept_out=kept_out, terms=terms):
                bit = (scalars[which] >> shift) & 1
                base = (m // size) * 2 * size + m % size
                for columns, total in terms:
                    kept_out[m, :, columns] = total(base + bit * size)
                    sent_out[m, :, columns] = total(base + (1 - bit) * size).astype(BF16)
                return carry

            lax.fori_loop(0, kept_out.shape[0], halves, 0)


HEAD_LANES = LANES


VECTOR_ROWS = (8 * D + FF) // 128


def row_norm(values):
    mean = jnp.mean(values, axis=1, keepdims=True)
    centered = values - mean
    variance = jnp.mean(centered * centered, axis=1, keepdims=True)
    inverse = lax.rsqrt(variance + NORM_EPS)
    return centered * inverse, inverse


def norm_input_gradient(upstream, values, gain):
    unit, inverse = row_norm(values)
    scaled = upstream * gain
    first = jnp.mean(scaled, axis=1, keepdims=True)
    second = jnp.mean(scaled * unit, axis=1, keepdims=True)
    return inverse * (scaled - first - unit * second), unit


def stack_rows(sums, rows):
    for place, row in enumerate(rows):
        total = jnp.sum(row, axis=0, keepdims=True)
        for part in range(D // 128):
            line = place * (D // 128) + part
            sums[line : line + 1, :] += total[:, part * 128 : (part + 1) * 128]


def middle_body(own, arrived, middle, cotangent, lines, grad_mid, grad_branch, sums):
    @pl.when(pl.program_id(0) == 0)
    def _():
        sums[...] = jnp.zeros_like(sums)

    upstream = own[...] + arrived[...].astype(F32)
    passed, unit = norm_input_gradient(upstream, middle[...], vector_row(lines, 2))
    outer = cotangent[...].astype(F32)
    total = outer + passed
    rounded = total.astype(BF16)
    grad_mid[...] = total
    grad_branch[...] = rounded
    stack_rows(sums, [upstream * unit, upstream, rounded.astype(F32), outer])


def first_body(own, arrived, across, tokens, grad_mid, lines, input_grad, sums):
    @pl.when(pl.program_id(0) == 0)
    def _():
        sums[...] = jnp.zeros_like(sums)

    upstream = own[...] + arrived[...].astype(F32) + across[...].astype(F32)
    passed, unit = norm_input_gradient(upstream, tokens[...].astype(F32), vector_row(lines, 0))
    input_grad[...] = (grad_mid[...] + passed).astype(BF16)
    stack_rows(sums, [upstream * unit, upstream])


def norm_backward(body, arrays, lines, outputs, name, markers=()):
    rows = arrays[0].shape[0]
    step = min(128, rows)
    tile = pl.BlockSpec((step, D), lambda i: (i, 0))
    row = pl.BlockSpec(lines.shape, lambda i: (0, 0))
    sums = pl.BlockSpec((24, 128), lambda i: (0, 0))
    count = len(arrays) + 1

    def whole(*refs):
        body(*refs[:count], *refs[count + len(markers) :])

    return pl.pallas_call(
        whole,
        grid=(rows // step,),
        out_shape=tuple(jax.ShapeDtypeStruct((rows, D), kind) for kind in outputs)
        + (jax.ShapeDtypeStruct((24, 128), F32),),
        in_specs=[tile] * len(arrays) + [row] + [LEFT] * len(markers),
        out_specs=tuple(tile for _ in outputs) + (sums,),
        compiler_params=pltpu.CompilerParams(vmem_limit_bytes=10 * 2**20),
        cost_estimate=cost(name),
        name=name,
    )(*arrays, lines, *markers)


def moments_body(*refs):
    payload, refs = refs[0], refs[1:]
    grads, firsts, seconds, masters = refs[0:4], refs[4:9], refs[9:14], refs[14:19]
    first_outs, second_outs, direction_outs = refs[20:25], refs[25:30], refs[30:35]
    clip = clip_of(payload)
    for place in range(5):
        gradient = grads[place][...] if place < 4 else payload[0:VECTOR_ROWS, :]
        master = masters[place][...]
        first_new, second_new, direction = direction_of(
            gradient, firsts[place][...], seconds[place][...], master, clip
        )
        first_outs[place][...] = first_new
        second_outs[place][...] = second_new
        direction_outs[place][...] = direction if place < 4 else master - VECTOR_RATE * direction


def clip_of(payload):
    vector = payload[0:VECTOR_ROWS, :]
    total = payload[VECTOR_ROWS : VECTOR_ROWS + 1, 0:1] + jnp.sum(
        jnp.sum(vector * vector, axis=1, keepdims=True), axis=0, keepdims=True
    )
    return jnp.minimum(1.0, 1.0 / jnp.sqrt(total))


def direction_of(gradient, first_old, second_old, master, clip):
    clipped = gradient * clip
    first_new = 0.5 * first_old + 0.5 * clipped
    second_new = 0.5 * second_old + 0.5 * clipped * clipped
    correction = 1.0 - 0.5**STEP
    direction = (
        first_new / correction / (jnp.sqrt(second_new / correction) + ADAM_EPS) + DECAY_RATE * master
    )
    return first_new, second_new, direction


def directions_body(*refs):
    payload, squares, refs = refs[0], refs[-1], refs[1:-1]
    grads, firsts, seconds, masters = refs[0:4], refs[4:8], refs[8:12], refs[12:16]
    clip = clip_of(payload)
    lane = lax.broadcasted_iota(jnp.int32, squares.shape, 1)
    row = lax.broadcasted_iota(jnp.int32, squares.shape, 0)
    found = jnp.zeros(squares.shape, F32)
    for place in range(4):
        master = masters[place][...]
        _, _, direction = direction_of(
            grads[place][...], firsts[place][...], seconds[place][...], master, clip
        )
        for offset, values in ((0, direction), (4, master)):
            square = jnp.sum(jnp.sum(values * values, axis=1, keepdims=True), axis=0, keepdims=True)
            found = found + jnp.where((lane == place + offset) & (row == 0), square, 0.0)
    squares[...] = found


def directions_step(payload, grads, firsts, seconds, masters):
    vmem = pl.BlockSpec(memory_space=pltpu.VMEM)
    return pl.pallas_call(
        directions_body,
        out_shape=jax.ShapeDtypeStruct((8, 128), F32),
        in_specs=[vmem] * 17,
        out_specs=vmem,
        compiler_params=pltpu.CompilerParams(vmem_limit_bytes=16 * 2**20),
        cost_estimate=cost("directions"),
        name="directions",
    )(payload, *grads, *firsts, *seconds, *masters)


def moments_step(payload, grads, firsts, seconds, masters, marker):
    vmem = pl.BlockSpec(memory_space=pltpu.VMEM)
    shapes = [jax.ShapeDtypeStruct(master.shape, F32) for master in masters]
    outs = pl.pallas_call(
        moments_body,
        out_shape=tuple(shapes * 3),
        in_specs=[vmem] * 21,
        out_specs=(vmem,) * 15,
        compiler_params=pltpu.CompilerParams(vmem_limit_bytes=16 * 2**20),
        cost_estimate=cost("moments"),
        name="moments",
    )(payload, *grads, *firsts, *seconds, *masters, marker)
    return outs[0:5], outs[5:10], outs[10:15]


def weights_body(*refs):
    squares, refs = refs[0], refs[1:]
    directions, masters, outs, lows = refs[0:4], refs[4:8], refs[8:12], refs[12:16]
    norms = refs[16]
    norms[...] = jnp.zeros_like(norms)
    weight = jnp.sqrt(squares[0:1, 4:8])
    update = jnp.sqrt(squares[0:1, 0:4])
    for place in range(4):
        ratio = MATRIX_RATE * (weight[:, place : place + 1] / update[:, place : place + 1])
        new = masters[place][...] - ratio * directions[place][...]
        outs[place][...] = new
        lows[place][...] = new.astype(BF16)
    norms[0:1, 0:4] = weight
    norms[1:2, 0:4] = update


def weights_step(squares, directions, masters):
    vmem = pl.BlockSpec(memory_space=pltpu.VMEM)
    outs = pl.pallas_call(
        weights_body,
        out_shape=tuple(jax.ShapeDtypeStruct(m.shape, F32) for m in masters)
        + tuple(jax.ShapeDtypeStruct(m.shape, BF16) for m in masters)
        + (jax.ShapeDtypeStruct((8, 128), F32),),
        in_specs=[vmem] * 9,
        out_specs=(vmem,) * 9,
        compiler_params=pltpu.CompilerParams(vmem_limit_bytes=60 * 2**20),
        cost_estimate=cost("weights"),
        name="weights",
    )(squares, *directions, *masters)
    return outs[0:4], outs[4:8], outs[8]


BOTH = ("batch", "head")
PARTNER = 1
ACROSS = 2


def dot(a, b, dims):
    return lax.dot_general(a, b, (dims, ((), ())), preferred_element_type=F32)


def swap(values, axis, mask):
    size = lax.axis_size(axis)
    return lax.ppermute(values, axis, [(place, place ^ mask) for place in range(size)])


def partner(values):
    return swap(values, "head", PARTNER)


def across(values):
    return swap(values, "head", ACROSS)


def batch_masks():
    return [1 << bit for bit in range((lax.axis_size("batch") - 1).bit_length())][::-1]


class Chain:
    def __init__(self, scalars, chunk, order, chips):
        self.scalars, self.values, self.order, self.chips = scalars, chunk[None], list(order), chips
        self.masks, self.flip, self.arrived = [0], 0, None

    def start(self):
        axis, mask = self.order.pop(0)
        self.flip = mask if not self.chips else (2 * mask if axis == "batch" else 1)
        self.arrived = swap(self.values, axis, mask)

    def pair(self):
        return self.values, self.arrived

    def take(self, joined):
        self.values = joined
        self.masks = self.masks + [mask ^ self.flip for mask in self.masks]
        self.arrived = None
        if self.order:
            self.start()

    def drain(self, left):
        while len(self.order) > left:
            self.take(join(self.scalars, [self.pair()], [0])[0])

    def halves(self, joined, orders):
        chains = []
        for values, order in zip(joined, orders):
            chain = Chain(self.scalars, values[0], order, self.chips)
            chain.values = values
            chain.masks = self.masks + [mask ^ self.flip for mask in self.masks]
            chain.start()
            chains.append(chain)
        return chains

    def parts(self, multiple, kinds=1):
        rows = self.values.shape[1] // kinds
        source = CHIP if self.chips else ROW
        arrays, masks = [self.values], [self.masks]
        if self.arrived is not None:
            arrays.append(self.arrived)
            masks.append([mask ^ self.flip for mask in self.masks])
        if rows % multiple == 0:
            return source, arrays, masks
        chunks = [array[r] for array in arrays for r in range(array.shape[0])]
        order = [mask for group in masks for mask in group]
        count = len(order)
        natural = jnp.stack([chunks[order.index(place)] for place in range(count)])
        size = 1
        while size < count:
            cut = natural.reshape((-1, 2, size) + natural.shape[1:])
            flipped = jnp.concatenate([cut[:, 1:], cut[:, :1]], axis=1)
            cut = jnp.where((self.scalars[source] & size) != 0, flipped, cut)
            natural = cut.reshape(natural.shape)
            size *= 2
        natural = natural.reshape(count, kinds, rows, -1).transpose(1, 0, 2, 3)
        return None, [natural.reshape(1, kinds * count * rows, -1)], [[0]]


def join_all(scalars, chains, extra=(), markers=()):
    pairs = [chain.pair() for chain in chains] + list(extra)
    joined = join(scalars, pairs, [0] * len(pairs), markers)
    for chain, values in zip(chains, joined):
        chain.take(values)
    return joined[len(chains) :]


def bit_source(bit):
    axis, mask = bit
    return (ROW, mask.bit_length() - 1) if axis == "batch" else (SIDE, 0)


class Reduce:
    def __init__(self, bits, order, *values):
        self.left, self.order, self.values, self.full = list(bits), list(order), values, None

    def split(self):
        bit = self.order.pop(0)
        size = 1 << (len(self.left) - 1 - self.left.index(bit))
        self.left.remove(bit)
        self.bit = bit
        return (*bit_source(bit), size)

    def begin(self, scalars):
        self.full = self.split()
        self.sources = []
        for values in self.values:
            self.send(scalars, values)

    def send(self, scalars, values):
        which, shift, size = self.full
        bit = (scalars[which] >> shift) & 1
        rows = values.shape[1:]
        cut = values.reshape((-1, 2, size) + rows)
        sent = lax.dynamic_index_in_dim(cut, 1 - bit, 1, keepdims=False).reshape((-1,) + rows)
        self.sources.append((values, swap(sent.astype(BF16), *self.bit)))

    def begin_with(self, *pairs):
        self.full = None
        self.sources = [(kept, swap(sent, *self.bit)) for sent, kept in pairs]

    def add_source(self, sent, kept):
        self.sources.append((kept, swap(sent, *self.bit)))

    @property
    def kept(self):
        return self.sources[0][0]


def reduce_all(scalars, chains, markers=()):
    plans, inputs, outs = [], [scalars], []
    for chain in chains:
        full = chain.full
        for source in chain.sources:
            inputs += source
        plan = chain.split() if chain.order else None
        plans.append(([full] * len(chain.sources), plan))
        count, rows, _ = chain.sources[0][1].shape
        columns = sum(arrived.shape[2] for _, arrived in chain.sources)
        if plan is None:
            outs.append(shape((count, rows, columns), F32))
        else:
            outs.append(shape((count // 2, rows, columns), BF16))
            outs.append(shape((count // 2, rows, columns), F32))
    found = list(call(partial(reduce_body, plans), inputs, outs, [], 16, "add_arrived", markers=markers))
    for chain, (_, plan) in zip(chains, plans):
        if plan is None:
            chain.values = found.pop(0)
        else:
            sent, kept = found.pop(0), found.pop(0)
            chain.begin_with((sent, kept))


def all_sum(values):
    for mask in (PARTNER, ACROSS):
        values = values + swap(values, "head", mask)
    masks = batch_masks()[::-1]
    if len(masks) % 2:
        values = values + swap(values, "batch", masks[0])
        masks = masks[1:]
    for low, high in zip(masks[::2], masks[1::2]):
        near = values + swap(values, "batch", low)
        far = swap(values, "batch", high) + swap(values, "batch", low | high)
        values = near + far
    return values


def block_permutation(slot, to_owner):
    rows, heads = lax.axis_size("batch"), lax.axis_size("head")
    total = rows * heads
    pairs = []
    for owner in range(total):
        place = (3 * owner + slot) % total
        holder = (place % rows) * heads + place // rows
        pairs.append((holder, owner) if to_owner else (owner, holder))
    return pairs


def holder_place():
    return lax.axis_size("batch") * lax.axis_index("head") + lax.axis_index("batch")


def blocks_to_holders(shard):
    blocks = shard.reshape(3, -1, D)
    return [lax.ppermute(blocks[slot], BOTH, block_permutation(slot, False)) for slot in range(3)]


def blocks_to_owners(blocks):
    total = lax.axis_size("batch") * lax.axis_size("head")
    place = holder_place()
    arrived = []
    for slot in range(3):
        kind = ((slot + 3 * total - place) * total) % 3
        sent = lax.dynamic_index_in_dim(blocks, kind, 0, keepdims=False)
        arrived.append(lax.ppermute(sent, BOTH, block_permutation(slot, True)))
    return jnp.concatenate(arrived, axis=0)


def on_device(
    tokens,
    cotangent,
    lengths,
    input_weight,
    output_weight,
    expand_weight,
    contract_weight,
    vector_params,
    input_first,
    input_second,
    output_first,
    output_second,
    expand_first,
    expand_second,
    contract_first,
    contract_second,
    vector_first,
    vector_second,
):
    rows_of_devices = lax.axis_size("batch")
    head_count = lax.axis_size("head")
    chips = rows_of_devices * head_count // 2
    here = lax.axis_index("head")
    core = here % 2
    side = here // 2
    width = D // head_count
    heads = width // HD
    piece = tokens.shape[0]
    docs = lengths.shape[1]
    hidden_block = FF // (2 * chips)
    half = FF // 2
    out_rows = output_weight.shape[0]
    total_devices = rows_of_devices * head_count
    batch_bits = [("batch", mask) for mask in batch_masks()]
    far, near = batch_bits[:-1], batch_bits[-1]
    side_bit = ("head", ACROSS)
    bits = batch_bits + [side_bit]
    bias_contract = vector_params[7 * D : 8 * D]

    def by_core(mine, other, axis):
        high = core == 1
        return jnp.stack([jnp.where(high, other, mine), jnp.where(high, mine, other)], axis=axis)

    def pick(values, index, axis):
        return lax.dynamic_index_in_dim(values, index, axis, keepdims=False)

    scalars, sequences = Places(), Places(lengths)
    lines = vector_params.reshape(VECTOR_ROWS, 128)

    *in_blocks, expand_low, output_mine, output_cut, contract_low, normed_own = prepare(
        scalars, input_weight, expand_weight, output_weight, contract_weight, tokens, lines
    )
    in_arrived = [
        lax.ppermute(block, BOTH, block_permutation(slot, False)) for slot, block in enumerate(in_blocks)
    ]
    expands = Chain(scalars, expand_low, far, True)
    expands.start()
    normed_across = across(normed_own)
    contract_cut = contract_low.reshape(out_rows, chips, 2, hidden_block)
    sent = jnp.concatenate([pick(contract_cut, 1 - core, 2).reshape(out_rows, half), output_cut], axis=1)
    columns_arrived = partner(sent)
    contract_mine = pick(contract_cut, core, 2).reshape(out_rows, half)
    contract_shard = by_core(contract_mine, columns_arrived[:, :half], 0).reshape(2 * out_rows, half)
    output_shard = by_core(output_mine, columns_arrived[:, half:], 0).reshape(2 * out_rows, 2 * width)
    contracts = Chain(scalars, contract_shard, [near, side_bit] + far, True)
    contracts.start()

    kinds = block_kinds(scalars, in_arrived, total_devices).reshape(-1, D)
    inputs = Chain(scalars, kinds, batch_bits, False)
    outputs = Chain(scalars, output_shard, far + [side_bit, near], True)
    inputs.start()
    outputs.start()
    inputs.drain(2)
    outputs.drain(3)
    join_all(scalars, [inputs, outputs, contracts], (), (expands.arrived,))
    expands.drain(1)
    (normed_mine,) = join_all(
        scalars, [inputs, outputs, contracts, expands], [(normed_own, normed_across)]
    )
    contracts.drain(1)
    normed_other = partner(normed_mine)

    def cores_first(vectors):
        hidden = vectors[:, 8 * D :].reshape(-1, chips, 2, hidden_block).transpose(0, 2, 1, 3)
        return jnp.concatenate([vectors[:, : 8 * D], hidden.reshape(-1, FF)], axis=1).reshape(-1, VECTOR_ROWS, 128)

    def cores_back(rows):
        vectors = rows.reshape(-1, 8 * D + FF)
        hidden = vectors[:, 8 * D :].reshape(-1, 2, chips, hidden_block).transpose(0, 2, 1, 3)
        return jnp.concatenate([vectors[:, : 8 * D], hidden.reshape(-1, FF)], axis=1)

    vector_state = cores_first(jnp.stack([vector_first, vector_second, vector_params]))
    projected, weight_in, joined = project(
        scalars,
        normed_mine,
        normed_other,
        lines,
        *inputs.parts(8, 3),
        [outputs.pair(), expands.pair()],
        [0, 2],
        (vector_state,),
    )
    outputs.take(joined[0])
    expands = expands.halves(joined[1:], ([near, side_bit], [side_bit, near]))

    keep_t, send_t, logs = attention_forward(sequences, projected, heads, 0, docs, piece, [], [])[0]
    across_t = across(send_t)
    cotangent_other = partner(cotangent)
    join_all(scalars, [*expands, contracts, outputs], (), (keep_t, cotangent_other))
    *branch_sent, branch_kept, output_own, output_across = branch(
        scalars, keep_t, across_t, *outputs.parts(16), (contracts.values,)
    )
    resid_mid, *normed_two = middle_norm(
        scalars, tokens, branch_kept, [partner(rows) for rows in branch_sent], lines
    )
    arrived_two = [partner(rows) for rows in normed_two]

    found = [chain.parts(16) for chain in expands]
    activated, slopes, expand_half, normed_pair, cotangent_pair = rise(
        scalars,
        (*normed_two, *arrived_two),
        (cotangent, cotangent_other),
        vector_state[2],
        [part[0] for part in found],
        [part[1] for part in found],
        [part[2] for part in found],
    )
    grad_hidden, normed_sent, normed_kept, out_sent, out_kept, hidden_sums = feed_forward(
        scalars, activated, slopes, expand_half, cotangent_pair, *contracts.parts(16)
    )
    normed_arrived = partner(normed_sent)
    out_arrived = partner(out_sent)
    block_out = (resid_mid + out_kept + out_arrived.astype(F32) + bias_contract).astype(BF16)

    expand_sum = Reduce(bits, [near] + far[-1:] + [side_bit] + far[:-1][::-1])
    contract_sum = Reduce(bits, far[-1:] + [side_bit, near] + far[:-1][::-1])
    output_sum = Reduce(bits, [side_bit] + far[-1:])
    sums = [expand_sum, contract_sum]
    aligned = hidden_block % 8 == 0 and 2 * out_rows % 8 == 0
    if aligned:
        plans = [chain.split() for chain in sums]
        contract_sum.begin_with(
            product_grad(scalars, cotangent_pair, activated, plans[1], chips, "contract_gradient")
        )
    else:
        expand_total = dot(grad_hidden, normed_pair, ((0,), (0,))).astype(BF16)
        contract_total = dot(cotangent_pair, activated, ((0,), (0,))).astype(BF16)
        expand_sum.values = (expand_total.reshape(chips, hidden_block, D),)
        contract_sum.values = (contract_total.reshape(chips, 2 * out_rows, half),)
        for chain in sums:
            chain.begin(scalars)
    grad_mid, grad_branch, middle_sums = norm_backward(
        middle_body,
        [normed_kept, normed_arrived, resid_mid, cotangent],
        lines,
        (F32, BF16),
        "middle_gradient",
        (contract_sum.kept,),
    )
    grads = (grad_branch, partner(grad_branch))
    if aligned:
        expand_sum.begin_with(
            product_grad(scalars, grad_hidden, normed_pair, plans[0], chips, "expand_gradient")
        )

    grad_keep_t, grad_sent_t = head_grads(scalars, grads, output_own, output_across, (expand_sum.kept,))
    grad_arrived_t = across(grad_sent_t)
    output_found = output_weight_grad(
        scalars, grads, keep_t, across_t, output_sum.split() if aligned else None, chips, (grad_sent_t,)
    )
    if aligned:
        output_sum.begin_with(output_found)
    else:
        output_sum.values = (output_found[0].reshape(chips, 2 * out_rows, 2 * width),)
        output_sum.begin(scalars)
    blocks = 4 * piece // BLOCK
    inputs = (sequences, projected, (keep_t, send_t), (grad_keep_t, grad_arrived_t), logs, heads, docs, piece)
    *before, _ = attention_backward(
        *inputs, (0, blocks // 2), (), [block_out, *(chain.kept for chain in (*sums, output_sum))]
    )
    reduce_all(scalars, [*sums, output_sum], (before[0],))
    grad_heads, _, _, head_sums = attention_backward(
        *inputs, (blocks // 2, blocks), before, [chain.kept for chain in sums]
    )

    contract_sum.sources += output_sum.sources
    reduce_all(scalars, sums, (grad_heads,))
    *far_sent, far_kept = first_grads(
        scalars, grad_heads, weight_in, (3, 2), (), [chain.kept for chain in sums]
    )
    far_arrived = [partner(rows) for rows in far_sent]
    in_found = input_weight_grad(
        scalars, grad_heads, normed_mine, normed_other, rows_of_devices, D // total_devices
    )
    in_sum = Reduce(batch_bits, far[-1:] + [near] + far[:-1][::-1])
    if len(in_found) == 2:
        in_sum.split()
        in_sum.begin_with(in_found)
    else:
        in_sum.values = (in_found[0].reshape(3 * rows_of_devices, -1, D),)
        in_sum.begin(scalars)
    reduce_all(scalars, sums, (in_sum.kept,))
    reduce_all(scalars, [in_sum], (sums[0].kept,))
    reduced_far, near_sent, near_kept = first_grads(
        scalars, grad_heads, weight_in, (1, 0), (far_kept, *far_arrived), (in_sum.kept,)
    )
    first_arrived = across(reduced_far)
    near_arrived = partner(near_sent)
    while sums[0].order:
        reduce_all(scalars, sums, (reduced_far,))
    reduce_all(scalars, sums, (reduced_far,))
    while in_sum.order:
        reduce_all(scalars, [in_sum], (expand_sum.values,))
    reduce_all(scalars, [in_sum], (first_arrived,))
    input_piece_grad = blocks_to_owners(in_sum.values)
    expand_grad = expand_sum.values.reshape(hidden_block, D)
    contract_mixed = contract_sum.values[0, :, :half]
    output_mixed = contract_sum.values[0, :, half:]

    def columns_other(mixed, parts):
        cut = mixed.reshape(2, out_rows, parts, -1)
        return pick(cut, core, 0), partner(pick(cut, 1 - core, 0))

    contract_grad = by_core(*columns_other(contract_mixed, chips), 2).reshape(out_rows, -1)
    output_grad = by_core(*columns_other(output_mixed, 2), 2).reshape(out_rows, -1)
    input_grad, first_sums = norm_backward(
        first_body,
        [near_kept, near_arrived, first_arrived, tokens, grad_mid],
        lines,
        (BF16,),
        "first_gradient",
    )

    masters = (input_weight, output_weight, expand_weight, contract_weight)
    gradients = [part.values for part in (in_sum, expand_sum, contract_sum)]
    payload = all_sum(
        make_payload(scalars, gradients, first_sums, middle_sums, head_sums, hidden_sums)
    )
    vector_grads = payload[:VECTOR_ROWS]
    grad_norm = jnp.sqrt(payload[VECTOR_ROWS, 0] + jnp.sum(vector_grads * vector_grads))
    shard_grads = (input_piece_grad, output_grad, expand_grad, contract_grad)
    firsts = (input_first, output_first, expand_first, contract_first)
    seconds = (input_second, output_second, expand_second, contract_second)
    squares = directions_step(payload, shard_grads, firsts, seconds, masters)
    first_new, second_new, directions = moments_step(
        payload,
        shard_grads,
        (*firsts, vector_state[0]),
        (*seconds, vector_state[1]),
        (*masters, vector_state[2]),
        squares,
    )
    squares = all_sum(squares)
    vector_news = cores_back(jnp.stack([first_new[4], second_new[4], directions[4]]))
    news, lows, norms = weights_step(squares, directions[:4], masters)
    results = []
    for position in range(4):
        results += [first_new[position], second_new[position], news[position], lows[position]]
    return (
        block_out,
        input_grad,
        grad_norm,
        norms[:2, :4].reshape(8),
        *results,
        vector_news[0],
        vector_news[1],
        vector_news[2],
    )


def solution(mesh):
    split = P(BOTH, None)
    return jax.shard_map(
        on_device,
        mesh=mesh,
        in_specs=(split, split, P("batch", None)) + (split,) * 4 + (P(),) + (split,) * 8 + (P(), P()),
        out_specs=(split, split, P(), P()) + (split,) * 16 + (P(), P(), P()),
        check_vma=False,
    )
```

```python
from functools import partial
import jax
import jax.numpy as jnp
from jax import lax
from jax.experimental import pallas as pl
from jax.experimental.pallas import tpu as pltpu
from jax.sharding import PartitionSpec as P

D = 768
HD = 64
FF = 3072
STEP = 5
NORM_EPS = 1e-05
ADAM_EPS = 1e-06
DECAY_RATE = 0.01
MATRIX_RATE = 0.5
VECTOR_RATE = 0.1
ROOT_TWO_OVER_PI = (2.0 / 3.141592653589793) ** 0.5
BLOCK = 256
LANES = 256
NT = (((1,), (1,)), ((), ()))
NN = (((1,), (0,)), ((), ()))
F32 = jnp.float32
BF16 = jnp.bfloat16


def mm(a, b, dims):
    return lax.dot_general(a, b, dims, preferred_element_type=F32)


def block_start(index, per_piece, me):
    piece = index // per_piece
    return pl.multiple_of(((piece ^ me) * per_piece + index % per_piece) * BLOCK, BLOCK)


def starts_of(scalars, docs, positions):
    first = jnp.zeros_like(positions)
    for doc in range(docs - 1):
        end = scalars[ENDS + doc]
        first = jnp.where(positions >= end, end, first)
    return first


def first_block(scalars, docs, index):
    position = index * BLOCK
    first = jnp.int32(0)
    for doc in range(docs - 1):
        end = scalars[ENDS + doc]
        first = jnp.where(position >= end, end, first)
    return first // BLOCK


def head_lanes(block, heads):
    if heads == 1:
        return [block]
    lane = lax.broadcasted_iota(jnp.int32, block.shape, 1) // HD
    return [jnp.where(lane == j, block, jnp.zeros_like(block)) for j in range(heads)]


def allowed_mask(index, key_block, doc_first):
    key = key_block * BLOCK + lax.broadcasted_iota(jnp.int32, (BLOCK, BLOCK), 0)
    if index is None:
        return key >= doc_first
    query = index * BLOCK + lax.broadcasted_iota(jnp.int32, (1, BLOCK), 1)
    return (key <= query) & (key >= doc_first)


def over_keys(first, last, key_step, state):
    pairs = (last - first) // 2

    def two(p, state):
        return key_step(first + 2 * p + 1, key_step(first + 2 * p, state))

    state = lax.fori_loop(0, pairs, two, state)
    return lax.fori_loop(first + 2 * pairs, last, key_step, state)


def group_lanes(group, kind):
    start = kind * LANES + group * HEAD_LANES
    return slice(start, start + HEAD_LANES)


def forward_body(heads, docs, per_piece, span, final, scalars, qkv, *refs):
    if span[0] > 0:
        refs = refs[2:]
    out_t, log_out, *ends, values_t = refs
    me = scalars[HERE]
    width = heads * HD

    def transpose_values(i, carry):
        v = qkv[pl.ds(block_start(i, per_piece, me), BLOCK), group_lanes(0, 2)]
        values_t[:, pl.ds(pl.multiple_of(i * BLOCK, BLOCK), BLOCK)] = v.T[:width]
        return carry

    lax.fori_loop(0, span[1], transpose_values, 0)

    def query_block(i, carry):
        row = block_start(i, per_piece, me)
        q_heads = head_lanes(qkv[pl.ds(row, BLOCK), group_lanes(0, 0)] * BF16(HD ** -0.5), heads)
        positions = i * BLOCK + lax.broadcasted_iota(jnp.int32, (1, BLOCK), 1)
        doc_first = starts_of(scalars, docs, positions)

        def key_step(kb, state, query=None):
            allowed = allowed_mask(query, kb, doc_first)
            k = qkv[pl.ds(block_start(kb, per_piece, me), BLOCK), group_lanes(0, 1)]
            column = pl.ds(pl.multiple_of(kb * BLOCK, BLOCK), BLOCK)
            new = []
            for j in range(heads):
                top, total, acc = state[j]
                s = jnp.where(allowed, mm(k, q_heads[j], NT), -1e30)
                top_new = jnp.maximum(top, jnp.max(s, axis=0, keepdims=True))
                p = jnp.exp(s - top_new)
                fade = jnp.exp(top - top_new)
                total = total * fade + jnp.sum(p, axis=0, keepdims=True)
                v_t = values_t[j * HD : (j + 1) * HD, column]
                acc = acc * fade + mm(v_t, p.astype(BF16), NN)
                new.append((top_new, total, acc))
            return tuple(new)

        init = tuple(
            (jnp.full((1, BLOCK), -1e30, F32), jnp.zeros((1, BLOCK), F32), jnp.zeros((HD, BLOCK), F32))
            for _ in range(heads)
        )
        state = key_step(i, init, i)
        state = lax.fori_loop(first_block(scalars, docs, i), i, key_step, state)
        column = pl.ds(row, BLOCK)
        for j in range(heads):
            top, total, acc = state[j]
            out_t[j * HD : (j + 1) * HD, column] = (acc / total).astype(BF16)
            log_out[j : j + 1, pl.ds(pl.multiple_of(i * BLOCK, BLOCK), BLOCK)] = top + jnp.log(total)
        return carry

    if span[0] == 0:
        log_out[...] = jnp.zeros_like(log_out)
    lax.fori_loop(span[0], span[1], query_block, 0)
    if final:
        half = out_t.shape[1] // 2
        ends[0][...] = out_t[:, :half]
        ends[1][...] = out_t[:, half:]


def attention_forward(scalars, qkv, heads, docs, piece, span, before=(), markers=()):
    rows = qkv.shape[0]
    width = heads * HD
    final = span[1] == rows // BLOCK
    inputs = [scalars, qkv, *before]
    outs = [shape((width, rows), BF16), shape((8, rows), F32)]
    return call(
        partial(forward_body, heads, docs, piece // BLOCK, span, final),
        inputs,
        outs + [shape((width, rows // 2), BF16)] * (2 * final),
        [pltpu.VMEM((width, rows), BF16)],
        14,
        "attention_forward",
        markers=markers,
        aliases={len(inputs) - 2 + i: i for i in range(2)} if before else {},
    )


def backward_body(
    heads, docs, per_piece, span, final, scalars, qkv, out_keep, out_send, grad_keep, grad_recv, logs, *refs
):
    if span[0] > 0:
        refs = refs[3:]
    grads, d_keys, d_values, sums, keys_t, out_t, grad_t = refs
    me = scalars[HERE]
    width = heads * HD
    scale = HD ** -0.5
    half = out_keep.shape[1]
    out_t[:, :half] = out_keep[...]
    out_t[:, half:] = out_send[...]
    grad_t[:, :half] = grad_keep[...]
    grad_t[:, half:] = grad_recv[...]
    if span[0] == 0:
        d_keys[...] = jnp.zeros_like(d_keys)
        d_values[...] = jnp.zeros_like(d_values)

    def transpose_keys(i, carry):
        k = qkv[pl.ds(block_start(i, per_piece, me), BLOCK), group_lanes(0, 1)]
        keys_t[:, pl.ds(pl.multiple_of(i * BLOCK, BLOCK), BLOCK)] = k.T[:width]
        return carry

    lax.fori_loop(0, span[1], transpose_keys, 0)

    def padded(rows, kind):
        return jnp.concatenate([rows, jnp.zeros((LANES - width, BLOCK), kind)], axis=0)

    def query_block(i, carry):
        row = block_start(i, per_piece, me)
        q_heads = head_lanes(qkv[pl.ds(row, BLOCK), group_lanes(0, 0)] * BF16(scale), heads)
        o_t = out_t[:, pl.ds(row, BLOCK)]
        g_t = grad_t[:, pl.ds(row, BLOCK)]
        product = o_t.astype(F32) * g_t.astype(F32)
        deltas = [jnp.sum(product[j * HD : (j + 1) * HD], axis=0, keepdims=True) for j in range(heads)]
        g_heads = head_lanes(padded(g_t, BF16).T, heads)
        natural = pl.ds(pl.multiple_of(i * BLOCK, BLOCK), BLOCK)
        log_rows = [logs[j : j + 1, natural] for j in range(heads)]
        positions = i * BLOCK + lax.broadcasted_iota(jnp.int32, (1, BLOCK), 1)
        doc_first = starts_of(scalars, docs, positions)

        def key_step(kb, d_q, query=None):
            allowed = allowed_mask(query, kb, doc_first)
            key_row = pl.ds(block_start(kb, per_piece, me), BLOCK)
            k = qkv[key_row, group_lanes(0, 1)]
            v = qkv[key_row, group_lanes(0, 2)]
            column = pl.ds(pl.multiple_of(kb * BLOCK, BLOCK), BLOCK)
            d_k = d_keys[key_row, :]
            d_v = d_values[key_row, :]
            new = []
            for j in range(heads):
                s = jnp.where(allowed, mm(k, q_heads[j], NT), -1e30)
                p = jnp.exp(s - log_rows[j])
                d_v = d_v + mm(p.astype(BF16), g_heads[j], NN)
                d_p = mm(v, g_heads[j], NT)
                d_s = (p * (d_p - deltas[j])).astype(BF16)
                d_k = d_k + mm(d_s, q_heads[j], NN)
                new.append(d_q[j] + mm(keys_t[j * HD : (j + 1) * HD, column], d_s, NN))
            d_keys[key_row, :] = d_k
            d_values[key_row, :] = d_v
            return tuple(new)

        d_q = key_step(i, tuple(jnp.zeros((HD, BLOCK), F32) for _ in range(heads)), i)
        d_q = over_keys(first_block(scalars, docs, i), i, key_step, d_q)
        stacked = padded(jnp.concatenate(d_q, axis=0), F32) * scale
        grads[pl.ds(row, BLOCK), 0:LANES] = stacked.T.astype(BF16)
        return carry

    lax.fori_loop(span[0], span[1], query_block, 0)
    sums[...] = jnp.zeros_like(sums)
    if final:
        grads[:, LANES : 2 * LANES] = d_keys[...].astype(BF16)
        grads[:, 2 * LANES : 3 * LANES] = d_values[...].astype(BF16)
        for line, kind in enumerate((0, 2)):
            columns = grads[:, kind * LANES : (kind + 1) * LANES].astype(F32)
            sums[line : line + 1, :] = jnp.sum(columns, axis=0, keepdims=True)


def attention_backward(scalars, qkv, outs, grads, logs, heads, docs, piece, span, before=(), markers=()):
    rows = qkv.shape[0]
    width = heads * HD
    final = span[1] == rows // BLOCK
    inputs = [scalars, qkv, *outs, *grads, logs, *before]
    return call(
        partial(backward_body, heads, docs, piece // BLOCK, span, final),
        inputs,
        [
            shape((rows, 3 * LANES), BF16),
            shape((rows, LANES), F32),
            shape((rows, LANES), F32),
            shape((8, LANES), F32),
        ],
        [pltpu.VMEM((width, rows), BF16)] * 3,
        19,
        "attention_backward",
        markers=markers,
        aliases={len(inputs) - 3 + i: i for i in range(3)} if before else {},
    )


MICROSECONDS = {
    "prepare": 2.8,
    "block_kinds": 0.5,
    "join": 1.2,
    "project": 5,
    "attention_forward": 8,
    "branch": 1.3,
    "middle_norm": 0.2,
    "rise": 0.1,
    "feed_forward": 11,
    "head_gradients": 0.2,
    "output_weight_gradient": 0.2,
    "attention_backward": 2,
    "first_norm_gradient": 0.5,
    "input_weight_gradient": 1,
    "add_arrived": 0.05,
    "middle_gradient": 0.4,
    "first_gradient": 2.5,
    "payload": 1,
    "expand_gradient": 0.4,
    "contract_gradient": 0.4,
    "moments": 2,
    "directions": 1,
    "weights": 1.5,
}
COST_SCALE = 1.0


def cost(name):
    flops = int(MICROSECONDS[name] * COST_SCALE * 1.0e9)
    return pl.CostEstimate(flops=flops, bytes_accessed=0, transcendentals=0)


VMEM = pl.BlockSpec(memory_space=pltpu.VMEM)
SMEM = pl.BlockSpec(memory_space=pltpu.SMEM)
LEFT = pl.BlockSpec(memory_space=pl.ANY)
TN = (((0,), (0,)), ((), ()))
HERE, CHIP, ROW, CORE, SIDE, PLACE = range(6)
ENDS = 6


class Places:
    def __init__(self, lengths=None):
        self.lengths = lengths

    def __getitem__(self, number):
        here, row = lax.axis_index("head"), lax.axis_index("batch")
        heads, rows = lax.axis_size("head"), lax.axis_size("batch")
        if number == HERE:
            return here
        if number == CHIP:
            return row * (heads // 2) + here // 2
        if number == ROW:
            return row
        if number == CORE:
            return here % 2
        if number == SIDE:
            return here // 2
        if number == PLACE:
            return rows * here + row
        return sum(self.lengths[0, doc] for doc in range(number - ENDS + 1))


def call(body, inputs, outputs, scratch, mib, name, markers=(), aliases={}):
    lengths, inputs = inputs[0].lengths, inputs[1:]
    lead = [] if lengths is None else [lengths]
    count = len(lead) + len(inputs)

    def whole(*refs):
        places = Places(refs[0] if lead else None)
        body(places, *refs[len(lead) : count], *refs[count + len(markers) :])

    return pl.pallas_call(
        whole,
        out_shape=tuple(outputs),
        in_specs=[SMEM] * len(lead) + [VMEM] * len(inputs) + [LEFT] * len(markers),
        out_specs=(VMEM,) * len(outputs),
        scratch_shapes=scratch,
        input_output_aliases=aliases,
        compiler_params=pltpu.CompilerParams(vmem_limit_bytes=mib * 2**20),
        cost_estimate=cost(name),
        name=name,
    )(*lead, *inputs, *markers)


def lines_row(lines, first, count):
    return jnp.concatenate([lines[pl.ds(first + i, 1), :] for i in range(count)], axis=1)


def vector_row(lines, number):
    return lines_row(lines, number * (D // 128), D // 128)


def heads_row(lines, number, here):
    width = D // lax.axis_size("head")
    row = lines_row(lines, number * (D // 128) + (width * here) // 128, LANES // 128)
    row = jnp.where((width * here) % 128 != 0, pltpu.roll(row, LANES - HD, 1), row)
    lane = lax.broadcasted_iota(jnp.int32, row.shape, 1)
    return jnp.where(lane < width, row, 0.0)


def shape(dims, kind):
    return jax.ShapeDtypeStruct(tuple(dims), kind)


def join_pairs(ins, outs, cuts):
    outs = list(outs)
    for i, cut in enumerate(cuts):
        own, arrived = ins[2 * i], ins[2 * i + 1]
        half = own.shape[0]
        if cut == 0:
            out = outs.pop(0)
            out[:half] = own[...]
            out[half:] = arrived[...]
            continue
        rows = own.shape[1] // cut
        for part in range(cut):
            out = outs.pop(0)
            out[:half] = own[:, part * rows : (part + 1) * rows]
            out[half:] = arrived[:, part * rows : (part + 1) * rows]


def join_body(cuts, scalars, *refs):
    count = 2 * len(cuts)
    join_pairs(refs[:count], refs[count:], cuts)


def join_shapes(pairs, cuts):
    shapes = []
    for (own, _), cut in zip(pairs, cuts):
        dims = (2 * own.shape[0],) + own.shape[1:]
        if cut == 0:
            shapes.append(shape(dims, own.dtype))
        else:
            shapes += [shape((dims[0], dims[1] // cut, dims[2]), own.dtype)] * cut
    return shapes


def join(scalars, pairs, cuts, markers=()):
    flat = [x for pair in pairs for x in pair]
    return call(
        partial(join_body, cuts), [scalars, *flat], join_shapes(pairs, cuts), [], 24, "join", markers=markers
    )


def prepare_body(scalars, weight_in, weight_expand, weight_out, weight_back, tokens, lines, *outs):
    blocks, (expand, mine, other, back, normed) = outs[:3], outs[3:]
    back[...] = weight_back[...].astype(BF16)
    rows = blocks[0].shape[0]
    for slot, out in enumerate(blocks):
        out[...] = weight_in[slot * rows : (slot + 1) * rows, :].astype(BF16)
    expand[...] = weight_expand[...].astype(BF16)
    quarter = D // 4
    wide = weight_out[...]
    even = jnp.concatenate([wide[:, :quarter], wide[:, 2 * quarter : 3 * quarter]], axis=1)
    odd = jnp.concatenate([wide[:, quarter : 2 * quarter], wide[:, 3 * quarter :]], axis=1)
    high = scalars[CORE] == 1
    mine[...] = jnp.where(high, odd, even).astype(BF16)
    other[...] = jnp.where(high, even, odd).astype(BF16)
    gain, shift = vector_row(lines, 0), vector_row(lines, 1)
    step = min(128, tokens.shape[0])
    for start in range(0, tokens.shape[0], step):
        unit, _ = row_norm(tokens[start : start + step, :].astype(F32))
        normed[start : start + step, :] = (unit * gain + shift).astype(BF16)


def prepare(scalars, weight_in, weight_expand, weight_out, weight_back, tokens, lines):
    rows, out_rows = weight_in.shape[0] // 3, weight_out.shape[0]
    return call(
        prepare_body,
        [scalars, weight_in, weight_expand, weight_out, weight_back, tokens, lines],
        [shape((rows, D), BF16)] * 3
        + [
            shape(weight_expand.shape, BF16),
            shape((out_rows, D // 2), BF16),
            shape((out_rows, D // 2), BF16),
            shape(weight_back.shape, BF16),
            shape(tokens.shape, BF16),
        ],
        [],
        60,
        "prepare",
    )


def kinds_body(total, scalars, first, second, third, out):
    place = scalars[PLACE]
    rows = first.shape[0]
    for slot, block in enumerate((first, second, third)):
        kind = ((slot + 3 * total - place) * total) % 3
        out[kind] = block[...]


def block_kinds(scalars, blocks, total):
    rows = blocks[0].shape[0]
    outs = [shape((3, rows, D), BF16)]
    return call(partial(kinds_body, total), [scalars, *blocks], outs, [], 8, "block_kinds")[0]


def spread(scalars, base, parts, masks, put):
    origin = scalars[base] if base is not None else 0
    for ref, own in zip(parts, masks):
        for r, mask in enumerate(own):
            put(origin ^ mask if base is not None else mask, ref[r])


def project_body(base, masks, cuts, scalars, mine, other, lines, *refs):
    parts, refs = refs[: len(masks)], refs[len(masks) :]
    pairs, refs = refs[: 2 * len(cuts)], refs[2 * len(cuts) :]
    out, weight_out, weight = refs[0], refs[1], refs[-1]
    join_pairs(pairs, refs[2:-1], cuts)
    weight[...] = jnp.zeros_like(weight)

    def put(place, chunk):
        rows = chunk.shape[0] // 3
        wide = chunk.astype(F32)
        for kind in range(3):
            start = kind * LANES + place * rows
            if base is not None:
                start = pl.multiple_of(start, 8)
            weight[pl.ds(start, rows), :] = wide[kind * rows : (kind + 1) * rows]

    spread(scalars, base, parts, masks, put)
    low = weight[...].astype(BF16)
    weight_out[...] = low
    piece = mine.shape[0] // 2
    here = scalars[HERE]
    bias = jnp.concatenate(
        [heads_row(lines, 4, here), jnp.zeros((1, LANES), F32), heads_row(lines, 5, here)], axis=1
    )
    for place, (source, lead) in enumerate(((mine, 0), (other, 0), (mine, piece), (other, piece))):
        rows = source[lead : lead + piece, :]
        out[place * piece : (place + 1) * piece, :] = (mm(rows, low, NT) + bias).astype(BF16)


def project(scalars, mine, other, lines, base, parts, masks, pairs, cuts, markers):
    rows = 2 * mine.shape[0]
    flat = [x for pair in pairs for x in pair]
    outs = [shape((rows, 3 * LANES), BF16), shape((3 * LANES, D), BF16), *join_shapes(pairs, cuts)]
    found = call(
        partial(project_body, base, masks, cuts),
        [scalars, mine, other, lines, *parts, *flat],
        outs,
        [pltpu.VMEM((3 * LANES, D), F32)],
        24,
        "project",
        markers=markers,
    )
    return found[0], found[1], found[2:]


def branch_body(base, masks, scalars, keep, across_t, *refs):
    parts, refs = refs[: len(masks)], refs[len(masks) :]
    sent_a, sent_b, kept, own_out, across_out, weight = refs
    width = own_out.shape[1]

    def put(place, chunk):
        rows = chunk.shape[0]
        start = pl.multiple_of(place * rows, 16) if base is not None else place * rows
        for group in range(2):
            weight[group, pl.ds(start, rows), :] = chunk[:, group * width : (group + 1) * width]

    spread(scalars, base, parts, masks, put)
    side = scalars[SIDE]
    own_out[...] = weight[side]
    across_out[...] = weight[1 - side]
    piece = kept.shape[0]
    def rows_of(columns):
        return mm(keep[:, columns].T, own_out[...], NT) + mm(across_t[:, columns].T, across_out[...], NT)

    half = piece // 2
    sent_a[...] = rows_of(slice(piece, piece + half)).astype(BF16)
    sent_b[...] = rows_of(slice(piece + half, 2 * piece)).astype(BF16)
    kept[...] = rows_of(slice(0, piece))


def middle_norm_body(scalars, tokens, kept, arrived_a, arrived_b, lines, middle, normed_a, normed_b):
    bias, gain, shift = vector_row(lines, 6), vector_row(lines, 2), vector_row(lines, 3)
    half = normed_a.shape[0]
    step = min(128, half)
    for lead, arrived, normed in ((0, arrived_a, normed_a), (half, arrived_b, normed_b)):
        for start in range(0, half, step):
            rows = slice(lead + start, lead + start + step)
            values = tokens[rows, :].astype(F32) + kept[rows, :]
            values = values + arrived[start : start + step, :].astype(F32) + bias
            middle[rows, :] = values
            unit, _ = row_norm(values)
            normed[start : start + step, :] = (unit * gain + shift).astype(BF16)


def middle_norm(scalars, tokens, kept, arrived, lines, markers):
    piece = tokens.shape[0]
    return call(
        middle_norm_body,
        [scalars, tokens, kept, *arrived, lines],
        [shape((piece, D), F32), shape((piece // 2, D), BF16), shape((piece // 2, D), BF16)],
        [],
        16,
        "middle_norm",
        markers,
    )


def branch(scalars, keep, across_t, base, parts, masks, markers):
    width, rows = keep.shape
    piece = rows // 2
    return call(
        partial(branch_body, base, masks),
        [scalars, keep, across_t, *parts],
        [shape((piece // 2, D), BF16)] * 2
        + [shape((piece, D), F32), shape((D, width), BF16), shape((D, width), BF16)],
        [pltpu.VMEM((2, D, width), BF16)],
        24,
        "branch",
        markers=markers,
    )


MLP_ROWS = 256
MLP_LANES = 512


def rise_body(bases, masks, scalars, own_a, own_b, other_a, other_b, grad_own, grad_other, lines, *refs):
    count = sum(map(len, masks))
    parts, (activated, slopes, expand, pair, grad_pair) = refs[:count], refs[count:]
    half = expand.shape[0]
    piece = grad_own.shape[0]
    for lead, rows in enumerate((own_a, own_b, other_a, other_b)):
        pair[lead * (piece // 2) : (lead + 1) * (piece // 2), :] = rows[...]
    grad_pair[:piece, :] = grad_own[...]
    grad_pair[piece:, :] = grad_other[...]
    bias = lines_row(lines, 8 * (D // 128) + scalars[CORE] * (half // 128), half // 128)

    def put_expand(index):
        def put(place, chunk):
            rows = chunk.shape[0]
            start = place * 2 * rows + index * rows
            if bases[index] is not None:
                start = pl.multiple_of(start, 16)
            expand[pl.ds(start, rows), :] = chunk

        return put

    taken = 0
    for index, own_masks in enumerate(masks):
        spread(scalars, bases[index], parts[taken : taken + len(own_masks)], own_masks, put_expand(index))
        taken += len(own_masks)
    step = min(MLP_ROWS, piece)

    def block(i, carry):
        rows = pl.ds(pl.multiple_of(i * step, step), step)
        normed = pair[rows, :]
        for lanes in range(0, half, MLP_LANES):
            span = slice(lanes, lanes + MLP_LANES)
            expanded = mm(normed, expand[span, :], NT) + bias[:, span]
            squared = expanded * expanded
            bent = jnp.tanh(ROOT_TWO_OVER_PI * (expanded + 0.044715 * (expanded * squared)))
            rise = 0.5 * (1.0 + bent)
            activated[rows, span] = (expanded * rise).astype(BF16)
            slopes[rows, span] = rise + (0.5 * ROOT_TWO_OVER_PI) * expanded * (1.0 - bent * bent) * (
                1.0 + (3.0 * 0.044715) * squared
            )
        return carry

    lax.fori_loop(0, 2 * piece // step, block, 0)


def rise(scalars, normed, grads, lines, bases, parts, masks):
    piece = grads[0].shape[0]
    half = FF // 2
    flat = [x for group in parts for x in group]
    return call(
        partial(rise_body, bases, masks),
        [scalars, *normed, *grads, lines, *flat],
        [
            shape((2 * piece, half), BF16),
            shape((2 * piece, half), F32),
            shape((half, D), BF16),
            shape((2 * piece, D), BF16),
            shape((2 * piece, D), BF16),
        ],
        [],
        14,
        "rise",
    )


def feed_body(base, masks, scalars, activated, slopes, expand, grad_pair, *refs):
    parts, refs = refs[: len(masks)], refs[len(masks) :]
    grad_hidden, normed_sent, normed_kept, out_sent, out_kept, sums, contract = refs
    half = expand.shape[0]
    piece = normed_kept.shape[0]

    def put_contract(place, chunk):
        rows = chunk.shape[0]
        start = pl.multiple_of(place * rows, 16) if base is not None else place * rows
        contract[pl.ds(start, rows), :] = chunk

    spread(scalars, base, parts, masks, put_contract)
    sums[...] = jnp.zeros_like(sums)
    step = min(MLP_ROWS, piece)

    def block(start, lead, normed_out, contract_out):
        rows = pl.ds(start, step)
        target = pl.ds(pl.multiple_of(lead + start, step), step)
        grad = grad_pair[target, :]
        back = jnp.zeros((step, D), F32)
        result = jnp.zeros((step, D), F32)
        for lanes in range(0, half, MLP_LANES):
            span = slice(lanes, lanes + MLP_LANES)
            hidden = (mm(grad, contract[:, span], NN) * slopes[target, span]).astype(BF16)
            grad_hidden[target, span] = hidden
            sums[0:1, span] += jnp.sum(hidden.astype(F32), axis=0, keepdims=True)
            back = back + mm(hidden, expand[span, :], NN)
            result = result + mm(activated[target, span], contract[:, span], NT)
        normed_out[rows, :] = back.astype(normed_out.dtype)
        contract_out[rows, :] = result.astype(contract_out.dtype)

    def own_block(i, carry):
        block(pl.multiple_of(i * step, step), 0, normed_kept, out_kept)
        return carry

    def other_block(i, carry):
        block(pl.multiple_of(i * step, step), piece, normed_sent, out_sent)
        return carry

    lax.fori_loop(0, piece // step, other_block, 0)
    lax.fori_loop(0, piece // step, own_block, 0)


def feed_forward(scalars, activated, slopes, expand, grad_pair, base, parts, masks):
    half = expand.shape[0]
    piece = grad_pair.shape[0] // 2
    return call(
        partial(feed_body, base, masks),
        [scalars, activated, slopes, expand, grad_pair, *parts],
        [
            shape((2 * piece, half), BF16),
            shape((piece, D), BF16),
            shape((piece, D), F32),
            shape((piece, D), BF16),
            shape((piece, D), F32),
            shape((8, half), F32),
        ],
        [pltpu.VMEM((D, half), BF16)],
        18,
        "feed_forward",
    )


def head_grads_body(scalars, own, other, weight_own, weight_across, keep, sent):
    piece = own.shape[0]
    for matrix, out in ((weight_across, sent), (weight_own, keep)):
        for place, rows in enumerate((own, other)):
            features = mm(rows[...], matrix[...], NN).T.astype(BF16)
            out[:, place * piece : (place + 1) * piece] = features


def head_grads(scalars, grads, weight_own, weight_across, markers):
    piece = grads[0].shape[0]
    outs = [shape((weight_own.shape[1], 2 * piece), BF16)] * 2
    return call(head_grads_body, [scalars, *grads, weight_own, weight_across], outs, [], 16, "head_gradients", markers)


def split_rows(total, plan, scalars, sent, kept):
    which, shift, size = plan
    bit = (scalars[which] >> shift) & 1
    rows = sent.shape[1]

    def one(m, carry):
        base = (m // size) * 2 * size + m % size
        for out, chosen in ((sent, 1 - bit), (kept, bit)):
            start = pl.multiple_of((base + chosen * size) * rows, 8)
            out[m] = total[pl.ds(start, rows), :].astype(out.dtype)
        return carry

    lax.fori_loop(0, sent.shape[0], one, 0)


def split_shapes(chips, rows, columns):
    dims = (chips // 2, rows, columns)
    return [shape(dims, BF16), shape(dims, F32)]


def output_weight_body(plan, scalars, own, other, keep, across_t, *refs):
    *outs, stacked, total = refs
    side = scalars[SIDE]
    piece = own.shape[0]
    width = keep.shape[0]
    for place, features in ((side, keep), (1 - side, across_t)):
        product = mm(features[:, :piece], own[...], NN) + mm(features[:, piece:], other[...], NN)
        stacked[pl.ds(pl.multiple_of(place * width, 8), width), :] = product
    total[...] = stacked[...].T
    if plan is None:
        outs[0][...] = total[...].astype(BF16)
    else:
        split_rows(total, plan, scalars, *outs)


def output_weight_grad(scalars, grads, keep, across_t, plan, chips, markers):
    width = keep.shape[0]
    outs = [shape((D, 2 * width), BF16)] if plan is None else split_shapes(chips, D // chips, 2 * width)
    return call(
        partial(output_weight_body, plan),
        [scalars, *grads, keep, across_t],
        outs,
        [pltpu.VMEM((2 * width, D), F32), pltpu.VMEM((D, 2 * width), F32)],
        16,
        "output_weight_gradient",
        markers=markers,
    )


def product_body(plan, lanes, scalars, left, right, sent, kept, total):
    for start in range(0, left.shape[1], lanes):
        block = left[:, start : start + lanes].T
        for column in range(0, right.shape[1], D):
            columns = slice(column, column + D)
            total[start : start + lanes, columns] = mm(block, right[:, columns], NN)
    split_rows(total, plan, scalars, sent, kept)


def product_grad(scalars, left, right, plan, chips, name, markers=()):
    rows, columns = left.shape[1], right.shape[1]
    return call(
        partial(product_body, plan, 256),
        [scalars, left, right],
        split_shapes(chips, rows // chips, columns),
        [pltpu.VMEM((rows, columns), F32)],
        24,
        name,
        markers=markers,
    )


def input_weight_body(aligned, rows_of_devices, scalars, grads, mine, other, *refs):
    total = refs[-1]
    piece = mine.shape[0] // 2
    step = min(MLP_ROWS, piece)
    total[...] = jnp.zeros_like(total)
    for place, (source, lead) in enumerate(((mine, 0), (other, 0), (mine, piece), (other, piece))):
        for start in range(0, piece, step):
            rows = grads[place * piece + start : place * piece + start + step, :]
            total[...] += mm(rows.T, source[lead + start : lead + start + step, :], NN)
    if not aligned:
        natural = refs[0]
        for kind in range(3):
            natural[kind] = total[kind * LANES : kind * LANES + natural.shape[1], :]
        return
    sent, kept = refs[0], refs[1]
    rows = sent.shape[1]
    bit = (scalars[ROW] >> 1) & 1
    count = rows_of_devices // 2
    for kind in range(3):
        for e in range(count):
            for out, chosen in ((sent, 1 - bit), (kept, bit)):
                start = kind * LANES + ((e // 2) * 4 + e % 2 + 2 * chosen) * rows
                out[kind * count + e] = total[pl.ds(pl.multiple_of(start, 8), rows), :].astype(out.dtype)


def input_weight_grad(scalars, grads, mine, other, rows_of_devices, block):
    aligned = block % 8 == 0
    part = (3 * rows_of_devices // 2, block, D)
    outs = [shape(part, BF16), shape(part, F32)]
    if not aligned:
        outs = [shape((3, block * rows_of_devices, D), F32)]
    return call(
        partial(input_weight_body, aligned, rows_of_devices),
        [scalars, grads, mine, other],
        outs,
        [pltpu.VMEM((3 * LANES, D), F32)],
        16,
        "input_weight_gradient",
    )


def first_grads_body(places, scalars, grads, weight, *refs):
    *far, kept = refs
    piece = kept.shape[0]
    half = piece // 2
    halves = len(far) == 2
    if halves:
        outs = ((0, far[0]), (half, far[1]))
    else:
        far_kept, arrived_a, arrived_b, reduced, whole = far
        outs = ((0, whole),)
        for lead, arrived in ((0, arrived_a), (half, arrived_b)):
            rows = slice(lead, lead + half)
            reduced[rows, :] = (far_kept[rows, :] + arrived[...].astype(F32)).astype(BF16)
    sent, stay = places
    for lead, out in outs:
        rows = grads[sent * piece + lead : sent * piece + lead + out.shape[0], :]
        out[...] = mm(rows, weight[...], NN).astype(BF16)
    kept[...] = mm(grads[stay * piece : (stay + 1) * piece, :], weight[...], NN)


def first_grads(scalars, grads, weight, places, far=(), markers=()):
    piece = grads.shape[0] // 4
    outs = [shape((piece, D), BF16)] * 2 if far else [shape((piece // 2, D), BF16)] * 2
    return call(
        partial(first_grads_body, places),
        [scalars, grads, weight, *far],
        outs + [shape((piece, D), F32)],
        [],
        16,
        "first_norm_gradient",
        markers=markers,
    )


def payload_body(hidden_rows, scalars, inputs, expand, contract, first, middle, heads, hidden, out):
    six = D // 128
    out[...] = jnp.zeros_like(out)
    out[: 2 * six, :] = first[: 2 * six, :]
    out[2 * six : 4 * six, :] = middle[: 2 * six, :]
    out[6 * six : 8 * six, :] = middle[2 * six : 4 * six, :]
    here = scalars[HERE]
    for line in range(2):
        row = heads[line : line + 1, :]
        row = jnp.where(here % 2 == 1, pltpu.roll(row, HD, 1), row)
        start = (4 + line) * six + (3 * here) // 2
        for part in range(2):
            out[pl.ds(start + part, 1), :] = row[:, part * 128 : (part + 1) * 128]
    for part in range(hidden_rows):
        line = 8 * six + scalars[CORE] * hidden_rows + part
        out[pl.ds(line, 1), :] = hidden[0:1, part * 128 : (part + 1) * 128]
    total = jnp.zeros((1, 1), F32)
    for gradients in (inputs, expand, contract):
        for i in range(gradients.shape[0]):
            values = gradients[i]
            rows = jnp.sum(values * values, axis=1, keepdims=True)
            total += jnp.sum(rows, axis=0, keepdims=True)
    lane = lax.broadcasted_iota(jnp.int32, (1, 128), 1)
    out[VECTOR_ROWS : VECTOR_ROWS + 1, :] = jnp.where(lane == 0, total, 0.0)


def make_payload(scalars, gradients, first, middle, heads, hidden):
    return call(
        partial(payload_body, hidden.shape[1] // 128),
        [scalars, *gradients, first, middle, heads, hidden],
        [shape((VECTOR_ROWS + 8, 128), F32)],
        [],
        12,
        "payload",
    )[0]


def reduce_body(plans, scalars, *refs):
    count = 2 * sum(len(sources) for sources, _ in plans)
    ins, outs = list(refs[:count]), list(refs[count:])
    for sources, split in plans:
        terms = []
        column = 0
        for full in sources:
            kept, arrived = ins.pop(0), ins.pop(0)
            columns = slice(column, column + arrived.shape[2])
            column += arrived.shape[2]

            def total(index, kept=kept, arrived=arrived, full=full):
                source = index
                if full is not None:
                    which, shift, size = full
                    bit = (scalars[which] >> shift) & 1
                    source = (index // size) * 2 * size + bit * size + index % size
                return kept[source].astype(F32) + arrived[index].astype(F32)

            terms.append((columns, total))
        if split is None:
            out = outs.pop(0)

            def whole(m, carry, out=out, terms=terms):
                for columns, total in terms:
                    out[m, :, columns] = total(m)
                return carry

            lax.fori_loop(0, out.shape[0], whole, 0)
        else:
            which, shift, size = split
            sent_out, kept_out = outs.pop(0), outs.pop(0)

            def halves(m, carry, sent_out=sent_out, kept_out=kept_out, terms=terms):
                bit = (scalars[which] >> shift) & 1
                base = (m // size) * 2 * size + m % size
                for columns, total in terms:
                    kept_out[m, :, columns] = total(base + bit * size)
                    sent_out[m, :, columns] = total(base + (1 - bit) * size).astype(BF16)
                return carry

            lax.fori_loop(0, kept_out.shape[0], halves, 0)


HEAD_LANES = LANES


VECTOR_ROWS = (8 * D + FF) // 128


def row_norm(values):
    mean = jnp.mean(values, axis=1, keepdims=True)
    centered = values - mean
    variance = jnp.mean(centered * centered, axis=1, keepdims=True)
    inverse = lax.rsqrt(variance + NORM_EPS)
    return centered * inverse, inverse


def norm_input_gradient(upstream, values, gain):
    unit, inverse = row_norm(values)
    scaled = upstream * gain
    first = jnp.mean(scaled, axis=1, keepdims=True)
    second = jnp.mean(scaled * unit, axis=1, keepdims=True)
    return inverse * (scaled - first - unit * second), unit


def stack_rows(sums, rows):
    for place, row in enumerate(rows):
        total = jnp.sum(row, axis=0, keepdims=True)
        for part in range(D // 128):
            line = place * (D // 128) + part
            sums[line : line + 1, :] += total[:, part * 128 : (part + 1) * 128]


def middle_body(own, arrived, middle, cotangent, lines, grad_mid, grad_branch, sums):
    @pl.when(pl.program_id(0) == 0)
    def _():
        sums[...] = jnp.zeros_like(sums)

    upstream = own[...] + arrived[...].astype(F32)
    passed, unit = norm_input_gradient(upstream, middle[...], vector_row(lines, 2))
    outer = cotangent[...].astype(F32)
    total = outer + passed
    rounded = total.astype(BF16)
    grad_mid[...] = total
    grad_branch[...] = rounded
    stack_rows(sums, [upstream * unit, upstream, rounded.astype(F32), outer])


def first_body(own, arrived, across, tokens, grad_mid, lines, input_grad, sums):
    @pl.when(pl.program_id(0) == 0)
    def _():
        sums[...] = jnp.zeros_like(sums)

    upstream = own[...] + arrived[...].astype(F32) + across[...].astype(F32)
    passed, unit = norm_input_gradient(upstream, tokens[...].astype(F32), vector_row(lines, 0))
    input_grad[...] = (grad_mid[...] + passed).astype(BF16)
    stack_rows(sums, [upstream * unit, upstream])


def norm_backward(body, arrays, lines, outputs, name, markers=()):
    rows = arrays[0].shape[0]
    step = min(128, rows)
    tile = pl.BlockSpec((step, D), lambda i: (i, 0))
    row = pl.BlockSpec(lines.shape, lambda i: (0, 0))
    sums = pl.BlockSpec((24, 128), lambda i: (0, 0))
    count = len(arrays) + 1

    def whole(*refs):
        body(*refs[:count], *refs[count + len(markers) :])

    return pl.pallas_call(
        whole,
        grid=(rows // step,),
        out_shape=tuple(jax.ShapeDtypeStruct((rows, D), kind) for kind in outputs)
        + (jax.ShapeDtypeStruct((24, 128), F32),),
        in_specs=[tile] * len(arrays) + [row] + [LEFT] * len(markers),
        out_specs=tuple(tile for _ in outputs) + (sums,),
        compiler_params=pltpu.CompilerParams(vmem_limit_bytes=10 * 2**20),
        cost_estimate=cost(name),
        name=name,
    )(*arrays, lines, *markers)


def moments_body(*refs):
    payload, refs = refs[0], refs[1:]
    grads, firsts, seconds, masters = refs[0:4], refs[4:9], refs[9:14], refs[14:19]
    first_outs, second_outs, direction_outs = refs[20:25], refs[25:30], refs[30:35]
    clip = clip_of(payload)
    for place in range(5):
        gradient = grads[place][...] if place < 4 else payload[0:VECTOR_ROWS, :]
        master = masters[place][...]
        first_new, second_new, direction = direction_of(
            gradient, firsts[place][...], seconds[place][...], master, clip
        )
        first_outs[place][...] = first_new
        second_outs[place][...] = second_new
        direction_outs[place][...] = direction if place < 4 else master - VECTOR_RATE * direction


def clip_of(payload):
    vector = payload[0:VECTOR_ROWS, :]
    total = payload[VECTOR_ROWS : VECTOR_ROWS + 1, 0:1] + jnp.sum(
        jnp.sum(vector * vector, axis=1, keepdims=True), axis=0, keepdims=True
    )
    return jnp.minimum(1.0, 1.0 / jnp.sqrt(total))


def direction_of(gradient, first_old, second_old, master, clip):
    clipped = gradient * clip
    first_new = 0.5 * first_old + 0.5 * clipped
    second_new = 0.5 * second_old + 0.5 * clipped * clipped
    correction = 1.0 - 0.5**STEP
    direction = (
        first_new / correction / (jnp.sqrt(second_new / correction) + ADAM_EPS) + DECAY_RATE * master
    )
    return first_new, second_new, direction


def directions_body(*refs):
    payload, squares, refs = refs[0], refs[-1], refs[1:-1]
    grads, firsts, seconds, masters = refs[0:4], refs[4:8], refs[8:12], refs[12:16]
    clip = clip_of(payload)
    lane = lax.broadcasted_iota(jnp.int32, squares.shape, 1)
    row = lax.broadcasted_iota(jnp.int32, squares.shape, 0)
    found = jnp.zeros(squares.shape, F32)
    for place in range(4):
        master = masters[place][...]
        _, _, direction = direction_of(
            grads[place][...], firsts[place][...], seconds[place][...], master, clip
        )
        for offset, values in ((0, direction), (4, master)):
            square = jnp.sum(jnp.sum(values * values, axis=1, keepdims=True), axis=0, keepdims=True)
            found = found + jnp.where((lane == place + offset) & (row == 0), square, 0.0)
    squares[...] = found


def directions_step(payload, grads, firsts, seconds, masters):
    vmem = pl.BlockSpec(memory_space=pltpu.VMEM)
    return pl.pallas_call(
        directions_body,
        out_shape=jax.ShapeDtypeStruct((8, 128), F32),
        in_specs=[vmem] * 17,
        out_specs=vmem,
        compiler_params=pltpu.CompilerParams(vmem_limit_bytes=16 * 2**20),
        cost_estimate=cost("directions"),
        name="directions",
    )(payload, *grads, *firsts, *seconds, *masters)


def moments_step(payload, grads, firsts, seconds, masters, marker):
    vmem = pl.BlockSpec(memory_space=pltpu.VMEM)
    shapes = [jax.ShapeDtypeStruct(master.shape, F32) for master in masters]
    outs = pl.pallas_call(
        moments_body,
        out_shape=tuple(shapes * 3),
        in_specs=[vmem] * 21,
        out_specs=(vmem,) * 15,
        compiler_params=pltpu.CompilerParams(vmem_limit_bytes=16 * 2**20),
        cost_estimate=cost("moments"),
        name="moments",
    )(payload, *grads, *firsts, *seconds, *masters, marker)
    return outs[0:5], outs[5:10], outs[10:15]


def weights_body(*refs):
    squares, refs = refs[0], refs[1:]
    directions, masters, outs, lows = refs[0:4], refs[4:8], refs[8:12], refs[12:16]
    norms = refs[16]
    norms[...] = jnp.zeros_like(norms)
    weight = jnp.sqrt(squares[0:1, 4:8])
    update = jnp.sqrt(squares[0:1, 0:4])
    for place in range(4):
        ratio = MATRIX_RATE * (weight[:, place : place + 1] / update[:, place : place + 1])
        new = masters[place][...] - ratio * directions[place][...]
        outs[place][...] = new
        lows[place][...] = new.astype(BF16)
    norms[0:1, 0:4] = weight
    norms[1:2, 0:4] = update


def weights_step(squares, directions, masters):
    vmem = pl.BlockSpec(memory_space=pltpu.VMEM)
    outs = pl.pallas_call(
        weights_body,
        out_shape=tuple(jax.ShapeDtypeStruct(m.shape, F32) for m in masters)
        + tuple(jax.ShapeDtypeStruct(m.shape, BF16) for m in masters)
        + (jax.ShapeDtypeStruct((8, 128), F32),),
        in_specs=[vmem] * 9,
        out_specs=(vmem,) * 9,
        compiler_params=pltpu.CompilerParams(vmem_limit_bytes=60 * 2**20),
        cost_estimate=cost("weights"),
        name="weights",
    )(squares, *directions, *masters)
    return outs[0:4], outs[4:8], outs[8]


BOTH = ("batch", "head")
PARTNER = 1
ACROSS = 2


def dot(a, b, dims):
    return lax.dot_general(a, b, (dims, ((), ())), preferred_element_type=F32)


def swap(values, axis, mask):
    size = lax.axis_size(axis)
    return lax.ppermute(values, axis, [(place, place ^ mask) for place in range(size)])


def partner(values):
    return swap(values, "head", PARTNER)


def across(values):
    return swap(values, "head", ACROSS)


def batch_masks():
    return [1 << bit for bit in range((lax.axis_size("batch") - 1).bit_length())][::-1]


class Chain:
    def __init__(self, scalars, chunk, order, chips):
        self.scalars, self.values, self.order, self.chips = scalars, chunk[None], list(order), chips
        self.masks, self.flip, self.arrived = [0], 0, None

    def start(self):
        axis, mask = self.order.pop(0)
        self.flip = mask if not self.chips else (2 * mask if axis == "batch" else 1)
        self.arrived = swap(self.values, axis, mask)

    def pair(self):
        return self.values, self.arrived

    def take(self, joined):
        self.values = joined
        self.masks = self.masks + [mask ^ self.flip for mask in self.masks]
        self.arrived = None
        if self.order:
            self.start()

    def drain(self, left):
        while len(self.order) > left:
            self.take(join(self.scalars, [self.pair()], [0])[0])

    def halves(self, joined, orders):
        chains = []
        for values, order in zip(joined, orders):
            chain = Chain(self.scalars, values[0], order, self.chips)
            chain.values = values
            chain.masks = self.masks + [mask ^ self.flip for mask in self.masks]
            chain.start()
            chains.append(chain)
        return chains

    def parts(self, multiple, kinds=1):
        rows = self.values.shape[1] // kinds
        source = CHIP if self.chips else ROW
        arrays, masks = [self.values], [self.masks]
        if self.arrived is not None:
            arrays.append(self.arrived)
            masks.append([mask ^ self.flip for mask in self.masks])
        if rows % multiple == 0:
            return source, arrays, masks
        chunks = [array[r] for array in arrays for r in range(array.shape[0])]
        order = [mask for group in masks for mask in group]
        count = len(order)
        natural = jnp.stack([chunks[order.index(place)] for place in range(count)])
        size = 1
        while size < count:
            cut = natural.reshape((-1, 2, size) + natural.shape[1:])
            flipped = jnp.concatenate([cut[:, 1:], cut[:, :1]], axis=1)
            cut = jnp.where((self.scalars[source] & size) != 0, flipped, cut)
            natural = cut.reshape(natural.shape)
            size *= 2
        natural = natural.reshape(count, kinds, rows, -1).transpose(1, 0, 2, 3)
        return None, [natural.reshape(1, kinds * count * rows, -1)], [[0]]


def join_all(scalars, chains, extra=(), markers=()):
    pairs = [chain.pair() for chain in chains] + list(extra)
    joined = join(scalars, pairs, [0] * len(pairs), markers)
    for chain, values in zip(chains, joined):
        chain.take(values)
    return joined[len(chains) :]


def bit_source(bit):
    axis, mask = bit
    return (ROW, mask.bit_length() - 1) if axis == "batch" else (SIDE, 0)


class Reduce:
    def __init__(self, bits, order, *values):
        self.left, self.order, self.values, self.full = list(bits), list(order), values, None

    def split(self):
        bit = self.order.pop(0)
        size = 1 << (len(self.left) - 1 - self.left.index(bit))
        self.left.remove(bit)
        self.bit = bit
        return (*bit_source(bit), size)

    def begin(self, scalars):
        self.full = self.split()
        self.sources = []
        for values in self.values:
            self.send(scalars, values)

    def send(self, scalars, values):
        which, shift, size = self.full
        bit = (scalars[which] >> shift) & 1
        rows = values.shape[1:]
        cut = values.reshape((-1, 2, size) + rows)
        sent = lax.dynamic_index_in_dim(cut, 1 - bit, 1, keepdims=False).reshape((-1,) + rows)
        self.sources.append((values, swap(sent.astype(BF16), *self.bit)))

    def begin_with(self, *pairs):
        self.full = None
        self.sources = [(kept, swap(sent, *self.bit)) for sent, kept in pairs]

    def add_source(self, sent, kept):
        self.sources.append((kept, swap(sent, *self.bit)))

    @property
    def kept(self):
        return self.sources[0][0]


def reduce_all(scalars, chains, markers=()):
    plans, inputs, outs = [], [scalars], []
    for chain in chains:
        full = chain.full
        for source in chain.sources:
            inputs += source
        plan = chain.split() if chain.order else None
        plans.append(([full] * len(chain.sources), plan))
        count, rows, _ = chain.sources[0][1].shape
        columns = sum(arrived.shape[2] for _, arrived in chain.sources)
        if plan is None:
            outs.append(shape((count, rows, columns), F32))
        else:
            outs.append(shape((count // 2, rows, columns), BF16))
            outs.append(shape((count // 2, rows, columns), F32))
    found = list(call(partial(reduce_body, plans), inputs, outs, [], 16, "add_arrived", markers=markers))
    for chain, (_, plan) in zip(chains, plans):
        if plan is None:
            chain.values = found.pop(0)
        else:
            sent, kept = found.pop(0), found.pop(0)
            chain.begin_with((sent, kept))


def all_sum(values):
    for mask in (PARTNER, ACROSS):
        values = values + swap(values, "head", mask)
    masks = batch_masks()[::-1]
    if len(masks) % 2:
        values = values + swap(values, "batch", masks[0])
        masks = masks[1:]
    for low, high in zip(masks[::2], masks[1::2]):
        near = values + swap(values, "batch", low)
        far = swap(values, "batch", high) + swap(values, "batch", low | high)
        values = near + far
    return values


def block_permutation(slot, to_owner):
    rows, heads = lax.axis_size("batch"), lax.axis_size("head")
    total = rows * heads
    pairs = []
    for owner in range(total):
        place = (3 * owner + slot) % total
        holder = (place % rows) * heads + place // rows
        pairs.append((holder, owner) if to_owner else (owner, holder))
    return pairs


def holder_place():
    return lax.axis_size("batch") * lax.axis_index("head") + lax.axis_index("batch")


def blocks_to_holders(shard):
    blocks = shard.reshape(3, -1, D)
    return [lax.ppermute(blocks[slot], BOTH, block_permutation(slot, False)) for slot in range(3)]


def blocks_to_owners(blocks):
    total = lax.axis_size("batch") * lax.axis_size("head")
    place = holder_place()
    arrived = []
    for slot in range(3):
        kind = ((slot + 3 * total - place) * total) % 3
        sent = lax.dynamic_index_in_dim(blocks, kind, 0, keepdims=False)
        arrived.append(lax.ppermute(sent, BOTH, block_permutation(slot, True)))
    return jnp.concatenate(arrived, axis=0)


def on_device(
    tokens,
    cotangent,
    lengths,
    input_weight,
    output_weight,
    expand_weight,
    contract_weight,
    vector_params,
    input_first,
    input_second,
    output_first,
    output_second,
    expand_first,
    expand_second,
    contract_first,
    contract_second,
    vector_first,
    vector_second,
):
    rows_of_devices = lax.axis_size("batch")
    head_count = lax.axis_size("head")
    chips = rows_of_devices * head_count // 2
    here = lax.axis_index("head")
    core = here % 2
    side = here // 2
    width = D // head_count
    heads = width // HD
    piece = tokens.shape[0]
    docs = lengths.shape[1]
    hidden_block = FF // (2 * chips)
    half = FF // 2
    out_rows = output_weight.shape[0]
    total_devices = rows_of_devices * head_count
    batch_bits = [("batch", mask) for mask in batch_masks()]
    far, near = batch_bits[:-1], batch_bits[-1]
    side_bit = ("head", ACROSS)
    bits = batch_bits + [side_bit]
    bias_contract = vector_params[7 * D : 8 * D]

    def by_core(mine, other, axis):
        high = core == 1
        return jnp.stack([jnp.where(high, other, mine), jnp.where(high, mine, other)], axis=axis)

    def pick(values, index, axis):
        return lax.dynamic_index_in_dim(values, index, axis, keepdims=False)

    scalars, sequences = Places(), Places(lengths)
    lines = vector_params.reshape(VECTOR_ROWS, 128)

    *in_blocks, expand_low, output_mine, output_cut, contract_low, normed_own = prepare(
        scalars, input_weight, expand_weight, output_weight, contract_weight, tokens, lines
    )
    in_arrived = [
        lax.ppermute(block, BOTH, block_permutation(slot, False)) for slot, block in enumerate(in_blocks)
    ]
    expands = Chain(scalars, expand_low, far, True)
    expands.start()
    normed_across = across(normed_own)
    contract_cut = contract_low.reshape(out_rows, chips, 2, hidden_block)
    sent = jnp.concatenate([pick(contract_cut, 1 - core, 2).reshape(out_rows, half), output_cut], axis=1)
    columns_arrived = partner(sent)
    contract_mine = pick(contract_cut, core, 2).reshape(out_rows, half)
    contract_shard = by_core(contract_mine, columns_arrived[:, :half], 0).reshape(2 * out_rows, half)
    output_shard = by_core(output_mine, columns_arrived[:, half:], 0).reshape(2 * out_rows, 2 * width)
    contracts = Chain(scalars, contract_shard, [near, side_bit] + far, True)
    contracts.start()

    def cores_first(vectors):
        hidden = vectors[:, 8 * D :].reshape(-1, chips, 2, hidden_block).transpose(0, 2, 1, 3)
        return jnp.concatenate([vectors[:, : 8 * D], hidden.reshape(-1, FF)], axis=1).reshape(-1, VECTOR_ROWS, 128)

    def cores_back(rows):
        vectors = rows.reshape(-1, 8 * D + FF)
        hidden = vectors[:, 8 * D :].reshape(-1, 2, chips, hidden_block).transpose(0, 2, 1, 3)
        return jnp.concatenate([vectors[:, : 8 * D], hidden.reshape(-1, FF)], axis=1)

    vector_state = cores_first(jnp.stack([vector_first, vector_second, vector_params]))
    kinds = block_kinds(scalars, in_arrived, total_devices).reshape(-1, D)
    inputs = Chain(scalars, kinds, batch_bits, False)
    outputs = Chain(scalars, output_shard, far + [side_bit, near], True)
    inputs.start()
    outputs.start()
    inputs.drain(2)
    outputs.drain(3)
    join_all(scalars, [inputs, outputs, contracts], (), (expands.arrived,))
    expands.drain(1)
    (normed_mine,) = join_all(
        scalars, [inputs, outputs, contracts, expands], [(normed_own, normed_across)], (vector_state,)
    )
    contracts.drain(1)
    normed_other = partner(normed_mine)

    projected, weight_in, joined = project(
        scalars,
        normed_mine,
        normed_other,
        lines,
        *inputs.parts(8, 3),
        [outputs.pair(), expands.pair()],
        [0, 2],
        (),
    )
    outputs.take(joined[0])
    expands = expands.halves(joined[1:], ([near, side_bit], [side_bit, near]))

    blocks = 4 * piece // BLOCK
    before = attention_forward(sequences, projected, heads, docs, piece, (0, blocks // 2))
    join_all(scalars, [*expands, contracts, outputs], (), (before[0],))
    _, logs, keep_t, send_t = attention_forward(
        sequences, projected, heads, docs, piece, (blocks // 2, blocks), before, (contracts.values,)
    )
    across_t = across(send_t)
    cotangent_other = partner(cotangent)
    *branch_sent, branch_kept, output_own, output_across = branch(
        scalars,
        keep_t,
        across_t,
        *outputs.parts(16),
        [expands[0].arrived, expands[1].arrived],
    )
    resid_mid, *normed_two = middle_norm(
        scalars,
        tokens,
        branch_kept,
        [partner(rows) for rows in branch_sent],
        lines,
        (contracts.arrived,),
    )
    arrived_two = [partner(rows) for rows in normed_two]

    found = [chain.parts(16) for chain in expands]
    activated, slopes, expand_half, normed_pair, cotangent_pair = rise(
        scalars,
        (*normed_two, *arrived_two),
        (cotangent, cotangent_other),
        vector_state[2],
        [part[0] for part in found],
        [part[1] for part in found],
        [part[2] for part in found],
    )
    grad_hidden, normed_sent, normed_kept, out_sent, out_kept, hidden_sums = feed_forward(
        scalars, activated, slopes, expand_half, cotangent_pair, *contracts.parts(16)
    )
    normed_arrived = partner(normed_sent)
    out_arrived = partner(out_sent)
    block_out = (resid_mid + out_kept + out_arrived.astype(F32) + bias_contract).astype(BF16)

    expand_sum = Reduce(bits, [near] + far[-1:] + [side_bit] + far[:-1][::-1])
    contract_sum = Reduce(bits, far[-1:] + [side_bit, near] + far[:-1][::-1])
    output_sum = Reduce(bits, [side_bit] + far[-1:])
    sums = [expand_sum, contract_sum]
    aligned = hidden_block % 8 == 0 and 2 * out_rows % 8 == 0
    if aligned:
        plans = [chain.split() for chain in sums]
        contract_sum.begin_with(
            product_grad(scalars, cotangent_pair, activated, plans[1], chips, "contract_gradient")
        )
    else:
        expand_total = dot(grad_hidden, normed_pair, ((0,), (0,))).astype(BF16)
        contract_total = dot(cotangent_pair, activated, ((0,), (0,))).astype(BF16)
        expand_sum.values = (expand_total.reshape(chips, hidden_block, D),)
        contract_sum.values = (contract_total.reshape(chips, 2 * out_rows, half),)
        for chain in sums:
            chain.begin(scalars)
    grad_mid, grad_branch, middle_sums = norm_backward(
        middle_body,
        [normed_kept, normed_arrived, resid_mid, cotangent],
        lines,
        (F32, BF16),
        "middle_gradient",
        (contract_sum.kept,),
    )
    grads = (grad_branch, partner(grad_branch))
    if aligned:
        expand_sum.begin_with(
            product_grad(scalars, grad_hidden, normed_pair, plans[0], chips, "expand_gradient")
        )

    grad_keep_t, grad_sent_t = head_grads(scalars, grads, output_own, output_across, (expand_sum.kept,))
    grad_arrived_t = across(grad_sent_t)
    output_found = output_weight_grad(
        scalars, grads, keep_t, across_t, output_sum.split() if aligned else None, chips, (grad_sent_t,)
    )
    if aligned:
        output_sum.begin_with(output_found)
    else:
        output_sum.values = (output_found[0].reshape(chips, 2 * out_rows, 2 * width),)
        output_sum.begin(scalars)
    inputs = (sequences, projected, (keep_t, send_t), (grad_keep_t, grad_arrived_t), logs, heads, docs, piece)
    *before, _ = attention_backward(
        *inputs, (0, blocks // 2), (), [block_out, *(chain.kept for chain in (*sums, output_sum))]
    )
    reduce_all(scalars, [*sums, output_sum], (before[0],))
    grad_heads, _, _, head_sums = attention_backward(
        *inputs, (blocks // 2, blocks), before, [chain.kept for chain in sums]
    )

    contract_sum.sources += output_sum.sources
    reduce_all(scalars, sums, (grad_heads,))
    *far_sent, far_kept = first_grads(
        scalars, grad_heads, weight_in, (3, 2), (), [chain.kept for chain in sums]
    )
    far_arrived = [partner(rows) for rows in far_sent]
    in_found = input_weight_grad(
        scalars, grad_heads, normed_mine, normed_other, rows_of_devices, D // total_devices
    )
    in_sum = Reduce(batch_bits, far[-1:] + [near] + far[:-1][::-1])
    if len(in_found) == 2:
        in_sum.split()
        in_sum.begin_with(in_found)
    else:
        in_sum.values = (in_found[0].reshape(3 * rows_of_devices, -1, D),)
        in_sum.begin(scalars)
    reduce_all(scalars, sums, (in_sum.kept,))
    reduce_all(scalars, [in_sum], (sums[0].kept,))
    reduced_far, near_sent, near_kept = first_grads(
        scalars, grad_heads, weight_in, (1, 0), (far_kept, *far_arrived), (in_sum.kept,)
    )
    first_arrived = across(reduced_far)
    near_arrived = partner(near_sent)
    while sums[0].order:
        reduce_all(scalars, sums, (reduced_far,))
    reduce_all(scalars, sums, (reduced_far,))
    while in_sum.order:
        reduce_all(scalars, [in_sum], (expand_sum.values,))
    reduce_all(scalars, [in_sum], (first_arrived,))
    input_piece_grad = blocks_to_owners(in_sum.values)
    expand_grad = expand_sum.values.reshape(hidden_block, D)
    contract_mixed = contract_sum.values[0, :, :half]
    output_mixed = contract_sum.values[0, :, half:]

    def columns_other(mixed, parts):
        cut = mixed.reshape(2, out_rows, parts, -1)
        return pick(cut, core, 0), partner(pick(cut, 1 - core, 0))

    contract_grad = by_core(*columns_other(contract_mixed, chips), 2).reshape(out_rows, -1)
    output_grad = by_core(*columns_other(output_mixed, 2), 2).reshape(out_rows, -1)
    input_grad, first_sums = norm_backward(
        first_body,
        [near_kept, near_arrived, first_arrived, tokens, grad_mid],
        lines,
        (BF16,),
        "first_gradient",
    )

    masters = (input_weight, output_weight, expand_weight, contract_weight)
    gradients = [part.values for part in (in_sum, expand_sum, contract_sum)]
    payload = all_sum(
        make_payload(scalars, gradients, first_sums, middle_sums, head_sums, hidden_sums)
    )
    vector_grads = payload[:VECTOR_ROWS]
    grad_norm = jnp.sqrt(payload[VECTOR_ROWS, 0] + jnp.sum(vector_grads * vector_grads))
    shard_grads = (input_piece_grad, output_grad, expand_grad, contract_grad)
    firsts = (input_first, output_first, expand_first, contract_first)
    seconds = (input_second, output_second, expand_second, contract_second)
    squares = directions_step(payload, shard_grads, firsts, seconds, masters)
    first_new, second_new, directions = moments_step(
        payload,
        shard_grads,
        (*firsts, vector_state[0]),
        (*seconds, vector_state[1]),
        (*masters, vector_state[2]),
        squares,
    )
    squares = all_sum(squares)
    vector_news = cores_back(jnp.stack([first_new[4], second_new[4], directions[4]]))
    news, lows, norms = weights_step(squares, directions[:4], masters)
    results = []
    for position in range(4):
        results += [first_new[position], second_new[position], news[position], lows[position]]
    return (
        block_out,
        input_grad,
        grad_norm,
        norms[:2, :4].reshape(8),
        *results,
        vector_news[0],
        vector_news[1],
        vector_news[2],
    )


def solution(mesh):
    split = P(BOTH, None)
    return jax.shard_map(
        on_device,
        mesh=mesh,
        in_specs=(split, split, P("batch", None)) + (split,) * 4 + (P(),) + (split,) * 8 + (P(), P()),
        out_specs=(split, split, P(), P()) + (split,) * 16 + (P(), P(), P()),
        check_vma=False,
    )
```

```python
from functools import partial
import jax
import jax.numpy as jnp
from jax import lax
from jax.experimental import pallas as pl
from jax.experimental.pallas import tpu as pltpu
from jax.sharding import PartitionSpec as P

D = 768
HD = 64
FF = 3072
STEP = 5
NORM_EPS = 1e-05
ADAM_EPS = 1e-06
DECAY_RATE = 0.01
MATRIX_RATE = 0.5
VECTOR_RATE = 0.1
ROOT_TWO_OVER_PI = (2.0 / 3.141592653589793) ** 0.5
BLOCK = 256
LANES = 256
NT = (((1,), (1,)), ((), ()))
NN = (((1,), (0,)), ((), ()))
F32 = jnp.float32
BF16 = jnp.bfloat16


def mm(a, b, dims):
    return lax.dot_general(a, b, dims, preferred_element_type=F32)


def block_start(index, per_piece, me):
    piece = index // per_piece
    return pl.multiple_of(((piece ^ me) * per_piece + index % per_piece) * BLOCK, BLOCK)


def starts_of(scalars, docs, positions):
    first = jnp.zeros_like(positions)
    for doc in range(docs - 1):
        end = scalars[ENDS + doc]
        first = jnp.where(positions >= end, end, first)
    return first


def first_block(scalars, docs, index):
    position = index * BLOCK
    first = jnp.int32(0)
    for doc in range(docs - 1):
        end = scalars[ENDS + doc]
        first = jnp.where(position >= end, end, first)
    return first // BLOCK


def head_lanes(block, heads):
    if heads == 1:
        return [block]
    lane = lax.broadcasted_iota(jnp.int32, block.shape, 1) // HD
    return [jnp.where(lane == j, block, jnp.zeros_like(block)) for j in range(heads)]


def allowed_mask(index, key_block, doc_first):
    key = key_block * BLOCK + lax.broadcasted_iota(jnp.int32, (BLOCK, BLOCK), 0)
    if index is None:
        return key >= doc_first
    query = index * BLOCK + lax.broadcasted_iota(jnp.int32, (1, BLOCK), 1)
    return (key <= query) & (key >= doc_first)


def over_keys(first, last, key_step, state):
    pairs = (last - first) // 2

    def two(p, state):
        return key_step(first + 2 * p + 1, key_step(first + 2 * p, state))

    state = lax.fori_loop(0, pairs, two, state)
    return lax.fori_loop(first + 2 * pairs, last, key_step, state)


def group_lanes(group, kind):
    start = kind * LANES + group * HEAD_LANES
    return slice(start, start + HEAD_LANES)


def forward_body(heads, docs, per_piece, span, final, scalars, qkv, *refs):
    if span[0] > 0:
        refs = refs[2:]
    out_t, log_out, *ends, values_t = refs
    me = scalars[HERE]
    width = heads * HD

    def transpose_values(i, carry):
        v = qkv[pl.ds(block_start(i, per_piece, me), BLOCK), group_lanes(0, 2)]
        values_t[:, pl.ds(pl.multiple_of(i * BLOCK, BLOCK), BLOCK)] = v.T[:width]
        return carry

    lax.fori_loop(0, span[1], transpose_values, 0)

    def query_block(i, carry):
        row = block_start(i, per_piece, me)
        q_heads = head_lanes(qkv[pl.ds(row, BLOCK), group_lanes(0, 0)] * BF16(HD ** -0.5), heads)
        positions = i * BLOCK + lax.broadcasted_iota(jnp.int32, (1, BLOCK), 1)
        doc_first = starts_of(scalars, docs, positions)

        def key_step(kb, state, query=None):
            allowed = allowed_mask(query, kb, doc_first)
            k = qkv[pl.ds(block_start(kb, per_piece, me), BLOCK), group_lanes(0, 1)]
            column = pl.ds(pl.multiple_of(kb * BLOCK, BLOCK), BLOCK)
            new = []
            for j in range(heads):
                top, total, acc = state[j]
                s = jnp.where(allowed, mm(k, q_heads[j], NT), -1e30)
                top_new = jnp.maximum(top, jnp.max(s, axis=0, keepdims=True))
                p = jnp.exp(s - top_new)
                fade = jnp.exp(top - top_new)
                total = total * fade + jnp.sum(p, axis=0, keepdims=True)
                v_t = values_t[j * HD : (j + 1) * HD, column]
                acc = acc * fade + mm(v_t, p.astype(BF16), NN)
                new.append((top_new, total, acc))
            return tuple(new)

        init = tuple(
            (jnp.full((1, BLOCK), -1e30, F32), jnp.zeros((1, BLOCK), F32), jnp.zeros((HD, BLOCK), F32))
            for _ in range(heads)
        )
        state = key_step(i, init, i)
        state = lax.fori_loop(first_block(scalars, docs, i), i, key_step, state)
        column = pl.ds(row, BLOCK)
        for j in range(heads):
            top, total, acc = state[j]
            out_t[j * HD : (j + 1) * HD, column] = (acc / total).astype(BF16)
            log_out[j : j + 1, pl.ds(pl.multiple_of(i * BLOCK, BLOCK), BLOCK)] = top + jnp.log(total)
        return carry

    if span[0] == 0:
        log_out[...] = jnp.zeros_like(log_out)
    lax.fori_loop(span[0], span[1], query_block, 0)
    if final:
        half = out_t.shape[1] // 2
        ends[0][...] = out_t[:, :half]
        ends[1][...] = out_t[:, half:]


def attention_forward(scalars, qkv, heads, docs, piece, span, before=(), markers=()):
    rows = qkv.shape[0]
    width = heads * HD
    final = span[1] == rows // BLOCK
    inputs = [scalars, qkv, *before]
    outs = [shape((width, rows), BF16), shape((8, rows), F32)]
    return call(
        partial(forward_body, heads, docs, piece // BLOCK, span, final),
        inputs,
        outs + [shape((width, rows // 2), BF16)] * (2 * final),
        [pltpu.VMEM((width, rows), BF16)],
        14,
        "attention_forward",
        markers=markers,
        aliases={len(inputs) - 2 + i: i for i in range(2)} if before else {},
    )


def backward_body(
    heads, docs, per_piece, span, final, scalars, qkv, out_keep, out_send, grad_keep, grad_recv, logs, *refs
):
    if span[0] > 0:
        refs = refs[3:]
    grads, d_keys, d_values, sums, keys_t, out_t, grad_t = refs
    me = scalars[HERE]
    width = heads * HD
    scale = HD ** -0.5
    half = out_keep.shape[1]
    out_t[:, :half] = out_keep[...]
    out_t[:, half:] = out_send[...]
    grad_t[:, :half] = grad_keep[...]
    grad_t[:, half:] = grad_recv[...]
    if span[0] == 0:
        d_keys[...] = jnp.zeros_like(d_keys)
        d_values[...] = jnp.zeros_like(d_values)

    def transpose_keys(i, carry):
        k = qkv[pl.ds(block_start(i, per_piece, me), BLOCK), group_lanes(0, 1)]
        keys_t[:, pl.ds(pl.multiple_of(i * BLOCK, BLOCK), BLOCK)] = k.T[:width]
        return carry

    lax.fori_loop(0, span[1], transpose_keys, 0)

    def padded(rows, kind):
        return jnp.concatenate([rows, jnp.zeros((LANES - width, BLOCK), kind)], axis=0)

    def query_block(i, carry):
        row = block_start(i, per_piece, me)
        q_heads = head_lanes(qkv[pl.ds(row, BLOCK), group_lanes(0, 0)] * BF16(scale), heads)
        o_t = out_t[:, pl.ds(row, BLOCK)]
        g_t = grad_t[:, pl.ds(row, BLOCK)]
        product = o_t.astype(F32) * g_t.astype(F32)
        deltas = [jnp.sum(product[j * HD : (j + 1) * HD], axis=0, keepdims=True) for j in range(heads)]
        g_heads = head_lanes(padded(g_t, BF16).T, heads)
        natural = pl.ds(pl.multiple_of(i * BLOCK, BLOCK), BLOCK)
        log_rows = [logs[j : j + 1, natural] for j in range(heads)]
        positions = i * BLOCK + lax.broadcasted_iota(jnp.int32, (1, BLOCK), 1)
        doc_first = starts_of(scalars, docs, positions)

        def key_step(kb, d_q, query=None):
            allowed = allowed_mask(query, kb, doc_first)
            key_row = pl.ds(block_start(kb, per_piece, me), BLOCK)
            k = qkv[key_row, group_lanes(0, 1)]
            v = qkv[key_row, group_lanes(0, 2)]
            column = pl.ds(pl.multiple_of(kb * BLOCK, BLOCK), BLOCK)
            d_k = d_keys[key_row, :]
            d_v = d_values[key_row, :]
            new = []
            for j in range(heads):
                s = jnp.where(allowed, mm(k, q_heads[j], NT), -1e30)
                p = jnp.exp(s - log_rows[j])
                d_v = d_v + mm(p.astype(BF16), g_heads[j], NN)
                d_p = mm(v, g_heads[j], NT)
                d_s = (p * (d_p - deltas[j])).astype(BF16)
                d_k = d_k + mm(d_s, q_heads[j], NN)
                new.append(d_q[j] + mm(keys_t[j * HD : (j + 1) * HD, column], d_s, NN))
            d_keys[key_row, :] = d_k
            d_values[key_row, :] = d_v
            return tuple(new)

        d_q = key_step(i, tuple(jnp.zeros((HD, BLOCK), F32) for _ in range(heads)), i)
        d_q = over_keys(first_block(scalars, docs, i), i, key_step, d_q)
        stacked = padded(jnp.concatenate(d_q, axis=0), F32) * scale
        grads[pl.ds(row, BLOCK), 0:LANES] = stacked.T.astype(BF16)
        return carry

    lax.fori_loop(span[0], span[1], query_block, 0)
    sums[...] = jnp.zeros_like(sums)
    if final:
        grads[:, LANES : 2 * LANES] = d_keys[...].astype(BF16)
        grads[:, 2 * LANES : 3 * LANES] = d_values[...].astype(BF16)
        for line, kind in enumerate((0, 2)):
            columns = grads[:, kind * LANES : (kind + 1) * LANES].astype(F32)
            sums[line : line + 1, :] = jnp.sum(columns, axis=0, keepdims=True)


def attention_backward(scalars, qkv, outs, grads, logs, heads, docs, piece, span, before=(), markers=()):
    rows = qkv.shape[0]
    width = heads * HD
    final = span[1] == rows // BLOCK
    inputs = [scalars, qkv, *outs, *grads, logs, *before]
    return call(
        partial(backward_body, heads, docs, piece // BLOCK, span, final),
        inputs,
        [
            shape((rows, 3 * LANES), BF16),
            shape((rows, LANES), F32),
            shape((rows, LANES), F32),
            shape((8, LANES), F32),
        ],
        [pltpu.VMEM((width, rows), BF16)] * 3,
        19,
        "attention_backward",
        markers=markers,
        aliases={len(inputs) - 3 + i: i for i in range(3)} if before else {},
    )


MICROSECONDS = {
    "prepare": 2.8,
    "block_kinds": 0.5,
    "join": 1.2,
    "project": 5,
    "attention_forward": 8,
    "branch": 1.3,
    "middle_norm": 0.2,
    "rise": 0.1,
    "feed_forward": 11,
    "head_gradients": 0.2,
    "output_weight_gradient": 0.2,
    "attention_backward": 2,
    "first_norm_gradient": 0.5,
    "input_weight_gradient": 1,
    "add_arrived": 0.05,
    "middle_gradient": 0.4,
    "first_gradient": 2.5,
    "payload": 1,
    "expand_gradient": 0.4,
    "contract_gradient": 0.4,
    "moments": 2,
    "directions": 1,
    "weights": 1.5,
}
COST_SCALE = 1.0


def cost(name):
    flops = int(MICROSECONDS[name] * COST_SCALE * 1.0e9)
    return pl.CostEstimate(flops=flops, bytes_accessed=0, transcendentals=0)


VMEM = pl.BlockSpec(memory_space=pltpu.VMEM)
SMEM = pl.BlockSpec(memory_space=pltpu.SMEM)
LEFT = pl.BlockSpec(memory_space=pl.ANY)
TN = (((0,), (0,)), ((), ()))
HERE, CHIP, ROW, CORE, SIDE, PLACE = range(6)
ENDS = 6


class Places:
    def __init__(self, lengths=None):
        self.lengths = lengths

    def __getitem__(self, number):
        here, row = lax.axis_index("head"), lax.axis_index("batch")
        heads, rows = lax.axis_size("head"), lax.axis_size("batch")
        if number == HERE:
            return here
        if number == CHIP:
            return row * (heads // 2) + here // 2
        if number == ROW:
            return row
        if number == CORE:
            return here % 2
        if number == SIDE:
            return here // 2
        if number == PLACE:
            return rows * here + row
        return sum(self.lengths[0, doc] for doc in range(number - ENDS + 1))


def call(body, inputs, outputs, scratch, mib, name, markers=(), aliases={}):
    lengths, inputs = inputs[0].lengths, inputs[1:]
    lead = [] if lengths is None else [lengths]
    count = len(lead) + len(inputs)

    def whole(*refs):
        places = Places(refs[0] if lead else None)
        body(places, *refs[len(lead) : count], *refs[count + len(markers) :])

    return pl.pallas_call(
        whole,
        out_shape=tuple(outputs),
        in_specs=[SMEM] * len(lead) + [VMEM] * len(inputs) + [LEFT] * len(markers),
        out_specs=(VMEM,) * len(outputs),
        scratch_shapes=scratch,
        input_output_aliases=aliases,
        compiler_params=pltpu.CompilerParams(vmem_limit_bytes=mib * 2**20),
        cost_estimate=cost(name),
        name=name,
    )(*lead, *inputs, *markers)


def lines_row(lines, first, count):
    return jnp.concatenate([lines[pl.ds(first + i, 1), :] for i in range(count)], axis=1)


def vector_row(lines, number):
    return lines_row(lines, number * (D // 128), D // 128)


def heads_row(lines, number, here):
    width = D // lax.axis_size("head")
    row = lines_row(lines, number * (D // 128) + (width * here) // 128, LANES // 128)
    row = jnp.where((width * here) % 128 != 0, pltpu.roll(row, LANES - HD, 1), row)
    lane = lax.broadcasted_iota(jnp.int32, row.shape, 1)
    return jnp.where(lane < width, row, 0.0)


def shape(dims, kind):
    return jax.ShapeDtypeStruct(tuple(dims), kind)


def join_pairs(ins, outs, cuts):
    outs = list(outs)
    for i, cut in enumerate(cuts):
        own, arrived = ins[2 * i], ins[2 * i + 1]
        half = own.shape[0]
        if cut == 0:
            out = outs.pop(0)
            out[:half] = own[...]
            out[half:] = arrived[...]
            continue
        rows = own.shape[1] // cut
        for part in range(cut):
            out = outs.pop(0)
            out[:half] = own[:, part * rows : (part + 1) * rows]
            out[half:] = arrived[:, part * rows : (part + 1) * rows]


def join_body(cuts, scalars, *refs):
    count = 2 * len(cuts)
    join_pairs(refs[:count], refs[count:], cuts)


def join_shapes(pairs, cuts):
    shapes = []
    for (own, _), cut in zip(pairs, cuts):
        dims = (2 * own.shape[0],) + own.shape[1:]
        if cut == 0:
            shapes.append(shape(dims, own.dtype))
        else:
            shapes += [shape((dims[0], dims[1] // cut, dims[2]), own.dtype)] * cut
    return shapes


def join(scalars, pairs, cuts, markers=()):
    flat = [x for pair in pairs for x in pair]
    return call(
        partial(join_body, cuts), [scalars, *flat], join_shapes(pairs, cuts), [], 24, "join", markers=markers
    )


def prepare_body(scalars, weight_in, weight_expand, weight_out, weight_back, tokens, lines, *outs):
    blocks, (expand, mine, other, back, normed) = outs[:3], outs[3:]
    back[...] = weight_back[...].astype(BF16)
    rows = blocks[0].shape[0]
    for slot, out in enumerate(blocks):
        out[...] = weight_in[slot * rows : (slot + 1) * rows, :].astype(BF16)
    expand[...] = weight_expand[...].astype(BF16)
    quarter = D // 4
    wide = weight_out[...]
    even = jnp.concatenate([wide[:, :quarter], wide[:, 2 * quarter : 3 * quarter]], axis=1)
    odd = jnp.concatenate([wide[:, quarter : 2 * quarter], wide[:, 3 * quarter :]], axis=1)
    high = scalars[CORE] == 1
    mine[...] = jnp.where(high, odd, even).astype(BF16)
    other[...] = jnp.where(high, even, odd).astype(BF16)
    gain, shift = vector_row(lines, 0), vector_row(lines, 1)
    step = min(128, tokens.shape[0])
    for start in range(0, tokens.shape[0], step):
        unit, _ = row_norm(tokens[start : start + step, :].astype(F32))
        normed[start : start + step, :] = (unit * gain + shift).astype(BF16)


def prepare(scalars, weight_in, weight_expand, weight_out, weight_back, tokens, lines):
    rows, out_rows = weight_in.shape[0] // 3, weight_out.shape[0]
    return call(
        prepare_body,
        [scalars, weight_in, weight_expand, weight_out, weight_back, tokens, lines],
        [shape((rows, D), BF16)] * 3
        + [
            shape(weight_expand.shape, BF16),
            shape((out_rows, D // 2), BF16),
            shape((out_rows, D // 2), BF16),
            shape(weight_back.shape, BF16),
            shape(tokens.shape, BF16),
        ],
        [],
        60,
        "prepare",
    )


def kinds_body(total, scalars, first, second, third, out):
    place = scalars[PLACE]
    rows = first.shape[0]
    for slot, block in enumerate((first, second, third)):
        kind = ((slot + 3 * total - place) * total) % 3
        out[kind] = block[...]


def block_kinds(scalars, blocks, total):
    rows = blocks[0].shape[0]
    outs = [shape((3, rows, D), BF16)]
    return call(partial(kinds_body, total), [scalars, *blocks], outs, [], 8, "block_kinds")[0]


def spread(scalars, base, parts, masks, put):
    origin = scalars[base] if base is not None else 0
    for ref, own in zip(parts, masks):
        for r, mask in enumerate(own):
            put(origin ^ mask if base is not None else mask, ref[r])


def project_body(base, masks, cuts, scalars, mine, other, lines, *refs):
    parts, refs = refs[: len(masks)], refs[len(masks) :]
    pairs, refs = refs[: 2 * len(cuts)], refs[2 * len(cuts) :]
    out, weight_out, weight = refs[0], refs[1], refs[-1]
    join_pairs(pairs, refs[2:-1], cuts)
    weight[...] = jnp.zeros_like(weight)

    def put(place, chunk):
        rows = chunk.shape[0] // 3
        wide = chunk.astype(F32)
        for kind in range(3):
            start = kind * LANES + place * rows
            if base is not None:
                start = pl.multiple_of(start, 8)
            weight[pl.ds(start, rows), :] = wide[kind * rows : (kind + 1) * rows]

    spread(scalars, base, parts, masks, put)
    low = weight[...].astype(BF16)
    weight_out[...] = low
    piece = mine.shape[0] // 2
    here = scalars[HERE]
    bias = jnp.concatenate(
        [heads_row(lines, 4, here), jnp.zeros((1, LANES), F32), heads_row(lines, 5, here)], axis=1
    )
    for place, (source, lead) in enumerate(((mine, 0), (other, 0), (mine, piece), (other, piece))):
        rows = source[lead : lead + piece, :]
        out[place * piece : (place + 1) * piece, :] = (mm(rows, low, NT) + bias).astype(BF16)


def project(scalars, mine, other, lines, base, parts, masks, pairs, cuts, markers):
    rows = 2 * mine.shape[0]
    flat = [x for pair in pairs for x in pair]
    outs = [shape((rows, 3 * LANES), BF16), shape((3 * LANES, D), BF16), *join_shapes(pairs, cuts)]
    found = call(
        partial(project_body, base, masks, cuts),
        [scalars, mine, other, lines, *parts, *flat],
        outs,
        [pltpu.VMEM((3 * LANES, D), F32)],
        24,
        "project",
        markers=markers,
    )
    return found[0], found[1], found[2:]


def branch_body(base, masks, scalars, keep, across_t, *refs):
    parts, refs = refs[: len(masks)], refs[len(masks) :]
    sent_a, sent_b, kept, own_out, across_out, weight = refs
    width = own_out.shape[1]

    def put(place, chunk):
        rows = chunk.shape[0]
        start = pl.multiple_of(place * rows, 16) if base is not None else place * rows
        for group in range(2):
            weight[group, pl.ds(start, rows), :] = chunk[:, group * width : (group + 1) * width]

    spread(scalars, base, parts, masks, put)
    side = scalars[SIDE]
    own_out[...] = weight[side]
    across_out[...] = weight[1 - side]
    piece = kept.shape[0]
    def rows_of(columns):
        return mm(keep[:, columns].T, own_out[...], NT) + mm(across_t[:, columns].T, across_out[...], NT)

    half = piece // 2
    sent_a[...] = rows_of(slice(piece, piece + half)).astype(BF16)
    sent_b[...] = rows_of(slice(piece + half, 2 * piece)).astype(BF16)
    kept[...] = rows_of(slice(0, piece))


def middle_norm_body(scalars, tokens, kept, arrived_a, arrived_b, lines, middle, normed_a, normed_b):
    bias, gain, shift = vector_row(lines, 6), vector_row(lines, 2), vector_row(lines, 3)
    half = normed_a.shape[0]
    step = min(128, half)
    for lead, arrived, normed in ((0, arrived_a, normed_a), (half, arrived_b, normed_b)):
        for start in range(0, half, step):
            rows = slice(lead + start, lead + start + step)
            values = tokens[rows, :].astype(F32) + kept[rows, :]
            values = values + arrived[start : start + step, :].astype(F32) + bias
            middle[rows, :] = values
            unit, _ = row_norm(values)
            normed[start : start + step, :] = (unit * gain + shift).astype(BF16)


def middle_norm(scalars, tokens, kept, arrived, lines, markers):
    piece = tokens.shape[0]
    return call(
        middle_norm_body,
        [scalars, tokens, kept, *arrived, lines],
        [shape((piece, D), F32), shape((piece // 2, D), BF16), shape((piece // 2, D), BF16)],
        [],
        16,
        "middle_norm",
        markers,
    )


def branch(scalars, keep, across_t, base, parts, masks, markers):
    width, rows = keep.shape
    piece = rows // 2
    return call(
        partial(branch_body, base, masks),
        [scalars, keep, across_t, *parts],
        [shape((piece // 2, D), BF16)] * 2
        + [shape((piece, D), F32), shape((D, width), BF16), shape((D, width), BF16)],
        [pltpu.VMEM((2, D, width), BF16)],
        24,
        "branch",
        markers=markers,
    )


MLP_ROWS = 256
MLP_LANES = 512


def rise_body(bases, masks, scalars, own_a, own_b, other_a, other_b, grad_own, grad_other, lines, *refs):
    count = sum(map(len, masks))
    parts, (activated, slopes, expand, pair, grad_pair) = refs[:count], refs[count:]
    half = expand.shape[0]
    piece = grad_own.shape[0]
    for lead, rows in enumerate((own_a, own_b, other_a, other_b)):
        pair[lead * (piece // 2) : (lead + 1) * (piece // 2), :] = rows[...]
    grad_pair[:piece, :] = grad_own[...]
    grad_pair[piece:, :] = grad_other[...]
    bias = lines_row(lines, 8 * (D // 128) + scalars[CORE] * (half // 128), half // 128)

    def put_expand(index):
        def put(place, chunk):
            rows = chunk.shape[0]
            start = place * 2 * rows + index * rows
            if bases[index] is not None:
                start = pl.multiple_of(start, 16)
            expand[pl.ds(start, rows), :] = chunk

        return put

    taken = 0
    for index, own_masks in enumerate(masks):
        spread(scalars, bases[index], parts[taken : taken + len(own_masks)], own_masks, put_expand(index))
        taken += len(own_masks)
    step = min(MLP_ROWS, piece)

    def block(i, carry):
        rows = pl.ds(pl.multiple_of(i * step, step), step)
        normed = pair[rows, :]
        for lanes in range(0, half, MLP_LANES):
            span = slice(lanes, lanes + MLP_LANES)
            expanded = mm(normed, expand[span, :], NT) + bias[:, span]
            squared = expanded * expanded
            bent = jnp.tanh(ROOT_TWO_OVER_PI * (expanded + 0.044715 * (expanded * squared)))
            rise = 0.5 * (1.0 + bent)
            activated[rows, span] = (expanded * rise).astype(BF16)
            slopes[rows, span] = rise + (0.5 * ROOT_TWO_OVER_PI) * expanded * (1.0 - bent * bent) * (
                1.0 + (3.0 * 0.044715) * squared
            )
        return carry

    lax.fori_loop(0, 2 * piece // step, block, 0)


def rise(scalars, normed, grads, lines, bases, parts, masks):
    piece = grads[0].shape[0]
    half = FF // 2
    flat = [x for group in parts for x in group]
    return call(
        partial(rise_body, bases, masks),
        [scalars, *normed, *grads, lines, *flat],
        [
            shape((2 * piece, half), BF16),
            shape((2 * piece, half), F32),
            shape((half, D), BF16),
            shape((2 * piece, D), BF16),
            shape((2 * piece, D), BF16),
        ],
        [],
        14,
        "rise",
    )


def feed_body(base, masks, scalars, activated, slopes, expand, grad_pair, *refs):
    parts, refs = refs[: len(masks)], refs[len(masks) :]
    grad_hidden, normed_sent, normed_kept, out_sent, out_kept, sums, contract = refs
    half = expand.shape[0]
    piece = normed_kept.shape[0]

    def put_contract(place, chunk):
        rows = chunk.shape[0]
        start = pl.multiple_of(place * rows, 16) if base is not None else place * rows
        contract[pl.ds(start, rows), :] = chunk

    spread(scalars, base, parts, masks, put_contract)
    sums[...] = jnp.zeros_like(sums)
    step = min(MLP_ROWS, piece)

    def block(start, lead, normed_out, contract_out):
        rows = pl.ds(start, step)
        target = pl.ds(pl.multiple_of(lead + start, step), step)
        grad = grad_pair[target, :]
        back = jnp.zeros((step, D), F32)
        result = jnp.zeros((step, D), F32)
        for lanes in range(0, half, MLP_LANES):
            span = slice(lanes, lanes + MLP_LANES)
            hidden = (mm(grad, contract[:, span], NN) * slopes[target, span]).astype(BF16)
            grad_hidden[target, span] = hidden
            sums[0:1, span] += jnp.sum(hidden.astype(F32), axis=0, keepdims=True)
            back = back + mm(hidden, expand[span, :], NN)
            result = result + mm(activated[target, span], contract[:, span], NT)
        normed_out[rows, :] = back.astype(normed_out.dtype)
        contract_out[rows, :] = result.astype(contract_out.dtype)

    def own_block(i, carry):
        block(pl.multiple_of(i * step, step), 0, normed_kept, out_kept)
        return carry

    def other_block(i, carry):
        block(pl.multiple_of(i * step, step), piece, normed_sent, out_sent)
        return carry

    lax.fori_loop(0, piece // step, other_block, 0)
    lax.fori_loop(0, piece // step, own_block, 0)


def feed_forward(scalars, activated, slopes, expand, grad_pair, base, parts, masks):
    half = expand.shape[0]
    piece = grad_pair.shape[0] // 2
    return call(
        partial(feed_body, base, masks),
        [scalars, activated, slopes, expand, grad_pair, *parts],
        [
            shape((2 * piece, half), BF16),
            shape((piece, D), BF16),
            shape((piece, D), F32),
            shape((piece, D), BF16),
            shape((piece, D), F32),
            shape((8, half), F32),
        ],
        [pltpu.VMEM((D, half), BF16)],
        18,
        "feed_forward",
    )


def head_grads_body(scalars, own, other, weight_own, weight_across, keep, sent):
    piece = own.shape[0]
    for matrix, out in ((weight_across, sent), (weight_own, keep)):
        for place, rows in enumerate((own, other)):
            features = mm(rows[...], matrix[...], NN).T.astype(BF16)
            out[:, place * piece : (place + 1) * piece] = features


def head_grads(scalars, grads, weight_own, weight_across, markers):
    piece = grads[0].shape[0]
    outs = [shape((weight_own.shape[1], 2 * piece), BF16)] * 2
    return call(head_grads_body, [scalars, *grads, weight_own, weight_across], outs, [], 16, "head_gradients", markers)


def split_rows(total, plan, scalars, sent, kept):
    which, shift, size = plan
    bit = (scalars[which] >> shift) & 1
    rows = sent.shape[1]

    def one(m, carry):
        base = (m // size) * 2 * size + m % size
        for out, chosen in ((sent, 1 - bit), (kept, bit)):
            start = pl.multiple_of((base + chosen * size) * rows, 8)
            out[m] = total[pl.ds(start, rows), :].astype(out.dtype)
        return carry

    lax.fori_loop(0, sent.shape[0], one, 0)


def split_shapes(chips, rows, columns):
    dims = (chips // 2, rows, columns)
    return [shape(dims, BF16), shape(dims, F32)]


def output_weight_body(plan, scalars, own, other, keep, across_t, *refs):
    *outs, stacked, total = refs
    side = scalars[SIDE]
    piece = own.shape[0]
    width = keep.shape[0]
    for place, features in ((side, keep), (1 - side, across_t)):
        product = mm(features[:, :piece], own[...], NN) + mm(features[:, piece:], other[...], NN)
        stacked[pl.ds(pl.multiple_of(place * width, 8), width), :] = product
    total[...] = stacked[...].T
    if plan is None:
        outs[0][...] = total[...].astype(BF16)
    else:
        split_rows(total, plan, scalars, *outs)


def output_weight_grad(scalars, grads, keep, across_t, plan, chips, markers):
    width = keep.shape[0]
    outs = [shape((D, 2 * width), BF16)] if plan is None else split_shapes(chips, D // chips, 2 * width)
    return call(
        partial(output_weight_body, plan),
        [scalars, *grads, keep, across_t],
        outs,
        [pltpu.VMEM((2 * width, D), F32), pltpu.VMEM((D, 2 * width), F32)],
        16,
        "output_weight_gradient",
        markers=markers,
    )


def product_body(plan, lanes, scalars, left, right, sent, kept, total):
    for start in range(0, left.shape[1], lanes):
        block = left[:, start : start + lanes].T
        for column in range(0, right.shape[1], D):
            columns = slice(column, column + D)
            total[start : start + lanes, columns] = mm(block, right[:, columns], NN)
    split_rows(total, plan, scalars, sent, kept)


def product_grad(scalars, left, right, plan, chips, name, markers=()):
    rows, columns = left.shape[1], right.shape[1]
    return call(
        partial(product_body, plan, 256),
        [scalars, left, right],
        split_shapes(chips, rows // chips, columns),
        [pltpu.VMEM((rows, columns), F32)],
        24,
        name,
        markers=markers,
    )


def input_weight_body(aligned, rows_of_devices, scalars, grads, mine, other, *refs):
    total = refs[-1]
    piece = mine.shape[0] // 2
    step = min(MLP_ROWS, piece)
    total[...] = jnp.zeros_like(total)
    for place, (source, lead) in enumerate(((mine, 0), (other, 0), (mine, piece), (other, piece))):
        for start in range(0, piece, step):
            rows = grads[place * piece + start : place * piece + start + step, :]
            total[...] += mm(rows.T, source[lead + start : lead + start + step, :], NN)
    if not aligned:
        natural = refs[0]
        for kind in range(3):
            natural[kind] = total[kind * LANES : kind * LANES + natural.shape[1], :]
        return
    sent, kept = refs[0], refs[1]
    rows = sent.shape[1]
    bit = (scalars[ROW] >> 1) & 1
    count = rows_of_devices // 2
    for kind in range(3):
        for e in range(count):
            for out, chosen in ((sent, 1 - bit), (kept, bit)):
                start = kind * LANES + ((e // 2) * 4 + e % 2 + 2 * chosen) * rows
                out[kind * count + e] = total[pl.ds(pl.multiple_of(start, 8), rows), :].astype(out.dtype)


def input_weight_grad(scalars, grads, mine, other, rows_of_devices, block):
    aligned = block % 8 == 0
    part = (3 * rows_of_devices // 2, block, D)
    outs = [shape(part, BF16), shape(part, F32)]
    if not aligned:
        outs = [shape((3, block * rows_of_devices, D), F32)]
    return call(
        partial(input_weight_body, aligned, rows_of_devices),
        [scalars, grads, mine, other],
        outs,
        [pltpu.VMEM((3 * LANES, D), F32)],
        16,
        "input_weight_gradient",
    )


def first_grads_body(places, scalars, grads, weight, *refs):
    *far, kept = refs
    piece = kept.shape[0]
    half = piece // 2
    halves = len(far) == 2
    if halves:
        outs = ((0, far[0]), (half, far[1]))
    else:
        far_kept, arrived_a, arrived_b, reduced, whole = far
        outs = ((0, whole),)
        for lead, arrived in ((0, arrived_a), (half, arrived_b)):
            rows = slice(lead, lead + half)
            reduced[rows, :] = (far_kept[rows, :] + arrived[...].astype(F32)).astype(BF16)
    sent, stay = places
    for lead, out in outs:
        rows = grads[sent * piece + lead : sent * piece + lead + out.shape[0], :]
        out[...] = mm(rows, weight[...], NN).astype(BF16)
    kept[...] = mm(grads[stay * piece : (stay + 1) * piece, :], weight[...], NN)


def first_grads(scalars, grads, weight, places, far=(), markers=()):
    piece = grads.shape[0] // 4
    outs = [shape((piece, D), BF16)] * 2 if far else [shape((piece // 2, D), BF16)] * 2
    return call(
        partial(first_grads_body, places),
        [scalars, grads, weight, *far],
        outs + [shape((piece, D), F32)],
        [],
        16,
        "first_norm_gradient",
        markers=markers,
    )


def payload_body(hidden_rows, scalars, inputs, expand, contract, first, middle, heads, hidden, out):
    six = D // 128
    out[...] = jnp.zeros_like(out)
    out[: 2 * six, :] = first[: 2 * six, :]
    out[2 * six : 4 * six, :] = middle[: 2 * six, :]
    out[6 * six : 8 * six, :] = middle[2 * six : 4 * six, :]
    here = scalars[HERE]
    for line in range(2):
        row = heads[line : line + 1, :]
        row = jnp.where(here % 2 == 1, pltpu.roll(row, HD, 1), row)
        start = (4 + line) * six + (3 * here) // 2
        for part in range(2):
            out[pl.ds(start + part, 1), :] = row[:, part * 128 : (part + 1) * 128]
    for part in range(hidden_rows):
        line = 8 * six + scalars[CORE] * hidden_rows + part
        out[pl.ds(line, 1), :] = hidden[0:1, part * 128 : (part + 1) * 128]
    total = jnp.zeros((1, 1), F32)
    for gradients in (inputs, expand, contract):
        for i in range(gradients.shape[0]):
            values = gradients[i]
            rows = jnp.sum(values * values, axis=1, keepdims=True)
            total += jnp.sum(rows, axis=0, keepdims=True)
    lane = lax.broadcasted_iota(jnp.int32, (1, 128), 1)
    out[VECTOR_ROWS : VECTOR_ROWS + 1, :] = jnp.where(lane == 0, total, 0.0)


def make_payload(scalars, gradients, first, middle, heads, hidden, markers):
    return call(
        partial(payload_body, hidden.shape[1] // 128),
        [scalars, *gradients, first, middle, heads, hidden],
        [shape((VECTOR_ROWS + 8, 128), F32)],
        [],
        12,
        "payload",
        markers,
    )[0]


def reduce_body(plans, scalars, *refs):
    count = 2 * sum(len(sources) for sources, _ in plans)
    ins, outs = list(refs[:count]), list(refs[count:])
    for sources, split in plans:
        terms = []
        column = 0
        for full in sources:
            kept, arrived = ins.pop(0), ins.pop(0)
            columns = slice(column, column + arrived.shape[2])
            column += arrived.shape[2]

            def total(index, kept=kept, arrived=arrived, full=full):
                source = index
                if full is not None:
                    which, shift, size = full
                    bit = (scalars[which] >> shift) & 1
                    source = (index // size) * 2 * size + bit * size + index % size
                return kept[source].astype(F32) + arrived[index].astype(F32)

            terms.append((columns, total))
        if split is None:
            out = outs.pop(0)

            def whole(m, carry, out=out, terms=terms):
                for columns, total in terms:
                    out[m, :, columns] = total(m)
                return carry

            lax.fori_loop(0, out.shape[0], whole, 0)
        else:
            which, shift, size = split
            sent_out, kept_out = outs.pop(0), outs.pop(0)

            def halves(m, carry, sent_out=sent_out, kept_out=kept_out, terms=terms):
                bit = (scalars[which] >> shift) & 1
                base = (m // size) * 2 * size + m % size
                for columns, total in terms:
                    kept_out[m, :, columns] = total(base + bit * size)
                    sent_out[m, :, columns] = total(base + (1 - bit) * size).astype(BF16)
                return carry

            lax.fori_loop(0, kept_out.shape[0], halves, 0)


HEAD_LANES = LANES


VECTOR_ROWS = (8 * D + FF) // 128


def row_norm(values):
    mean = jnp.mean(values, axis=1, keepdims=True)
    centered = values - mean
    variance = jnp.mean(centered * centered, axis=1, keepdims=True)
    inverse = lax.rsqrt(variance + NORM_EPS)
    return centered * inverse, inverse


def norm_input_gradient(upstream, values, gain):
    unit, inverse = row_norm(values)
    scaled = upstream * gain
    first = jnp.mean(scaled, axis=1, keepdims=True)
    second = jnp.mean(scaled * unit, axis=1, keepdims=True)
    return inverse * (scaled - first - unit * second), unit


def stack_rows(sums, rows):
    for place, row in enumerate(rows):
        total = jnp.sum(row, axis=0, keepdims=True)
        for part in range(D // 128):
            line = place * (D // 128) + part
            sums[line : line + 1, :] += total[:, part * 128 : (part + 1) * 128]


def middle_body(own, arrived, middle, cotangent, lines, grad_mid, grad_branch, sums):
    @pl.when(pl.program_id(0) == 0)
    def _():
        sums[...] = jnp.zeros_like(sums)

    upstream = own[...] + arrived[...].astype(F32)
    passed, unit = norm_input_gradient(upstream, middle[...], vector_row(lines, 2))
    outer = cotangent[...].astype(F32)
    total = outer + passed
    rounded = total.astype(BF16)
    grad_mid[...] = total
    grad_branch[...] = rounded
    stack_rows(sums, [upstream * unit, upstream, rounded.astype(F32), outer])


def first_body(own, arrived, across, tokens, grad_mid, lines, input_grad, sums):
    @pl.when(pl.program_id(0) == 0)
    def _():
        sums[...] = jnp.zeros_like(sums)

    upstream = own[...] + arrived[...].astype(F32) + across[...].astype(F32)
    passed, unit = norm_input_gradient(upstream, tokens[...].astype(F32), vector_row(lines, 0))
    input_grad[...] = (grad_mid[...] + passed).astype(BF16)
    stack_rows(sums, [upstream * unit, upstream])


def norm_backward(body, arrays, lines, outputs, name, markers=()):
    rows = arrays[0].shape[0]
    step = min(256, rows)
    tile = pl.BlockSpec((step, D), lambda i: (i, 0))
    row = pl.BlockSpec(lines.shape, lambda i: (0, 0))
    sums = pl.BlockSpec((24, 128), lambda i: (0, 0))
    count = len(arrays) + 1

    def whole(*refs):
        body(*refs[:count], *refs[count + len(markers) :])

    return pl.pallas_call(
        whole,
        grid=(rows // step,),
        out_shape=tuple(jax.ShapeDtypeStruct((rows, D), kind) for kind in outputs)
        + (jax.ShapeDtypeStruct((24, 128), F32),),
        in_specs=[tile] * len(arrays) + [row] + [LEFT] * len(markers),
        out_specs=tuple(tile for _ in outputs) + (sums,),
        compiler_params=pltpu.CompilerParams(vmem_limit_bytes=14 * 2**20),
        cost_estimate=cost(name),
        name=name,
    )(*arrays, lines, *markers)


def moments_body(*refs):
    payload, refs = refs[0], refs[1:]
    grads, firsts, seconds, masters = refs[0:4], refs[4:9], refs[9:14], refs[14:19]
    first_outs, second_outs, direction_outs = refs[20:25], refs[25:30], refs[30:35]
    clip = clip_of(payload)
    for place in range(5):
        gradient = grads[place][...] if place < 4 else payload[0:VECTOR_ROWS, :]
        master = masters[place][...]
        first_new, second_new, direction = direction_of(
            gradient, firsts[place][...], seconds[place][...], master, clip
        )
        first_outs[place][...] = first_new
        second_outs[place][...] = second_new
        direction_outs[place][...] = direction if place < 4 else master - VECTOR_RATE * direction


def clip_of(payload):
    vector = payload[0:VECTOR_ROWS, :]
    total = payload[VECTOR_ROWS : VECTOR_ROWS + 1, 0:1] + jnp.sum(
        jnp.sum(vector * vector, axis=1, keepdims=True), axis=0, keepdims=True
    )
    return jnp.minimum(1.0, 1.0 / jnp.sqrt(total))


def direction_of(gradient, first_old, second_old, master, clip):
    clipped = gradient * clip
    first_new = 0.5 * first_old + 0.5 * clipped
    second_new = 0.5 * second_old + 0.5 * clipped * clipped
    correction = 1.0 - 0.5**STEP
    direction = (
        first_new / correction / (jnp.sqrt(second_new / correction) + ADAM_EPS) + DECAY_RATE * master
    )
    return first_new, second_new, direction


def directions_body(*refs):
    payload, squares, refs = refs[0], refs[-1], refs[1:-1]
    grads, firsts, seconds, masters = refs[0:4], refs[4:8], refs[8:12], refs[12:16]
    clip = clip_of(payload)
    lane = lax.broadcasted_iota(jnp.int32, squares.shape, 1)
    row = lax.broadcasted_iota(jnp.int32, squares.shape, 0)
    found = jnp.zeros(squares.shape, F32)
    for place in range(4):
        master = masters[place][...]
        _, _, direction = direction_of(
            grads[place][...], firsts[place][...], seconds[place][...], master, clip
        )
        for offset, values in ((0, direction), (4, master)):
            square = jnp.sum(jnp.sum(values * values, axis=1, keepdims=True), axis=0, keepdims=True)
            found = found + jnp.where((lane == place + offset) & (row == 0), square, 0.0)
    squares[...] = found


def directions_step(payload, grads, firsts, seconds, masters):
    vmem = pl.BlockSpec(memory_space=pltpu.VMEM)
    return pl.pallas_call(
        directions_body,
        out_shape=jax.ShapeDtypeStruct((8, 128), F32),
        in_specs=[vmem] * 17,
        out_specs=vmem,
        compiler_params=pltpu.CompilerParams(vmem_limit_bytes=16 * 2**20),
        cost_estimate=cost("directions"),
        name="directions",
    )(payload, *grads, *firsts, *seconds, *masters)


def moments_step(payload, grads, firsts, seconds, masters, marker):
    vmem = pl.BlockSpec(memory_space=pltpu.VMEM)
    shapes = [jax.ShapeDtypeStruct(master.shape, F32) for master in masters]
    outs = pl.pallas_call(
        moments_body,
        out_shape=tuple(shapes * 3),
        in_specs=[vmem] * 21,
        out_specs=(vmem,) * 15,
        compiler_params=pltpu.CompilerParams(vmem_limit_bytes=16 * 2**20),
        cost_estimate=cost("moments"),
        name="moments",
    )(payload, *grads, *firsts, *seconds, *masters, marker)
    return outs[0:5], outs[5:10], outs[10:15]


def weights_body(*refs):
    squares, refs = refs[0], refs[1:]
    directions, masters, outs, lows = refs[0:4], refs[4:8], refs[8:12], refs[12:16]
    norms = refs[16]
    norms[...] = jnp.zeros_like(norms)
    weight = jnp.sqrt(squares[0:1, 4:8])
    update = jnp.sqrt(squares[0:1, 0:4])
    for place in range(4):
        ratio = MATRIX_RATE * (weight[:, place : place + 1] / update[:, place : place + 1])
        new = masters[place][...] - ratio * directions[place][...]
        outs[place][...] = new
        lows[place][...] = new.astype(BF16)
    norms[0:1, 0:4] = weight
    norms[1:2, 0:4] = update


def weights_step(squares, directions, masters):
    vmem = pl.BlockSpec(memory_space=pltpu.VMEM)
    outs = pl.pallas_call(
        weights_body,
        out_shape=tuple(jax.ShapeDtypeStruct(m.shape, F32) for m in masters)
        + tuple(jax.ShapeDtypeStruct(m.shape, BF16) for m in masters)
        + (jax.ShapeDtypeStruct((8, 128), F32),),
        in_specs=[vmem] * 9,
        out_specs=(vmem,) * 9,
        compiler_params=pltpu.CompilerParams(vmem_limit_bytes=60 * 2**20),
        cost_estimate=cost("weights"),
        name="weights",
    )(squares, *directions, *masters)
    return outs[0:4], outs[4:8], outs[8]


BOTH = ("batch", "head")
PARTNER = 1
ACROSS = 2


def dot(a, b, dims):
    return lax.dot_general(a, b, (dims, ((), ())), preferred_element_type=F32)


def swap(values, axis, mask):
    size = lax.axis_size(axis)
    return lax.ppermute(values, axis, [(place, place ^ mask) for place in range(size)])


def partner(values):
    return swap(values, "head", PARTNER)


def across(values):
    return swap(values, "head", ACROSS)


def batch_masks():
    return [1 << bit for bit in range((lax.axis_size("batch") - 1).bit_length())][::-1]


class Chain:
    def __init__(self, scalars, chunk, order, chips):
        self.scalars, self.values, self.order, self.chips = scalars, chunk[None], list(order), chips
        self.masks, self.flip, self.arrived = [0], 0, None

    def start(self):
        axis, mask = self.order.pop(0)
        self.flip = mask if not self.chips else (2 * mask if axis == "batch" else 1)
        self.arrived = swap(self.values, axis, mask)

    def pair(self):
        return self.values, self.arrived

    def take(self, joined):
        self.values = joined
        self.masks = self.masks + [mask ^ self.flip for mask in self.masks]
        self.arrived = None
        if self.order:
            self.start()

    def drain(self, left):
        while len(self.order) > left:
            self.take(join(self.scalars, [self.pair()], [0])[0])

    def halves(self, joined, orders):
        chains = []
        for values, order in zip(joined, orders):
            chain = Chain(self.scalars, values[0], order, self.chips)
            chain.values = values
            chain.masks = self.masks + [mask ^ self.flip for mask in self.masks]
            chain.start()
            chains.append(chain)
        return chains

    def parts(self, multiple, kinds=1):
        rows = self.values.shape[1] // kinds
        source = CHIP if self.chips else ROW
        arrays, masks = [self.values], [self.masks]
        if self.arrived is not None:
            arrays.append(self.arrived)
            masks.append([mask ^ self.flip for mask in self.masks])
        if rows % multiple == 0:
            return source, arrays, masks
        chunks = [array[r] for array in arrays for r in range(array.shape[0])]
        order = [mask for group in masks for mask in group]
        count = len(order)
        natural = jnp.stack([chunks[order.index(place)] for place in range(count)])
        size = 1
        while size < count:
            cut = natural.reshape((-1, 2, size) + natural.shape[1:])
            flipped = jnp.concatenate([cut[:, 1:], cut[:, :1]], axis=1)
            cut = jnp.where((self.scalars[source] & size) != 0, flipped, cut)
            natural = cut.reshape(natural.shape)
            size *= 2
        natural = natural.reshape(count, kinds, rows, -1).transpose(1, 0, 2, 3)
        return None, [natural.reshape(1, kinds * count * rows, -1)], [[0]]


def join_all(scalars, chains, extra=(), markers=()):
    pairs = [chain.pair() for chain in chains] + list(extra)
    joined = join(scalars, pairs, [0] * len(pairs), markers)
    for chain, values in zip(chains, joined):
        chain.take(values)
    return joined[len(chains) :]


def bit_source(bit):
    axis, mask = bit
    return (ROW, mask.bit_length() - 1) if axis == "batch" else (SIDE, 0)


class Reduce:
    def __init__(self, bits, order, *values):
        self.left, self.order, self.values, self.full = list(bits), list(order), values, None

    def split(self):
        bit = self.order.pop(0)
        size = 1 << (len(self.left) - 1 - self.left.index(bit))
        self.left.remove(bit)
        self.bit = bit
        return (*bit_source(bit), size)

    def begin(self, scalars):
        self.full = self.split()
        self.sources = []
        for values in self.values:
            self.send(scalars, values)

    def send(self, scalars, values):
        which, shift, size = self.full
        bit = (scalars[which] >> shift) & 1
        rows = values.shape[1:]
        cut = values.reshape((-1, 2, size) + rows)
        sent = lax.dynamic_index_in_dim(cut, 1 - bit, 1, keepdims=False).reshape((-1,) + rows)
        self.sources.append((values, swap(sent.astype(BF16), *self.bit)))

    def begin_with(self, *pairs):
        self.full = None
        self.sources = [(kept, swap(sent, *self.bit)) for sent, kept in pairs]

    def add_source(self, sent, kept):
        self.sources.append((kept, swap(sent, *self.bit)))

    @property
    def kept(self):
        return self.sources[0][0]


def reduce_all(scalars, chains, markers=()):
    plans, inputs, outs = [], [scalars], []
    for chain in chains:
        full = chain.full
        for source in chain.sources:
            inputs += source
        plan = chain.split() if chain.order else None
        plans.append(([full] * len(chain.sources), plan))
        count, rows, _ = chain.sources[0][1].shape
        columns = sum(arrived.shape[2] for _, arrived in chain.sources)
        if plan is None:
            outs.append(shape((count, rows, columns), F32))
        else:
            outs.append(shape((count // 2, rows, columns), BF16))
            outs.append(shape((count // 2, rows, columns), F32))
    found = list(call(partial(reduce_body, plans), inputs, outs, [], 16, "add_arrived", markers=markers))
    for chain, (_, plan) in zip(chains, plans):
        if plan is None:
            chain.values = found.pop(0)
        else:
            sent, kept = found.pop(0), found.pop(0)
            chain.begin_with((sent, kept))


def all_sum(values):
    for mask in (PARTNER, ACROSS):
        values = values + swap(values, "head", mask)
    masks = batch_masks()[::-1]
    if len(masks) % 2:
        values = values + swap(values, "batch", masks[0])
        masks = masks[1:]
    for low, high in zip(masks[::2], masks[1::2]):
        near = values + swap(values, "batch", low)
        far = swap(values, "batch", high) + swap(values, "batch", low | high)
        values = near + far
    return values


def block_permutation(slot, to_owner):
    rows, heads = lax.axis_size("batch"), lax.axis_size("head")
    total = rows * heads
    pairs = []
    for owner in range(total):
        place = (3 * owner + slot) % total
        holder = (place % rows) * heads + place // rows
        pairs.append((holder, owner) if to_owner else (owner, holder))
    return pairs


def holder_place():
    return lax.axis_size("batch") * lax.axis_index("head") + lax.axis_index("batch")


def blocks_to_holders(shard):
    blocks = shard.reshape(3, -1, D)
    return [lax.ppermute(blocks[slot], BOTH, block_permutation(slot, False)) for slot in range(3)]


def blocks_to_owners(blocks):
    total = lax.axis_size("batch") * lax.axis_size("head")
    place = holder_place()
    arrived = []
    for slot in range(3):
        kind = ((slot + 3 * total - place) * total) % 3
        sent = lax.dynamic_index_in_dim(blocks, kind, 0, keepdims=False)
        arrived.append(lax.ppermute(sent, BOTH, block_permutation(slot, True)))
    return jnp.concatenate(arrived, axis=0)


def on_device(
    tokens,
    cotangent,
    lengths,
    input_weight,
    output_weight,
    expand_weight,
    contract_weight,
    vector_params,
    input_first,
    input_second,
    output_first,
    output_second,
    expand_first,
    expand_second,
    contract_first,
    contract_second,
    vector_first,
    vector_second,
):
    rows_of_devices = lax.axis_size("batch")
    head_count = lax.axis_size("head")
    chips = rows_of_devices * head_count // 2
    here = lax.axis_index("head")
    core = here % 2
    side = here // 2
    width = D // head_count
    heads = width // HD
    piece = tokens.shape[0]
    docs = lengths.shape[1]
    hidden_block = FF // (2 * chips)
    half = FF // 2
    out_rows = output_weight.shape[0]
    total_devices = rows_of_devices * head_count
    batch_bits = [("batch", mask) for mask in batch_masks()]
    far, near = batch_bits[:-1], batch_bits[-1]
    side_bit = ("head", ACROSS)
    bits = batch_bits + [side_bit]
    bias_contract = vector_params[7 * D : 8 * D]

    def by_core(mine, other, axis):
        high = core == 1
        return jnp.stack([jnp.where(high, other, mine), jnp.where(high, mine, other)], axis=axis)

    def pick(values, index, axis):
        return lax.dynamic_index_in_dim(values, index, axis, keepdims=False)

    scalars, sequences = Places(), Places(lengths)
    lines = vector_params.reshape(VECTOR_ROWS, 128)

    *in_blocks, expand_low, output_mine, output_cut, contract_low, normed_own = prepare(
        scalars, input_weight, expand_weight, output_weight, contract_weight, tokens, lines
    )
    in_arrived = [
        lax.ppermute(block, BOTH, block_permutation(slot, False)) for slot, block in enumerate(in_blocks)
    ]
    expands = Chain(scalars, expand_low, far, True)
    expands.start()
    normed_across = across(normed_own)
    contract_cut = contract_low.reshape(out_rows, chips, 2, hidden_block)
    sent = jnp.concatenate([pick(contract_cut, 1 - core, 2).reshape(out_rows, half), output_cut], axis=1)
    columns_arrived = partner(sent)
    contract_mine = pick(contract_cut, core, 2).reshape(out_rows, half)
    contract_shard = by_core(contract_mine, columns_arrived[:, :half], 0).reshape(2 * out_rows, half)
    output_shard = by_core(output_mine, columns_arrived[:, half:], 0).reshape(2 * out_rows, 2 * width)
    contracts = Chain(scalars, contract_shard, [near, side_bit] + far, True)
    contracts.start()

    def cores_first(vectors):
        hidden = vectors[:, 8 * D :].reshape(-1, chips, 2, hidden_block).transpose(0, 2, 1, 3)
        return jnp.concatenate([vectors[:, : 8 * D], hidden.reshape(-1, FF)], axis=1).reshape(-1, VECTOR_ROWS, 128)

    def cores_back(rows):
        vectors = rows.reshape(-1, 8 * D + FF)
        hidden = vectors[:, 8 * D :].reshape(-1, 2, chips, hidden_block).transpose(0, 2, 1, 3)
        return jnp.concatenate([vectors[:, : 8 * D], hidden.reshape(-1, FF)], axis=1)

    vector_state = cores_first(jnp.stack([vector_first, vector_second, vector_params]))
    kinds = block_kinds(scalars, in_arrived, total_devices).reshape(-1, D)
    inputs = Chain(scalars, kinds, batch_bits, False)
    outputs = Chain(scalars, output_shard, far + [side_bit, near], True)
    inputs.start()
    outputs.start()
    inputs.drain(2)
    outputs.drain(3)
    join_all(scalars, [inputs, outputs, contracts], (), (expands.arrived,))
    expands.drain(1)
    (normed_mine,) = join_all(
        scalars, [inputs, outputs, contracts, expands], [(normed_own, normed_across)], (vector_state,)
    )
    contracts.drain(1)
    normed_other = partner(normed_mine)

    projected, weight_in, joined = project(
        scalars,
        normed_mine,
        normed_other,
        lines,
        *inputs.parts(8, 3),
        [outputs.pair(), expands.pair()],
        [0, 2],
        (),
    )
    outputs.take(joined[0])
    expands = expands.halves(joined[1:], ([near, side_bit], [side_bit, near]))

    blocks = 4 * piece // BLOCK
    before = attention_forward(sequences, projected, heads, docs, piece, (0, blocks // 2))
    join_all(scalars, [*expands, contracts, outputs], (), (before[0],))
    _, logs, keep_t, send_t = attention_forward(
        sequences, projected, heads, docs, piece, (blocks // 2, blocks), before, (contracts.values,)
    )
    across_t = across(send_t)
    cotangent_other = partner(cotangent)
    *branch_sent, branch_kept, output_own, output_across = branch(
        scalars,
        keep_t,
        across_t,
        *outputs.parts(16),
        [expands[0].arrived, expands[1].arrived],
    )
    resid_mid, *normed_two = middle_norm(
        scalars,
        tokens,
        branch_kept,
        [partner(rows) for rows in branch_sent],
        lines,
        (contracts.arrived,),
    )
    arrived_two = [partner(rows) for rows in normed_two]

    found = [chain.parts(16) for chain in expands]
    activated, slopes, expand_half, normed_pair, cotangent_pair = rise(
        scalars,
        (*normed_two, *arrived_two),
        (cotangent, cotangent_other),
        vector_state[2],
        [part[0] for part in found],
        [part[1] for part in found],
        [part[2] for part in found],
    )
    grad_hidden, normed_sent, normed_kept, out_sent, out_kept, hidden_sums = feed_forward(
        scalars, activated, slopes, expand_half, cotangent_pair, *contracts.parts(16)
    )
    normed_arrived = partner(normed_sent)
    out_arrived = partner(out_sent)
    block_out = (resid_mid + out_kept + out_arrived.astype(F32) + bias_contract).astype(BF16)

    expand_sum = Reduce(bits, [near] + far[-1:] + [side_bit] + far[:-1][::-1])
    contract_sum = Reduce(bits, far[-1:] + [side_bit, near] + far[:-1][::-1])
    output_sum = Reduce(bits, [side_bit] + far[-1:])
    sums = [expand_sum, contract_sum]
    aligned = hidden_block % 8 == 0 and 2 * out_rows % 8 == 0
    if aligned:
        plans = [chain.split() for chain in sums]
        contract_sum.begin_with(
            product_grad(scalars, cotangent_pair, activated, plans[1], chips, "contract_gradient")
        )
    else:
        expand_total = dot(grad_hidden, normed_pair, ((0,), (0,))).astype(BF16)
        contract_total = dot(cotangent_pair, activated, ((0,), (0,))).astype(BF16)
        expand_sum.values = (expand_total.reshape(chips, hidden_block, D),)
        contract_sum.values = (contract_total.reshape(chips, 2 * out_rows, half),)
        for chain in sums:
            chain.begin(scalars)
    grad_mid, grad_branch, middle_sums = norm_backward(
        middle_body,
        [normed_kept, normed_arrived, resid_mid, cotangent],
        lines,
        (F32, BF16),
        "middle_gradient",
        (contract_sum.kept,),
    )
    grads = (grad_branch, partner(grad_branch))
    if aligned:
        expand_sum.begin_with(
            product_grad(scalars, grad_hidden, normed_pair, plans[0], chips, "expand_gradient")
        )

    grad_keep_t, grad_sent_t = head_grads(scalars, grads, output_own, output_across, (expand_sum.kept,))
    grad_arrived_t = across(grad_sent_t)
    output_found = output_weight_grad(
        scalars, grads, keep_t, across_t, output_sum.split() if aligned else None, chips, (grad_sent_t,)
    )
    if aligned:
        output_sum.begin_with(output_found)
    else:
        output_sum.values = (output_found[0].reshape(chips, 2 * out_rows, 2 * width),)
        output_sum.begin(scalars)
    inputs = (sequences, projected, (keep_t, send_t), (grad_keep_t, grad_arrived_t), logs, heads, docs, piece)
    *before, _ = attention_backward(
        *inputs, (0, blocks // 2), (), [block_out, *(chain.kept for chain in (*sums, output_sum))]
    )
    reduce_all(scalars, [*sums, output_sum], (before[0],))
    grad_heads, _, _, head_sums = attention_backward(
        *inputs, (blocks // 2, blocks), before, [chain.kept for chain in sums]
    )

    contract_sum.sources += output_sum.sources
    reduce_all(scalars, sums, (grad_heads,))
    *far_sent, far_kept = first_grads(
        scalars, grad_heads, weight_in, (3, 2), (), [chain.kept for chain in sums]
    )
    far_arrived = [partner(rows) for rows in far_sent]
    in_found = input_weight_grad(
        scalars, grad_heads, normed_mine, normed_other, rows_of_devices, D // total_devices
    )
    in_sum = Reduce(batch_bits, far[-1:] + [near] + far[:-1][::-1])
    if len(in_found) == 2:
        in_sum.split()
        in_sum.begin_with(in_found)
    else:
        in_sum.values = (in_found[0].reshape(3 * rows_of_devices, -1, D),)
        in_sum.begin(scalars)
    reduce_all(scalars, sums, (in_sum.kept,))
    reduce_all(scalars, [in_sum], (sums[0].kept,))
    reduced_far, near_sent, near_kept = first_grads(
        scalars, grad_heads, weight_in, (1, 0), (far_kept, *far_arrived), (in_sum.kept,)
    )
    first_arrived = across(reduced_far)
    near_arrived = partner(near_sent)
    while sums[0].order:
        reduce_all(scalars, sums, (reduced_far,))
    reduce_all(scalars, sums, (reduced_far,))
    while in_sum.order:
        reduce_all(scalars, [in_sum], (expand_sum.values,))
    reduce_all(scalars, [in_sum], (first_arrived,))
    input_piece_grad = blocks_to_owners(in_sum.values)
    expand_grad = expand_sum.values.reshape(hidden_block, D)
    contract_mixed = contract_sum.values[0, :, :half]
    output_mixed = contract_sum.values[0, :, half:]

    def columns_other(mixed, parts):
        cut = mixed.reshape(2, out_rows, parts, -1)
        return pick(cut, core, 0), partner(pick(cut, 1 - core, 0))

    contract_grad = by_core(*columns_other(contract_mixed, chips), 2).reshape(out_rows, -1)
    output_grad = by_core(*columns_other(output_mixed, 2), 2).reshape(out_rows, -1)
    input_grad, first_sums = norm_backward(
        first_body,
        [near_kept, near_arrived, first_arrived, tokens, grad_mid],
        lines,
        (BF16,),
        "first_gradient",
    )

    masters = (input_weight, output_weight, expand_weight, contract_weight)
    gradients = [part.values for part in (in_sum, expand_sum, contract_sum)]
    payload = all_sum(
        make_payload(
            scalars,
            gradients,
            first_sums,
            middle_sums,
            head_sums,
            hidden_sums,
            (input_piece_grad, contract_grad, output_grad),
        )
    )
    vector_grads = payload[:VECTOR_ROWS]
    grad_norm = jnp.sqrt(payload[VECTOR_ROWS, 0] + jnp.sum(vector_grads * vector_grads))
    shard_grads = (input_piece_grad, output_grad, expand_grad, contract_grad)
    firsts = (input_first, output_first, expand_first, contract_first)
    seconds = (input_second, output_second, expand_second, contract_second)
    squares = directions_step(payload, shard_grads, firsts, seconds, masters)
    first_new, second_new, directions = moments_step(
        payload,
        shard_grads,
        (*firsts, vector_state[0]),
        (*seconds, vector_state[1]),
        (*masters, vector_state[2]),
        squares,
    )
    squares = all_sum(squares)
    vector_news = cores_back(jnp.stack([first_new[4], second_new[4], directions[4]]))
    news, lows, norms = weights_step(squares, directions[:4], masters)
    results = []
    for position in range(4):
        results += [first_new[position], second_new[position], news[position], lows[position]]
    return (
        block_out,
        input_grad,
        grad_norm,
        norms[:2, :4].reshape(8),
        *results,
        vector_news[0],
        vector_news[1],
        vector_news[2],
    )


def solution(mesh):
    split = P(BOTH, None)
    return jax.shard_map(
        on_device,
        mesh=mesh,
        in_specs=(split, split, P("batch", None)) + (split,) * 4 + (P(),) + (split,) * 8 + (P(), P()),
        out_specs=(split, split, P(), P()) + (split,) * 16 + (P(), P(), P()),
        check_vma=False,
    )
```

```python
from functools import partial
import jax
import jax.numpy as jnp
from jax import lax
from jax.experimental import pallas as pl
from jax.experimental.pallas import tpu as pltpu
from jax.sharding import PartitionSpec as P

D = 768
HD = 64
FF = 3072
STEP = 5
NORM_EPS = 1e-05
ADAM_EPS = 1e-06
DECAY_RATE = 0.01
MATRIX_RATE = 0.5
VECTOR_RATE = 0.1
ROOT_TWO_OVER_PI = (2.0 / 3.141592653589793) ** 0.5
BLOCK = 256
LANES = 256
NT = (((1,), (1,)), ((), ()))
NN = (((1,), (0,)), ((), ()))
F32 = jnp.float32
BF16 = jnp.bfloat16


def mm(a, b, dims):
    return lax.dot_general(a, b, dims, preferred_element_type=F32)


def block_start(index, per_piece, me):
    piece = index // per_piece
    return pl.multiple_of(((piece ^ me) * per_piece + index % per_piece) * BLOCK, BLOCK)


def starts_of(scalars, docs, positions):
    first = jnp.zeros_like(positions)
    for doc in range(docs - 1):
        end = scalars[ENDS + doc]
        first = jnp.where(positions >= end, end, first)
    return first


def first_block(scalars, docs, index):
    position = index * BLOCK
    first = jnp.int32(0)
    for doc in range(docs - 1):
        end = scalars[ENDS + doc]
        first = jnp.where(position >= end, end, first)
    return first // BLOCK


def head_lanes(block, heads):
    if heads == 1:
        return [block]
    lane = lax.broadcasted_iota(jnp.int32, block.shape, 1) // HD
    return [jnp.where(lane == j, block, jnp.zeros_like(block)) for j in range(heads)]


def allowed_mask(index, key_block, doc_first):
    key = key_block * BLOCK + lax.broadcasted_iota(jnp.int32, (BLOCK, BLOCK), 0)
    if index is None:
        return key >= doc_first
    query = index * BLOCK + lax.broadcasted_iota(jnp.int32, (1, BLOCK), 1)
    return (key <= query) & (key >= doc_first)


def over_keys(first, last, key_step, state):
    pairs = (last - first) // 2

    def two(p, state):
        return key_step(first + 2 * p + 1, key_step(first + 2 * p, state))

    state = lax.fori_loop(0, pairs, two, state)
    return lax.fori_loop(first + 2 * pairs, last, key_step, state)


def group_lanes(group, kind):
    start = kind * LANES + group * HEAD_LANES
    return slice(start, start + HEAD_LANES)


def forward_body(heads, docs, per_piece, span, final, scalars, qkv, *refs):
    if span[0] > 0:
        refs = refs[2:]
    out_t, log_out, *ends, values_t = refs
    me = scalars[HERE]
    width = heads * HD

    def transpose_values(i, carry):
        v = qkv[pl.ds(block_start(i, per_piece, me), BLOCK), group_lanes(0, 2)]
        values_t[:, pl.ds(pl.multiple_of(i * BLOCK, BLOCK), BLOCK)] = v.T[:width]
        return carry

    lax.fori_loop(0, span[1], transpose_values, 0)

    def query_block(i, carry):
        row = block_start(i, per_piece, me)
        q_heads = head_lanes(qkv[pl.ds(row, BLOCK), group_lanes(0, 0)] * BF16(HD ** -0.5), heads)
        positions = i * BLOCK + lax.broadcasted_iota(jnp.int32, (1, BLOCK), 1)
        doc_first = starts_of(scalars, docs, positions)

        def key_step(kb, state, query=None):
            allowed = allowed_mask(query, kb, doc_first)
            k = qkv[pl.ds(block_start(kb, per_piece, me), BLOCK), group_lanes(0, 1)]
            column = pl.ds(pl.multiple_of(kb * BLOCK, BLOCK), BLOCK)
            new = []
            for j in range(heads):
                top, total, acc = state[j]
                s = jnp.where(allowed, mm(k, q_heads[j], NT), -1e30)
                top_new = jnp.maximum(top, jnp.max(s, axis=0, keepdims=True))
                p = jnp.exp(s - top_new)
                fade = jnp.exp(top - top_new)
                total = total * fade + jnp.sum(p, axis=0, keepdims=True)
                v_t = values_t[j * HD : (j + 1) * HD, column]
                acc = acc * fade + mm(v_t, p.astype(BF16), NN)
                new.append((top_new, total, acc))
            return tuple(new)

        init = tuple(
            (jnp.full((1, BLOCK), -1e30, F32), jnp.zeros((1, BLOCK), F32), jnp.zeros((HD, BLOCK), F32))
            for _ in range(heads)
        )
        state = key_step(i, init, i)
        state = lax.fori_loop(first_block(scalars, docs, i), i, key_step, state)
        column = pl.ds(row, BLOCK)
        for j in range(heads):
            top, total, acc = state[j]
            out_t[j * HD : (j + 1) * HD, column] = (acc / total).astype(BF16)
            log_out[j : j + 1, pl.ds(pl.multiple_of(i * BLOCK, BLOCK), BLOCK)] = top + jnp.log(total)
        return carry

    if span[0] == 0:
        log_out[...] = jnp.zeros_like(log_out)
    lax.fori_loop(span[0], span[1], query_block, 0)
    if final:
        half = out_t.shape[1] // 2
        ends[0][...] = out_t[:, :half]
        ends[1][...] = out_t[:, half:]


def attention_forward(scalars, qkv, heads, docs, piece, span, before=(), markers=()):
    rows = qkv.shape[0]
    width = heads * HD
    final = span[1] == rows // BLOCK
    inputs = [scalars, qkv, *before]
    outs = [shape((width, rows), BF16), shape((8, rows), F32)]
    return call(
        partial(forward_body, heads, docs, piece // BLOCK, span, final),
        inputs,
        outs + [shape((width, rows // 2), BF16)] * (2 * final),
        [pltpu.VMEM((width, rows), BF16)],
        14,
        "attention_forward",
        markers=markers,
        aliases={len(inputs) - 2 + i: i for i in range(2)} if before else {},
    )


def backward_body(
    heads, docs, per_piece, span, final, scalars, qkv, out_keep, out_send, grad_keep, grad_recv, logs, *refs
):
    if span[0] > 0:
        refs = refs[3:]
    grads, d_keys, d_values, sums, keys_t, out_t, grad_t = refs
    me = scalars[HERE]
    width = heads * HD
    scale = HD ** -0.5
    half = out_keep.shape[1]
    out_t[:, :half] = out_keep[...]
    out_t[:, half:] = out_send[...]
    grad_t[:, :half] = grad_keep[...]
    grad_t[:, half:] = grad_recv[...]
    if span[0] == 0:
        d_keys[...] = jnp.zeros_like(d_keys)
        d_values[...] = jnp.zeros_like(d_values)

    def transpose_keys(i, carry):
        k = qkv[pl.ds(block_start(i, per_piece, me), BLOCK), group_lanes(0, 1)]
        keys_t[:, pl.ds(pl.multiple_of(i * BLOCK, BLOCK), BLOCK)] = k.T[:width]
        return carry

    lax.fori_loop(0, span[1], transpose_keys, 0)

    def padded(rows, kind):
        return jnp.concatenate([rows, jnp.zeros((LANES - width, BLOCK), kind)], axis=0)

    def query_block(i, carry):
        row = block_start(i, per_piece, me)
        q_heads = head_lanes(qkv[pl.ds(row, BLOCK), group_lanes(0, 0)] * BF16(scale), heads)
        o_t = out_t[:, pl.ds(row, BLOCK)]
        g_t = grad_t[:, pl.ds(row, BLOCK)]
        product = o_t.astype(F32) * g_t.astype(F32)
        deltas = [jnp.sum(product[j * HD : (j + 1) * HD], axis=0, keepdims=True) for j in range(heads)]
        g_heads = head_lanes(padded(g_t, BF16).T, heads)
        natural = pl.ds(pl.multiple_of(i * BLOCK, BLOCK), BLOCK)
        log_rows = [logs[j : j + 1, natural] for j in range(heads)]
        positions = i * BLOCK + lax.broadcasted_iota(jnp.int32, (1, BLOCK), 1)
        doc_first = starts_of(scalars, docs, positions)

        def key_step(kb, d_q, query=None):
            allowed = allowed_mask(query, kb, doc_first)
            key_row = pl.ds(block_start(kb, per_piece, me), BLOCK)
            k = qkv[key_row, group_lanes(0, 1)]
            v = qkv[key_row, group_lanes(0, 2)]
            column = pl.ds(pl.multiple_of(kb * BLOCK, BLOCK), BLOCK)
            d_k = d_keys[key_row, :]
            d_v = d_values[key_row, :]
            new = []
            for j in range(heads):
                s = jnp.where(allowed, mm(k, q_heads[j], NT), -1e30)
                p = jnp.exp(s - log_rows[j])
                d_v = d_v + mm(p.astype(BF16), g_heads[j], NN)
                d_p = mm(v, g_heads[j], NT)
                d_s = (p * (d_p - deltas[j])).astype(BF16)
                d_k = d_k + mm(d_s, q_heads[j], NN)
                new.append(d_q[j] + mm(keys_t[j * HD : (j + 1) * HD, column], d_s, NN))
            d_keys[key_row, :] = d_k
            d_values[key_row, :] = d_v
            return tuple(new)

        d_q = key_step(i, tuple(jnp.zeros((HD, BLOCK), F32) for _ in range(heads)), i)
        d_q = over_keys(first_block(scalars, docs, i), i, key_step, d_q)
        stacked = padded(jnp.concatenate(d_q, axis=0), F32) * scale
        grads[pl.ds(row, BLOCK), 0:LANES] = stacked.T.astype(BF16)
        return carry

    lax.fori_loop(span[0], span[1], query_block, 0)
    sums[...] = jnp.zeros_like(sums)
    if final:
        grads[:, LANES : 2 * LANES] = d_keys[...].astype(BF16)
        grads[:, 2 * LANES : 3 * LANES] = d_values[...].astype(BF16)
        for line, kind in enumerate((0, 2)):
            columns = grads[:, kind * LANES : (kind + 1) * LANES].astype(F32)
            sums[line : line + 1, :] = jnp.sum(columns, axis=0, keepdims=True)


def attention_backward(scalars, qkv, outs, grads, logs, heads, docs, piece, span, before=(), markers=()):
    rows = qkv.shape[0]
    width = heads * HD
    final = span[1] == rows // BLOCK
    inputs = [scalars, qkv, *outs, *grads, logs, *before]
    return call(
        partial(backward_body, heads, docs, piece // BLOCK, span, final),
        inputs,
        [
            shape((rows, 3 * LANES), BF16),
            shape((rows, LANES), F32),
            shape((rows, LANES), F32),
            shape((8, LANES), F32),
        ],
        [pltpu.VMEM((width, rows), BF16)] * 3,
        19,
        "attention_backward",
        markers=markers,
        aliases={len(inputs) - 3 + i: i for i in range(3)} if before else {},
    )


MICROSECONDS = {
    "prepare": 2.8,
    "block_kinds": 0.5,
    "join": 1.2,
    "project": 5,
    "attention_forward": 8,
    "branch": 1.3,
    "middle_norm": 0.2,
    "rise": 0.1,
    "feed_forward": 11,
    "head_gradients": 0.2,
    "output_weight_gradient": 0.2,
    "attention_backward": 2,
    "first_norm_gradient": 0.5,
    "input_weight_gradient": 1,
    "add_arrived": 0.05,
    "middle_gradient": 0.4,
    "first_gradient": 2.5,
    "payload": 1,
    "expand_gradient": 0.4,
    "contract_gradient": 0.4,
    "moments": 2,
    "directions": 1,
    "weights": 1.5,
}
COST_SCALE = 1.0


def cost(name):
    flops = int(MICROSECONDS[name] * COST_SCALE * 1.0e9)
    return pl.CostEstimate(flops=flops, bytes_accessed=0, transcendentals=0)


VMEM = pl.BlockSpec(memory_space=pltpu.VMEM)
SMEM = pl.BlockSpec(memory_space=pltpu.SMEM)
LEFT = pl.BlockSpec(memory_space=pl.ANY)
TN = (((0,), (0,)), ((), ()))
HERE, CHIP, ROW, CORE, SIDE, PLACE = range(6)
ENDS = 6


class Places:
    def __init__(self, lengths=None):
        self.lengths = lengths

    def __getitem__(self, number):
        here, row = lax.axis_index("head"), lax.axis_index("batch")
        heads, rows = lax.axis_size("head"), lax.axis_size("batch")
        if number == HERE:
            return here
        if number == CHIP:
            return row * (heads // 2) + here // 2
        if number == ROW:
            return row
        if number == CORE:
            return here % 2
        if number == SIDE:
            return here // 2
        if number == PLACE:
            return rows * here + row
        return sum(self.lengths[0, doc] for doc in range(number - ENDS + 1))


def call(body, inputs, outputs, scratch, mib, name, markers=(), aliases={}):
    lengths, inputs = inputs[0].lengths, inputs[1:]
    lead = [] if lengths is None else [lengths]
    count = len(lead) + len(inputs)

    def whole(*refs):
        places = Places(refs[0] if lead else None)
        body(places, *refs[len(lead) : count], *refs[count + len(markers) :])

    return pl.pallas_call(
        whole,
        out_shape=tuple(outputs),
        in_specs=[SMEM] * len(lead) + [VMEM] * len(inputs) + [LEFT] * len(markers),
        out_specs=(VMEM,) * len(outputs),
        scratch_shapes=scratch,
        input_output_aliases=aliases,
        compiler_params=pltpu.CompilerParams(vmem_limit_bytes=mib * 2**20),
        cost_estimate=cost(name),
        name=name,
    )(*lead, *inputs, *markers)


def lines_row(lines, first, count):
    return jnp.concatenate([lines[pl.ds(first + i, 1), :] for i in range(count)], axis=1)


def vector_row(lines, number):
    return lines_row(lines, number * (D // 128), D // 128)


def heads_row(lines, number, here):
    width = D // lax.axis_size("head")
    row = lines_row(lines, number * (D // 128) + (width * here) // 128, LANES // 128)
    row = jnp.where((width * here) % 128 != 0, pltpu.roll(row, LANES - HD, 1), row)
    lane = lax.broadcasted_iota(jnp.int32, row.shape, 1)
    return jnp.where(lane < width, row, 0.0)


def shape(dims, kind):
    return jax.ShapeDtypeStruct(tuple(dims), kind)


def join_pairs(ins, outs, cuts):
    outs = list(outs)
    for i, cut in enumerate(cuts):
        own, arrived = ins[2 * i], ins[2 * i + 1]
        half = own.shape[0]
        if cut == 0:
            out = outs.pop(0)
            out[:half] = own[...]
            out[half:] = arrived[...]
            continue
        rows = own.shape[1] // cut
        for part in range(cut):
            out = outs.pop(0)
            out[:half] = own[:, part * rows : (part + 1) * rows]
            out[half:] = arrived[:, part * rows : (part + 1) * rows]


def join_body(cuts, scalars, *refs):
    count = 2 * len(cuts)
    join_pairs(refs[:count], refs[count:], cuts)


def join_shapes(pairs, cuts):
    shapes = []
    for (own, _), cut in zip(pairs, cuts):
        dims = (2 * own.shape[0],) + own.shape[1:]
        if cut == 0:
            shapes.append(shape(dims, own.dtype))
        else:
            shapes += [shape((dims[0], dims[1] // cut, dims[2]), own.dtype)] * cut
    return shapes


def join(scalars, pairs, cuts, markers=()):
    flat = [x for pair in pairs for x in pair]
    return call(
        partial(join_body, cuts), [scalars, *flat], join_shapes(pairs, cuts), [], 24, "join", markers=markers
    )


def prepare_body(scalars, weight_in, weight_expand, weight_out, weight_back, tokens, lines, *outs):
    blocks, (expand, mine, other, back, normed) = outs[:3], outs[3:]
    back[...] = weight_back[...].astype(BF16)
    rows = blocks[0].shape[0]
    for slot, out in enumerate(blocks):
        out[...] = weight_in[slot * rows : (slot + 1) * rows, :].astype(BF16)
    expand[...] = weight_expand[...].astype(BF16)
    quarter = D // 4
    wide = weight_out[...]
    even = jnp.concatenate([wide[:, :quarter], wide[:, 2 * quarter : 3 * quarter]], axis=1)
    odd = jnp.concatenate([wide[:, quarter : 2 * quarter], wide[:, 3 * quarter :]], axis=1)
    high = scalars[CORE] == 1
    mine[...] = jnp.where(high, odd, even).astype(BF16)
    other[...] = jnp.where(high, even, odd).astype(BF16)
    gain, shift = vector_row(lines, 0), vector_row(lines, 1)
    step = min(128, tokens.shape[0])
    for start in range(0, tokens.shape[0], step):
        unit, _ = row_norm(tokens[start : start + step, :].astype(F32))
        normed[start : start + step, :] = (unit * gain + shift).astype(BF16)


def prepare(scalars, weight_in, weight_expand, weight_out, weight_back, tokens, lines):
    rows, out_rows = weight_in.shape[0] // 3, weight_out.shape[0]
    return call(
        prepare_body,
        [scalars, weight_in, weight_expand, weight_out, weight_back, tokens, lines],
        [shape((rows, D), BF16)] * 3
        + [
            shape(weight_expand.shape, BF16),
            shape((out_rows, D // 2), BF16),
            shape((out_rows, D // 2), BF16),
            shape(weight_back.shape, BF16),
            shape(tokens.shape, BF16),
        ],
        [],
        60,
        "prepare",
    )


def kinds_body(total, scalars, first, second, third, out):
    place = scalars[PLACE]
    rows = first.shape[0]
    for slot, block in enumerate((first, second, third)):
        kind = ((slot + 3 * total - place) * total) % 3
        out[kind] = block[...]


def block_kinds(scalars, blocks, total):
    rows = blocks[0].shape[0]
    outs = [shape((3, rows, D), BF16)]
    return call(partial(kinds_body, total), [scalars, *blocks], outs, [], 8, "block_kinds")[0]


def spread(scalars, base, parts, masks, put):
    origin = scalars[base] if base is not None else 0
    for ref, own in zip(parts, masks):
        for r, mask in enumerate(own):
            put(origin ^ mask if base is not None else mask, ref[r])


def project_body(base, masks, cuts, scalars, mine, other, lines, *refs):
    parts, refs = refs[: len(masks)], refs[len(masks) :]
    pairs, refs = refs[: 2 * len(cuts)], refs[2 * len(cuts) :]
    out, weight_out, weight = refs[0], refs[1], refs[-1]
    join_pairs(pairs, refs[2:-1], cuts)
    weight[...] = jnp.zeros_like(weight)

    def put(place, chunk):
        rows = chunk.shape[0] // 3
        wide = chunk.astype(F32)
        for kind in range(3):
            start = kind * LANES + place * rows
            if base is not None:
                start = pl.multiple_of(start, 8)
            weight[pl.ds(start, rows), :] = wide[kind * rows : (kind + 1) * rows]

    spread(scalars, base, parts, masks, put)
    low = weight[...].astype(BF16)
    weight_out[...] = low
    piece = mine.shape[0] // 2
    here = scalars[HERE]
    bias = jnp.concatenate(
        [heads_row(lines, 4, here), jnp.zeros((1, LANES), F32), heads_row(lines, 5, here)], axis=1
    )
    for place, (source, lead) in enumerate(((mine, 0), (other, 0), (mine, piece), (other, piece))):
        rows = source[lead : lead + piece, :]
        out[place * piece : (place + 1) * piece, :] = (mm(rows, low, NT) + bias).astype(BF16)


def project(scalars, mine, other, lines, base, parts, masks, pairs, cuts, markers):
    rows = 2 * mine.shape[0]
    flat = [x for pair in pairs for x in pair]
    outs = [shape((rows, 3 * LANES), BF16), shape((3 * LANES, D), BF16), *join_shapes(pairs, cuts)]
    found = call(
        partial(project_body, base, masks, cuts),
        [scalars, mine, other, lines, *parts, *flat],
        outs,
        [pltpu.VMEM((3 * LANES, D), F32)],
        24,
        "project",
        markers=markers,
    )
    return found[0], found[1], found[2:]


def branch_body(base, masks, scalars, keep, across_t, *refs):
    parts, refs = refs[: len(masks)], refs[len(masks) :]
    sent_a, sent_b, kept, own_out, across_out, weight = refs
    width = own_out.shape[1]

    def put(place, chunk):
        rows = chunk.shape[0]
        start = pl.multiple_of(place * rows, 16) if base is not None else place * rows
        for group in range(2):
            weight[group, pl.ds(start, rows), :] = chunk[:, group * width : (group + 1) * width]

    spread(scalars, base, parts, masks, put)
    side = scalars[SIDE]
    own_out[...] = weight[side]
    across_out[...] = weight[1 - side]
    piece = kept.shape[0]
    def rows_of(columns):
        return mm(keep[:, columns].T, own_out[...], NT) + mm(across_t[:, columns].T, across_out[...], NT)

    half = piece // 2
    sent_a[...] = rows_of(slice(piece, piece + half)).astype(BF16)
    sent_b[...] = rows_of(slice(piece + half, 2 * piece)).astype(BF16)
    kept[...] = rows_of(slice(0, piece))


def middle_norm_body(scalars, tokens, kept, arrived_a, arrived_b, lines, middle, normed_a, normed_b):
    bias, gain, shift = vector_row(lines, 6), vector_row(lines, 2), vector_row(lines, 3)
    half = normed_a.shape[0]
    step = min(128, half)
    for lead, arrived, normed in ((0, arrived_a, normed_a), (half, arrived_b, normed_b)):
        for start in range(0, half, step):
            rows = slice(lead + start, lead + start + step)
            values = tokens[rows, :].astype(F32) + kept[rows, :]
            values = values + arrived[start : start + step, :].astype(F32) + bias
            middle[rows, :] = values
            unit, _ = row_norm(values)
            normed[start : start + step, :] = (unit * gain + shift).astype(BF16)


def middle_norm(scalars, tokens, kept, arrived, lines, markers):
    piece = tokens.shape[0]
    return call(
        middle_norm_body,
        [scalars, tokens, kept, *arrived, lines],
        [shape((piece, D), F32), shape((piece // 2, D), BF16), shape((piece // 2, D), BF16)],
        [],
        16,
        "middle_norm",
        markers,
    )


def branch(scalars, keep, across_t, base, parts, masks, markers):
    width, rows = keep.shape
    piece = rows // 2
    return call(
        partial(branch_body, base, masks),
        [scalars, keep, across_t, *parts],
        [shape((piece // 2, D), BF16)] * 2
        + [shape((piece, D), F32), shape((D, width), BF16), shape((D, width), BF16)],
        [pltpu.VMEM((2, D, width), BF16)],
        24,
        "branch",
        markers=markers,
    )


MLP_ROWS = 256
MLP_LANES = 512


def rise_body(bases, masks, scalars, own_a, own_b, other_a, other_b, grad_own, grad_other, lines, *refs):
    count = sum(map(len, masks))
    parts, (activated, slopes, expand, pair, grad_pair) = refs[:count], refs[count:]
    half = expand.shape[0]
    piece = grad_own.shape[0]
    for lead, rows in enumerate((own_a, own_b, other_a, other_b)):
        pair[lead * (piece // 2) : (lead + 1) * (piece // 2), :] = rows[...]
    grad_pair[:piece, :] = grad_own[...]
    grad_pair[piece:, :] = grad_other[...]
    bias = lines_row(lines, 8 * (D // 128) + scalars[CORE] * (half // 128), half // 128)

    def put_expand(index):
        def put(place, chunk):
            rows = chunk.shape[0]
            start = place * 2 * rows + index * rows
            if bases[index] is not None:
                start = pl.multiple_of(start, 16)
            expand[pl.ds(start, rows), :] = chunk

        return put

    taken = 0
    for index, own_masks in enumerate(masks):
        spread(scalars, bases[index], parts[taken : taken + len(own_masks)], own_masks, put_expand(index))
        taken += len(own_masks)
    step = min(MLP_ROWS, piece)

    def block(i, carry):
        rows = pl.ds(pl.multiple_of(i * step, step), step)
        normed = pair[rows, :]
        for lanes in range(0, half, MLP_LANES):
            span = slice(lanes, lanes + MLP_LANES)
            expanded = mm(normed, expand[span, :], NT) + bias[:, span]
            squared = expanded * expanded
            bent = jnp.tanh(ROOT_TWO_OVER_PI * (expanded + 0.044715 * (expanded * squared)))
            rise = 0.5 * (1.0 + bent)
            activated[rows, span] = (expanded * rise).astype(BF16)
            slopes[rows, span] = rise + (0.5 * ROOT_TWO_OVER_PI) * expanded * (1.0 - bent * bent) * (
                1.0 + (3.0 * 0.044715) * squared
            )
        return carry

    lax.fori_loop(0, 2 * piece // step, block, 0)


def rise(scalars, normed, grads, lines, bases, parts, masks):
    piece = grads[0].shape[0]
    half = FF // 2
    flat = [x for group in parts for x in group]
    return call(
        partial(rise_body, bases, masks),
        [scalars, *normed, *grads, lines, *flat],
        [
            shape((2 * piece, half), BF16),
            shape((2 * piece, half), F32),
            shape((half, D), BF16),
            shape((2 * piece, D), BF16),
            shape((2 * piece, D), BF16),
        ],
        [],
        14,
        "rise",
    )


def feed_body(base, masks, scalars, activated, slopes, expand, grad_pair, *refs):
    parts, refs = refs[: len(masks)], refs[len(masks) :]
    grad_hidden, normed_sent, normed_kept, out_sent, out_kept, sums, contract = refs
    half = expand.shape[0]
    piece = normed_kept.shape[0]

    def put_contract(place, chunk):
        rows = chunk.shape[0]
        start = pl.multiple_of(place * rows, 16) if base is not None else place * rows
        contract[pl.ds(start, rows), :] = chunk

    spread(scalars, base, parts, masks, put_contract)
    sums[...] = jnp.zeros_like(sums)
    step = min(MLP_ROWS, piece)

    def block(start, lead, normed_out, contract_out):
        rows = pl.ds(start, step)
        target = pl.ds(pl.multiple_of(lead + start, step), step)
        grad = grad_pair[target, :]
        back = jnp.zeros((step, D), F32)
        result = jnp.zeros((step, D), F32)
        for lanes in range(0, half, MLP_LANES):
            span = slice(lanes, lanes + MLP_LANES)
            hidden = (mm(grad, contract[:, span], NN) * slopes[target, span]).astype(BF16)
            grad_hidden[target, span] = hidden
            sums[0:1, span] += jnp.sum(hidden.astype(F32), axis=0, keepdims=True)
            back = back + mm(hidden, expand[span, :], NN)
            result = result + mm(activated[target, span], contract[:, span], NT)
        normed_out[rows, :] = back.astype(normed_out.dtype)
        contract_out[rows, :] = result.astype(contract_out.dtype)

    def own_block(i, carry):
        block(pl.multiple_of(i * step, step), 0, normed_kept, out_kept)
        return carry

    def other_block(i, carry):
        block(pl.multiple_of(i * step, step), piece, normed_sent, out_sent)
        return carry

    lax.fori_loop(0, piece // step, other_block, 0)
    lax.fori_loop(0, piece // step, own_block, 0)


def feed_forward(scalars, activated, slopes, expand, grad_pair, base, parts, masks):
    half = expand.shape[0]
    piece = grad_pair.shape[0] // 2
    return call(
        partial(feed_body, base, masks),
        [scalars, activated, slopes, expand, grad_pair, *parts],
        [
            shape((2 * piece, half), BF16),
            shape((piece, D), BF16),
            shape((piece, D), F32),
            shape((piece, D), BF16),
            shape((piece, D), F32),
            shape((8, half), F32),
        ],
        [pltpu.VMEM((D, half), BF16)],
        18,
        "feed_forward",
    )


def head_grads_body(scalars, own, other, weight_own, weight_across, keep, sent):
    piece = own.shape[0]
    for matrix, out in ((weight_across, sent), (weight_own, keep)):
        for place, rows in enumerate((own, other)):
            features = mm(rows[...], matrix[...], NN).T.astype(BF16)
            out[:, place * piece : (place + 1) * piece] = features


def head_grads(scalars, grads, weight_own, weight_across, markers):
    piece = grads[0].shape[0]
    outs = [shape((weight_own.shape[1], 2 * piece), BF16)] * 2
    return call(head_grads_body, [scalars, *grads, weight_own, weight_across], outs, [], 16, "head_gradients", markers)


def split_rows(total, plan, scalars, sent, kept):
    which, shift, size = plan
    bit = (scalars[which] >> shift) & 1
    rows = sent.shape[1]

    def one(m, carry):
        base = (m // size) * 2 * size + m % size
        for out, chosen in ((sent, 1 - bit), (kept, bit)):
            start = pl.multiple_of((base + chosen * size) * rows, 8)
            out[m] = total[pl.ds(start, rows), :].astype(out.dtype)
        return carry

    lax.fori_loop(0, sent.shape[0], one, 0)


def split_shapes(chips, rows, columns):
    dims = (chips // 2, rows, columns)
    return [shape(dims, BF16), shape(dims, F32)]


def output_weight_body(plan, scalars, own, other, keep, across_t, *refs):
    *outs, stacked, total = refs
    side = scalars[SIDE]
    piece = own.shape[0]
    width = keep.shape[0]
    for place, features in ((side, keep), (1 - side, across_t)):
        product = mm(features[:, :piece], own[...], NN) + mm(features[:, piece:], other[...], NN)
        stacked[pl.ds(pl.multiple_of(place * width, 8), width), :] = product
    total[...] = stacked[...].T
    if plan is None:
        outs[0][...] = total[...].astype(BF16)
    else:
        split_rows(total, plan, scalars, *outs)


def output_weight_grad(scalars, grads, keep, across_t, plan, chips, markers):
    width = keep.shape[0]
    outs = [shape((D, 2 * width), BF16)] if plan is None else split_shapes(chips, D // chips, 2 * width)
    return call(
        partial(output_weight_body, plan),
        [scalars, *grads, keep, across_t],
        outs,
        [pltpu.VMEM((2 * width, D), F32), pltpu.VMEM((D, 2 * width), F32)],
        16,
        "output_weight_gradient",
        markers=markers,
    )


def product_body(plan, lanes, scalars, left, right, sent, kept, total):
    for start in range(0, left.shape[1], lanes):
        block = left[:, start : start + lanes].T
        for column in range(0, right.shape[1], D):
            columns = slice(column, column + D)
            total[start : start + lanes, columns] = mm(block, right[:, columns], NN)
    split_rows(total, plan, scalars, sent, kept)


def product_grad(scalars, left, right, plan, chips, name, markers=()):
    rows, columns = left.shape[1], right.shape[1]
    return call(
        partial(product_body, plan, 256),
        [scalars, left, right],
        split_shapes(chips, rows // chips, columns),
        [pltpu.VMEM((rows, columns), F32)],
        24,
        name,
        markers=markers,
    )


def input_weight_body(aligned, rows_of_devices, scalars, grads, mine, other, *refs):
    total = refs[-1]
    piece = mine.shape[0] // 2
    step = min(MLP_ROWS, piece)
    total[...] = jnp.zeros_like(total)
    for place, (source, lead) in enumerate(((mine, 0), (other, 0), (mine, piece), (other, piece))):
        for start in range(0, piece, step):
            rows = grads[place * piece + start : place * piece + start + step, :]
            total[...] += mm(rows.T, source[lead + start : lead + start + step, :], NN)
    if not aligned:
        natural = refs[0]
        for kind in range(3):
            natural[kind] = total[kind * LANES : kind * LANES + natural.shape[1], :]
        return
    sent, kept = refs[0], refs[1]
    rows = sent.shape[1]
    bit = (scalars[ROW] >> 1) & 1
    count = rows_of_devices // 2
    for kind in range(3):
        for e in range(count):
            for out, chosen in ((sent, 1 - bit), (kept, bit)):
                start = kind * LANES + ((e // 2) * 4 + e % 2 + 2 * chosen) * rows
                out[kind * count + e] = total[pl.ds(pl.multiple_of(start, 8), rows), :].astype(out.dtype)


def input_weight_grad(scalars, grads, mine, other, rows_of_devices, block):
    aligned = block % 8 == 0
    part = (3 * rows_of_devices // 2, block, D)
    outs = [shape(part, BF16), shape(part, F32)]
    if not aligned:
        outs = [shape((3, block * rows_of_devices, D), F32)]
    return call(
        partial(input_weight_body, aligned, rows_of_devices),
        [scalars, grads, mine, other],
        outs,
        [pltpu.VMEM((3 * LANES, D), F32)],
        16,
        "input_weight_gradient",
    )


def first_grads_body(places, scalars, grads, weight, *refs):
    *far, kept = refs
    piece = kept.shape[0]
    half = piece // 2
    halves = len(far) == 2
    if halves:
        outs = ((0, far[0]), (half, far[1]))
    else:
        far_kept, arrived_a, arrived_b, reduced, whole = far
        outs = ((0, whole),)
        for lead, arrived in ((0, arrived_a), (half, arrived_b)):
            rows = slice(lead, lead + half)
            reduced[rows, :] = (far_kept[rows, :].astype(F32) + arrived[...].astype(F32)).astype(BF16)
    sent, stay = places
    for lead, out in outs:
        rows = grads[sent * piece + lead : sent * piece + lead + out.shape[0], :]
        out[...] = mm(rows, weight[...], NN).astype(BF16)
    kept[...] = mm(grads[stay * piece : (stay + 1) * piece, :], weight[...], NN).astype(BF16)


def first_grads(scalars, grads, weight, places, far=(), markers=()):
    piece = grads.shape[0] // 4
    outs = [shape((piece, D), BF16)] * 2 if far else [shape((piece // 2, D), BF16)] * 2
    return call(
        partial(first_grads_body, places),
        [scalars, grads, weight, *far],
        outs + [shape((piece, D), BF16)],
        [],
        16,
        "first_norm_gradient",
        markers=markers,
    )


def payload_body(hidden_rows, scalars, inputs, expand, contract, first, middle, heads, hidden, out):
    six = D // 128
    out[...] = jnp.zeros_like(out)
    out[: 2 * six, :] = first[: 2 * six, :]
    out[2 * six : 4 * six, :] = middle[: 2 * six, :]
    out[6 * six : 8 * six, :] = middle[2 * six : 4 * six, :]
    here = scalars[HERE]
    for line in range(2):
        row = heads[line : line + 1, :]
        row = jnp.where(here % 2 == 1, pltpu.roll(row, HD, 1), row)
        start = (4 + line) * six + (3 * here) // 2
        for part in range(2):
            out[pl.ds(start + part, 1), :] = row[:, part * 128 : (part + 1) * 128]
    for part in range(hidden_rows):
        line = 8 * six + scalars[CORE] * hidden_rows + part
        out[pl.ds(line, 1), :] = hidden[0:1, part * 128 : (part + 1) * 128]
    total = jnp.zeros((1, 1), F32)
    for gradients in (inputs, expand, contract):
        for i in range(gradients.shape[0]):
            values = gradients[i]
            rows = jnp.sum(values * values, axis=1, keepdims=True)
            total += jnp.sum(rows, axis=0, keepdims=True)
    lane = lax.broadcasted_iota(jnp.int32, (1, 128), 1)
    out[VECTOR_ROWS : VECTOR_ROWS + 1, :] = jnp.where(lane == 0, total, 0.0)


def make_payload(scalars, gradients, first, middle, heads, hidden, markers):
    return call(
        partial(payload_body, hidden.shape[1] // 128),
        [scalars, *gradients, first, middle, heads, hidden],
        [shape((VECTOR_ROWS + 8, 128), F32)],
        [],
        12,
        "payload",
        markers,
    )[0]


def reduce_body(plans, scalars, *refs):
    count = 2 * sum(len(sources) for sources, _ in plans)
    ins, outs = list(refs[:count]), list(refs[count:])
    for sources, split in plans:
        terms = []
        column = 0
        for full in sources:
            kept, arrived = ins.pop(0), ins.pop(0)
            columns = slice(column, column + arrived.shape[2])
            column += arrived.shape[2]

            def total(index, kept=kept, arrived=arrived, full=full):
                source = index
                if full is not None:
                    which, shift, size = full
                    bit = (scalars[which] >> shift) & 1
                    source = (index // size) * 2 * size + bit * size + index % size
                return kept[source].astype(F32) + arrived[index].astype(F32)

            terms.append((columns, total))
        if split is None:
            out = outs.pop(0)

            def whole(m, carry, out=out, terms=terms):
                for columns, total in terms:
                    out[m, :, columns] = total(m)
                return carry

            lax.fori_loop(0, out.shape[0], whole, 0)
        else:
            which, shift, size = split
            sent_out, kept_out = outs.pop(0), outs.pop(0)

            def halves(m, carry, sent_out=sent_out, kept_out=kept_out, terms=terms):
                bit = (scalars[which] >> shift) & 1
                base = (m // size) * 2 * size + m % size
                for columns, total in terms:
                    kept_out[m, :, columns] = total(base + bit * size)
                    sent_out[m, :, columns] = total(base + (1 - bit) * size).astype(BF16)
                return carry

            lax.fori_loop(0, kept_out.shape[0], halves, 0)


HEAD_LANES = LANES


VECTOR_ROWS = (8 * D + FF) // 128


def row_norm(values):
    mean = jnp.mean(values, axis=1, keepdims=True)
    centered = values - mean
    variance = jnp.mean(centered * centered, axis=1, keepdims=True)
    inverse = lax.rsqrt(variance + NORM_EPS)
    return centered * inverse, inverse


def norm_input_gradient(upstream, values, gain):
    unit, inverse = row_norm(values)
    scaled = upstream * gain
    first = jnp.mean(scaled, axis=1, keepdims=True)
    second = jnp.mean(scaled * unit, axis=1, keepdims=True)
    return inverse * (scaled - first - unit * second), unit


def stack_rows(sums, rows):
    for place, row in enumerate(rows):
        total = jnp.sum(row, axis=0, keepdims=True)
        for part in range(D // 128):
            line = place * (D // 128) + part
            sums[line : line + 1, :] += total[:, part * 128 : (part + 1) * 128]


def middle_body(own, arrived, middle, cotangent, lines, grad_mid, grad_branch, sums):
    @pl.when(pl.program_id(0) == 0)
    def _():
        sums[...] = jnp.zeros_like(sums)

    upstream = own[...] + arrived[...].astype(F32)
    passed, unit = norm_input_gradient(upstream, middle[...], vector_row(lines, 2))
    outer = cotangent[...].astype(F32)
    total = outer + passed
    rounded = total.astype(BF16)
    grad_mid[...] = total
    grad_branch[...] = rounded
    stack_rows(sums, [upstream * unit, upstream, rounded.astype(F32), outer])


def first_body(own, arrived, across, tokens, grad_mid, lines, input_grad, sums):
    @pl.when(pl.program_id(0) == 0)
    def _():
        sums[...] = jnp.zeros_like(sums)

    upstream = own[...].astype(F32) + arrived[...].astype(F32) + across[...].astype(F32)
    passed, unit = norm_input_gradient(upstream, tokens[...].astype(F32), vector_row(lines, 0))
    input_grad[...] = (grad_mid[...] + passed).astype(BF16)
    stack_rows(sums, [upstream * unit, upstream])


def norm_backward(body, arrays, lines, outputs, name, markers=()):
    rows = arrays[0].shape[0]
    step = min(256, rows)
    tile = pl.BlockSpec((step, D), lambda i: (i, 0))
    row = pl.BlockSpec(lines.shape, lambda i: (0, 0))
    sums = pl.BlockSpec((24, 128), lambda i: (0, 0))
    count = len(arrays) + 1

    def whole(*refs):
        body(*refs[:count], *refs[count + len(markers) :])

    return pl.pallas_call(
        whole,
        grid=(rows // step,),
        out_shape=tuple(jax.ShapeDtypeStruct((rows, D), kind) for kind in outputs)
        + (jax.ShapeDtypeStruct((24, 128), F32),),
        in_specs=[tile] * len(arrays) + [row] + [LEFT] * len(markers),
        out_specs=tuple(tile for _ in outputs) + (sums,),
        compiler_params=pltpu.CompilerParams(vmem_limit_bytes=14 * 2**20),
        cost_estimate=cost(name),
        name=name,
    )(*arrays, lines, *markers)


def moments_body(*refs):
    payload, refs = refs[0], refs[1:]
    grads, firsts, seconds, masters = refs[0:4], refs[4:9], refs[9:14], refs[14:19]
    first_outs, second_outs, direction_outs = refs[20:25], refs[25:30], refs[30:35]
    clip = clip_of(payload)
    for place in range(5):
        gradient = grads[place][...] if place < 4 else payload[0:VECTOR_ROWS, :]
        master = masters[place][...]
        first_new, second_new, direction = direction_of(
            gradient, firsts[place][...], seconds[place][...], master, clip
        )
        first_outs[place][...] = first_new
        second_outs[place][...] = second_new
        direction_outs[place][...] = direction if place < 4 else master - VECTOR_RATE * direction


def clip_of(payload):
    vector = payload[0:VECTOR_ROWS, :]
    total = payload[VECTOR_ROWS : VECTOR_ROWS + 1, 0:1] + jnp.sum(
        jnp.sum(vector * vector, axis=1, keepdims=True), axis=0, keepdims=True
    )
    return jnp.minimum(1.0, 1.0 / jnp.sqrt(total))


def direction_of(gradient, first_old, second_old, master, clip):
    clipped = gradient * clip
    first_new = 0.5 * first_old + 0.5 * clipped
    second_new = 0.5 * second_old + 0.5 * clipped * clipped
    correction = 1.0 - 0.5**STEP
    direction = (
        first_new / correction / (jnp.sqrt(second_new / correction) + ADAM_EPS) + DECAY_RATE * master
    )
    return first_new, second_new, direction


def directions_body(*refs):
    payload, squares, refs = refs[0], refs[-1], refs[1:-1]
    grads, firsts, seconds, masters = refs[0:4], refs[4:8], refs[8:12], refs[12:16]
    clip = clip_of(payload)
    lane = lax.broadcasted_iota(jnp.int32, squares.shape, 1)
    row = lax.broadcasted_iota(jnp.int32, squares.shape, 0)
    found = jnp.zeros(squares.shape, F32)
    for place in range(4):
        master = masters[place][...]
        _, _, direction = direction_of(
            grads[place][...], firsts[place][...], seconds[place][...], master, clip
        )
        for offset, values in ((0, direction), (4, master)):
            square = jnp.sum(jnp.sum(values * values, axis=1, keepdims=True), axis=0, keepdims=True)
            found = found + jnp.where((lane == place + offset) & (row == 0), square, 0.0)
    squares[...] = found


def directions_step(payload, grads, firsts, seconds, masters):
    vmem = pl.BlockSpec(memory_space=pltpu.VMEM)
    return pl.pallas_call(
        directions_body,
        out_shape=jax.ShapeDtypeStruct((8, 128), F32),
        in_specs=[vmem] * 17,
        out_specs=vmem,
        compiler_params=pltpu.CompilerParams(vmem_limit_bytes=16 * 2**20),
        cost_estimate=cost("directions"),
        name="directions",
    )(payload, *grads, *firsts, *seconds, *masters)


def moments_step(payload, grads, firsts, seconds, masters, marker):
    vmem = pl.BlockSpec(memory_space=pltpu.VMEM)
    shapes = [jax.ShapeDtypeStruct(master.shape, F32) for master in masters]
    outs = pl.pallas_call(
        moments_body,
        out_shape=tuple(shapes * 3),
        in_specs=[vmem] * 21,
        out_specs=(vmem,) * 15,
        compiler_params=pltpu.CompilerParams(vmem_limit_bytes=16 * 2**20),
        cost_estimate=cost("moments"),
        name="moments",
    )(payload, *grads, *firsts, *seconds, *masters, marker)
    return outs[0:5], outs[5:10], outs[10:15]


def weights_body(*refs):
    squares, refs = refs[0], refs[1:]
    directions, masters, outs, lows = refs[0:4], refs[4:8], refs[8:12], refs[12:16]
    norms = refs[16]
    norms[...] = jnp.zeros_like(norms)
    weight = jnp.sqrt(squares[0:1, 4:8])
    update = jnp.sqrt(squares[0:1, 0:4])
    for place in range(4):
        ratio = MATRIX_RATE * (weight[:, place : place + 1] / update[:, place : place + 1])
        new = masters[place][...] - ratio * directions[place][...]
        outs[place][...] = new
        lows[place][...] = new.astype(BF16)
    norms[0:1, 0:4] = weight
    norms[1:2, 0:4] = update


def weights_step(squares, directions, masters):
    vmem = pl.BlockSpec(memory_space=pltpu.VMEM)
    outs = pl.pallas_call(
        weights_body,
        out_shape=tuple(jax.ShapeDtypeStruct(m.shape, F32) for m in masters)
        + tuple(jax.ShapeDtypeStruct(m.shape, BF16) for m in masters)
        + (jax.ShapeDtypeStruct((8, 128), F32),),
        in_specs=[vmem] * 9,
        out_specs=(vmem,) * 9,
        compiler_params=pltpu.CompilerParams(vmem_limit_bytes=60 * 2**20),
        cost_estimate=cost("weights"),
        name="weights",
    )(squares, *directions, *masters)
    return outs[0:4], outs[4:8], outs[8]


BOTH = ("batch", "head")
PARTNER = 1
ACROSS = 2


def dot(a, b, dims):
    return lax.dot_general(a, b, (dims, ((), ())), preferred_element_type=F32)


def swap(values, axis, mask):
    size = lax.axis_size(axis)
    return lax.ppermute(values, axis, [(place, place ^ mask) for place in range(size)])


def partner(values):
    return swap(values, "head", PARTNER)


def across(values):
    return swap(values, "head", ACROSS)


def batch_masks():
    return [1 << bit for bit in range((lax.axis_size("batch") - 1).bit_length())][::-1]


class Chain:
    def __init__(self, scalars, chunk, order, chips):
        self.scalars, self.values, self.order, self.chips = scalars, chunk[None], list(order), chips
        self.masks, self.flip, self.arrived = [0], 0, None

    def start(self):
        axis, mask = self.order.pop(0)
        self.flip = mask if not self.chips else (2 * mask if axis == "batch" else 1)
        self.arrived = swap(self.values, axis, mask)

    def pair(self):
        return self.values, self.arrived

    def take(self, joined):
        self.values = joined
        self.masks = self.masks + [mask ^ self.flip for mask in self.masks]
        self.arrived = None
        if self.order:
            self.start()

    def drain(self, left):
        while len(self.order) > left:
            self.take(join(self.scalars, [self.pair()], [0])[0])

    def halves(self, joined, orders):
        chains = []
        for values, order in zip(joined, orders):
            chain = Chain(self.scalars, values[0], order, self.chips)
            chain.values = values
            chain.masks = self.masks + [mask ^ self.flip for mask in self.masks]
            chain.start()
            chains.append(chain)
        return chains

    def parts(self, multiple, kinds=1):
        rows = self.values.shape[1] // kinds
        source = CHIP if self.chips else ROW
        arrays, masks = [self.values], [self.masks]
        if self.arrived is not None:
            arrays.append(self.arrived)
            masks.append([mask ^ self.flip for mask in self.masks])
        if rows % multiple == 0:
            return source, arrays, masks
        chunks = [array[r] for array in arrays for r in range(array.shape[0])]
        order = [mask for group in masks for mask in group]
        count = len(order)
        natural = jnp.stack([chunks[order.index(place)] for place in range(count)])
        size = 1
        while size < count:
            cut = natural.reshape((-1, 2, size) + natural.shape[1:])
            flipped = jnp.concatenate([cut[:, 1:], cut[:, :1]], axis=1)
            cut = jnp.where((self.scalars[source] & size) != 0, flipped, cut)
            natural = cut.reshape(natural.shape)
            size *= 2
        natural = natural.reshape(count, kinds, rows, -1).transpose(1, 0, 2, 3)
        return None, [natural.reshape(1, kinds * count * rows, -1)], [[0]]


def join_all(scalars, chains, extra=(), markers=()):
    pairs = [chain.pair() for chain in chains] + list(extra)
    joined = join(scalars, pairs, [0] * len(pairs), markers)
    for chain, values in zip(chains, joined):
        chain.take(values)
    return joined[len(chains) :]


def bit_source(bit):
    axis, mask = bit
    return (ROW, mask.bit_length() - 1) if axis == "batch" else (SIDE, 0)


class Reduce:
    def __init__(self, bits, order, *values):
        self.left, self.order, self.values, self.full = list(bits), list(order), values, None

    def split(self):
        bit = self.order.pop(0)
        size = 1 << (len(self.left) - 1 - self.left.index(bit))
        self.left.remove(bit)
        self.bit = bit
        return (*bit_source(bit), size)

    def begin(self, scalars):
        self.full = self.split()
        self.sources = []
        for values in self.values:
            self.send(scalars, values)

    def send(self, scalars, values):
        which, shift, size = self.full
        bit = (scalars[which] >> shift) & 1
        rows = values.shape[1:]
        cut = values.reshape((-1, 2, size) + rows)
        sent = lax.dynamic_index_in_dim(cut, 1 - bit, 1, keepdims=False).reshape((-1,) + rows)
        self.sources.append((values, swap(sent.astype(BF16), *self.bit)))

    def begin_with(self, *pairs):
        self.full = None
        self.sources = [(kept, swap(sent, *self.bit)) for sent, kept in pairs]

    def add_source(self, sent, kept):
        self.sources.append((kept, swap(sent, *self.bit)))

    @property
    def kept(self):
        return self.sources[0][0]


def reduce_all(scalars, chains, markers=()):
    plans, inputs, outs = [], [scalars], []
    for chain in chains:
        full = chain.full
        for source in chain.sources:
            inputs += source
        plan = chain.split() if chain.order else None
        plans.append(([full] * len(chain.sources), plan))
        count, rows, _ = chain.sources[0][1].shape
        columns = sum(arrived.shape[2] for _, arrived in chain.sources)
        if plan is None:
            outs.append(shape((count, rows, columns), F32))
        else:
            outs.append(shape((count // 2, rows, columns), BF16))
            outs.append(shape((count // 2, rows, columns), F32))
    found = list(call(partial(reduce_body, plans), inputs, outs, [], 16, "add_arrived", markers=markers))
    for chain, (_, plan) in zip(chains, plans):
        if plan is None:
            chain.values = found.pop(0)
        else:
            sent, kept = found.pop(0), found.pop(0)
            chain.begin_with((sent, kept))


def all_sum(values):
    for mask in (PARTNER, ACROSS):
        values = values + swap(values, "head", mask)
    masks = batch_masks()[::-1]
    if len(masks) % 2:
        values = values + swap(values, "batch", masks[0])
        masks = masks[1:]
    for low, high in zip(masks[::2], masks[1::2]):
        near = values + swap(values, "batch", low)
        far = swap(values, "batch", high) + swap(values, "batch", low | high)
        values = near + far
    return values


def block_permutation(slot, to_owner):
    rows, heads = lax.axis_size("batch"), lax.axis_size("head")
    total = rows * heads
    pairs = []
    for owner in range(total):
        place = (3 * owner + slot) % total
        holder = (place % rows) * heads + place // rows
        pairs.append((holder, owner) if to_owner else (owner, holder))
    return pairs


def holder_place():
    return lax.axis_size("batch") * lax.axis_index("head") + lax.axis_index("batch")


def blocks_to_holders(shard):
    blocks = shard.reshape(3, -1, D)
    return [lax.ppermute(blocks[slot], BOTH, block_permutation(slot, False)) for slot in range(3)]


def blocks_to_owners(blocks):
    total = lax.axis_size("batch") * lax.axis_size("head")
    place = holder_place()
    arrived = []
    for slot in range(3):
        kind = ((slot + 3 * total - place) * total) % 3
        sent = lax.dynamic_index_in_dim(blocks, kind, 0, keepdims=False)
        arrived.append(lax.ppermute(sent, BOTH, block_permutation(slot, True)))
    return jnp.concatenate(arrived, axis=0)


def on_device(
    tokens,
    cotangent,
    lengths,
    input_weight,
    output_weight,
    expand_weight,
    contract_weight,
    vector_params,
    input_first,
    input_second,
    output_first,
    output_second,
    expand_first,
    expand_second,
    contract_first,
    contract_second,
    vector_first,
    vector_second,
):
    rows_of_devices = lax.axis_size("batch")
    head_count = lax.axis_size("head")
    chips = rows_of_devices * head_count // 2
    here = lax.axis_index("head")
    core = here % 2
    side = here // 2
    width = D // head_count
    heads = width // HD
    piece = tokens.shape[0]
    docs = lengths.shape[1]
    hidden_block = FF // (2 * chips)
    half = FF // 2
    out_rows = output_weight.shape[0]
    total_devices = rows_of_devices * head_count
    batch_bits = [("batch", mask) for mask in batch_masks()]
    far, near = batch_bits[:-1], batch_bits[-1]
    side_bit = ("head", ACROSS)
    bits = batch_bits + [side_bit]
    bias_contract = vector_params[7 * D : 8 * D]

    def by_core(mine, other, axis):
        high = core == 1
        return jnp.stack([jnp.where(high, other, mine), jnp.where(high, mine, other)], axis=axis)

    def pick(values, index, axis):
        return lax.dynamic_index_in_dim(values, index, axis, keepdims=False)

    scalars, sequences = Places(), Places(lengths)
    lines = vector_params.reshape(VECTOR_ROWS, 128)

    *in_blocks, expand_low, output_mine, output_cut, contract_low, normed_own = prepare(
        scalars, input_weight, expand_weight, output_weight, contract_weight, tokens, lines
    )
    in_arrived = [
        lax.ppermute(block, BOTH, block_permutation(slot, False)) for slot, block in enumerate(in_blocks)
    ]
    expands = Chain(scalars, expand_low, far, True)
    expands.start()
    normed_across = across(normed_own)
    contract_cut = contract_low.reshape(out_rows, chips, 2, hidden_block)
    sent = jnp.concatenate([pick(contract_cut, 1 - core, 2).reshape(out_rows, half), output_cut], axis=1)
    columns_arrived = partner(sent)
    contract_mine = pick(contract_cut, core, 2).reshape(out_rows, half)
    contract_shard = by_core(contract_mine, columns_arrived[:, :half], 0).reshape(2 * out_rows, half)
    output_shard = by_core(output_mine, columns_arrived[:, half:], 0).reshape(2 * out_rows, 2 * width)
    contracts = Chain(scalars, contract_shard, [near, side_bit] + far, True)
    contracts.start()

    def cores_first(vectors):
        hidden = vectors[:, 8 * D :].reshape(-1, chips, 2, hidden_block).transpose(0, 2, 1, 3)
        return jnp.concatenate([vectors[:, : 8 * D], hidden.reshape(-1, FF)], axis=1).reshape(-1, VECTOR_ROWS, 128)

    def cores_back(rows):
        vectors = rows.reshape(-1, 8 * D + FF)
        hidden = vectors[:, 8 * D :].reshape(-1, 2, chips, hidden_block).transpose(0, 2, 1, 3)
        return jnp.concatenate([vectors[:, : 8 * D], hidden.reshape(-1, FF)], axis=1)

    vector_state = cores_first(jnp.stack([vector_first, vector_second, vector_params]))
    kinds = block_kinds(scalars, in_arrived, total_devices).reshape(-1, D)
    inputs = Chain(scalars, kinds, batch_bits, False)
    outputs = Chain(scalars, output_shard, far + [side_bit, near], True)
    inputs.start()
    outputs.start()
    inputs.drain(2)
    outputs.drain(3)
    join_all(scalars, [inputs, outputs, contracts], (), (expands.arrived,))
    expands.drain(1)
    (normed_mine,) = join_all(
        scalars, [inputs, outputs, contracts, expands], [(normed_own, normed_across)], (vector_state,)
    )
    contracts.drain(1)
    normed_other = partner(normed_mine)

    projected, weight_in, joined = project(
        scalars,
        normed_mine,
        normed_other,
        lines,
        *inputs.parts(8, 3),
        [outputs.pair(), expands.pair()],
        [0, 2],
        (),
    )
    outputs.take(joined[0])
    expands = expands.halves(joined[1:], ([near, side_bit], [side_bit, near]))

    blocks = 4 * piece // BLOCK
    before = attention_forward(sequences, projected, heads, docs, piece, (0, blocks // 2))
    join_all(scalars, [*expands, contracts, outputs], (), (before[0],))
    _, logs, keep_t, send_t = attention_forward(
        sequences, projected, heads, docs, piece, (blocks // 2, blocks), before, (contracts.values,)
    )
    across_t = across(send_t)
    cotangent_other = partner(cotangent)
    *branch_sent, branch_kept, output_own, output_across = branch(
        scalars,
        keep_t,
        across_t,
        *outputs.parts(16),
        [expands[0].arrived, expands[1].arrived],
    )
    resid_mid, *normed_two = middle_norm(
        scalars,
        tokens,
        branch_kept,
        [partner(rows) for rows in branch_sent],
        lines,
        (contracts.arrived,),
    )
    arrived_two = [partner(rows) for rows in normed_two]

    found = [chain.parts(16) for chain in expands]
    activated, slopes, expand_half, normed_pair, cotangent_pair = rise(
        scalars,
        (*normed_two, *arrived_two),
        (cotangent, cotangent_other),
        vector_state[2],
        [part[0] for part in found],
        [part[1] for part in found],
        [part[2] for part in found],
    )
    grad_hidden, normed_sent, normed_kept, out_sent, out_kept, hidden_sums = feed_forward(
        scalars, activated, slopes, expand_half, cotangent_pair, *contracts.parts(16)
    )
    normed_arrived = partner(normed_sent)
    out_arrived = partner(out_sent)
    block_out = (resid_mid + out_kept + out_arrived.astype(F32) + bias_contract).astype(BF16)

    expand_sum = Reduce(bits, [near] + far[-1:] + [side_bit] + far[:-1][::-1])
    contract_sum = Reduce(bits, far[-1:] + [side_bit, near] + far[:-1][::-1])
    output_sum = Reduce(bits, [side_bit] + far[-1:])
    sums = [expand_sum, contract_sum]
    aligned = hidden_block % 8 == 0 and 2 * out_rows % 8 == 0
    if aligned:
        plans = [chain.split() for chain in sums]
        contract_sum.begin_with(
            product_grad(scalars, cotangent_pair, activated, plans[1], chips, "contract_gradient")
        )
    else:
        expand_total = dot(grad_hidden, normed_pair, ((0,), (0,))).astype(BF16)
        contract_total = dot(cotangent_pair, activated, ((0,), (0,))).astype(BF16)
        expand_sum.values = (expand_total.reshape(chips, hidden_block, D),)
        contract_sum.values = (contract_total.reshape(chips, 2 * out_rows, half),)
        for chain in sums:
            chain.begin(scalars)
    grad_mid, grad_branch, middle_sums = norm_backward(
        middle_body,
        [normed_kept, normed_arrived, resid_mid, cotangent],
        lines,
        (F32, BF16),
        "middle_gradient",
        (contract_sum.kept,),
    )
    grads = (grad_branch, partner(grad_branch))
    if aligned:
        expand_sum.begin_with(
            product_grad(scalars, grad_hidden, normed_pair, plans[0], chips, "expand_gradient")
        )

    grad_keep_t, grad_sent_t = head_grads(scalars, grads, output_own, output_across, (expand_sum.kept,))
    grad_arrived_t = across(grad_sent_t)
    output_found = output_weight_grad(
        scalars, grads, keep_t, across_t, output_sum.split() if aligned else None, chips, (grad_sent_t,)
    )
    if aligned:
        output_sum.begin_with(output_found)
    else:
        output_sum.values = (output_found[0].reshape(chips, 2 * out_rows, 2 * width),)
        output_sum.begin(scalars)
    inputs = (sequences, projected, (keep_t, send_t), (grad_keep_t, grad_arrived_t), logs, heads, docs, piece)
    *before, _ = attention_backward(
        *inputs, (0, blocks // 2), (), [block_out, *(chain.kept for chain in (*sums, output_sum))]
    )
    reduce_all(scalars, [*sums, output_sum], (before[0],))
    grad_heads, _, _, head_sums = attention_backward(
        *inputs, (blocks // 2, blocks), before, [chain.kept for chain in sums]
    )

    contract_sum.sources += output_sum.sources
    reduce_all(scalars, sums, (grad_heads,))
    *far_sent, far_kept = first_grads(
        scalars, grad_heads, weight_in, (3, 2), (), [chain.kept for chain in sums]
    )
    far_arrived = [partner(rows) for rows in far_sent]
    in_found = input_weight_grad(
        scalars, grad_heads, normed_mine, normed_other, rows_of_devices, D // total_devices
    )
    in_sum = Reduce(batch_bits, far[-1:] + [near] + far[:-1][::-1])
    if len(in_found) == 2:
        in_sum.split()
        in_sum.begin_with(in_found)
    else:
        in_sum.values = (in_found[0].reshape(3 * rows_of_devices, -1, D),)
        in_sum.begin(scalars)
    reduce_all(scalars, sums, (in_sum.kept,))
    reduce_all(scalars, [in_sum], (sums[0].kept,))
    reduced_far, near_sent, near_kept = first_grads(
        scalars, grad_heads, weight_in, (1, 0), (far_kept, *far_arrived), (in_sum.kept,)
    )
    first_arrived = across(reduced_far)
    near_arrived = partner(near_sent)
    while sums[0].order:
        reduce_all(scalars, sums, (reduced_far,))
    reduce_all(scalars, sums, (reduced_far,))
    while in_sum.order:
        reduce_all(scalars, [in_sum], (expand_sum.values,))
    reduce_all(scalars, [in_sum], (first_arrived,))
    input_piece_grad = blocks_to_owners(in_sum.values)
    expand_grad = expand_sum.values.reshape(hidden_block, D)
    contract_mixed = contract_sum.values[0, :, :half]
    output_mixed = contract_sum.values[0, :, half:]

    def columns_other(mixed, parts):
        cut = mixed.reshape(2, out_rows, parts, -1)
        return pick(cut, core, 0), partner(pick(cut, 1 - core, 0))

    contract_grad = by_core(*columns_other(contract_mixed, chips), 2).reshape(out_rows, -1)
    output_grad = by_core(*columns_other(output_mixed, 2), 2).reshape(out_rows, -1)
    input_grad, first_sums = norm_backward(
        first_body,
        [near_kept, near_arrived, first_arrived, tokens, grad_mid],
        lines,
        (BF16,),
        "first_gradient",
    )

    masters = (input_weight, output_weight, expand_weight, contract_weight)
    gradients = [part.values for part in (in_sum, expand_sum, contract_sum)]
    payload = all_sum(
        make_payload(
            scalars,
            gradients,
            first_sums,
            middle_sums,
            head_sums,
            hidden_sums,
            (input_piece_grad, contract_grad, output_grad),
        )
    )
    vector_grads = payload[:VECTOR_ROWS]
    grad_norm = jnp.sqrt(payload[VECTOR_ROWS, 0] + jnp.sum(vector_grads * vector_grads))
    shard_grads = (input_piece_grad, output_grad, expand_grad, contract_grad)
    firsts = (input_first, output_first, expand_first, contract_first)
    seconds = (input_second, output_second, expand_second, contract_second)
    squares = directions_step(payload, shard_grads, firsts, seconds, masters)
    first_new, second_new, directions = moments_step(
        payload,
        shard_grads,
        (*firsts, vector_state[0]),
        (*seconds, vector_state[1]),
        (*masters, vector_state[2]),
        squares,
    )
    squares = all_sum(squares)
    vector_news = cores_back(jnp.stack([first_new[4], second_new[4], directions[4]]))
    news, lows, norms = weights_step(squares, directions[:4], masters)
    results = []
    for position in range(4):
        results += [first_new[position], second_new[position], news[position], lows[position]]
    return (
        block_out,
        input_grad,
        grad_norm,
        norms[:2, :4].reshape(8),
        *results,
        vector_news[0],
        vector_news[1],
        vector_news[2],
    )


def solution(mesh):
    split = P(BOTH, None)
    return jax.shard_map(
        on_device,
        mesh=mesh,
        in_specs=(split, split, P("batch", None)) + (split,) * 4 + (P(),) + (split,) * 8 + (P(), P()),
        out_specs=(split, split, P(), P()) + (split,) * 16 + (P(), P(), P()),
        check_vma=False,
    )
```
